32 devices in a mesh: rep: 4 (over y, x), shard: 8 (over z, core).
Axes of the slice: x: 2, y: 2, z: 4, core: 2. Of those that a mesh axis runs over, the one named last changes fastest.
Arguments:
- byte_ids: int32 [128, 1024], P(('rep', 'shard')), may hold values from 0 to 258
- lengths: int32 [128], P(('rep', 'shard')), may hold values from 1 to 1024, 81920 in all
- target: int32 [128], P(('rep', 'shard')), may hold values from 0 to 127, as said below
- rel_bucket: int32 [1023], replicated, may hold values from 0 to 31
- cotangent: bfloat16 [128, 512, 768], P(('rep', 'shard')), may hold values from -6 to 6
- embed: bfloat16 [259, 768], P(None, 'shard'), may hold values from -6 to 6
- conv_w: bfloat16 [4, 768], P(None, 'shard'), may hold values from -3 to 3
- score_w: bfloat16 [768], P('shard'), may hold values from -0.59765625 to 0.59765625
- gain_attn: bfloat16 [768], P('shard'), may hold values from 0.5 to 1.5
- attn_in: bfloat16 [768, 2304], P('shard'), may hold values from -0.09375 to 0.09375
- attn_out: bfloat16 [768, 768], P('shard'), may hold values from -2.5 to 2.5
- gain_ffn: bfloat16 [768], P('shard'), may hold values from 0.5 to 1.5
- ffn_in: bfloat16 [768, 4096], P('shard'), may hold values from -0.21875 to 0.21875
- ffn_out: bfloat16 [2048, 768], P('shard'), may hold values from -0.125 to 0.125
- rel_table: bfloat16 [32, 12], P('shard'), may hold values from -4 to 4
Outputs:
- out: bfloat16 [128, 512, 768], P(('rep', 'shard'))
- input_grad: bfloat16 [128, 1024, 768], P(('rep', 'shard'))
- embed_grad: float32 [259, 768], P(None, 'shard')
- conv_grad: float32 [4, 768], P(None, 'shard')
- score_grad: float32 [768], P('shard')
- gain_attn_grad: float32 [768], P('shard')
- attn_in_grad: float32 [768, 2304], P('shard')
- attn_out_grad: float32 [768, 768], P('shard')
- gain_ffn_grad: float32 [768], P('shard')
- ffn_in_grad: float32 [768, 4096], P('shard')
- ffn_out_grad: float32 [2048, 768], P('shard')
- rel_table_grad: float32 [32, 12], P('shard')
The draws below stay inside these ranges and needn't reach their ends.
Inputs may be any that keep to these rules, and one draw needn't show every extreme that they name: target is a permutation. Sequence number (r * 8 + s) * 4 + k is dealt to slot target % 4 of device target // 4 (devices numbered rep-major); that device has the same shard index s, and the 4 sequences of one device go to 4 different devices. `lengths`: the longest sequence fills its slot.
All inputs are finite; a program needn't handle non-finite values. No bound on the sum of `lengths` on one device may be relied on, other than what follows from the above.
Results may differ from the reference program's by a relative error of at most 0.015.
Values may be sent and summed in bfloat16 or wider, within the bound.
A program may use at most 576 MiB of HBM per device.

```python
import math
import jax
import jax.numpy as jnp
import numpy as np
from jax import lax

D = 768
HEADS = 12
HEAD_DIM = 64
FF = 2048
VOCAB = 259
BUCKETS = 32
BLOCKS = 4
CONV = 4
MAXLEN = 1024
TOK = 512
SEQ_DEV = 4
REPLICAS = 4
SHARDS = 8
SEQS = 128


def column_perms(key, count, length):
    return jax.vmap(lambda subkey: jax.random.permutation(subkey, length))(jax.random.split(key, count))


def draw_target(key, part):
    first, second, third, fourth = jax.random.split(key, 4)
    spread = column_perms(first, SHARDS, REPLICAS)
    landing = column_perms(second, SHARDS, REPLICAS)
    offsets = column_perms(third, SHARDS, REPLICAS)[:, :SEQ_DEV]
    slot_order = column_perms(fourth, SHARDS * REPLICAS, SEQ_DEV).reshape(SHARDS, REPLICAS, SEQ_DEV)
    rep_index = jnp.arange(REPLICAS)[:, None, None]
    shard_index = jnp.arange(SHARDS)[None, :, None]
    seq_index = jnp.arange(SEQ_DEV)[None, None, :]
    turned = (spread[shard_index, rep_index] + offsets[shard_index, seq_index]) % REPLICAS
    dest_rep = landing[shard_index, turned]
    dest_slot = slot_order[shard_index, dest_rep, seq_index]
    return ((dest_rep * SHARDS + shard_index) * SEQ_DEV + dest_slot).reshape(-1).astype(jnp.int32)


def with_ends(values, stream_key, smallest, high):
    place = [jax.random.randint(jax.random.fold_in(stream_key, axis), (), 0, length) for axis, length in enumerate(values.shape)]
    longest = values.shape.index(max(values.shape))
    next_to = place[:longest] + [(place[longest] + 1) % values.shape[longest]] + place[longest + 1:]
    return values.at[tuple(place)].set(smallest).at[tuple(next_to)].set(high)


def steps_of(own_key, extent, cuts, smallest, high):
    def one(axis_at, shards_of):
        steps = jax.random.uniform(jax.random.fold_in(jax.random.fold_in(own_key, 6), axis_at), (shards_of,), jnp.float32, smallest / len(cuts), high / len(cuts))
        return jnp.repeat(jnp.exp(steps), extent[axis_at] // shards_of).reshape((-1,) + (1,) * (len(extent) - axis_at - 1))

    level = one(*cuts[0])
    for cut in cuts[1:]:
        level = level * one(*cut)
    return level


def profile(count, total, limit, skew):
    portions = [(1 << 20) // math.isqrt(grade ** skew) + 1 for grade in range(2, count + 1)]
    surplus, given = total - limit - (count - 1), [1] * (count - 1)
    while surplus > 0:
        movable = [i for i in range(count - 1) if given[i] < limit]
        pool, left = sum([portions[i] for i in movable]), surplus
        for i in movable:
            more = min(limit - given[i], max(1, left * portions[i] // pool), surplus)
            given[i] = given[i] + more
            surplus = surplus - more
    return np.array([limit] + given)


def ragged_sizes(key, number_of, total, bound, skew):
    if number_of == 2:
        one = jax.random.randint(key, (), max(1, total - bound), min(bound, total - 1) + 1)
        return jnp.stack([one, total - one])
    tallies = jnp.asarray(profile(number_of, total, bound, skew), jnp.int32)
    couples = (number_of - 1) // 2
    donor, sink = tallies[1:1 + 2 * couples:2], tallies[2:2 + 2 * couples:2]
    room = jnp.minimum(donor - 1, bound - sink)
    moved = jax.random.randint(jax.random.fold_in(key, 1), (couples,), 0, 1 << 20) % (room + 1)
    tallies = tallies.at[1:1 + 2 * couples:2].set(donor - moved).at[2:2 + 2 * couples:2].set(sink + moved)
    return tallies[jax.random.permutation(jax.random.fold_in(key, 2), number_of)]


def gaussian(rng, shape, deviation, reach, shards=(), kind=jnp.bfloat16):
    entries = deviation * jax.random.normal(rng, shape, jnp.float32)
    if shards:
        entries = entries * steps_of(rng, shape, shards, -0.22, 0.18)
    return jnp.clip(entries, -reach, reach).astype(kind)


def setup_inputs(seed: int = 0) -> dict:
    key_list = jax.random.split(jax.random.key(seed), 16)
    return {
        "byte_ids": with_ends(jax.random.randint(key_list[0], (SEQS, MAXLEN), 0, VOCAB), jax.random.fold_in(key_list[0], 1), 0, VOCAB - 1).astype(jnp.int32),
        "lengths": ragged_sizes(key_list[1], SEQS, SEQS * MAXLEN * 5 // 8, MAXLEN, 2).astype(jnp.int32),
        "target": draw_target(jax.random.fold_in(key_list[15], 71), 0),
        "rel_bucket": with_ends(jax.random.randint(key_list[3], (2 * TOK - 1,), 0, BUCKETS), jax.random.fold_in(key_list[3], 1), 0, BUCKETS - 1).astype(jnp.int32),
        "cotangent": gaussian(key_list[4], (SEQS, TOK, D), 1.0, 6.0, ((0, 32),)),
        "embed": gaussian(key_list[5], (VOCAB, D), 1.0, 6.0, ((1, 8),)),
        "conv_w": gaussian(key_list[6], (CONV, D), 0.5, 3.0, ((1, 8),)),
        "score_w": gaussian(key_list[7], (D,), 0.1, 0.59765625, ((0, 8),)),
        "gain_attn": jnp.clip(1.0 + 0.1 * jax.random.normal(key_list[8], (D,), jnp.float32), 0.5, 1.5).astype(jnp.bfloat16),
        "attn_in": gaussian(key_list[9], (D, 3 * D), (5 * D) ** -0.5, 0.09375, ((0, 8),)),
        "attn_out": gaussian(key_list[10], (D, D), (max(D // 128, 1)) ** -0.5, 2.5, ((0, 8),)),
        "gain_ffn": jnp.clip(1.0 + 0.1 * jax.random.normal(key_list[11], (D,), jnp.float32), 0.5, 1.5).astype(jnp.bfloat16),
        "ffn_in": gaussian(key_list[12], (D, 2 * FF), D ** -0.5, 0.21875, ((0, 8),)),
        "ffn_out": gaussian(key_list[13], (FF, D), FF ** -0.5, 0.125, ((0, 8),)),
        "rel_table": gaussian(key_list[14], (BUCKETS, HEADS), 1.0, 4.0, ((0, 8),)),
    }


epsilon = 1e-06
masked_score = -1000000000.0

@jax.custom_vjp
def low(v):
    return lax.optimization_barrier(v.astype(jnp.bfloat16)).astype(jnp.float32)

@jax.custom_vjp
def low_back(v):
    return v

def low_keep(v):
    return (low(v), None)

def low_pass(kept, grad):
    return (grad,)

def back_keep(v):
    return (v, None)

def back_low(kept, grad):
    return (low(grad),)
low.defvjp(low_keep, low_pass)
low_back.defvjp(back_keep, back_low)

def gbst_pool(embedded, conv_w, score_w, byte_mask):
    groups, length, features = embedded.shape
    masked = embedded * byte_mask[..., None]
    padded = jnp.pad(masked, ((0, 0), (0, CONV - 1), (0, 0)))
    convolved = conv_w[0] * padded[:, 0:length]
    for offset in range(1, CONV):
        convolved = convolved + conv_w[offset] * padded[:, offset:offset + length]
    block_means = []
    for block_size in range(1, BLOCKS + 1):
        block_total = -(-length // block_size)
        extra = block_total * block_size - length
        block_sums = jnp.pad(convolved, ((0, 0), (0, extra), (0, 0))).reshape(groups, block_total, block_size, features).sum(axis=2)
        block_counts = jnp.pad(byte_mask, ((0, 0), (0, extra))).reshape(groups, block_total, block_size).sum(axis=2)
        block_mean = block_sums / jnp.maximum(block_counts, 1.0)[..., None]
        block_means.append(jnp.repeat(block_mean, block_size, axis=1)[:, :length])
    size_score = jnp.stack([lax.optimization_barrier(jnp.sum(block_mean * score_w, axis=-1)) for block_mean in block_means], axis=-1)
    size_weight = jax.nn.softmax(size_score, axis=-1)
    mixture = size_weight[..., 0:1] * block_means[0]
    for block_index in range(1, BLOCKS):
        mixture = mixture + size_weight[..., block_index:block_index + 1] * block_means[block_index]
    pair_rows = mixture.reshape(groups, length // 2, 2, features)
    pair_mask = byte_mask.reshape(groups, length // 2, 2)
    return lax.optimization_barrier(jnp.sum(pair_rows * pair_mask[..., None], axis=2)) / jnp.maximum(lax.optimization_barrier(jnp.sum(pair_mask, axis=2)), 1.0)[..., None]

def rms_norm(values, gain):
    return values * lax.rsqrt(lax.optimization_barrier(jnp.mean(values * values, axis=-1, keepdims=True)) + epsilon) * gain

def relative_bias(table, rel_bucket, tokens):
    bucket_hits = (jnp.arange(table.shape[0])[:, None] == rel_bucket[None, :]).astype(jnp.float32)
    per_distance = lax.dot_general(table, bucket_hits, (((0,), (0,)), ((), ())), precision=lax.Precision.HIGHEST, preferred_element_type=jnp.float32)
    span = 2 * tokens - 1
    copies = jnp.tile(per_distance, (1, tokens))
    window = lax.slice_in_dim(copies, tokens - 1, tokens - 1 + tokens * (span - 1), axis=1)
    return window.reshape(per_distance.shape[0], tokens, span - 1)[:, :, :tokens]

def gated_gelu(gate, upward):
    return jax.nn.gelu(gate, approximate=True) * upward

def highest(left, right):
    return jnp.dot(left, right, precision=lax.Precision.HIGHEST, preferred_element_type=jnp.float32)

def block_forward(embedded, params, byte_mask, token_mask, rel_bucket):
    conv_f, score_f, gain_one, weight_in, weight_out, gain_two, ffn_first, ffn_second, table = params
    groups = embedded.shape[0]
    hidden = gbst_pool(low_back(embedded), conv_f, score_f, byte_mask)
    normed = low(rms_norm(hidden, gain_one))
    qkv = low_back(low(highest(normed, weight_in)))
    query = qkv[..., 0:D].reshape(groups, TOK, HEADS, HEAD_DIM)
    key_rows = qkv[..., D:2 * D].reshape(groups, TOK, HEADS, HEAD_DIM)
    value = qkv[..., 2 * D:3 * D].reshape(groups, TOK, HEADS, HEAD_DIM)
    raw = low_back(jnp.einsum('gqhe,gkhe->ghqk', query, key_rows, precision=lax.Precision.HIGHEST))
    bias = relative_bias(table, rel_bucket, TOK)
    scores = jnp.where(token_mask[:, None, None, :] > 0, raw + bias[None], masked_score)
    prob = low(jax.nn.softmax(scores, axis=-1))
    context = low_back(low(jnp.einsum('ghqk,gkhe->gqhe', prob, value, precision=lax.Precision.HIGHEST))).reshape(groups, TOK, D)
    attended = hidden + low_back(highest(context, weight_out))
    ffn_normed = low(rms_norm(attended, gain_two))
    gate_up = low_back(highest(ffn_normed, ffn_first))
    activated = low(gated_gelu(gate_up[..., :FF], gate_up[..., FF:]))
    return (attended + highest(activated, ffn_second)) * token_mask[..., None]

def reference(byte_ids, lengths, target, rel_bucket, cotangent, embed, conv_w, score_w, gain_attn, attn_in, attn_out, gain_ffn, ffn_in, ffn_out, rel_table):
    params = tuple((weight.astype(jnp.float32) for weight in (conv_w, score_w, gain_attn, attn_in, attn_out, gain_ffn, ffn_in, ffn_out, rel_table)))
    embed_f = embed.astype(jnp.float32)
    positions = jnp.arange(MAXLEN)
    cot_seq = cotangent[target]
    group_total = SEQS // SEQ_DEV
    inputs = (byte_ids.reshape(group_total, SEQ_DEV, MAXLEN), lengths.reshape(group_total, SEQ_DEV), cot_seq.reshape(group_total, SEQ_DEV, TOK, D))

    def group_step(totals, pieces):
        group_ids, group_lengths, group_cot = pieces
        byte_mask = (positions[None, :] < group_lengths[:, None]).astype(jnp.float32)
        token_mask = byte_mask[:, ::2]

        def lookup(table):
            return table[group_ids] * byte_mask[..., None]

        def layer(embedded, weights):
            return block_forward(embedded, weights, byte_mask, token_mask, rel_bucket)
        embedded, lookup_back = jax.vjp(lookup, embed_f)
        result, pull = jax.vjp(layer, embedded, params)
        d_embedded, d_params = pull(group_cot.astype(jnp.float32))
        d_embed, = lookup_back(d_embedded)
        totals = jax.tree.map(jnp.add, totals, (d_embed,) + tuple(d_params))
        return (totals, (result.astype(jnp.bfloat16), d_embedded.astype(jnp.bfloat16)))
    zeros = (jnp.zeros_like(embed_f),) + tuple((jnp.zeros_like(weight) for weight in params))
    totals, (results, d_inputs) = lax.scan(group_step, zeros, inputs)
    return (results.reshape(SEQS, TOK, D), d_inputs.reshape(SEQS, MAXLEN, D), totals[0], totals[1], totals[2], totals[3], totals[4], totals[5], totals[6], totals[7], totals[8], totals[9])
```

```python
import jax
import jax.numpy as jnp
from jax import lax
from jax.experimental import pallas as pl
from jax.experimental.pallas import tpu as pltpu
from jax.sharding import PartitionSpec as P

D = 768
VOCAB = 259
VPAD = 384
VROWS = 272
MAXLEN = 1024
TOK = 512
LANES = 128
QN = 88
R = 12
P_ROWS = QN * R
T_ROWS = 528
LT = D // LANES
epsilon = 1e-06
f32 = jnp.float32
bf16 = jnp.bfloat16


def lane_iota(rows):
    return lax.broadcasted_iota(jnp.int32, (rows, LANES), 1)


def group_matrix(b):
    row = lax.broadcasted_iota(jnp.int32, (LANES, LANES), 0)
    col = lax.broadcasted_iota(jnp.int32, (LANES, LANES), 1)
    return jnp.where((row // b == col // b) & (row < R) & (col < R), 1.0, 0.0).astype(f32)


def exact_dot(a, b):
    return jnp.dot(a, b, precision=lax.Precision.HIGHEST, preferred_element_type=f32)


def place(columns, rows):
    lanes = lane_iota(rows)
    out = jnp.zeros((rows, LANES), f32)
    for r, column in enumerate(columns):
        out = jnp.where(lanes == r, column, out)
    return out


def gbst_masks(length):
    q = lax.broadcasted_iota(jnp.int32, (QN, LANES), 0)
    r = lax.broadcasted_iota(jnp.int32, (QN, LANES), 1)
    mask = jnp.where((q * R + r < length) & (r < R), 1.0, 0.0).astype(f32)
    inverse = [1.0 / jnp.maximum(exact_dot(mask, group_matrix(b)), 1.0) for b in (2, 3, 4)]
    pair = exact_dot(mask, group_matrix(2))
    alpha = mask / jnp.maximum(pair, 1.0)
    return mask, inverse, alpha


def gbst_weights(s1, inverse):
    sizes = [s1] + [exact_dot(s1, group_matrix(b)) * inv for b, inv in zip((2, 3, 4), inverse)]
    top = jnp.maximum(jnp.maximum(sizes[0], sizes[1]), jnp.maximum(sizes[2], sizes[3]))
    parts = [jnp.exp(s - top) for s in sizes]
    total = parts[0] + parts[1] + parts[2] + parts[3]
    return [p / total for p in parts]


def gbst_coefs(weights, inverse, alpha):
    a1 = weights[0] * alpha
    a2 = weights[1] * alpha * inverse[0]
    a3 = weights[2] * alpha * inverse[1]
    a4 = weights[3] * alpha * inverse[2]
    pair = group_matrix(2)
    a4s = exact_dot(a4, pair)
    own = a1 + exact_dot(a2, pair) + a4s
    return own, a3, a4s


def column(x, r):
    return jnp.broadcast_to(x[:, r : r + 1], (x.shape[0], LANES))


def hits_of(ids_col):
    lanes = lax.broadcasted_iota(jnp.int32, (P_ROWS, VPAD), 1)
    return jnp.where(ids_col == lanes, 1.0, 0.0).astype(bf16)


def load_e(e_ref, r, lt):
    lanes = pl.ds(lt * LANES, LANES)
    if r < R:
        return e_ref[pl.ds(r * QN, QN), lanes]
    return e_ref[pl.ds((r - R) * QN + 1, QN), lanes]


def gbst_fwd_kernel(len_ref, ids_ref, table_ref, conv_ref, vec_ref, hidden_ref, normed_ref, c_ref, w_ref, e_ref, hid_ref, s_ref, k_ref):
    length = len_ref[pl.program_id(0)]
    hits = hits_of(ids_ref[0])
    e_ref[pl.ds(0, P_ROWS), :] = jnp.dot(hits, table_ref[...], preferred_element_type=f32)
    e_ref[pl.ds(P_ROWS, 8), :] = jnp.zeros((8, D), f32)
    for lt in range(LT):
        lanes = pl.ds(lt * LANES, LANES)
        taps = [jnp.broadcast_to(conv_ref[j : j + 1, lanes], (QN, LANES)) for j in range(4)]
        sw = jnp.broadcast_to(vec_ref[0:1, lanes], (QN, LANES))
        for r in range(R):
            c = taps[0] * load_e(e_ref, r, lt)
            for j in range(1, 4):
                c = c + taps[j] * load_e(e_ref, r + j, lt)
            c_ref[0, pl.ds(r * QN, QN), lanes] = c
            part = c * sw
            rows = pl.ds(r * QN, QN)
            s_ref[rows, :] = part if lt == 0 else s_ref[rows, :] + part
    s1 = place([jnp.sum(s_ref[pl.ds(r * QN, QN), :], axis=1, keepdims=True) for r in range(R)], QN)
    mask, inverse, alpha = gbst_masks(length)
    weights = gbst_weights(s1, inverse)
    for b in range(4):
        w_ref[0, b] = weights[b]
    own, a3, a4s = gbst_coefs(weights, inverse, alpha)
    n = 0
    for r in range(R):
        k_ref[r] = column(own, r)
        k_ref[R + r] = column(a3, r)
    for k in range(6):
        k_ref[2 * R + k] = column(a4s, 2 * k)
    for lt in range(LT):
        lanes = pl.ds(lt * LANES, LANES)
        for half in range(2):
            c = [c_ref[0, pl.ds((half * 6 + r) * QN, QN), lanes] for r in range(6)]
            base = half * 6
            s3 = [c[0] + c[1] + c[2], c[3] + c[4] + c[5]]
            for k in range(3):
                tok = half * 3 + k
                other = tok ^ 1
                rows = pl.ds(2 * other * QN, QN)
                rows1 = pl.ds((2 * other + 1) * QN, QN)
                s2 = c_ref[0, rows, lanes] + c_ref[0, rows1, lanes]
                h = k_ref[2 * tok] * c[2 * k] + k_ref[2 * tok + 1] * c[2 * k + 1] + k_ref[2 * R + tok] * s2
                if k == 1:
                    h = h + k_ref[R + 2 * tok] * s3[0] + k_ref[R + 2 * tok + 1] * s3[1]
                else:
                    h = h + (k_ref[R + 2 * tok] + k_ref[R + 2 * tok + 1]) * s3[0 if k == 0 else 1]
                hid_ref[lt, pl.ds(tok, QN, stride=6), :] = h
    total = jnp.zeros((TOK, LANES), f32)
    for lt in range(LT):
        x = hid_ref[lt, 0:TOK, :]
        total = total + x * x
    scale = lax.rsqrt(jnp.sum(total, axis=1, keepdims=True) * (1.0 / D) + epsilon)
    for lt in range(LT):
        lanes = pl.ds(lt * LANES, LANES)
        x = hid_ref[lt, 0:TOK, :]
        hidden_ref[:, lanes] = x
        normed_ref[:, lanes] = (x * scale * vec_ref[1:2, lanes]).astype(bf16)


def gbst_forward(lengths, ids_col, table, conv_w, vecs):
    seqs = ids_col.shape[0]
    grid_spec = pltpu.PrefetchScalarGridSpec(
        num_scalar_prefetch=1,
        grid=(seqs,),
        in_specs=[
            pl.BlockSpec((1, P_ROWS, 1), lambda s, n: (s, 0, 0)),
            pl.BlockSpec((VPAD, D), lambda s, n: (0, 0)),
            pl.BlockSpec((4, D), lambda s, n: (0, 0)),
            pl.BlockSpec((3, D), lambda s, n: (0, 0)),
        ],
        out_specs=[
            pl.BlockSpec((TOK, D), lambda s, n: (s, 0)),
            pl.BlockSpec((TOK, D), lambda s, n: (s, 0)),
            pl.BlockSpec((1, P_ROWS, D), lambda s, n: (s, 0, 0)),
            pl.BlockSpec((1, 4, QN, LANES), lambda s, n: (s, 0, 0, 0)),
        ],
        scratch_shapes=[
            pltpu.VMEM((P_ROWS + 8, D), f32),
            pltpu.VMEM((LT, T_ROWS, LANES), f32),
            pltpu.VMEM((P_ROWS, LANES), f32),
            pltpu.VMEM((2 * R + 6, QN, LANES), f32),
        ],
    )
    return pl.pallas_call(
        gbst_fwd_kernel,
        grid_spec=grid_spec,
        out_shape=[
            jax.ShapeDtypeStruct((seqs * TOK, D), f32),
            jax.ShapeDtypeStruct((seqs * TOK, D), bf16),
            jax.ShapeDtypeStruct((seqs, P_ROWS, D), f32),
            jax.ShapeDtypeStruct((seqs, 4, QN, LANES), f32),
        ],
        compiler_params=pltpu.CompilerParams(vmem_limit_bytes=48 << 20),
        name="gbst_forward",
    )(lengths, ids_col, table, conv_w, vecs)


def gbst_bwd_kernel(len_ref, ids_ref, row_ref, table_ref, conv_ref, vec_ref, dh_ref, c_ref, w_ref,
                    ig_ref, ge_ref, gc_ref, gs_ref, e_ref, dt_ref, dc_ref, s_ref, k_ref, igs_ref):
    seq = pl.program_id(0)
    length = len_ref[seq]

    @pl.when(seq == 0)
    def _():
        ge_ref[...] = jnp.zeros_like(ge_ref)
        gc_ref[...] = jnp.zeros_like(gc_ref)
        gs_ref[...] = jnp.zeros_like(gs_ref)

    hits = hits_of(ids_ref[0])
    e_ref[pl.ds(0, P_ROWS), :] = jnp.dot(hits, table_ref[...], preferred_element_type=f32)
    e_ref[pl.ds(P_ROWS, 8), :] = jnp.zeros((8, D), f32)
    for lt in range(LT):
        dt_ref[lt, 0:TOK, :] = dh_ref[:, pl.ds(lt * LANES, LANES)]
        dt_ref[lt, TOK:T_ROWS, :] = jnp.zeros((T_ROWS - TOK, LANES), f32)
    for lt in range(LT):
        lanes = pl.ds(lt * LANES, LANES)
        for half in range(2):
            c = [c_ref[0, pl.ds((half * 6 + r) * QN, QN), lanes] for r in range(6)]
            s3 = [c[0] + c[1] + c[2], c[3] + c[4] + c[5]]
            for k in range(3):
                tok = half * 3 + k
                other = tok ^ 1
                dh = dt_ref[lt, pl.ds(tok, QN, stride=6), :]
                s2 = c_ref[0, pl.ds(2 * other * QN, QN), lanes] + c_ref[0, pl.ds((2 * other + 1) * QN, QN), lanes]
                parts = [
                    (2 * tok, dh * c[2 * k]),
                    (2 * tok + 1, dh * c[2 * k + 1]),
                    (2 * R + tok, dh * s2),
                    (R + 2 * tok, dh * s3[0 if k < 2 else 1]),
                ]
                if k == 1:
                    parts.append((R + 2 * tok + 1, dh * s3[1]))
                for slot, part in parts:
                    s_ref[slot] = part if lt == 0 else s_ref[slot] + part

    def total(slot):
        return jnp.sum(s_ref[slot], axis=1, keepdims=True)

    d1, d3, dother = [], [], []
    for tok in range(6):
        d1 += [total(2 * tok), total(2 * tok + 1)]
        first = total(R + 2 * tok)
        d3 += [first, total(R + 2 * tok + 1) if tok % 3 == 1 else first]
        o = total(2 * R + tok)
        dother += [o, o]
    d1, d3, dother = place(d1, QN), place(d3, QN), place(dother, QN)
    mask, inverse, alpha = gbst_masks(length)
    weights = [w_ref[0, b] for b in range(4)]
    d2 = exact_dot(d1, group_matrix(2))
    g = [alpha * d1, alpha * d2 * inverse[0], alpha * d3 * inverse[1], alpha * (d2 + dother) * inverse[2]]
    mean = weights[0] * g[0] + weights[1] * g[1] + weights[2] * g[2] + weights[3] * g[3]
    d_size = [w * (x - mean) for w, x in zip(weights, g)]
    coef = d_size[0]
    for b, inv in zip((2, 3, 4), inverse):
        coef = coef + exact_dot(d_size[b - 1] * inv, group_matrix(b))
    own, a3, a4s = gbst_coefs(weights, inverse, alpha)
    for r in range(R):
        k_ref[r] = column(own, r)
        k_ref[R + r] = column(a3, r)
        k_ref[2 * R + r] = column(coef, r)
        k_ref[3 * R + r] = column(mask, r)
    for k in range(6):
        k_ref[4 * R + k] = column(a4s, 2 * k)

    for lt in range(LT):
        lanes = pl.ds(lt * LANES, LANES)
        taps = [jnp.broadcast_to(conv_ref[j : j + 1, lanes], (QN, LANES)) for j in range(4)]
        sw = jnp.broadcast_to(vec_ref[0:1, lanes], (QN, LANES))
        gs = jnp.zeros((QN, LANES), f32)
        gc = [jnp.zeros((QN, LANES), f32) for _ in range(4)]
        for half in range(2):
            dh = [dt_ref[lt, pl.ds(half * 3 + k, QN, stride=6), :] for k in range(3)]
            a = R + half * 6
            t3 = [
                (k_ref[a] + k_ref[a + 1]) * dh[0] + k_ref[a + 2] * dh[1],
                k_ref[a + 3] * dh[1] + (k_ref[a + 4] + k_ref[a + 5]) * dh[2],
            ]
            for k in range(3):
                tok = half * 3 + k
                other = tok ^ 1
                dother_h = dt_ref[lt, pl.ds(other, QN, stride=6), :]
                cross = k_ref[4 * R + other] * dother_h
                for e in range(2):
                    r = 2 * tok + e
                    cf = k_ref[2 * R + r]
                    dc = k_ref[r] * dh[k] + cross + t3[(r % 6) // 3] + cf * sw
                    gs = gs + cf * c_ref[0, pl.ds(r * QN, QN), lanes]
                    dc_ref[r, pl.ds(8, QN), :] = dc
                    for j in range(4):
                        gc[j] = gc[j] + dc * load_e(e_ref, r + j, lt)
        gs_ref[0:1, lanes] += jnp.sum(gs, axis=0, keepdims=True)
        for j in range(4):
            gc_ref[j : j + 1, lanes] += jnp.sum(gc[j], axis=0, keepdims=True)
        for r in range(R):
            dc_ref[r, 0:8, :] = jnp.zeros((8, LANES), f32)
        for r in range(R):
            x = taps[0] * dc_ref[r, pl.ds(8, QN), :]
            for j in range(1, 4):
                back = dc_ref[r - j, pl.ds(8, QN), :] if r >= j else dc_ref[r - j + R, pl.ds(7, QN), :]
                x = x + taps[j] * back
            igs_ref[lt, pl.ds(r, QN, stride=R), :] = x * k_ref[3 * R + r]
    for lt in range(LT):
        lanes = pl.ds(lt * LANES, LANES)
        ig_ref[0, :, lanes] = igs_ref[lt, 0:MAXLEN, :].astype(bf16)
    vocab = lax.broadcasted_iota(jnp.int32, (VROWS, MAXLEN), 0)
    row_hits = jnp.where(vocab == row_ref[0], 1.0, 0.0).astype(bf16)
    ge_ref[...] += jnp.dot(row_hits, ig_ref[0], preferred_element_type=f32)


def gbst_backward(lengths, ids_col, ids_row, table, conv_w, vecs, d_hidden, c, w):
    seqs = ids_col.shape[0]
    grid_spec = pltpu.PrefetchScalarGridSpec(
        num_scalar_prefetch=1,
        grid=(seqs,),
        in_specs=[
            pl.BlockSpec((1, P_ROWS, 1), lambda s, n: (s, 0, 0)),
            pl.BlockSpec((1, 1, MAXLEN), lambda s, n: (s, 0, 0)),
            pl.BlockSpec((VPAD, D), lambda s, n: (0, 0)),
            pl.BlockSpec((4, D), lambda s, n: (0, 0)),
            pl.BlockSpec((3, D), lambda s, n: (0, 0)),
            pl.BlockSpec((TOK, D), lambda s, n: (s, 0)),
            pl.BlockSpec((1, P_ROWS, D), lambda s, n: (s, 0, 0)),
            pl.BlockSpec((1, 4, QN, LANES), lambda s, n: (s, 0, 0, 0)),
        ],
        out_specs=[
            pl.BlockSpec((1, MAXLEN, D), lambda s, n: (s, 0, 0)),
            pl.BlockSpec((VROWS, D), lambda s, n: (0, 0)),
            pl.BlockSpec((4, D), lambda s, n: (0, 0)),
            pl.BlockSpec((1, D), lambda s, n: (0, 0)),
        ],
        scratch_shapes=[
            pltpu.VMEM((P_ROWS + 8, D), f32),
            pltpu.VMEM((LT, T_ROWS, LANES), f32),
            pltpu.VMEM((R, QN + 8, LANES), f32),
            pltpu.VMEM((2 * R + 6, QN, LANES), f32),
            pltpu.VMEM((4 * R + 6, QN, LANES), f32),
            pltpu.VMEM((LT, P_ROWS, LANES), f32),
        ],
    )
    return pl.pallas_call(
        gbst_bwd_kernel,
        grid_spec=grid_spec,
        out_shape=[
            jax.ShapeDtypeStruct((seqs, MAXLEN, D), bf16),
            jax.ShapeDtypeStruct((VROWS, D), f32),
            jax.ShapeDtypeStruct((4, D), f32),
            jax.ShapeDtypeStruct((1, D), f32),
        ],
        compiler_params=pltpu.CompilerParams(vmem_limit_bytes=56 << 20),
        name="gbst_backward",
    )(lengths, ids_col, ids_row, table, conv_w, vecs, d_hidden, c, w)


def byte_columns(byte_ids, lengths):
    seqs = byte_ids.shape[0]
    live = jnp.arange(MAXLEN)[None, :] < lengths[:, None]
    ids = jnp.where(live, byte_ids, -1)
    wide = jnp.pad(ids, ((0, 0), (0, P_ROWS - MAXLEN)), constant_values=-1)
    ids_col = wide.reshape(seqs, QN, R).transpose(0, 2, 1).reshape(seqs, P_ROWS, 1)
    return ids_col, ids.reshape(seqs, 1, MAXLEN)


HEADS = 12
HD = 64
BUCKETS = 32
SPAN = 1024
PAIRS = HEADS // 2
QC = 256
dead_score = -1e9


def nt(a, b):
    return lax.dot_general(a, b, (((1,), (1,)), ((), ())), preferred_element_type=f32)


def nn(a, b):
    return jnp.dot(a, b, preferred_element_type=f32)


def bucket_rows(rel_bucket):
    back = jnp.pad(rel_bucket[::-1], (8, 0))
    rows = [
        jnp.concatenate([back[8 + TOK - 1 - s : 8 + 2 * TOK - 1 - s], back[7 - s : 7 - s + TOK]])
        for s in range(8)
    ]
    return jnp.concatenate(rows)


def bucket_hits(rel_bucket):
    return jnp.arange(BUCKETS)[:, None] == bucket_rows(rel_bucket)[None, :]


def build_bias(z_ref, bt_ref):
    for h in range(2):
        z = z_ref[h]
        for g in range(TOK // 8):
            bt_ref[h, pl.ds(8 * g, 8), :] = (z if g == 0 else pltpu.roll(z, 8 * g, 1))[:, :TOK]


def head_parts(k, q, length, h):
    lanes = lax.broadcasted_iota(jnp.int32, (TOK, LANES), 1)
    rows = lax.broadcasted_iota(jnp.int32, (TOK, LANES), 0)
    spare = HD * (1 - h)
    own = (lanes < HD) if h == 0 else (lanes >= HD)
    dead = jnp.where(2 * rows < length, 0.0, dead_score)
    kf = jnp.where(own, k.astype(f32), jnp.where(lanes == spare, dead, 0.0)).astype(bf16)
    qf = jnp.where(lanes == spare, 1.0, q.astype(f32)).astype(bf16)
    return kf, qf


def attn_fwd_kernel(len_ref, q_ref, k_ref, v_ref, z_ref, ctx_ref, lse_ref, bt_ref):
    length = len_ref[pl.program_id(1)]

    @pl.when(pl.program_id(1) == 0)
    def _():
        build_bias(z_ref, bt_ref)

    q, k, v = q_ref[...], k_ref[...], v_ref[...]
    vt = v.astype(f32).T.astype(bf16)
    outs = []
    for h in range(2):
        kf, qf = head_parts(k, q, length, h)
        pieces = []
        for c in range(TOK // QC):
            cols = slice(c * QC, (c + 1) * QC)
            s = nt(kf, qf[cols]) + bt_ref[h, :, cols]
            top = jnp.max(s, axis=0, keepdims=True)
            p = jnp.exp(s - top)
            total = jnp.sum(p, axis=0, keepdims=True)
            lse_ref[0, 0, h : h + 1, cols] = top + jnp.log(total)
            pieces.append(nn(vt[h * HD : (h + 1) * HD], p.astype(bf16)) * (1.0 / total))
        outs.append(jnp.concatenate(pieces, axis=1))
    ctx_ref[...] = jnp.concatenate(outs, axis=0).T.astype(bf16)


def attn_forward(lengths, qkv, z):
    seqs = qkv.shape[0] // TOK
    spec = lambda off: pl.BlockSpec((TOK, LANES), lambda hp, s, n: (s, off + hp))
    return pl.pallas_call(
        attn_fwd_kernel,
        grid_spec=pltpu.PrefetchScalarGridSpec(
            num_scalar_prefetch=1,
            grid=(PAIRS, seqs),
            in_specs=[spec(0), spec(PAIRS), spec(2 * PAIRS), pl.BlockSpec((2, 8, SPAN), lambda hp, s, n: (hp, 0, 0))],
            out_specs=[spec(0), pl.BlockSpec((1, 1, 2, TOK), lambda hp, s, n: (hp, s, 0, 0))],
            scratch_shapes=[pltpu.VMEM((2, TOK, TOK), f32)],
        ),
        out_shape=[
            jax.ShapeDtypeStruct((seqs * TOK, D), bf16),
            jax.ShapeDtypeStruct((PAIRS, seqs, 2, TOK), f32),
        ],
        compiler_params=pltpu.CompilerParams(vmem_limit_bytes=40 << 20),
        name="attn_forward",
    )(lengths, qkv, qkv, qkv, z)


def attn_bwd_kernel(len_ref, q_ref, k_ref, v_ref, do_ref, o_ref, lse_ref, z_ref, dqkv_ref, gz_ref, bt_ref, g_ref):
    s_id = pl.program_id(1)
    length = len_ref[s_id]

    @pl.when(s_id == 0)
    def _():
        build_bias(z_ref, bt_ref)
        g_ref[...] = jnp.zeros_like(g_ref)

    q, k, v, do = q_ref[...], k_ref[...], v_ref[...], do_ref[...]
    kt = k.astype(f32).T.astype(bf16)
    lanes8 = lax.broadcasted_iota(jnp.int32, (8, LANES), 1)
    rows8 = lax.broadcasted_iota(jnp.int32, (8, LANES), 0)
    pick = jnp.where(lanes8 // HD == rows8, 1.0, 0.0).astype(f32)
    delta = lax.dot_general(
        pick, do.astype(f32) * o_ref[...].astype(f32), (((1,), (1,)), ((), ())),
        precision=lax.Precision.HIGHEST, preferred_element_type=f32)
    lanes = lax.broadcasted_iota(jnp.int32, (TOK, LANES), 1)
    dq_t, dk, dv = [], [], []
    for h in range(2):
        kf, qf = head_parts(k, q, length, h)
        own = (lanes < HD) if h == 0 else (lanes >= HD)
        vf = jnp.where(own, v.astype(f32), 0.0).astype(bf16)
        pieces, dk_h, dv_h = [], None, None
        for c in range(TOK // QC):
            cols = slice(c * QC, (c + 1) * QC)
            s = nt(kf, qf[cols]) + bt_ref[h, :, cols]
            p = jnp.exp(s - lse_ref[0, 0, h : h + 1, cols])
            ds = p * (nt(vf, do[cols]) - delta[h : h + 1, cols])
            g_ref[h, :, cols] += ds
            low = ds.astype(bf16)
            dv_c = nn(p.astype(bf16), do[cols])
            dk_c = nn(low, q[cols])
            dv_h = dv_c if dv_h is None else dv_h + dv_c
            dk_h = dk_c if dk_h is None else dk_h + dk_c
            pieces.append(nn(kt[h * HD : (h + 1) * HD], low))
        dq_t.append(jnp.concatenate(pieces, axis=1))
        dk.append(dk_h)
        dv.append(dv_h)
    dqkv_ref[0] = jnp.concatenate(dq_t, axis=0).T.astype(bf16)
    dqkv_ref[1] = jnp.where(lanes < HD, dk[0], dk[1]).astype(bf16)
    dqkv_ref[2] = jnp.where(lanes < HD, dv[0], dv[1]).astype(bf16)

    @pl.when(s_id == pl.num_programs(1) - 1)
    def _():
        zero = jnp.zeros((8, SPAN - TOK), f32)
        for h in range(2):
            total = jnp.zeros((8, SPAN), f32)
            for g in range(TOK // 8):
                piece = jnp.concatenate([g_ref[h, pl.ds(8 * g, 8), :], zero], axis=1)
                total = total + (piece if g == 0 else pltpu.roll(piece, SPAN - 8 * g, 1))
            gz_ref[h] = total


def attn_backward(lengths, qkv, d_ctx, ctx, lse, z):
    seqs = qkv.shape[0] // TOK
    spec = lambda off: pl.BlockSpec((TOK, LANES), lambda hp, s, n: (s, off + hp))
    return pl.pallas_call(
        attn_bwd_kernel,
        grid_spec=pltpu.PrefetchScalarGridSpec(
            num_scalar_prefetch=1,
            grid=(PAIRS, seqs),
            in_specs=[
                spec(0), spec(PAIRS), spec(2 * PAIRS), spec(0), spec(0),
                pl.BlockSpec((1, 1, 2, TOK), lambda hp, s, n: (hp, s, 0, 0)),
                pl.BlockSpec((2, 8, SPAN), lambda hp, s, n: (hp, 0, 0)),
            ],
            out_specs=[
                pl.BlockSpec((3, TOK, LANES), lambda hp, s, n: (0, s, hp)),
                pl.BlockSpec((2, 8, SPAN), lambda hp, s, n: (hp, 0, 0)),
            ],
            scratch_shapes=[pltpu.VMEM((2, TOK, TOK), f32), pltpu.VMEM((2, TOK, TOK), f32)],
        ),
        out_shape=[
            jax.ShapeDtypeStruct((3, seqs * TOK, D), bf16),
            jax.ShapeDtypeStruct((HEADS, 8, SPAN), f32),
        ],
        compiler_params=pltpu.CompilerParams(vmem_limit_bytes=48 << 20),
        name="attn_backward",
    )(lengths, qkv, qkv, qkv, d_ctx, ctx, lse, z)


FF = 2048
FT = 256
RC = 512


def row_mask(length):
    rows = lax.broadcasted_iota(jnp.int32, (TOK, 1), 0)
    return jnp.where(2 * rows < length, 1.0, 0.0).astype(f32)


def rms_scale(x):
    return lax.rsqrt(jnp.sum(x * x, axis=1, keepdims=True) * (1.0 / D) + epsilon)


def post_kernel(ctx_ref, w_ref, hidden_ref, vec_ref, att_ref, low_ref):
    att = hidden_ref[...] + nn(ctx_ref[...], w_ref[...])
    att_ref[...] = att
    low_ref[...] = (att * rms_scale(att) * vec_ref[2:3, :]).astype(bf16)


def rows_spec(width=D):
    return pl.BlockSpec((TOK, width), lambda s, *n: (s, 0))


def whole(*shape):
    return pl.BlockSpec(shape, lambda s, *n: (0,) * len(shape))


def post_attention(ctx, attn_out, hidden, vecs):
    rows = ctx.shape[0]
    return pl.pallas_call(
        post_kernel,
        grid=(rows // TOK,),
        in_specs=[rows_spec(), whole(D, D), rows_spec(), whole(3, D)],
        out_specs=[rows_spec(), rows_spec()],
        out_shape=[jax.ShapeDtypeStruct((rows, D), f32), jax.ShapeDtypeStruct((rows, D), bf16)],
        compiler_params=pltpu.CompilerParams(vmem_limit_bytes=32 << 20),
        name="post_attention",
    )(ctx, attn_out, hidden, vecs)


def gelu_parts(v):
    c = 0.7978845608
    v2 = v * v
    t = jnp.tanh(v * (c + (c * 0.044715) * v2))
    half = 0.5 + 0.5 * t
    gelu = v * half
    slope = half + (0.5 * v) * (1.0 - t * t) * (c + (3.0 * c * 0.044715) * v2)
    return gelu, slope


def ffn_kernel(x_ref, do_ref, wg_ref, wu_ref, wo_ref, y_ref, dx_ref, gg_ref, gu_ref, go_ref,
               xt_ref, dt_ref, a_ref, dg_ref, du_ref):
    f = pl.program_id(0)
    rows_total = x_ref.shape[0]

    @pl.when(f == 0)
    def _():
        for r in range(0, rows_total, RC):
            xt_ref[:, r : r + RC] = x_ref[r : r + RC, :].T
            dt_ref[:, r : r + RC] = do_ref[r : r + RC, :].T
        y_ref[...] = jnp.zeros_like(y_ref)
        dx_ref[...] = jnp.zeros_like(dx_ref)

    wg, wu, wo = wg_ref[...], wu_ref[...], wo_ref[...]
    for r in range(0, rows_total, RC):
        rows = pl.ds(r, RC)
        x, d = x_ref[rows, :], do_ref[rows, :]
        gelu, slope = gelu_parts(nn(x, wg))
        up = nn(x, wu)
        da = nt(d, wo)
        act = (gelu * up).astype(bf16)
        dg = (da * up * slope).astype(bf16)
        du = (da * gelu).astype(bf16)
        a_ref[rows, :] = act
        dg_ref[rows, :] = dg
        du_ref[rows, :] = du
        y_ref[rows, :] += nn(act, wo)
        dx_ref[rows, :] += nt(dg, wg) + nt(du, wu)
    gg_ref[...] = nn(xt_ref[...], dg_ref[...]).astype(bf16)
    gu_ref[...] = nn(xt_ref[...], du_ref[...]).astype(bf16)
    go_ref[...] = nn(dt_ref[...], a_ref[...]).T.astype(bf16)


def ffn(x, d_out, ffn_in, ffn_out):
    rows = x.shape[0]
    tiles = FF // FT
    return pl.pallas_call(
        ffn_kernel,
        grid=(tiles,),
        in_specs=[
            pl.BlockSpec((rows, D), lambda f: (0, 0), pipeline_mode=pl.Buffered(1)),
            pl.BlockSpec((rows, D), lambda f: (0, 0), pipeline_mode=pl.Buffered(1)),
            pl.BlockSpec((D, FT), lambda f: (0, f)),
            pl.BlockSpec((D, FT), lambda f: (0, tiles + f)),
            pl.BlockSpec((FT, D), lambda f: (f, 0)),
        ],
        out_specs=[
            pl.BlockSpec((rows, D), lambda f: (0, 0), pipeline_mode=pl.Buffered(1)),
            pl.BlockSpec((rows, D), lambda f: (0, 0), pipeline_mode=pl.Buffered(1)),
            pl.BlockSpec((D, FT), lambda f: (0, f)),
            pl.BlockSpec((D, FT), lambda f: (0, f)),
            pl.BlockSpec((FT, D), lambda f: (f, 0)),
        ],
        out_shape=[
            jax.ShapeDtypeStruct((rows, D), f32),
            jax.ShapeDtypeStruct((rows, D), f32),
            jax.ShapeDtypeStruct((D, FF), bf16),
            jax.ShapeDtypeStruct((D, FF), bf16),
            jax.ShapeDtypeStruct((FF, D), bf16),
        ],
        scratch_shapes=[
            pltpu.VMEM((D, rows), bf16),
            pltpu.VMEM((D, rows), bf16),
            pltpu.VMEM((rows, FT), bf16),
            pltpu.VMEM((rows, FT), bf16),
            pltpu.VMEM((rows, FT), bf16),
        ],
        compiler_params=pltpu.CompilerParams(vmem_limit_bytes=58 << 20),
        name="ffn_both_ways",
    )(x, d_out, ffn_in, ffn_in, ffn_out)


def norm_back(x, grad, gain):
    r = rms_scale(x)
    n = x * r
    u = gain * grad
    mean = jnp.sum(n * u, axis=1, keepdims=True) * (1.0 / D)
    return r * (u - n * mean), jnp.sum(n * grad, axis=0, keepdims=True)


def mid_kernel(len_ref, att_ref, y_ref, dx_ref, do_ref, ctx_ref, w_ref, vec_ref,
               out_ref, datt_ref, dctx_ref, gw_ref, gg_ref, acc_ref):
    s = pl.program_id(0)

    @pl.when(s == 0)
    def _():
        acc_ref[...] = jnp.zeros_like(acc_ref)
        gg_ref[...] = jnp.zeros_like(gg_ref)

    att = att_ref[...]
    out_ref[...] = ((att + y_ref[...]) * row_mask(len_ref[s])).astype(bf16)
    back, gain_grad = norm_back(att, dx_ref[...], vec_ref[2:3, :])
    gg_ref[...] += gain_grad
    d_att = do_ref[...].astype(f32) + back
    datt_ref[...] = d_att
    low = d_att.astype(bf16)
    dctx_ref[...] = nt(low, w_ref[...]).astype(bf16)
    acc_ref[...] += nn(ctx_ref[...].T, low)

    @pl.when(s == pl.num_programs(0) - 1)
    def _():
        gw_ref[...] = acc_ref[...].astype(bf16)


def mid_backward(lengths, att, y, dx, d_out, ctx, attn_out, vecs):
    rows = att.shape[0]
    return pl.pallas_call(
        mid_kernel,
        grid_spec=pltpu.PrefetchScalarGridSpec(
            num_scalar_prefetch=1,
            grid=(rows // TOK,),
            in_specs=[rows_spec()] * 5 + [whole(D, D), whole(3, D)],
            out_specs=[rows_spec(), rows_spec(), rows_spec(), whole(D, D), whole(1, D)],
            scratch_shapes=[pltpu.VMEM((D, D), f32)],
        ),
        out_shape=[
            jax.ShapeDtypeStruct((rows, D), bf16),
            jax.ShapeDtypeStruct((rows, D), f32),
            jax.ShapeDtypeStruct((rows, D), bf16),
            jax.ShapeDtypeStruct((D, D), bf16),
            jax.ShapeDtypeStruct((1, D), f32),
        ],
        compiler_params=pltpu.CompilerParams(vmem_limit_bytes=48 << 20),
        name="mid_backward",
    )(lengths, att, y, dx, d_out, ctx, attn_out, vecs)


def qkv_back_kernel(dqkv_ref, w_ref, normed_ref, hidden_ref, datt_ref, vec_ref, dh_ref, gw_ref, gg_ref, acc_ref):
    s = pl.program_id(0)

    @pl.when(s == 0)
    def _():
        acc_ref[...] = jnp.zeros_like(acc_ref)
        gg_ref[...] = jnp.zeros_like(gg_ref)

    nt_rows = normed_ref[...].T
    dn = jnp.zeros((TOK, D), f32)
    for i in range(3):
        piece = dqkv_ref[i]
        cols = pl.ds(i * D, D)
        dn = dn + nt(piece, w_ref[:, cols])
        acc_ref[:, cols] += nn(nt_rows, piece)
    back, gain_grad = norm_back(hidden_ref[...], dn, vec_ref[1:2, :])
    gg_ref[...] += gain_grad
    dh_ref[...] = datt_ref[...] + back

    @pl.when(s == pl.num_programs(0) - 1)
    def _():
        gw_ref[...] = acc_ref[...].astype(bf16)


def qkv_backward(dqkv, attn_in, normed, hidden, d_att, vecs):
    rows = normed.shape[0]
    return pl.pallas_call(
        qkv_back_kernel,
        grid=(rows // TOK,),
        in_specs=[
            pl.BlockSpec((3, TOK, D), lambda s: (0, s, 0)),
            whole(D, 3 * D), rows_spec(), rows_spec(), rows_spec(), whole(3, D),
        ],
        out_specs=[rows_spec(), whole(D, 3 * D), whole(1, D)],
        out_shape=[
            jax.ShapeDtypeStruct((rows, D), f32),
            jax.ShapeDtypeStruct((D, 3 * D), bf16),
            jax.ShapeDtypeStruct((1, D), f32),
        ],
        scratch_shapes=[pltpu.VMEM((D, 3 * D), f32)],
        compiler_params=pltpu.CompilerParams(vmem_limit_bytes=56 << 20),
        name="qkv_backward",
    )(dqkv, attn_in, normed, hidden, d_att, vecs)


def gather_small(embed, conv_w, score_w, gain_attn, gain_ffn, rel_table):
    shards = lax.axis_size("shard")
    width = embed.shape[1]
    table_row = jnp.pad(rel_table.reshape(1, -1), ((0, 0), (0, width - rel_table.size)))
    packed = jnp.concatenate(
        [embed, conv_w, score_w[None], gain_attn[None], gain_ffn[None], table_row], axis=0
    )
    full = lax.all_gather(packed, "shard", axis=1, tiled=True)
    table = full[VOCAB : VOCAB + 4]
    vecs = full[VOCAB + 4 : VOCAB + 7].astype(f32)
    rel = full[VOCAB + 7].reshape(shards, width)[:, : rel_table.size].reshape(BUCKETS, HEADS)
    return jnp.pad(full[:VOCAB], ((0, VPAD - VOCAB), (0, 0))), table.astype(f32), vecs, rel


def own_order_cotangent(target, cotangent, lengths):
    replicas = lax.axis_size("rep")
    shards = lax.axis_size("shard")
    rep = lax.axis_index("rep")
    seqs = cotangent.shape[0]
    dest_rep = target // seqs // shards
    dest_slot = target % seqs
    wanted = jnp.where(dest_rep[None, :] == jnp.arange(replicas)[:, None], dest_slot[None, :] + 1, 0).sum(axis=1)
    slots = lax.all_to_all(wanted, "rep", split_axis=0, concat_axis=0, tiled=True) - 1

    def pick(slot):
        out = cotangent[0]
        for k in range(1, seqs):
            out = jnp.where(slot == k, cotangent[k], out)
        return out

    pieces = []
    for shift in range(replicas):
        sent = pick(slots[(rep + shift) % replicas])
        if shift:
            sent = lax.ppermute(sent, "rep", [(r, (r + shift) % replicas) for r in range(replicas)])
        pieces.append(sent)
    rows = []
    for k in range(seqs):
        shift = (rep - dest_rep[k]) % replicas
        row = pieces[0]
        for j in range(1, replicas):
            row = jnp.where(shift == j, pieces[j], row)
        live = 2 * jnp.arange(TOK) < lengths[k]
        rows.append(jnp.where(live[:, None], row, jnp.zeros((), bf16)))
    return jnp.concatenate(rows, axis=0)


def scatter_sum(grad, dim):
    part = lax.psum_scatter(grad.astype(bf16), "shard", scatter_dimension=dim, tiled=True)
    return lax.psum(part, "rep").astype(f32)


def body(
    byte_ids, lengths, target, rel_bucket, cotangent, embed, conv_w, score_w, gain_attn,
    attn_in, attn_out, gain_ffn, ffn_in, ffn_out, rel_table,
):
    seqs = byte_ids.shape[0]
    rows = seqs * TOK
    shards = lax.axis_size("shard")
    width = embed.shape[1]
    table, taps, vecs, rel = gather_small(embed, conv_w, score_w, gain_attn, gain_ffn, rel_table)
    attn_in_full = lax.all_gather(attn_in, "shard", axis=0, tiled=True)
    attn_out_full = lax.all_gather(attn_out, "shard", axis=0, tiled=True)
    ffn_in_full = lax.all_gather(ffn_in, "shard", axis=0, tiled=True)
    ffn_out_full = lax.all_gather(ffn_out, "shard", axis=0, tiled=True)
    d_out = own_order_cotangent(target, cotangent, lengths)
    ids_col, ids_row = byte_columns(byte_ids, lengths)
    hits = bucket_hits(rel_bucket)
    z = lax.dot_general(
        rel, hits.astype(bf16), (((0,), (0,)), ((), ())), preferred_element_type=f32
    ).reshape(HEADS, 8, SPAN)

    hidden, normed, convolved, weights = gbst_forward(lengths, ids_col, table, taps, vecs)
    qkv = jnp.dot(normed, attn_in_full, preferred_element_type=f32).astype(bf16)
    ctx, lse = attn_forward(lengths, qkv, z)
    attended, low = post_attention(ctx, attn_out_full, hidden, vecs)
    y, d_low, g_gate, g_up, g_ffn_out = ffn(low, d_out, ffn_in_full, ffn_out_full)
    out, d_att, d_ctx, g_attn_out, g_gain_ffn = mid_backward(
        lengths, attended, y, d_low, d_out, ctx, attn_out_full, vecs
    )
    dqkv, gz = attn_backward(lengths, qkv, d_ctx, ctx, lse, z)
    d_hidden, g_attn_in, g_gain_attn = qkv_backward(dqkv, attn_in_full, normed, hidden, d_att, vecs)
    input_grad, g_embed, g_conv, g_score = gbst_backward(
        lengths, ids_col, ids_row, table, taps, vecs, d_hidden, convolved, weights
    )
    g_table = lax.dot_general(
        hits.astype(f32), gz.reshape(HEADS, -1), (((1,), (1,)), ((), ())),
        precision=lax.Precision.HIGHEST, preferred_element_type=f32,
    )
    s_gate = scatter_sum(g_gate, 0)
    s_up = scatter_sum(g_up, 0)
    s_ffn_out = scatter_sum(g_ffn_out, 0)
    s_attn_out = scatter_sum(g_attn_out, 0)
    s_attn_in = scatter_sum(g_attn_in, 0)
    per = g_table.size // shards
    table_rows = jnp.pad(g_table.reshape(shards, per), ((0, 0), (0, width - per))).reshape(1, D)
    small = jnp.concatenate(
        [g_embed[:VOCAB], g_conv, g_score, g_gain_attn, g_gain_ffn, table_rows], axis=0
    )
    s_small = lax.psum(lax.psum_scatter(small, "shard", scatter_dimension=1, tiled=True), "rep")
    return (
        out.reshape(seqs, TOK, D),
        input_grad,
        s_small[:VOCAB],
        s_small[VOCAB : VOCAB + 4],
        s_small[VOCAB + 4],
        s_small[VOCAB + 5],
        s_attn_in,
        s_attn_out,
        s_small[VOCAB + 6],
        jnp.concatenate([s_gate, s_up], axis=1),
        s_ffn_out,
        s_small[VOCAB + 7, :per].reshape(rel_table.shape),
    )


def solution(mesh):
    in_specs = (
        P(("rep", "shard"), None), P(("rep", "shard")), P(("rep", "shard")), P(),
        P(("rep", "shard"), None, None), P(None, "shard"), P(None, "shard"), P("shard"), P("shard"),
        P("shard", None), P("shard", None), P("shard"), P("shard", None), P("shard", None), P("shard", None),
    )
    out_specs = (
        P(("rep", "shard"), None, None), P(("rep", "shard"), None, None), P(None, "shard"), P(None, "shard"),
        P("shard"), P("shard"), P("shard", None), P("shard", None), P("shard"), P("shard", None),
        P("shard", None), P("shard", None),
    )
    return jax.shard_map(body, mesh=mesh, in_specs=in_specs, out_specs=out_specs, check_vma=False)
```

```python
import jax
import jax.numpy as jnp
from jax import lax
from jax.experimental import pallas as pl
from jax.experimental.pallas import tpu as pltpu
from jax.sharding import PartitionSpec as P

D = 768
VOCAB = 259
VPAD = 384
VROWS = 272
SMALL = 384
MAXLEN = 1024
TOK = 512
LANES = 128
QN = 88
R = 12
P_ROWS = QN * R
T_ROWS = 528
LT = D // LANES
epsilon = 1e-06
f32 = jnp.float32
bf16 = jnp.bfloat16


def cost(us, mib):
    return pl.CostEstimate(flops=int(us * 1e9), bytes_accessed=mib << 20, transcendentals=0)


def lane_iota(rows):
    return lax.broadcasted_iota(jnp.int32, (rows, LANES), 1)


def group_matrix(b):
    row = lax.broadcasted_iota(jnp.int32, (LANES, LANES), 0)
    col = lax.broadcasted_iota(jnp.int32, (LANES, LANES), 1)
    return jnp.where((row // b == col // b) & (row < R) & (col < R), 1.0, 0.0).astype(f32)


def exact_dot(a, b):
    return jnp.dot(a, b, precision=lax.Precision.HIGHEST, preferred_element_type=f32)


def place(columns, rows):
    lanes = lane_iota(rows)
    out = jnp.zeros((rows, LANES), f32)
    for r, column in enumerate(columns):
        out = jnp.where(lanes == r, column, out)
    return out


def gbst_masks(length):
    q = lax.broadcasted_iota(jnp.int32, (QN, LANES), 0)
    r = lax.broadcasted_iota(jnp.int32, (QN, LANES), 1)
    mask = jnp.where((q * R + r < length) & (r < R), 1.0, 0.0).astype(f32)
    inverse = [1.0 / jnp.maximum(exact_dot(mask, group_matrix(b)), 1.0) for b in (2, 3, 4)]
    pair = exact_dot(mask, group_matrix(2))
    alpha = mask / jnp.maximum(pair, 1.0)
    return mask, inverse, alpha


def gbst_weights(s1, inverse):
    sizes = [s1] + [exact_dot(s1, group_matrix(b)) * inv for b, inv in zip((2, 3, 4), inverse)]
    top = jnp.maximum(jnp.maximum(sizes[0], sizes[1]), jnp.maximum(sizes[2], sizes[3]))
    parts = [jnp.exp(s - top) for s in sizes]
    total = parts[0] + parts[1] + parts[2] + parts[3]
    return [p / total for p in parts]


def gbst_coefs(weights, inverse, alpha):
    a1 = weights[0] * alpha
    a2 = weights[1] * alpha * inverse[0]
    a3 = weights[2] * alpha * inverse[1]
    a4 = weights[3] * alpha * inverse[2]
    pair = group_matrix(2)
    a4s = exact_dot(a4, pair)
    own = a1 + exact_dot(a2, pair) + a4s
    return own, a3, a4s


def column(x, r):
    return jnp.broadcast_to(x[:, r : r + 1], (x.shape[0], LANES))


def hits_of(ids_col):
    lanes = lax.broadcasted_iota(jnp.int32, (P_ROWS, VPAD), 1)
    return jnp.where(ids_col == lanes, 1.0, 0.0).astype(bf16)


def load_e(e_ref, r, lt):
    lanes = pl.ds(lt * LANES, LANES)
    if r < R:
        return e_ref[pl.ds(r * QN, QN), lanes]
    return e_ref[pl.ds((r - R) * QN + 1, QN), lanes]


def gbst_fwd_kernel(len_ref, ids_ref, table_ref, conv_ref, vec_ref, hidden_ref, normed_ref, c_ref, w_ref, e_ref, hid_ref, s_ref, k_ref):
    length = len_ref[pl.program_id(0)]
    hits = hits_of(ids_ref[0])
    e_ref[pl.ds(0, P_ROWS), :] = jnp.dot(hits, table_ref[...], preferred_element_type=f32)
    e_ref[pl.ds(P_ROWS, 8), :] = jnp.zeros((8, D), f32)
    for lt in range(LT):
        lanes = pl.ds(lt * LANES, LANES)
        taps = [jnp.broadcast_to(conv_ref[j : j + 1, lanes], (QN, LANES)) for j in range(4)]
        sw = jnp.broadcast_to(vec_ref[0:1, lanes], (QN, LANES))
        for r in range(R):
            c = taps[0] * load_e(e_ref, r, lt)
            for j in range(1, 4):
                c = c + taps[j] * load_e(e_ref, r + j, lt)
            c_ref[0, pl.ds(r * QN, QN), lanes] = c
            part = c * sw
            rows = pl.ds(r * QN, QN)
            s_ref[rows, :] = part if lt == 0 else s_ref[rows, :] + part
    s1 = place([jnp.sum(s_ref[pl.ds(r * QN, QN), :], axis=1, keepdims=True) for r in range(R)], QN)
    mask, inverse, alpha = gbst_masks(length)
    weights = gbst_weights(s1, inverse)
    for b in range(4):
        w_ref[0, b] = weights[b]
    own, a3, a4s = gbst_coefs(weights, inverse, alpha)
    n = 0
    for r in range(R):
        k_ref[r] = column(own, r)
        k_ref[R + r] = column(a3, r)
    for k in range(6):
        k_ref[2 * R + k] = column(a4s, 2 * k)
    for lt in range(LT):
        lanes = pl.ds(lt * LANES, LANES)
        for half in range(2):
            c = [c_ref[0, pl.ds((half * 6 + r) * QN, QN), lanes] for r in range(6)]
            base = half * 6
            s3 = [c[0] + c[1] + c[2], c[3] + c[4] + c[5]]
            for k in range(3):
                tok = half * 3 + k
                other = tok ^ 1
                rows = pl.ds(2 * other * QN, QN)
                rows1 = pl.ds((2 * other + 1) * QN, QN)
                s2 = c_ref[0, rows, lanes] + c_ref[0, rows1, lanes]
                h = k_ref[2 * tok] * c[2 * k] + k_ref[2 * tok + 1] * c[2 * k + 1] + k_ref[2 * R + tok] * s2
                if k == 1:
                    h = h + k_ref[R + 2 * tok] * s3[0] + k_ref[R + 2 * tok + 1] * s3[1]
                else:
                    h = h + (k_ref[R + 2 * tok] + k_ref[R + 2 * tok + 1]) * s3[0 if k == 0 else 1]
                hid_ref[lt, pl.ds(tok, QN, stride=6), :] = h
    total = jnp.zeros((TOK, LANES), f32)
    for lt in range(LT):
        x = hid_ref[lt, 0:TOK, :]
        total = total + x * x
    scale = lax.rsqrt(jnp.sum(total, axis=1, keepdims=True) * (1.0 / D) + epsilon)
    for lt in range(LT):
        lanes = pl.ds(lt * LANES, LANES)
        x = hid_ref[lt, 0:TOK, :]
        hidden_ref[:, lanes] = x
        normed_ref[:, lanes] = (x * scale * vec_ref[1:2, lanes]).astype(bf16)


def gbst_forward(lengths, ids_col, table, conv_w, vecs):
    seqs = ids_col.shape[0]
    grid_spec = pltpu.PrefetchScalarGridSpec(
        num_scalar_prefetch=1,
        grid=(seqs,),
        in_specs=[
            pl.BlockSpec((1, P_ROWS, 1), lambda s, n: (s, 0, 0)),
            pl.BlockSpec((VPAD, D), lambda s, n: (0, 0)),
            pl.BlockSpec((4, D), lambda s, n: (0, 0)),
            pl.BlockSpec((3, D), lambda s, n: (0, 0)),
        ],
        out_specs=[
            pl.BlockSpec((TOK, D), lambda s, n: (s, 0)),
            pl.BlockSpec((TOK, D), lambda s, n: (s, 0)),
            pl.BlockSpec((1, P_ROWS, D), lambda s, n: (s, 0, 0)),
            pl.BlockSpec((1, 4, QN, LANES), lambda s, n: (s, 0, 0, 0)),
        ],
        scratch_shapes=[
            pltpu.VMEM((P_ROWS + 8, D), f32),
            pltpu.VMEM((LT, T_ROWS, LANES), f32),
            pltpu.VMEM((P_ROWS, LANES), f32),
            pltpu.VMEM((2 * R + 6, QN, LANES), f32),
        ],
    )
    return pl.pallas_call(
        gbst_fwd_kernel,
        grid_spec=grid_spec,
        out_shape=[
            jax.ShapeDtypeStruct((seqs * TOK, D), f32),
            jax.ShapeDtypeStruct((seqs * TOK, D), bf16),
            jax.ShapeDtypeStruct((seqs, P_ROWS, D), f32),
            jax.ShapeDtypeStruct((seqs, 4, QN, LANES), f32),
        ],
        compiler_params=pltpu.CompilerParams(vmem_limit_bytes=48 << 20),
        cost_estimate=cost(18, 30),
        name="gbst_forward",
    )(lengths, ids_col, table, conv_w, vecs)


def gbst_bwd_kernel(len_ref, ids_ref, row_ref, table_ref, conv_ref, vec_ref, dh_ref, c_ref, w_ref, more_ref,
                    ig_ref, small_ref, ge_ref, e_ref, dt_ref, dc_ref, s_ref, k_ref, igs_ref):
    seq = pl.program_id(0)
    length = len_ref[seq]

    @pl.when(seq == 0)
    def _():
        ge_ref[...] = jnp.zeros_like(ge_ref)

    hits = hits_of(ids_ref[0])
    e_ref[pl.ds(0, P_ROWS), :] = jnp.dot(hits, table_ref[...], preferred_element_type=f32)
    e_ref[pl.ds(P_ROWS, 8), :] = jnp.zeros((8, D), f32)
    for lt in range(LT):
        dt_ref[lt, 0:TOK, :] = dh_ref[:, pl.ds(lt * LANES, LANES)]
        dt_ref[lt, TOK:T_ROWS, :] = jnp.zeros((T_ROWS - TOK, LANES), f32)
    for lt in range(LT):
        lanes = pl.ds(lt * LANES, LANES)
        for half in range(2):
            c = [c_ref[0, pl.ds((half * 6 + r) * QN, QN), lanes] for r in range(6)]
            s3 = [c[0] + c[1] + c[2], c[3] + c[4] + c[5]]
            for k in range(3):
                tok = half * 3 + k
                other = tok ^ 1
                dh = dt_ref[lt, pl.ds(tok, QN, stride=6), :]
                s2 = c_ref[0, pl.ds(2 * other * QN, QN), lanes] + c_ref[0, pl.ds((2 * other + 1) * QN, QN), lanes]
                parts = [
                    (2 * tok, dh * c[2 * k]),
                    (2 * tok + 1, dh * c[2 * k + 1]),
                    (2 * R + tok, dh * s2),
                    (R + 2 * tok, dh * s3[0 if k < 2 else 1]),
                ]
                if k == 1:
                    parts.append((R + 2 * tok + 1, dh * s3[1]))
                for slot, part in parts:
                    s_ref[slot] = part if lt == 0 else s_ref[slot] + part

    def total(slot):
        return jnp.sum(s_ref[slot], axis=1, keepdims=True)

    d1, d3, dother = [], [], []
    for tok in range(6):
        d1 += [total(2 * tok), total(2 * tok + 1)]
        first = total(R + 2 * tok)
        d3 += [first, total(R + 2 * tok + 1) if tok % 3 == 1 else first]
        o = total(2 * R + tok)
        dother += [o, o]
    d1, d3, dother = place(d1, QN), place(d3, QN), place(dother, QN)
    mask, inverse, alpha = gbst_masks(length)
    weights = [w_ref[0, b] for b in range(4)]
    d2 = exact_dot(d1, group_matrix(2))
    g = [alpha * d1, alpha * d2 * inverse[0], alpha * d3 * inverse[1], alpha * (d2 + dother) * inverse[2]]
    mean = weights[0] * g[0] + weights[1] * g[1] + weights[2] * g[2] + weights[3] * g[3]
    d_size = [w * (x - mean) for w, x in zip(weights, g)]
    coef = d_size[0]
    for b, inv in zip((2, 3, 4), inverse):
        coef = coef + exact_dot(d_size[b - 1] * inv, group_matrix(b))
    own, a3, a4s = gbst_coefs(weights, inverse, alpha)
    for r in range(R):
        k_ref[r] = column(own, r)
        k_ref[R + r] = column(a3, r)
        k_ref[2 * R + r] = column(coef, r)
        k_ref[3 * R + r] = column(mask, r)
    for k in range(6):
        k_ref[4 * R + k] = column(a4s, 2 * k)

    for lt in range(LT):
        lanes = pl.ds(lt * LANES, LANES)
        taps = [jnp.broadcast_to(conv_ref[j : j + 1, lanes], (QN, LANES)) for j in range(4)]
        sw = jnp.broadcast_to(vec_ref[0:1, lanes], (QN, LANES))
        gs = jnp.zeros((QN, LANES), f32)
        gc = [jnp.zeros((QN, LANES), f32) for _ in range(4)]
        for half in range(2):
            dh = [dt_ref[lt, pl.ds(half * 3 + k, QN, stride=6), :] for k in range(3)]
            a = R + half * 6
            t3 = [
                (k_ref[a] + k_ref[a + 1]) * dh[0] + k_ref[a + 2] * dh[1],
                k_ref[a + 3] * dh[1] + (k_ref[a + 4] + k_ref[a + 5]) * dh[2],
            ]
            for k in range(3):
                tok = half * 3 + k
                other = tok ^ 1
                dother_h = dt_ref[lt, pl.ds(other, QN, stride=6), :]
                cross = k_ref[4 * R + other] * dother_h
                for e in range(2):
                    r = 2 * tok + e
                    cf = k_ref[2 * R + r]
                    dc = k_ref[r] * dh[k] + cross + t3[(r % 6) // 3] + cf * sw
                    gs = gs + cf * c_ref[0, pl.ds(r * QN, QN), lanes]
                    dc_ref[r, pl.ds(8, QN), :] = dc
                    for j in range(4):
                        gc[j] = gc[j] + dc * load_e(e_ref, r + j, lt)
        ge_ref[VROWS + 4 : VROWS + 5, lanes] += jnp.sum(gs, axis=0, keepdims=True)
        for j in range(4):
            ge_ref[VROWS + j : VROWS + j + 1, lanes] += jnp.sum(gc[j], axis=0, keepdims=True)
        for r in range(R):
            dc_ref[r, 0:8, :] = jnp.zeros((8, LANES), f32)
        for r in range(R):
            x = taps[0] * dc_ref[r, pl.ds(8, QN), :]
            for j in range(1, 4):
                back = dc_ref[r - j, pl.ds(8, QN), :] if r >= j else dc_ref[r - j + R, pl.ds(7, QN), :]
                x = x + taps[j] * back
            igs_ref[lt, pl.ds(r, QN, stride=R), :] = x * k_ref[3 * R + r]
    for lt in range(LT):
        lanes = pl.ds(lt * LANES, LANES)
        ig_ref[0, :, lanes] = igs_ref[lt, 0:MAXLEN, :].astype(bf16)
    vocab = lax.broadcasted_iota(jnp.int32, (VROWS, MAXLEN), 0)
    row_hits = jnp.where(vocab == row_ref[0], 1.0, 0.0).astype(bf16)
    ge_ref[0:VROWS, :] += jnp.dot(row_hits, ig_ref[0], preferred_element_type=f32)

    @pl.when(seq == pl.num_programs(0) - 1)
    def _():
        ge_ref[VROWS + 5 : VROWS + 8, :] = more_ref[...]
        for lt in range(LT):
            lanes = pl.ds(lt * LANES, LANES)
            small_ref[lanes, :] = ge_ref[:, lanes].T.astype(bf16)


def gbst_backward(lengths, ids_col, ids_row, table, conv_w, vecs, d_hidden, c, w, more):
    seqs = ids_col.shape[0]
    grid_spec = pltpu.PrefetchScalarGridSpec(
        num_scalar_prefetch=1,
        grid=(seqs,),
        in_specs=[
            pl.BlockSpec((1, P_ROWS, 1), lambda s, n: (s, 0, 0)),
            pl.BlockSpec((1, 1, MAXLEN), lambda s, n: (s, 0, 0)),
            pl.BlockSpec((VPAD, D), lambda s, n: (0, 0)),
            pl.BlockSpec((4, D), lambda s, n: (0, 0)),
            pl.BlockSpec((3, D), lambda s, n: (0, 0)),
            pl.BlockSpec((TOK, D), lambda s, n: (s, 0)),
            pl.BlockSpec((1, P_ROWS, D), lambda s, n: (s, 0, 0)),
            pl.BlockSpec((1, 4, QN, LANES), lambda s, n: (s, 0, 0, 0)),
            pl.BlockSpec((3, D), lambda s, n: (0, 0)),
        ],
        out_specs=[
            pl.BlockSpec((1, MAXLEN, D), lambda s, n: (s, 0, 0)),
            pl.BlockSpec((D, SMALL), lambda s, n: (0, 0)),
        ],
        scratch_shapes=[
            pltpu.VMEM((SMALL, D), f32),
            pltpu.VMEM((P_ROWS + 8, D), f32),
            pltpu.VMEM((LT, T_ROWS, LANES), f32),
            pltpu.VMEM((R, QN + 8, LANES), f32),
            pltpu.VMEM((2 * R + 6, QN, LANES), f32),
            pltpu.VMEM((4 * R + 6, QN, LANES), f32),
            pltpu.VMEM((LT, P_ROWS, LANES), f32),
        ],
    )
    return pl.pallas_call(
        gbst_bwd_kernel,
        grid_spec=grid_spec,
        out_shape=[
            jax.ShapeDtypeStruct((seqs, MAXLEN, D), bf16),
            jax.ShapeDtypeStruct((D, SMALL), bf16),
        ],
        compiler_params=pltpu.CompilerParams(vmem_limit_bytes=56 << 20),
        cost_estimate=cost(31, 40),
        name="gbst_backward",
    )(lengths, ids_col, ids_row, table, conv_w, vecs, d_hidden, c, w, more)


def byte_columns(byte_ids, lengths):
    seqs = byte_ids.shape[0]
    live = jnp.arange(MAXLEN)[None, :] < lengths[:, None]
    ids = jnp.where(live, byte_ids, -1)
    wide = jnp.pad(ids, ((0, 0), (0, P_ROWS - MAXLEN)), constant_values=-1)
    ids_col = wide.reshape(seqs, QN, R).transpose(0, 2, 1).reshape(seqs, P_ROWS, 1)
    return ids_col, ids.reshape(seqs, 1, MAXLEN)


HEADS = 12
HD = 64
BUCKETS = 32
SPAN = 1024
PAIRS = HEADS // 2
QC = 256
dead_score = -1e9


def nt(a, b):
    return lax.dot_general(a, b, (((1,), (1,)), ((), ())), preferred_element_type=f32)


def nn(a, b):
    return jnp.dot(a, b, preferred_element_type=f32)


def bucket_rows(rel_bucket):
    back = jnp.pad(rel_bucket[::-1], (8, 0))
    rows = [
        jnp.concatenate([back[8 + TOK - 1 - s : 8 + 2 * TOK - 1 - s], back[7 - s : 7 - s + TOK]])
        for s in range(8)
    ]
    return jnp.concatenate(rows)


def bucket_hits(rel_bucket):
    return jnp.arange(BUCKETS)[:, None] == bucket_rows(rel_bucket)[None, :]


def build_bias(z_ref, bt_ref):
    for h in range(2):
        z = z_ref[h]
        for g in range(TOK // 8):
            bt_ref[h, pl.ds(8 * g, 8), :] = (z if g == 0 else pltpu.roll(z, 8 * g, 1))[:, :TOK]


def head_parts(k, q, length, h):
    lanes = lax.broadcasted_iota(jnp.int32, (TOK, LANES), 1)
    rows = lax.broadcasted_iota(jnp.int32, (TOK, LANES), 0)
    spare = HD * (1 - h)
    own = (lanes < HD) if h == 0 else (lanes >= HD)
    dead = jnp.where(2 * rows < length, 0.0, dead_score)
    kf = jnp.where(own, k.astype(f32), jnp.where(lanes == spare, dead, 0.0)).astype(bf16)
    qf = jnp.where(lanes == spare, 1.0, q.astype(f32)).astype(bf16)
    return kf, qf


def attn_fwd_kernel(len_ref, q_ref, k_ref, v_ref, z_ref, ctx_ref, lse_ref, bt_ref):
    length = len_ref[pl.program_id(1)]

    @pl.when(pl.program_id(1) == 0)
    def _():
        build_bias(z_ref, bt_ref)

    q, k, v = q_ref[...], k_ref[...], v_ref[...]
    vt = v.astype(f32).T.astype(bf16)
    outs = []
    for h in range(2):
        kf, qf = head_parts(k, q, length, h)
        pieces = []
        for c in range(TOK // QC):
            cols = slice(c * QC, (c + 1) * QC)
            s = nt(kf, qf[cols]) + bt_ref[h, :, cols]
            top = jnp.max(s, axis=0, keepdims=True)
            p = jnp.exp(s - top)
            total = jnp.sum(p, axis=0, keepdims=True)
            lse_ref[0, 0, h : h + 1, cols] = top + jnp.log(total)
            pieces.append(nn(vt[h * HD : (h + 1) * HD], p.astype(bf16)) * (1.0 / total))
        outs.append(jnp.concatenate(pieces, axis=1))
    ctx_ref[...] = jnp.concatenate(outs, axis=0).T.astype(bf16)


def attn_forward(lengths, qkv, z):
    seqs = qkv.shape[0] // TOK
    spec = lambda off: pl.BlockSpec((TOK, LANES), lambda hp, s, n: (s, off + hp))
    return pl.pallas_call(
        attn_fwd_kernel,
        grid_spec=pltpu.PrefetchScalarGridSpec(
            num_scalar_prefetch=1,
            grid=(PAIRS, seqs),
            in_specs=[spec(0), spec(PAIRS), spec(2 * PAIRS), pl.BlockSpec((2, 8, SPAN), lambda hp, s, n: (hp, 0, 0))],
            out_specs=[spec(0), pl.BlockSpec((1, 1, 2, TOK), lambda hp, s, n: (hp, s, 0, 0))],
            scratch_shapes=[pltpu.VMEM((2, TOK, TOK), f32)],
        ),
        out_shape=[
            jax.ShapeDtypeStruct((seqs * TOK, D), bf16),
            jax.ShapeDtypeStruct((PAIRS, seqs, 2, TOK), f32),
        ],
        compiler_params=pltpu.CompilerParams(vmem_limit_bytes=40 << 20),
        cost_estimate=cost(45, 20),
        name="attn_forward",
    )(lengths, qkv, qkv, qkv, z)


def attn_bwd_kernel(len_ref, q_ref, k_ref, v_ref, do_ref, o_ref, lse_ref, z_ref, dqkv_ref, gz_ref, bt_ref, g_ref):
    s_id = pl.program_id(1)
    length = len_ref[s_id]

    @pl.when(s_id == 0)
    def _():
        build_bias(z_ref, bt_ref)
        g_ref[...] = jnp.zeros_like(g_ref)

    q, k, v, do = q_ref[...], k_ref[...], v_ref[...], do_ref[...]
    kt = k.astype(f32).T.astype(bf16)
    lanes8 = lax.broadcasted_iota(jnp.int32, (8, LANES), 1)
    rows8 = lax.broadcasted_iota(jnp.int32, (8, LANES), 0)
    pick = jnp.where(lanes8 // HD == rows8, 1.0, 0.0).astype(f32)
    delta = lax.dot_general(
        pick, do.astype(f32) * o_ref[...].astype(f32), (((1,), (1,)), ((), ())),
        precision=lax.Precision.HIGHEST, preferred_element_type=f32)
    lanes = lax.broadcasted_iota(jnp.int32, (TOK, LANES), 1)
    dq_t, dk, dv = [], [], []
    for h in range(2):
        kf, qf = head_parts(k, q, length, h)
        own = (lanes < HD) if h == 0 else (lanes >= HD)
        vf = jnp.where(own, v.astype(f32), 0.0).astype(bf16)
        pieces, dk_h, dv_h = [], None, None
        for c in range(TOK // QC):
            cols = slice(c * QC, (c + 1) * QC)
            s = nt(kf, qf[cols]) + bt_ref[h, :, cols]
            p = jnp.exp(s - lse_ref[0, 0, h : h + 1, cols])
            ds = p * (nt(vf, do[cols]) - delta[h : h + 1, cols])
            g_ref[h, :, cols] += ds
            low = ds.astype(bf16)
            dv_c = nn(p.astype(bf16), do[cols])
            dk_c = nn(low, q[cols])
            dv_h = dv_c if dv_h is None else dv_h + dv_c
            dk_h = dk_c if dk_h is None else dk_h + dk_c
            pieces.append(nn(kt[h * HD : (h + 1) * HD], low))
        dq_t.append(jnp.concatenate(pieces, axis=1))
        dk.append(dk_h)
        dv.append(dv_h)
    dqkv_ref[0] = jnp.concatenate(dq_t, axis=0).T.astype(bf16)
    dqkv_ref[1] = jnp.where(lanes < HD, dk[0], dk[1]).astype(bf16)
    dqkv_ref[2] = jnp.where(lanes < HD, dv[0], dv[1]).astype(bf16)

    @pl.when(s_id == pl.num_programs(1) - 1)
    def _():
        zero = jnp.zeros((8, SPAN - TOK), f32)
        for h in range(2):
            total = jnp.zeros((8, SPAN), f32)
            for g in range(TOK // 8):
                piece = jnp.concatenate([g_ref[h, pl.ds(8 * g, 8), :], zero], axis=1)
                total = total + (piece if g == 0 else pltpu.roll(piece, SPAN - 8 * g, 1))
            gz_ref[h] = total


def attn_backward(lengths, qkv, d_ctx, ctx, lse, z):
    seqs = qkv.shape[0] // TOK
    spec = lambda off: pl.BlockSpec((TOK, LANES), lambda hp, s, n: (s, off + hp))
    return pl.pallas_call(
        attn_bwd_kernel,
        grid_spec=pltpu.PrefetchScalarGridSpec(
            num_scalar_prefetch=1,
            grid=(PAIRS, seqs),
            in_specs=[
                spec(0), spec(PAIRS), spec(2 * PAIRS), spec(0), spec(0),
                pl.BlockSpec((1, 1, 2, TOK), lambda hp, s, n: (hp, s, 0, 0)),
                pl.BlockSpec((2, 8, SPAN), lambda hp, s, n: (hp, 0, 0)),
            ],
            out_specs=[
                pl.BlockSpec((3, TOK, LANES), lambda hp, s, n: (0, s, hp)),
                pl.BlockSpec((2, 8, SPAN), lambda hp, s, n: (hp, 0, 0)),
            ],
            scratch_shapes=[pltpu.VMEM((2, TOK, TOK), f32), pltpu.VMEM((2, TOK, TOK), f32)],
        ),
        out_shape=[
            jax.ShapeDtypeStruct((3, seqs * TOK, D), bf16),
            jax.ShapeDtypeStruct((HEADS, 8, SPAN), f32),
        ],
        compiler_params=pltpu.CompilerParams(vmem_limit_bytes=48 << 20),
        cost_estimate=cost(50, 30),
        name="attn_backward",
    )(lengths, qkv, qkv, qkv, d_ctx, ctx, lse, z)


FF = 2048
FT = 256
RC = 512


def row_mask(length):
    rows = lax.broadcasted_iota(jnp.int32, (TOK, 1), 0)
    return jnp.where(2 * rows < length, 1.0, 0.0).astype(f32)


def rms_scale(x):
    return lax.rsqrt(jnp.sum(x * x, axis=1, keepdims=True) * (1.0 / D) + epsilon)


def post_kernel(ctx_ref, w_ref, hidden_ref, vec_ref, att_ref, low_ref):
    att = hidden_ref[...] + nn(ctx_ref[...], w_ref[...])
    att_ref[...] = att
    low_ref[...] = (att * rms_scale(att) * vec_ref[2:3, :]).astype(bf16)


def rows_spec(width=D):
    return pl.BlockSpec((TOK, width), lambda s, *n: (s, 0))


def whole(*shape):
    return pl.BlockSpec(shape, lambda s, *n: (0,) * len(shape))


def post_attention(ctx, attn_out, hidden, vecs):
    rows = ctx.shape[0]
    return pl.pallas_call(
        post_kernel,
        grid=(rows // TOK,),
        in_specs=[rows_spec(), whole(D, D), rows_spec(), whole(3, D)],
        out_specs=[rows_spec(), rows_spec()],
        out_shape=[jax.ShapeDtypeStruct((rows, D), f32), jax.ShapeDtypeStruct((rows, D), bf16)],
        compiler_params=pltpu.CompilerParams(vmem_limit_bytes=32 << 20),
        cost_estimate=cost(4, 20),
        name="post_attention",
    )(ctx, attn_out, hidden, vecs)


def gelu_parts(v):
    c = 0.7978845608
    v2 = v * v
    t = jnp.tanh(v * (c + (c * 0.044715) * v2))
    half = 0.5 + 0.5 * t
    gelu = v * half
    slope = half + (0.5 * v) * (1.0 - t * t) * (c + (3.0 * c * 0.044715) * v2)
    return gelu, slope


def ffn_kernel(x_ref, do_ref, wg_ref, wu_ref, wo_ref, y_ref, dx_ref, grad_ref,
               xt_ref, dt_ref, a_ref, dg_ref, du_ref, gu_ref, go_ref, sems):
    f = pl.program_id(0)
    steps = pl.num_programs(0)
    rows_total = x_ref.shape[0]
    shards, part = gu_ref.shape[1], gu_ref.shape[2]
    owners, deep = go_ref.shape[1], go_ref.shape[2]
    base = (FF // 2 // FT) * part

    def copies(slot, step):
        return (
            pltpu.make_async_copy(
                gu_ref.at[slot], grad_ref.at[:, pl.ds(step * part, part), :], sems.at[0, slot]),
            pltpu.make_async_copy(
                go_ref.at[slot], grad_ref.at[pl.ds(step * owners, owners), pl.ds(base, deep), :], sems.at[1, slot]),
        )

    @pl.when(f == 0)
    def _():
        for r in range(0, rows_total, RC):
            xt_ref[:, r : r + RC] = x_ref[r : r + RC, :].T
            dt_ref[:, r : r + RC] = do_ref[r : r + RC, :].T
        y_ref[...] = jnp.zeros_like(y_ref)
        dx_ref[...] = jnp.zeros_like(dx_ref)

    wg, wu, wo = wg_ref[...], wu_ref[...], wo_ref[...]
    for r in range(0, rows_total, RC):
        rows = pl.ds(r, RC)
        x, d = x_ref[rows, :], do_ref[rows, :]
        gelu, slope = gelu_parts(nn(x, wg))
        up = nn(x, wu)
        da = nt(d, wo)
        act = (gelu * up).astype(bf16)
        dg = (da * up * slope).astype(bf16)
        du = (da * gelu).astype(bf16)
        a_ref[rows, :] = act
        dg_ref[rows, :] = dg
        du_ref[rows, :] = du
        y_ref[rows, :] += nn(act, wo)
        dx_ref[rows, :] += nt(dg, wg) + nt(du, wu)
    slot = lax.rem(f, 2)

    @pl.when(f >= 2)
    def _():
        for copy in copies(slot, f - 2):
            copy.wait()

    d_rows = part // 2
    gu_ref[slot, :, 0:d_rows, :] = nn(xt_ref[...], dg_ref[...]).astype(bf16).reshape(shards, d_rows, FT)
    gu_ref[slot, :, d_rows:part, :] = nn(xt_ref[...], du_ref[...]).astype(bf16).reshape(shards, d_rows, FT)
    go = nn(dt_ref[...], a_ref[...]).T.astype(bf16)
    third = deep // 3
    for i in range(3):
        go_ref[slot, :, i * third : (i + 1) * third, :] = go[:, i * FT : (i + 1) * FT].reshape(owners, third, FT)
    for copy in copies(slot, f):
        copy.start()

    @pl.when(f == steps - 1)
    def _():
        for copy in copies(1 - slot, f - 1) + copies(slot, f):
            copy.wait()


def ffn_half(x, d_out, ffn_in, ffn_out, shards):
    rows = x.shape[0]
    tiles = FF // 2 // FT
    part = 2 * D // shards
    hs = FF // 2 // shards
    owners = FT // hs
    still = lambda f: (0, 0)
    return pl.pallas_call(
        ffn_kernel,
        grid=(tiles,),
        in_specs=[
            pl.BlockSpec((rows, D), still, pipeline_mode=pl.Buffered(1)),
            pl.BlockSpec((rows, D), still, pipeline_mode=pl.Buffered(1)),
            pl.BlockSpec((D, FT), lambda f: (0, f)),
            pl.BlockSpec((D, FT), lambda f: (0, tiles + f)),
            pl.BlockSpec((FT, D), lambda f: (f, 0)),
        ],
        out_specs=[
            pl.BlockSpec((rows, D), still, pipeline_mode=pl.Buffered(1)),
            pl.BlockSpec((rows, D), still, pipeline_mode=pl.Buffered(1)),
            pl.BlockSpec(memory_space=pl.ANY),
        ],
        out_shape=[
            jax.ShapeDtypeStruct((rows, D), f32),
            jax.ShapeDtypeStruct((rows, D), f32),
            jax.ShapeDtypeStruct((shards, tiles * part + 3 * hs, FT), bf16),
        ],
        scratch_shapes=[
            pltpu.VMEM((D, rows), bf16),
            pltpu.VMEM((D, rows), bf16),
            pltpu.VMEM((rows, FT), bf16),
            pltpu.VMEM((rows, FT), bf16),
            pltpu.VMEM((rows, FT), bf16),
            pltpu.VMEM((2, shards, part, FT), bf16),
            pltpu.VMEM((2, owners, 3 * hs, FT), bf16),
            pltpu.SemaphoreType.DMA((2, 2)),
        ],
        compiler_params=pltpu.CompilerParams(vmem_limit_bytes=58 << 20),
        cost_estimate=cost(38, 40),
        name="ffn_both_ways",
    )(x, d_out, ffn_in, ffn_in, ffn_out)


def norm_back(x, grad, gain):
    r = rms_scale(x)
    n = x * r
    u = gain * grad
    mean = jnp.sum(n * u, axis=1, keepdims=True) * (1.0 / D)
    return r * (u - n * mean), jnp.sum(n * grad, axis=0, keepdims=True)


def mid_kernel(len_ref, att_ref, y_ref, y2_ref, dx_ref, dx2_ref, do_ref, ctx_ref, w_ref, vec_ref,
               out_ref, datt_ref, dctx_ref, gw_ref, gg_ref, acc_ref):
    s = pl.program_id(0)

    @pl.when(s == 0)
    def _():
        acc_ref[...] = jnp.zeros_like(acc_ref)
        gg_ref[...] = jnp.zeros_like(gg_ref)

    att = att_ref[...]
    out_ref[...] = ((att + y_ref[...] + y2_ref[...]) * row_mask(len_ref[s])).astype(bf16)
    back, gain_grad = norm_back(att, dx_ref[...] + dx2_ref[...], vec_ref[2:3, :])
    gg_ref[...] += gain_grad
    d_att = do_ref[...].astype(f32) + back
    datt_ref[...] = d_att
    low = d_att.astype(bf16)
    dctx_ref[...] = nt(low, w_ref[...]).astype(bf16)
    acc_ref[...] += nn(ctx_ref[...].T, low)

    @pl.when(s == pl.num_programs(0) - 1)
    def _():
        gw_ref[...] = acc_ref[...].astype(bf16)


def mid_backward(lengths, att, y, y2, dx, dx2, d_out, ctx, attn_out, vecs):
    rows = att.shape[0]
    return pl.pallas_call(
        mid_kernel,
        grid_spec=pltpu.PrefetchScalarGridSpec(
            num_scalar_prefetch=1,
            grid=(rows // TOK,),
            in_specs=[rows_spec()] * 7 + [whole(D, D), whole(3, D)],
            out_specs=[rows_spec(), rows_spec(), rows_spec(), whole(D, D), whole(1, D)],
            scratch_shapes=[pltpu.VMEM((D, D), f32)],
        ),
        out_shape=[
            jax.ShapeDtypeStruct((rows, D), bf16),
            jax.ShapeDtypeStruct((rows, D), f32),
            jax.ShapeDtypeStruct((rows, D), bf16),
            jax.ShapeDtypeStruct((D, D), bf16),
            jax.ShapeDtypeStruct((1, D), f32),
        ],
        compiler_params=pltpu.CompilerParams(vmem_limit_bytes=48 << 20),
        cost_estimate=cost(14, 50),
        name="mid_backward",
    )(lengths, att, y, y2, dx, dx2, d_out, ctx, attn_out, vecs)


def qkv_back_kernel(dqkv_ref, w_ref, normed_ref, hidden_ref, datt_ref, vec_ref, dh_ref, gw_ref, gg_ref, acc_ref):
    s = pl.program_id(0)

    @pl.when(s == 0)
    def _():
        acc_ref[...] = jnp.zeros_like(acc_ref)
        gg_ref[...] = jnp.zeros_like(gg_ref)

    nt_rows = normed_ref[...].T
    dn = jnp.zeros((TOK, D), f32)
    for i in range(3):
        piece = dqkv_ref[i]
        cols = pl.ds(i * D, D)
        dn = dn + nt(piece, w_ref[:, cols])
        acc_ref[:, cols] += nn(nt_rows, piece)
    back, gain_grad = norm_back(hidden_ref[...], dn, vec_ref[1:2, :])
    gg_ref[...] += gain_grad
    dh_ref[...] = datt_ref[...] + back

    @pl.when(s == pl.num_programs(0) - 1)
    def _():
        gw_ref[...] = acc_ref[...].astype(bf16)


def qkv_backward(dqkv, attn_in, normed, hidden, d_att, vecs):
    rows = normed.shape[0]
    return pl.pallas_call(
        qkv_back_kernel,
        grid=(rows // TOK,),
        in_specs=[
            pl.BlockSpec((3, TOK, D), lambda s: (0, s, 0)),
            whole(D, 3 * D), rows_spec(), rows_spec(), rows_spec(), whole(3, D),
        ],
        out_specs=[rows_spec(), whole(D, 3 * D), whole(1, D)],
        out_shape=[
            jax.ShapeDtypeStruct((rows, D), f32),
            jax.ShapeDtypeStruct((D, 3 * D), bf16),
            jax.ShapeDtypeStruct((1, D), f32),
        ],
        scratch_shapes=[pltpu.VMEM((D, 3 * D), f32)],
        compiler_params=pltpu.CompilerParams(vmem_limit_bytes=56 << 20),
        cost_estimate=cost(22, 50),
        name="qkv_backward",
    )(dqkv, attn_in, normed, hidden, d_att, vecs)


MESH = pl.DeviceIdType.MESH


def greet(peers):
    barrier = pltpu.get_barrier_semaphore()
    for peer in peers:
        pl.semaphore_signal(barrier, inc=1, device_id=peer, device_id_type=MESH)
    pl.semaphore_wait(barrier, len(peers))


def gather_kernel(shards, own_ref, out_ref, all_ref, send_sem, recv_sem):
    rep, me = lax.axis_index("rep"), lax.axis_index("shard")
    peers = [(rep, lax.rem(me + i, shards)) for i in range(1, shards)]
    greet(peers)
    copies = []
    for i, peer in enumerate(peers):
        copy = pltpu.make_async_remote_copy(
            src_ref=own_ref, dst_ref=all_ref.at[me], send_sem=send_sem.at[i], recv_sem=recv_sem.at[i],
            device_id=peer, device_id_type=MESH)
        copy.start()
        copies.append(copy)
    all_ref[me] = own_ref[...]
    for copy in copies:
        copy.wait()
    rows = own_ref.shape[0]
    for s in range(0, shards, 2):
        pair = jnp.concatenate([all_ref[s].astype(f32), all_ref[s + 1].astype(f32)], axis=0)
        out_ref[s // 2] = pair.T.astype(bf16)


def gather_columns(own, shards):
    rows = own.shape[0]
    out = pl.pallas_call(
        lambda *refs: gather_kernel(shards, *refs),
        out_shape=jax.ShapeDtypeStruct((shards // 2, SMALL, 2 * rows), bf16),
        in_specs=[pl.BlockSpec(memory_space=pltpu.VMEM)],
        out_specs=pl.BlockSpec(memory_space=pltpu.VMEM),
        scratch_shapes=[
            pltpu.VMEM((shards, rows, SMALL), bf16),
            pltpu.SemaphoreType.DMA((shards - 1,)),
            pltpu.SemaphoreType.DMA((shards - 1,)),
        ],
        compiler_params=pltpu.CompilerParams(collective_id=1, has_side_effects=True),
        name="gather_columns",
    )(own)
    return out.transpose(1, 0, 2).reshape(SMALL, shards * rows)


def finish_kernel(replicas, shards, piece_ref, small_ref, out_ref, got_ref, held_ref, other_ref,
                  send_sem, recv_sem, send2_sem, recv2_sem):
    rep, me = lax.axis_index("rep"), lax.axis_index("shard")
    wide = piece_ref.shape[2]
    half = piece_ref.shape[1]
    bits = [1 << b for b in range(replicas.bit_length() - 1)]
    peers = [(rep, lax.rem(me + i, shards)) for i in range(1, shards)]
    partners = {}
    for bit in bits:
        down = lax.rem(rep // bit, 2)
        partners[bit] = (rep + bit - 2 * bit * down, me)
    greet(peers + [partners[bit] for bit in bits])
    copies = []
    for i, peer in enumerate(peers):
        copy = pltpu.make_async_remote_copy(
            src_ref=small_ref.at[peer[1]], dst_ref=got_ref.at[i], send_sem=send_sem.at[i],
            recv_sem=recv_sem.at[i], device_id=peer, device_id_type=MESH)
        copy.start()
        copies.append(copy)
    held_ref[0, :, :, 0:wide] = piece_ref[...]
    total = small_ref[me].astype(f32)
    for i, copy in enumerate(copies):
        copy.wait()
        total = total + got_ref[i].astype(f32)
    held_ref[0, :, :, wide:] = total.astype(bf16)
    for t in range(len(bits)):
        copies = []
        for h, order in enumerate((bits, bits[::-1])):
            copy = pltpu.make_async_remote_copy(
                src_ref=held_ref.at[t, h], dst_ref=other_ref.at[t, h], send_sem=send2_sem.at[t, h],
                recv_sem=recv2_sem.at[t, h], device_id=partners[order[t]], device_id_type=MESH)
            copy.start()
            copies.append(copy)
        for h, copy in enumerate(copies):
            copy.wait()
            total = held_ref[t, h].astype(f32) + other_ref[t, h].astype(f32)
            if t == len(bits) - 1:
                out_ref[h] = total
            else:
                held_ref[t + 1, h] = total.astype(bf16)


def finish(piece, small, replicas, shards):
    rows, wide = piece.shape
    half = rows // 2
    steps = replicas.bit_length() - 1
    vmem = pl.BlockSpec(memory_space=pltpu.VMEM)
    out = pl.pallas_call(
        lambda *refs: finish_kernel(replicas, shards, *refs),
        out_shape=jax.ShapeDtypeStruct((2, half, wide + SMALL), f32),
        in_specs=[vmem, vmem],
        out_specs=vmem,
        scratch_shapes=[
            pltpu.VMEM((shards - 1, 2, half, SMALL), bf16),
            pltpu.VMEM((steps, 2, half, wide + SMALL), bf16),
            pltpu.VMEM((steps, 2, half, wide + SMALL), bf16),
            pltpu.SemaphoreType.DMA((shards - 1,)),
            pltpu.SemaphoreType.DMA((shards - 1,)),
            pltpu.SemaphoreType.DMA((steps, 2)),
            pltpu.SemaphoreType.DMA((steps, 2)),
        ],
        compiler_params=pltpu.CompilerParams(
            collective_id=2, has_side_effects=True, vmem_limit_bytes=32 << 20),
        cost_estimate=cost(20, 4),
        name="finish_sums",
    )(piece.reshape(2, half, wide), small.reshape(shards, 2, half, SMALL))
    return out.reshape(rows, wide + SMALL)


def gather_small(embed, conv_w, score_w, gain_attn, gain_ffn, rel_table):
    shards = lax.axis_size("shard")
    width = embed.shape[1]
    table_row = jnp.pad(rel_table.reshape(1, -1), ((0, 0), (0, width - rel_table.size)))
    packed = jnp.concatenate(
        [embed, conv_w, score_w[None], gain_attn[None], gain_ffn[None], table_row], axis=0
    )
    full = gather_columns(jnp.pad(packed, ((0, SMALL - packed.shape[0]), (0, 0))).T, shards)
    taps = full[VOCAB : VOCAB + 4].astype(f32)
    vecs = full[VOCAB + 4 : VOCAB + 7].astype(f32)
    rel = full[VOCAB + 7].reshape(shards, width)[:, : rel_table.size].reshape(BUCKETS, HEADS)
    return full, taps, vecs, rel


def own_order_cotangent(target, cotangent, lengths):
    replicas = lax.axis_size("rep")
    shards = lax.axis_size("shard")
    rep = lax.axis_index("rep")
    seqs = cotangent.shape[0]
    dest_rep = target // seqs // shards
    dest_slot = target % seqs
    wanted = jnp.where(dest_rep[None, :] == jnp.arange(replicas)[:, None], dest_slot[None, :] + 1, 0).sum(axis=1)
    slots = lax.all_to_all(wanted, "rep", split_axis=0, concat_axis=0, tiled=True) - 1

    def pick(slot):
        out = cotangent[0]
        for k in range(1, seqs):
            out = jnp.where(slot == k, cotangent[k], out)
        return out

    pieces = []
    for shift in range(replicas):
        sent = pick(slots[(rep + shift) % replicas])
        if shift:
            sent = lax.ppermute(sent, "rep", [(r, (r + shift) % replicas) for r in range(replicas)])
        pieces.append(sent)
    rows = []
    for k in range(seqs):
        shift = (rep - dest_rep[k]) % replicas
        row = pieces[0]
        for j in range(1, replicas):
            row = jnp.where(shift == j, pieces[j], row)
        live = 2 * jnp.arange(TOK) < lengths[k]
        rows.append(jnp.where(live[:, None], row, jnp.zeros((), bf16)))
    return jnp.concatenate(rows, axis=0)


def butterfly(x):
    replicas = lax.axis_size("rep")
    bits = [1 << b for b in range(replicas.bit_length() - 1)]
    half = x.shape[0] // 2
    parts = []
    for piece, order in ((x[:half], bits), (x[half:], bits[::-1])):
        for bit in order:
            other = lax.ppermute(piece, "rep", [(r, r ^ bit) for r in range(replicas)])
            piece = (piece.astype(f32) + other.astype(f32)).astype(f32 if bit == order[-1] else bf16)
        parts.append(piece)
    return jnp.concatenate(parts, axis=0)


def scatter_sum(grad):
    return lax.psum_scatter(grad, "shard", scatter_dimension=0, tiled=True)


def halves_of_ffn(ffn_in, ffn_out, shards):
    hs = FF // 2 // shards
    wide = ffn_in.reshape(ffn_in.shape[0], 2, shards, 2, hs)
    return [(wide[:, :, :, h].reshape(-1, FF), ffn_out[h * hs : (h + 1) * hs]) for h in range(2)]


def ffn_shard_grads(sums, shards):
    hs = FF // 2 // shards
    deep = D // shards
    tiles = FF // 2 // FT
    first, second = [], []
    for total in sums:
        cut = tiles * 2 * deep
        cols = total[:cut].reshape(tiles, 2, deep, FT).transpose(2, 1, 0, 3)
        first.append(cols.reshape(deep, 2, shards, 1, hs))
        second.append(total[cut:].reshape(3, hs, FT).transpose(1, 0, 2).reshape(hs, D))
    return jnp.concatenate(first, axis=3).reshape(deep, 2 * FF), jnp.concatenate(second, axis=0)


def body(
    byte_ids, lengths, target, rel_bucket, cotangent, embed, conv_w, score_w, gain_attn,
    attn_in, attn_out, gain_ffn, ffn_in, ffn_out, rel_table,
):
    seqs = byte_ids.shape[0]
    rows = seqs * TOK
    shards = lax.axis_size("shard")
    width = embed.shape[1]
    table, taps, vecs, rel = gather_small(embed, conv_w, score_w, gain_attn, gain_ffn, rel_table)
    attn_in_full = lax.all_gather(attn_in, "shard", axis=0, tiled=True)
    attn_out_full = lax.all_gather(attn_out, "shard", axis=0, tiled=True)
    gathered = []
    for part_in, part_out in halves_of_ffn(ffn_in, ffn_out, shards):
        gathered.append(
            (
                lax.all_gather(part_in, "shard", axis=0, tiled=True),
                lax.all_gather(part_out, "shard", axis=0, tiled=True),
            )
        )
    d_out = own_order_cotangent(target, cotangent, lengths)
    ids_col, ids_row = byte_columns(byte_ids, lengths)
    hits = bucket_hits(rel_bucket)
    z = lax.dot_general(
        rel, hits.astype(bf16), (((0,), (0,)), ((), ())), preferred_element_type=f32
    ).reshape(HEADS, 8, SPAN)

    hidden, normed, convolved, weights = gbst_forward(lengths, ids_col, table, taps, vecs)
    qkv = jnp.dot(normed, attn_in_full, preferred_element_type=f32).astype(bf16)
    ctx, lse = attn_forward(lengths, qkv, z)
    attended, low = post_attention(ctx, attn_out_full, hidden, vecs)
    y1, dx1, g_half1 = ffn_half(low, d_out, *gathered[0], shards)
    y2, dx2, g_half2 = ffn_half(low, d_out, *gathered[1], shards)
    s_halves = [scatter_sum(g.reshape(-1, FT)) for g in (g_half1, g_half2)]
    out, d_att, d_ctx, g_attn_out, g_gain_ffn = mid_backward(
        lengths, attended, y1, y2, dx1, dx2, d_out, ctx, attn_out_full, vecs
    )
    s_attn_out = scatter_sum(g_attn_out)
    d_ctx, s_halves[0] = lax.optimization_barrier((d_ctx, s_halves[0]))
    s_halves[0] = butterfly(s_halves[0])
    dqkv, gz = attn_backward(lengths, qkv, d_ctx, ctx, lse, z)
    dqkv, s_halves = lax.optimization_barrier((dqkv, s_halves))
    s_halves[1] = butterfly(s_halves[1])
    d_hidden, g_attn, g_gain_attn = qkv_backward(
        dqkv, attn_in_full, normed, hidden, d_att, vecs
    )
    d_hidden, s_halves, s_attn_out = lax.optimization_barrier((d_hidden, s_halves, s_attn_out))
    s_attn_out = butterfly(s_attn_out)
    g_table = lax.dot_general(
        hits.astype(f32), gz.reshape(HEADS, -1), (((1,), (1,)), ((), ())),
        precision=lax.Precision.HIGHEST, preferred_element_type=f32,
    )
    per = g_table.size // shards
    table_row = jnp.pad(g_table.reshape(shards, per), ((0, 0), (0, width - per))).reshape(1, D)
    more = jnp.concatenate([g_gain_attn, g_gain_ffn, table_row], axis=0)
    p_attn_in = scatter_sum(g_attn)
    input_grad, small = gbst_backward(
        lengths, ids_col, ids_row, table, taps, vecs, d_hidden, convolved, weights, more
    )
    sums = finish(p_attn_in, small, lax.axis_size("rep"), shards)
    s_attn_in = sums[:, : 3 * D]
    s_small = sums[:, 3 * D :].T
    s_ffn_in, s_ffn_out = ffn_shard_grads(s_halves, shards)
    return (
        out.reshape(seqs, TOK, D),
        input_grad,
        s_small[:VOCAB],
        s_small[VROWS : VROWS + 4],
        s_small[VROWS + 4],
        s_small[VROWS + 5],
        s_attn_in,
        s_attn_out,
        s_small[VROWS + 6],
        s_ffn_in,
        s_ffn_out,
        s_small[VROWS + 7, :per].reshape(rel_table.shape),
    )


def solution(mesh):
    in_specs = (
        P(("rep", "shard"), None), P(("rep", "shard")), P(("rep", "shard")), P(),
        P(("rep", "shard"), None, None), P(None, "shard"), P(None, "shard"), P("shard"), P("shard"),
        P("shard", None), P("shard", None), P("shard"), P("shard", None), P("shard", None), P("shard", None),
    )
    out_specs = (
        P(("rep", "shard"), None, None), P(("rep", "shard"), None, None), P(None, "shard"), P(None, "shard"),
        P("shard"), P("shard"), P("shard", None), P("shard", None), P("shard"), P("shard", None),
        P("shard", None), P("shard", None),
    )
    return jax.shard_map(body, mesh=mesh, in_specs=in_specs, out_specs=out_specs, check_vma=False)
```

```python
import jax
import jax.numpy as jnp
from jax import lax
from jax.experimental import pallas as pl
from jax.experimental.pallas import tpu as pltpu
from jax.sharding import PartitionSpec as P

D = 768
VOCAB = 259
VPAD = 384
VROWS = 272
VMEM_LIMIT = 60 << 20
SMALL = 384
MAXLEN = 1024
TOK = 512
LANES = 128
QN = 88
R = 12
P_ROWS = QN * R
T_ROWS = 528
LT = D // LANES
epsilon = 1e-06
f32 = jnp.float32
bf16 = jnp.bfloat16


def cost(us, mib):
    return pl.CostEstimate(flops=int(us * 1e9), bytes_accessed=mib << 20, transcendentals=0)


def lane_iota(rows):
    return lax.broadcasted_iota(jnp.int32, (rows, LANES), 1)


def group_matrix(b):
    row = lax.broadcasted_iota(jnp.int32, (LANES, LANES), 0)
    col = lax.broadcasted_iota(jnp.int32, (LANES, LANES), 1)
    return jnp.where((row // b == col // b) & (row < R) & (col < R), 1.0, 0.0).astype(f32)


def exact_dot(a, b):
    return jnp.dot(a, b, precision=lax.Precision.HIGHEST, preferred_element_type=f32)


def place(columns, rows):
    lanes = lane_iota(rows)
    out = jnp.zeros((rows, LANES), f32)
    for r, column in enumerate(columns):
        out = jnp.where(lanes == r, column, out)
    return out


def gbst_masks(length):
    q = lax.broadcasted_iota(jnp.int32, (QN, LANES), 0)
    r = lax.broadcasted_iota(jnp.int32, (QN, LANES), 1)
    mask = jnp.where((q * R + r < length) & (r < R), 1.0, 0.0).astype(f32)
    inverse = [1.0 / jnp.maximum(exact_dot(mask, group_matrix(b)), 1.0) for b in (2, 3, 4)]
    pair = exact_dot(mask, group_matrix(2))
    alpha = mask / jnp.maximum(pair, 1.0)
    return mask, inverse, alpha


def gbst_weights(s1, inverse):
    sizes = [s1] + [exact_dot(s1, group_matrix(b)) * inv for b, inv in zip((2, 3, 4), inverse)]
    top = jnp.maximum(jnp.maximum(sizes[0], sizes[1]), jnp.maximum(sizes[2], sizes[3]))
    parts = [jnp.exp(s - top) for s in sizes]
    total = parts[0] + parts[1] + parts[2] + parts[3]
    return [p / total for p in parts]


def gbst_coefs(weights, inverse, alpha):
    a1 = weights[0] * alpha
    a2 = weights[1] * alpha * inverse[0]
    a3 = weights[2] * alpha * inverse[1]
    a4 = weights[3] * alpha * inverse[2]
    pair = group_matrix(2)
    a4s = exact_dot(a4, pair)
    own = a1 + exact_dot(a2, pair) + a4s
    return own, a3, a4s


def column(x, r):
    return jnp.broadcast_to(x[:, r : r + 1], (x.shape[0], LANES))


def hits_of(ids_col):
    lanes = lax.broadcasted_iota(jnp.int32, (P_ROWS, VPAD), 1)
    return jnp.where(ids_col == lanes, 1.0, 0.0).astype(bf16)


def load_e(e_ref, r, lt):
    lanes = pl.ds(lt * LANES, LANES)
    if r < R:
        return e_ref[pl.ds(r * QN, QN), lanes]
    return e_ref[pl.ds((r - R) * QN + 1, QN), lanes]


def gbst_fwd_kernel(len_ref, ids_ref, table_ref, conv_ref, vec_ref, hidden_ref, normed_ref, turned_ref, c_ref, w_ref, e_ref, hid_ref, s_ref, k_ref):
    length = len_ref[pl.program_id(0)]
    hits = hits_of(ids_ref[0])
    e_ref[pl.ds(0, P_ROWS), :] = jnp.dot(hits, table_ref[...], preferred_element_type=f32)
    e_ref[pl.ds(P_ROWS, 8), :] = jnp.zeros((8, D), f32)
    for lt in range(LT):
        lanes = pl.ds(lt * LANES, LANES)
        taps = [jnp.broadcast_to(conv_ref[j : j + 1, lanes], (QN, LANES)) for j in range(4)]
        sw = jnp.broadcast_to(vec_ref[0:1, lanes], (QN, LANES))
        for r in range(R):
            c = taps[0] * load_e(e_ref, r, lt)
            for j in range(1, 4):
                c = c + taps[j] * load_e(e_ref, r + j, lt)
            c_ref[0, pl.ds(r * QN, QN), lanes] = c
            part = c * sw
            rows = pl.ds(r * QN, QN)
            s_ref[rows, :] = part if lt == 0 else s_ref[rows, :] + part
    s1 = place([jnp.sum(s_ref[pl.ds(r * QN, QN), :], axis=1, keepdims=True) for r in range(R)], QN)
    mask, inverse, alpha = gbst_masks(length)
    weights = gbst_weights(s1, inverse)
    for b in range(4):
        w_ref[0, b] = weights[b]
    own, a3, a4s = gbst_coefs(weights, inverse, alpha)
    n = 0
    for r in range(R):
        k_ref[r] = column(own, r)
        k_ref[R + r] = column(a3, r)
    for k in range(6):
        k_ref[2 * R + k] = column(a4s, 2 * k)
    for lt in range(LT):
        lanes = pl.ds(lt * LANES, LANES)
        for half in range(2):
            c = [c_ref[0, pl.ds((half * 6 + r) * QN, QN), lanes] for r in range(6)]
            base = half * 6
            s3 = [c[0] + c[1] + c[2], c[3] + c[4] + c[5]]
            for k in range(3):
                tok = half * 3 + k
                other = tok ^ 1
                rows = pl.ds(2 * other * QN, QN)
                rows1 = pl.ds((2 * other + 1) * QN, QN)
                s2 = c_ref[0, rows, lanes] + c_ref[0, rows1, lanes]
                h = k_ref[2 * tok] * c[2 * k] + k_ref[2 * tok + 1] * c[2 * k + 1] + k_ref[2 * R + tok] * s2
                if k == 1:
                    h = h + k_ref[R + 2 * tok] * s3[0] + k_ref[R + 2 * tok + 1] * s3[1]
                else:
                    h = h + (k_ref[R + 2 * tok] + k_ref[R + 2 * tok + 1]) * s3[0 if k == 0 else 1]
                hid_ref[lt, pl.ds(tok, QN, stride=6), :] = h
    total = jnp.zeros((TOK, LANES), f32)
    for lt in range(LT):
        x = hid_ref[lt, 0:TOK, :]
        total = total + x * x
    scale = lax.rsqrt(jnp.sum(total, axis=1, keepdims=True) * (1.0 / D) + epsilon)
    for lt in range(LT):
        lanes = pl.ds(lt * LANES, LANES)
        x = hid_ref[lt, 0:TOK, :]
        hidden_ref[:, lanes] = x
        normed = (x * scale * vec_ref[1:2, lanes]).astype(bf16)
        normed_ref[:, lanes] = normed
        turned_ref[lanes, :] = normed.T


def gbst_forward(lengths, ids_col, table, conv_w, vecs):
    seqs = ids_col.shape[0]
    grid_spec = pltpu.PrefetchScalarGridSpec(
        num_scalar_prefetch=1,
        grid=(seqs,),
        in_specs=[
            pl.BlockSpec((1, P_ROWS, 1), lambda s, n: (s, 0, 0)),
            pl.BlockSpec((VPAD, D), lambda s, n: (0, 0)),
            pl.BlockSpec((4, D), lambda s, n: (0, 0)),
            pl.BlockSpec((3, D), lambda s, n: (0, 0)),
        ],
        out_specs=[
            pl.BlockSpec((TOK, D), lambda s, n: (s, 0)),
            pl.BlockSpec((TOK, D), lambda s, n: (s, 0)),
            pl.BlockSpec((D, TOK), lambda s, n: (0, s)),
            pl.BlockSpec((1, P_ROWS, D), lambda s, n: (s, 0, 0)),
            pl.BlockSpec((1, 4, QN, LANES), lambda s, n: (s, 0, 0, 0)),
        ],
        scratch_shapes=[
            pltpu.VMEM((P_ROWS + 8, D), f32),
            pltpu.VMEM((LT, T_ROWS, LANES), f32),
            pltpu.VMEM((P_ROWS, LANES), f32),
            pltpu.VMEM((2 * R + 6, QN, LANES), f32),
        ],
    )
    return pl.pallas_call(
        gbst_fwd_kernel,
        grid_spec=grid_spec,
        out_shape=[
            jax.ShapeDtypeStruct((seqs * TOK, D), f32),
            jax.ShapeDtypeStruct((seqs * TOK, D), bf16),
            jax.ShapeDtypeStruct((D, seqs * TOK), bf16),
            jax.ShapeDtypeStruct((seqs, P_ROWS, D), f32),
            jax.ShapeDtypeStruct((seqs, 4, QN, LANES), f32),
        ],
        compiler_params=pltpu.CompilerParams(vmem_limit_bytes=VMEM_LIMIT),
        cost_estimate=cost(18, 30),
        name="gbst_forward",
    )(lengths, ids_col, table, conv_w, vecs)


def gbst_bwd_kernel(len_ref, ids_ref, row_ref, table_ref, conv_ref, vec_ref, dh_ref, c_ref, w_ref, more_ref,
                    ig_ref, small_ref, ge_ref, e_ref, dt_ref, dc_ref, s_ref, k_ref, igs_ref):
    seq = pl.program_id(0)
    length = len_ref[seq]

    @pl.when(seq == 0)
    def _():
        ge_ref[...] = jnp.zeros_like(ge_ref)

    hits = hits_of(ids_ref[0])
    e_ref[pl.ds(0, P_ROWS), :] = jnp.dot(hits, table_ref[...], preferred_element_type=f32)
    e_ref[pl.ds(P_ROWS, 8), :] = jnp.zeros((8, D), f32)
    for lt in range(LT):
        dt_ref[lt, 0:TOK, :] = dh_ref[:, pl.ds(lt * LANES, LANES)]
        dt_ref[lt, TOK:T_ROWS, :] = jnp.zeros((T_ROWS - TOK, LANES), f32)
    for lt in range(LT):
        lanes = pl.ds(lt * LANES, LANES)
        for half in range(2):
            c = [c_ref[0, pl.ds((half * 6 + r) * QN, QN), lanes] for r in range(6)]
            s3 = [c[0] + c[1] + c[2], c[3] + c[4] + c[5]]
            for k in range(3):
                tok = half * 3 + k
                other = tok ^ 1
                dh = dt_ref[lt, pl.ds(tok, QN, stride=6), :]
                s2 = c_ref[0, pl.ds(2 * other * QN, QN), lanes] + c_ref[0, pl.ds((2 * other + 1) * QN, QN), lanes]
                parts = [
                    (2 * tok, dh * c[2 * k]),
                    (2 * tok + 1, dh * c[2 * k + 1]),
                    (2 * R + tok, dh * s2),
                    (R + 2 * tok, dh * s3[0 if k < 2 else 1]),
                ]
                if k == 1:
                    parts.append((R + 2 * tok + 1, dh * s3[1]))
                for slot, part in parts:
                    s_ref[slot] = part if lt == 0 else s_ref[slot] + part

    def total(slot):
        return jnp.sum(s_ref[slot], axis=1, keepdims=True)

    d1, d3, dother = [], [], []
    for tok in range(6):
        d1 += [total(2 * tok), total(2 * tok + 1)]
        first = total(R + 2 * tok)
        d3 += [first, total(R + 2 * tok + 1) if tok % 3 == 1 else first]
        o = total(2 * R + tok)
        dother += [o, o]
    d1, d3, dother = place(d1, QN), place(d3, QN), place(dother, QN)
    mask, inverse, alpha = gbst_masks(length)
    weights = [w_ref[0, b] for b in range(4)]
    d2 = exact_dot(d1, group_matrix(2))
    g = [alpha * d1, alpha * d2 * inverse[0], alpha * d3 * inverse[1], alpha * (d2 + dother) * inverse[2]]
    mean = weights[0] * g[0] + weights[1] * g[1] + weights[2] * g[2] + weights[3] * g[3]
    d_size = [w * (x - mean) for w, x in zip(weights, g)]
    coef = d_size[0]
    for b, inv in zip((2, 3, 4), inverse):
        coef = coef + exact_dot(d_size[b - 1] * inv, group_matrix(b))
    own, a3, a4s = gbst_coefs(weights, inverse, alpha)
    for r in range(R):
        k_ref[r] = column(own, r)
        k_ref[R + r] = column(a3, r)
        k_ref[2 * R + r] = column(coef, r)
        k_ref[3 * R + r] = column(mask, r)
    for k in range(6):
        k_ref[4 * R + k] = column(a4s, 2 * k)

    for lt in range(LT):
        lanes = pl.ds(lt * LANES, LANES)
        taps = [jnp.broadcast_to(conv_ref[j : j + 1, lanes], (QN, LANES)) for j in range(4)]
        sw = jnp.broadcast_to(vec_ref[0:1, lanes], (QN, LANES))
        gs = jnp.zeros((QN, LANES), f32)
        gc = [jnp.zeros((QN, LANES), f32) for _ in range(4)]
        for half in range(2):
            dh = [dt_ref[lt, pl.ds(half * 3 + k, QN, stride=6), :] for k in range(3)]
            a = R + half * 6
            t3 = [
                (k_ref[a] + k_ref[a + 1]) * dh[0] + k_ref[a + 2] * dh[1],
                k_ref[a + 3] * dh[1] + (k_ref[a + 4] + k_ref[a + 5]) * dh[2],
            ]
            for k in range(3):
                tok = half * 3 + k
                other = tok ^ 1
                dother_h = dt_ref[lt, pl.ds(other, QN, stride=6), :]
                cross = k_ref[4 * R + other] * dother_h
                for e in range(2):
                    r = 2 * tok + e
                    cf = k_ref[2 * R + r]
                    dc = k_ref[r] * dh[k] + cross + t3[(r % 6) // 3] + cf * sw
                    gs = gs + cf * c_ref[0, pl.ds(r * QN, QN), lanes]
                    dc_ref[r, pl.ds(8, QN), :] = dc
                    for j in range(4):
                        gc[j] = gc[j] + dc * load_e(e_ref, r + j, lt)
        ge_ref[VROWS + 4 : VROWS + 5, lanes] += jnp.sum(gs, axis=0, keepdims=True)
        for j in range(4):
            ge_ref[VROWS + j : VROWS + j + 1, lanes] += jnp.sum(gc[j], axis=0, keepdims=True)
        for r in range(R):
            dc_ref[r, 0:8, :] = jnp.zeros((8, LANES), f32)
        for r in range(R):
            x = taps[0] * dc_ref[r, pl.ds(8, QN), :]
            for j in range(1, 4):
                back = dc_ref[r - j, pl.ds(8, QN), :] if r >= j else dc_ref[r - j + R, pl.ds(7, QN), :]
                x = x + taps[j] * back
            igs_ref[lt, pl.ds(r, QN, stride=R), :] = x * k_ref[3 * R + r]
    for lt in range(LT):
        lanes = pl.ds(lt * LANES, LANES)
        ig_ref[0, :, lanes] = igs_ref[lt, 0:MAXLEN, :].astype(bf16)
    vocab = lax.broadcasted_iota(jnp.int32, (VROWS, MAXLEN), 0)
    row_hits = jnp.where(vocab == row_ref[0], 1.0, 0.0).astype(bf16)
    ge_ref[0:VROWS, :] += jnp.dot(row_hits, ig_ref[0], preferred_element_type=f32)

    @pl.when(seq == pl.num_programs(0) - 1)
    def _():
        ge_ref[VROWS + 5 : VROWS + 8, :] = more_ref[...]
        for lt in range(LT):
            lanes = pl.ds(lt * LANES, LANES)
            small_ref[lanes, :] = ge_ref[:, lanes].T.astype(bf16)


def gbst_backward(lengths, ids_col, ids_row, table, conv_w, vecs, d_hidden, c, w, more):
    seqs = ids_col.shape[0]
    grid_spec = pltpu.PrefetchScalarGridSpec(
        num_scalar_prefetch=1,
        grid=(seqs,),
        in_specs=[
            pl.BlockSpec((1, P_ROWS, 1), lambda s, n: (s, 0, 0)),
            pl.BlockSpec((1, 1, MAXLEN), lambda s, n: (s, 0, 0)),
            pl.BlockSpec((VPAD, D), lambda s, n: (0, 0)),
            pl.BlockSpec((4, D), lambda s, n: (0, 0)),
            pl.BlockSpec((3, D), lambda s, n: (0, 0)),
            pl.BlockSpec((TOK, D), lambda s, n: (s, 0)),
            pl.BlockSpec((1, P_ROWS, D), lambda s, n: (s, 0, 0)),
            pl.BlockSpec((1, 4, QN, LANES), lambda s, n: (s, 0, 0, 0)),
            pl.BlockSpec((3, D), lambda s, n: (0, 0)),
        ],
        out_specs=[
            pl.BlockSpec((1, MAXLEN, D), lambda s, n: (s, 0, 0)),
            pl.BlockSpec((D, SMALL), lambda s, n: (0, 0)),
        ],
        scratch_shapes=[
            pltpu.VMEM((SMALL, D), f32),
            pltpu.VMEM((P_ROWS + 8, D), f32),
            pltpu.VMEM((LT, T_ROWS, LANES), f32),
            pltpu.VMEM((R, QN + 8, LANES), f32),
            pltpu.VMEM((2 * R + 6, QN, LANES), f32),
            pltpu.VMEM((4 * R + 6, QN, LANES), f32),
            pltpu.VMEM((LT, P_ROWS, LANES), f32),
        ],
    )
    return pl.pallas_call(
        gbst_bwd_kernel,
        grid_spec=grid_spec,
        out_shape=[
            jax.ShapeDtypeStruct((seqs, MAXLEN, D), bf16),
            jax.ShapeDtypeStruct((D, SMALL), bf16),
        ],
        compiler_params=pltpu.CompilerParams(vmem_limit_bytes=VMEM_LIMIT),
        cost_estimate=cost(31, 40),
        name="gbst_backward",
    )(lengths, ids_col, ids_row, table, conv_w, vecs, d_hidden, c, w, more)


def byte_columns(byte_ids, lengths):
    seqs = byte_ids.shape[0]
    live = jnp.arange(MAXLEN)[None, :] < lengths[:, None]
    ids = jnp.where(live, byte_ids, -1)
    wide = jnp.pad(ids, ((0, 0), (0, P_ROWS - MAXLEN)), constant_values=-1)
    ids_col = wide.reshape(seqs, QN, R).transpose(0, 2, 1).reshape(seqs, P_ROWS, 1)
    return ids_col, ids.reshape(seqs, 1, MAXLEN)


HEADS = 12
HD = 64
BUCKETS = 32
SPAN = 1024
HB = 4
WIDE = HB * HD
GROUPS = HEADS // HB
dead_score = -1e9


def nt(a, b):
    return lax.dot_general(a, b, (((1,), (1,)), ((), ())), preferred_element_type=f32)


def nn(a, b):
    return jnp.dot(a, b, preferred_element_type=f32)


def bucket_rows(buckets):
    back = jnp.pad(buckets, (8, 0))
    rows = [
        jnp.concatenate([back[8 + TOK - 1 - s : 8 + 2 * TOK - 1 - s], back[7 - s : 7 - s + TOK]])
        for s in range(8)
    ]
    return jnp.concatenate(rows)


def bucket_hits(buckets):
    return jnp.arange(BUCKETS)[:, None] == bucket_rows(buckets)[None, :]


def build_bias(z_ref, bt_ref):
    for h in range(HB):
        z = z_ref[h]
        for g in range(TOK // 8):
            bt_ref[h, pl.ds(8 * g, 8), :] = (z if g == 0 else pltpu.roll(z, 8 * g, 1))[:, :TOK]


def own_lanes(h):
    return lax.broadcasted_iota(jnp.int32, (TOK, WIDE), 1) // HD == h


def head_parts(k, q, length, h):
    lanes = lax.broadcasted_iota(jnp.int32, (TOK, WIDE), 1)
    rows = lax.broadcasted_iota(jnp.int32, (TOK, WIDE), 0)
    spare = HD * (h + 1) % WIDE
    dead = jnp.where(2 * rows < length, 0.0, dead_score)
    kf = jnp.where(lanes // HD == h, k.astype(f32), jnp.where(lanes == spare, dead, 0.0)).astype(bf16)
    qf = jnp.where(lanes == spare, 1.0, q.astype(f32)).astype(bf16)
    return kf, qf


def join_heads(parts):
    out = parts[0]
    for h in range(1, HB):
        out = jnp.where(own_lanes(h), parts[h], out)
    return out.astype(bf16)


def attn_fwd_kernel(len_ref, q_ref, k_ref, v_ref, z_ref, ctx_ref, lse_ref, bias_ref):
    length = len_ref[pl.program_id(1)]

    @pl.when(pl.program_id(1) == 0)
    def _():
        build_bias(z_ref, bias_ref)

    q, k, v = q_ref[...], k_ref[...], v_ref[...]

    def score(h):
        kf, qf = head_parts(k, q, length, h)
        return nt(qf, kf) + bias_ref[h]

    outs = []
    lanes = lax.broadcasted_iota(jnp.int32, (TOK, LANES), 1)
    lse = jnp.zeros((TOK, LANES), f32)
    s = score(0)
    for h in range(HB):
        later = score(h + 1) if h + 1 < HB else None
        top = jnp.max(s, axis=1, keepdims=True)
        p = jnp.exp(s - top)
        total = jnp.sum(p, axis=1, keepdims=True)
        outs.append(nn(p.astype(bf16), v) * (1.0 / total))
        lse = jnp.where(lanes == h, top + jnp.log(total), lse)
        s = later
    ctx_ref[...] = join_heads(outs)
    lse_ref[0, 0] = lse.T[0:8]


def attn_forward(lengths, qkv, z):
    seqs = qkv.shape[0] // TOK
    spec = lambda off: pl.BlockSpec((TOK, WIDE), lambda hp, s, n: (s, off + hp))
    return pl.pallas_call(
        attn_fwd_kernel,
        grid_spec=pltpu.PrefetchScalarGridSpec(
            num_scalar_prefetch=1,
            grid=(GROUPS, seqs),
            in_specs=[spec(0), spec(GROUPS), spec(2 * GROUPS), pl.BlockSpec((HB, 8, SPAN), lambda hp, s, n: (hp, 0, 0))],
            out_specs=[spec(0), pl.BlockSpec((1, 1, 8, TOK), lambda hp, s, n: (hp, s, 0, 0))],
            scratch_shapes=[pltpu.VMEM((HB, TOK, TOK), f32)],
        ),
        out_shape=[
            jax.ShapeDtypeStruct((seqs * TOK, D), bf16),
            jax.ShapeDtypeStruct((GROUPS, seqs, 8, TOK), f32),
        ],
        compiler_params=pltpu.CompilerParams(vmem_limit_bytes=VMEM_LIMIT),
        cost_estimate=cost(27, 20),
        name="attn_forward",
    )(lengths, qkv, qkv, qkv, z)


def attn_bwd_kernel(len_ref, q_ref, k_ref, v_ref, do_ref, o_ref, lse_ref, z_ref, dqkv_ref, gz_ref, bt_ref, g_ref):
    s_id = pl.program_id(1)
    length = len_ref[s_id]

    @pl.when(s_id == 0)
    def _():
        build_bias(z_ref, bt_ref)
        g_ref[...] = jnp.zeros_like(g_ref)

    q, k, v, do = q_ref[...], k_ref[...], v_ref[...], do_ref[...]
    kt = k.astype(f32).T.astype(bf16)
    lanes8 = lax.broadcasted_iota(jnp.int32, (8, WIDE), 1)
    rows8 = lax.broadcasted_iota(jnp.int32, (8, WIDE), 0)
    pick = jnp.where(lanes8 // HD == rows8, 1.0, 0.0).astype(bf16)
    prod = do.astype(f32) * o_ref[...].astype(f32)
    upper = prod.astype(bf16)
    delta = nt(pick, upper) + nt(pick, (prod - upper.astype(f32)).astype(bf16))
    dq, dk, dv = [], [], []

    def first(h):
        kf, qf = head_parts(k, q, length, h)
        vf = jnp.where(own_lanes(h), v.astype(f32), 0.0).astype(bf16)
        return nt(kf, qf) + bt_ref[h], nt(vf, do)

    now = first(0)
    for h in range(HB):
        later = first(h + 1) if h + 1 < HB else None
        s, d_prob = now
        p = jnp.exp(s - lse_ref[0, 0, h : h + 1, :])
        ds = p * (d_prob - delta[h : h + 1, :])
        g_ref[h] += ds
        low = ds.astype(bf16)
        dv.append(nn(p.astype(bf16), do))
        dk.append(nn(low, q))
        dq.append(nn(kt[h * HD : (h + 1) * HD], low))
        now = later
    dqkv_ref[0] = jnp.concatenate(dq, axis=0).T.astype(bf16)
    dqkv_ref[1] = join_heads(dk)
    dqkv_ref[2] = join_heads(dv)

    @pl.when(s_id == pl.num_programs(1) - 1)
    def _():
        for h in range(HB):
            total = jnp.zeros((8, SPAN), f32)
            for g in range(LANES // 8):
                tiles = [jnp.zeros((8, LANES), f32) for _ in range(SPAN // LANES)]
                for j in range(TOK // LANES):
                    x = g_ref[h, pl.ds(LANES * j + 8 * g, 8), :]
                    for t in range(TOK // LANES):
                        n = (t - j) % (SPAN // LANES)
                        tiles[n] = tiles[n] + x[:, t * LANES : (t + 1) * LANES]
                piece = jnp.concatenate(tiles, axis=1)
                total = total + (piece if g == 0 else pltpu.roll(piece, SPAN - 8 * g, 1))
            gz_ref[h] = total


def attn_backward(lengths, qkv, d_ctx, ctx, lse, z):
    seqs = qkv.shape[0] // TOK
    spec = lambda off: pl.BlockSpec((TOK, WIDE), lambda hp, s, n: (s, off + hp))
    return pl.pallas_call(
        attn_bwd_kernel,
        grid_spec=pltpu.PrefetchScalarGridSpec(
            num_scalar_prefetch=1,
            grid=(GROUPS, seqs),
            in_specs=[
                spec(0), spec(GROUPS), spec(2 * GROUPS), spec(0), spec(0),
                pl.BlockSpec((1, 1, 8, TOK), lambda hp, s, n: (hp, s, 0, 0)),
                pl.BlockSpec((HB, 8, SPAN), lambda hp, s, n: (hp, 0, 0)),
            ],
            out_specs=[
                pl.BlockSpec((3, TOK, WIDE), lambda hp, s, n: (0, s, hp)),
                pl.BlockSpec((HB, 8, SPAN), lambda hp, s, n: (hp, 0, 0)),
            ],
            scratch_shapes=[pltpu.VMEM((HB, TOK, TOK), f32), pltpu.VMEM((HB, TOK, TOK), f32)],
        ),
        out_shape=[
            jax.ShapeDtypeStruct((3, seqs * TOK, D), bf16),
            jax.ShapeDtypeStruct((HEADS, 8, SPAN), f32),
        ],
        compiler_params=pltpu.CompilerParams(vmem_limit_bytes=VMEM_LIMIT),
        cost_estimate=cost(46, 30),
        name="attn_backward",
    )(lengths, qkv, qkv, qkv, d_ctx, ctx, lse, z)


FF = 2048
FT = 256
RC = 512
MT = 256


def rms_scale(x):
    return lax.rsqrt(jnp.sum(x * x, axis=1, keepdims=True) * (1.0 / D) + epsilon)


def post_kernel(ctx_ref, w_ref, hidden_ref, vec_ref, do_ref, att_ref, low_ref, low_t_ref, do_t_ref):
    att = hidden_ref[...] + nn(ctx_ref[...], w_ref[...])
    att_ref[...] = att
    low = (att * rms_scale(att) * vec_ref[2:3, :]).astype(bf16)
    low_ref[...] = low
    low_t_ref[...] = low.T
    do_t_ref[...] = do_ref[...].T


def rows_spec(width=D):
    return pl.BlockSpec((TOK, width), lambda s, *n: (s, 0))


def whole(*shape):
    return pl.BlockSpec(shape, lambda s, *n: (0,) * len(shape))


def out_block():
    return pl.BlockSpec((D, D), lambda s, *n: (0, 3))


def post_attention(ctx, attn_w, hidden, vecs, d_out):
    rows = ctx.shape[0]
    cols_spec = pl.BlockSpec((D, TOK), lambda s: (0, s))
    return pl.pallas_call(
        post_kernel,
        grid=(rows // TOK,),
        in_specs=[rows_spec(), out_block(), rows_spec(), whole(3, D), rows_spec()],
        out_specs=[rows_spec(), rows_spec(), cols_spec, cols_spec],
        out_shape=[
            jax.ShapeDtypeStruct((rows, D), f32),
            jax.ShapeDtypeStruct((rows, D), bf16),
            jax.ShapeDtypeStruct((D, rows), bf16),
            jax.ShapeDtypeStruct((D, rows), bf16),
        ],
        compiler_params=pltpu.CompilerParams(vmem_limit_bytes=VMEM_LIMIT),
        cost_estimate=cost(6, 30),
        name="post_attention",
    )(ctx, attn_w, hidden, vecs, d_out)


def gelu_parts(v):
    c = 0.7978845608
    v2 = v * v
    t = jnp.tanh(v * (c + (c * 0.044715) * v2))
    half = 0.5 + 0.5 * t
    gelu = v * half
    slope = half + (0.5 * v) * (1.0 - t * t) * (c + (3.0 * c * 0.044715) * v2)
    return gelu, slope


def ffn_steps(x_any, d_any, xt_any, dt_any, wgu_ref, wo_ref, grad_ref, y_any, dx_any,
              x_ref, d_ref, xt_ref, dt_ref, y_ref, dx_ref, a_ref, dg_ref, du_ref, gu_ref, go_ref, in_sem, out_sem, sems):
    f = pl.program_id(0)
    steps = FF // 2 // FT
    rows_total = x_ref.shape[0]
    chunks = rows_total // RC
    shards, part = gu_ref.shape[1], gu_ref.shape[2]
    owners, deep = go_ref.shape[1], go_ref.shape[2]
    base = steps * part

    def copies(slot, step):
        return (
            pltpu.make_async_copy(
                gu_ref.at[slot], grad_ref.at[:, pl.ds(step * part, part), :], sems.at[0, slot]),
            pltpu.make_async_copy(
                go_ref.at[slot], grad_ref.at[pl.ds(step * owners, owners), pl.ds(base, deep), :], sems.at[1, slot]),
        )

    def row_loads(i):
        rows = pl.ds(i * RC, RC)
        return (
            pltpu.make_async_copy(x_any.at[rows], x_ref.at[rows], in_sem.at[0, i]),
            pltpu.make_async_copy(d_any.at[rows], d_ref.at[rows], in_sem.at[1, i]),
        )

    def turned_loads():
        return (
            pltpu.make_async_copy(xt_any, xt_ref, in_sem.at[2, 0]),
            pltpu.make_async_copy(dt_any, dt_ref, in_sem.at[2, 1]),
        )

    def row_stores(i):
        rows = pl.ds(i * RC, RC)
        return (
            pltpu.make_async_copy(y_ref.at[rows], y_any.at[rows], out_sem.at[0, i]),
            pltpu.make_async_copy(dx_ref.at[rows], dx_any.at[rows], out_sem.at[1, i]),
        )

    @pl.when(f == 0)
    def _():
        for i in range(chunks):
            for copy in row_loads(i):
                copy.start()
        for copy in turned_loads():
            copy.start()
        y_ref[...] = jnp.zeros_like(y_ref)
        dx_ref[...] = jnp.zeros_like(dx_ref)

    d_rows = part // 2
    third = deep // 3
    wg = wgu_ref[:, 0:d_rows, :].reshape(D, FT)
    wu = wgu_ref[:, d_rows:part, :].reshape(D, FT)
    wo = jnp.concatenate(
        [wo_ref[:, i * third : (i + 1) * third, :].reshape(FT, FT) for i in range(3)], axis=1)

    @pl.when(f == 0)
    def _():
        for i in range(chunks):
            for copy in row_loads(i):
                copy.wait()

    for i in range(chunks):
        rows = pl.ds(i * RC, RC)
        x, d = x_ref[rows, :], d_ref[rows, :]
        gelu, slope = gelu_parts(nn(x, wg))
        up = nn(x, wu)
        da = nt(d, wo)
        act = (gelu * up).astype(bf16)
        dg = (da * up * slope).astype(bf16)
        du = (da * gelu).astype(bf16)
        a_ref[rows, :] = act
        dg_ref[rows, :] = dg
        du_ref[rows, :] = du
        y_ref[rows, :] += nn(act, wo)
        dx_ref[rows, :] += nt(dg, wg) + nt(du, wu)
    if y_any is not None:

        @pl.when(f == steps - 1)
        def _():
            for i in range(chunks):
                for copy in row_stores(i):
                    copy.start()

    slot = lax.rem(f, 2)

    @pl.when(f == 0)
    def _():
        for copy in turned_loads():
            copy.wait()

    @pl.when(f >= 2)
    def _():
        for copy in copies(slot, f - 2):
            copy.wait()

    gu_ref[slot, :, 0:d_rows, :] = nn(xt_ref[...], dg_ref[...]).astype(bf16).reshape(shards, d_rows, FT)
    gu_ref[slot, :, d_rows:part, :] = nn(xt_ref[...], du_ref[...]).astype(bf16).reshape(shards, d_rows, FT)
    go = nn(dt_ref[...], a_ref[...]).T.astype(bf16)
    for i in range(3):
        go_ref[slot, :, i * third : (i + 1) * third, :] = go[:, i * FT : (i + 1) * FT].reshape(owners, third, FT)
    for copy in copies(slot, f):
        copy.start()

    @pl.when(f == steps - 1)
    def _():
        for copy in copies(1 - slot, f - 1) + copies(slot, f):
            copy.wait()
        if y_any is not None:
            for i in range(chunks):
                for copy in row_stores(i):
                    copy.wait()


def first_kernel(x, d, xt, dt, wgu, wo, grad, y, dx, *scratch):
    ffn_steps(x, d, xt, dt, wgu, wo, grad, y, dx, *scratch)


def second_kernel(len_ref, x, d, xt, dt, wgu, wo, att_ref, y1_ref, dx1_ref, do_ref, ctx_ref, w_ref, vec_ref,
                  grad, out_ref, datt_ref, dctx_ref, gw_ref, gg_ref, acc_ref, *scratch):
    f = pl.program_id(0)
    steps = FF // 2 // FT

    @pl.when(f == 0)
    def _():
        acc_ref[...] = jnp.zeros_like(acc_ref)
        gg_ref[...] = jnp.zeros_like(gg_ref)

    @pl.when(f < steps)
    def _():
        ffn_steps(x, d, xt, dt, wgu, wo, grad, None, None, *scratch)

    @pl.when(f >= steps)
    def _():
        tile = f - steps
        y_ref, dx_ref = scratch[4], scratch[5]
        rows = pl.ds(pl.multiple_of(tile * MT, MT), MT)
        per = TOK // MT
        length = len_ref[tile // per]
        place_in = lax.rem(tile, per) * MT + lax.broadcasted_iota(jnp.int32, (MT, 1), 0)
        live = jnp.where(2 * place_in < length, 1.0, 0.0).astype(f32)
        att = att_ref[...]
        out_ref[...] = ((att + y1_ref[...] + y_ref[rows, :]) * live).astype(bf16)
        back, gain_grad = norm_back(att, dx1_ref[...] + dx_ref[rows, :], vec_ref[2:3, :])
        gg_ref[...] += gain_grad
        d_att = do_ref[...].astype(f32) + back
        datt_ref[...] = d_att
        low = d_att.astype(bf16)
        dctx_ref[...] = nt(low, w_ref[...]).astype(bf16)
        acc_ref[...] += nn(ctx_ref[...].T, low)

    @pl.when(f == pl.num_programs(0) - 1)
    def _():
        gw_ref[...] = acc_ref[...].astype(bf16)


def ffn_scratch(rows, shards):
    part, hs = 2 * D // shards, FF // 2 // shards
    return [
        pltpu.VMEM((rows, D), bf16),
        pltpu.VMEM((rows, D), bf16),
        pltpu.VMEM((D, rows), bf16),
        pltpu.VMEM((D, rows), bf16),
        pltpu.VMEM((rows, D), f32),
        pltpu.VMEM((rows, D), f32),
        pltpu.VMEM((rows, FT), bf16),
        pltpu.VMEM((rows, FT), bf16),
        pltpu.VMEM((rows, FT), bf16),
        pltpu.VMEM((2, shards, part, FT), bf16),
        pltpu.VMEM((2, FT // hs, 3 * hs, FT), bf16),
        pltpu.SemaphoreType.DMA((3, max(2, rows // RC))),
        pltpu.SemaphoreType.DMA((2, rows // RC)),
        pltpu.SemaphoreType.DMA((2, 2)),
    ]


def ffn_specs(tiles, shards):
    last = lambda f: jnp.minimum(f, tiles - 1)
    part, hs = 2 * D // shards, FF // 2 // shards
    return [pl.BlockSpec(memory_space=pl.ANY)] * 4 + [
        pl.BlockSpec((shards, part, FT), lambda f, *n: (0, last(f), 0)),
        pl.BlockSpec((FT // hs, 3 * hs, FT), lambda f, *n: (last(f), 2, 0)),
    ]


def grad_shape(shards):
    part, hs = 2 * D // shards, FF // 2 // shards
    return jax.ShapeDtypeStruct((shards, FF // 2 // FT * part + 3 * hs, FT), bf16)


def ffn_first(x, d_out, xt, dt, pack, shards):
    rows = x.shape[0]
    tiles = FF // 2 // FT
    anywhere = pl.BlockSpec(memory_space=pl.ANY)
    return pl.pallas_call(
        first_kernel,
        grid=(tiles,),
        in_specs=ffn_specs(tiles, shards),
        out_specs=[anywhere] * 3,
        out_shape=[
            grad_shape(shards),
            jax.ShapeDtypeStruct((rows, D), f32),
            jax.ShapeDtypeStruct((rows, D), f32),
        ],
        scratch_shapes=ffn_scratch(rows, shards),
        compiler_params=pltpu.CompilerParams(vmem_limit_bytes=VMEM_LIMIT),
        cost_estimate=cost(36, 40),
        name="ffn_first",
    )(x, d_out, xt, dt, pack, pack)


def ffn_second(lengths, x, d_out, xt, dt, pack, att, y1, dx1, ctx, attn_w, vecs, shards):
    rows = x.shape[0]
    tiles = FF // 2 // FT
    tile_rows = pl.BlockSpec((MT, D), lambda f, n: (jnp.maximum(f - tiles, 0), 0))
    return pl.pallas_call(
        second_kernel,
        grid_spec=pltpu.PrefetchScalarGridSpec(
            num_scalar_prefetch=1,
            grid=(tiles + rows // MT,),
            in_specs=ffn_specs(tiles, shards) + [tile_rows] * 5 + [out_block(), whole(3, D)],
            out_specs=[pl.BlockSpec(memory_space=pl.ANY), tile_rows, tile_rows, tile_rows, whole(D, D), whole(1, D)],
            scratch_shapes=[pltpu.VMEM((D, D), f32)] + ffn_scratch(rows, shards),
        ),
        out_shape=[
            grad_shape(shards),
            jax.ShapeDtypeStruct((rows, D), bf16),
            jax.ShapeDtypeStruct((rows, D), f32),
            jax.ShapeDtypeStruct((rows, D), bf16),
            jax.ShapeDtypeStruct((D, D), bf16),
            jax.ShapeDtypeStruct((1, D), f32),
        ],
        compiler_params=pltpu.CompilerParams(vmem_limit_bytes=VMEM_LIMIT),
        cost_estimate=cost(46, 60),
        name="ffn_second",
    )(lengths, x, d_out, xt, dt, pack, pack, att, y1, dx1, d_out, ctx, attn_w, vecs)


def norm_back(x, grad, gain):
    r = rms_scale(x)
    n = x * r
    u = gain * grad
    mean = jnp.sum(n * u, axis=1, keepdims=True) * (1.0 / D)
    return r * (u - n * mean), jnp.sum(n * grad, axis=0, keepdims=True)


def qkv_grad_kernel(dqkv_ref, normed_t_ref, go_ref, gw_ref):
    i = pl.program_id(0)

    @pl.when(i < 3)
    def _():
        gw_ref[...] = nn(normed_t_ref[...], dqkv_ref[0]).astype(bf16)

    @pl.when(i == 3)
    def _():
        gw_ref[...] = go_ref[...]


def qkv_grad(dqkv, normed_t, g_attn_out):
    rows = normed_t.shape[1]
    return pl.pallas_call(
        qkv_grad_kernel,
        grid=(4,),
        in_specs=[
            pl.BlockSpec((1, rows, D), lambda i: (jnp.minimum(i, 2), 0, 0)),
            whole(D, rows), whole(D, D),
        ],
        out_specs=pl.BlockSpec((D, D), lambda i: (0, i)),
        out_shape=jax.ShapeDtypeStruct((D, 4 * D), bf16),
        compiler_params=pltpu.CompilerParams(vmem_limit_bytes=VMEM_LIMIT),
        cost_estimate=cost(11, 20),
        name="qkv_grad",
    )(dqkv, normed_t, g_attn_out)


def qkv_back_kernel(dqkv_ref, w_ref, hidden_ref, datt_ref, vec_ref, dh_ref, gg_ref):
    @pl.when(pl.program_id(0) == 0)
    def _():
        gg_ref[...] = jnp.zeros_like(gg_ref)

    dn = nt(dqkv_ref[0], w_ref[:, 0:D])
    for i in range(1, 3):
        dn = dn + nt(dqkv_ref[i], w_ref[:, i * D : (i + 1) * D])
    back, gain_grad = norm_back(hidden_ref[...], dn, vec_ref[1:2, :])
    gg_ref[...] += gain_grad
    dh_ref[...] = datt_ref[...] + back


def qkv_backward(dqkv, attn_w, hidden, d_att, vecs):
    rows = hidden.shape[0]
    tile = pl.BlockSpec((MT, D), lambda s: (s, 0))
    return pl.pallas_call(
        qkv_back_kernel,
        grid=(rows // MT,),
        in_specs=[
            pl.BlockSpec((3, MT, D), lambda s: (0, s, 0)),
            pl.BlockSpec((D, 3 * D), lambda s: (0, 0)),
            tile, tile, whole(3, D),
        ],
        out_specs=[tile, whole(1, D)],
        out_shape=[jax.ShapeDtypeStruct((rows, D), f32), jax.ShapeDtypeStruct((1, D), f32)],
        compiler_params=pltpu.CompilerParams(vmem_limit_bytes=VMEM_LIMIT),
        cost_estimate=cost(14, 40),
        name="qkv_backward",
    )(dqkv, attn_w, hidden, d_att, vecs)


MESH = pl.DeviceIdType.MESH


def greet(peers):
    barrier = pltpu.get_barrier_semaphore()
    for peer in peers:
        pl.semaphore_signal(barrier, inc=1, device_id=peer, device_id_type=MESH)
    pl.semaphore_wait(barrier, len(peers))


def gather_kernel(replicas, shards, own_ref, wanted_ref, out_ref, slots_ref, all_ref, send_sem, recv_sem):
    rep, me = lax.axis_index("rep"), lax.axis_index("shard")
    peers = [(rep, lax.rem(me + i, shards)) for i in range(1, shards)]
    others = [(lax.rem(rep + i, replicas), me) for i in range(1, replicas)]
    greet(peers + others)
    copies = []
    for i, peer in enumerate(peers + others):
        near = i < len(peers)
        copy = pltpu.make_async_remote_copy(
            src_ref=own_ref if near else wanted_ref, dst_ref=all_ref.at[me] if near else slots_ref.at[rep],
            send_sem=send_sem.at[i], recv_sem=recv_sem.at[i], device_id=peer, device_id_type=MESH)
        copy.start()
        copies.append(copy)
    all_ref[me] = own_ref[...]
    slots_ref[rep] = wanted_ref[...]
    for copy in copies:
        copy.wait()
    for s in range(0, shards, 2):
        pair = jnp.concatenate([all_ref[s].astype(f32), all_ref[s + 1].astype(f32)], axis=0)
        out_ref[s // 2] = pair.T.astype(bf16)


def gather_columns(own, wanted, replicas, shards):
    rows = own.shape[0]
    vmem = pl.BlockSpec(memory_space=pltpu.VMEM)
    out, slots = pl.pallas_call(
        lambda *refs: gather_kernel(replicas, shards, *refs),
        out_shape=[
            jax.ShapeDtypeStruct((shards // 2, SMALL, 2 * rows), bf16),
            jax.ShapeDtypeStruct((replicas, 8, 128), jnp.int32),
        ],
        in_specs=[vmem, vmem],
        out_specs=[vmem, vmem],
        scratch_shapes=[
            pltpu.VMEM((shards, rows, SMALL), bf16),
            pltpu.SemaphoreType.DMA((shards + replicas - 2,)),
            pltpu.SemaphoreType.DMA((shards + replicas - 2,)),
        ],
        compiler_params=pltpu.CompilerParams(collective_id=1, has_side_effects=True, vmem_limit_bytes=VMEM_LIMIT),
        cost_estimate=cost(6, 2),
        name="gather_columns",
    )(own, wanted)
    return out.transpose(1, 0, 2).reshape(SMALL, shards * rows), slots[:, 0, :replicas]


def finish_kernel(replicas, shards, piece_ref, small_ref, out_ref, got_ref, held_ref, other_ref,
                  send_sem, recv_sem, send2_sem, recv2_sem):
    rep, me = lax.axis_index("rep"), lax.axis_index("shard")
    wide = piece_ref.shape[2]
    half = piece_ref.shape[1]
    bits = [1 << b for b in range(replicas.bit_length() - 1)]
    peers = [(rep, lax.rem(me + i, shards)) for i in range(1, shards)]
    partners = {}
    for bit in bits:
        down = lax.rem(rep // bit, 2)
        partners[bit] = (rep + bit - 2 * bit * down, me)
    greet(peers + [partners[bit] for bit in bits])
    copies = []
    for i, peer in enumerate(peers):
        copy = pltpu.make_async_remote_copy(
            src_ref=small_ref.at[peer[1]], dst_ref=got_ref.at[i], send_sem=send_sem.at[i],
            recv_sem=recv_sem.at[i], device_id=peer, device_id_type=MESH)
        copy.start()
        copies.append(copy)
    held_ref[0, :, :, 0:wide] = piece_ref[...]
    total = small_ref[me].astype(f32)
    for i, copy in enumerate(copies):
        copy.wait()
        total = total + got_ref[i].astype(f32)
    held_ref[0, :, :, wide:] = total.astype(bf16)
    for t in range(len(bits)):
        copies = []
        for h, order in enumerate((bits, bits[::-1])):
            copy = pltpu.make_async_remote_copy(
                src_ref=held_ref.at[t, h], dst_ref=other_ref.at[t, h], send_sem=send2_sem.at[t, h],
                recv_sem=recv2_sem.at[t, h], device_id=partners[order[t]], device_id_type=MESH)
            copy.start()
            copies.append(copy)
        for h, copy in enumerate(copies):
            copy.wait()
            total = held_ref[t, h].astype(f32) + other_ref[t, h].astype(f32)
            if t == len(bits) - 1:
                out_ref[h] = total
            else:
                held_ref[t + 1, h] = total.astype(bf16)


def finish(piece, small, replicas, shards):
    rows, wide = piece.shape
    half = rows // 2
    steps = replicas.bit_length() - 1
    vmem = pl.BlockSpec(memory_space=pltpu.VMEM)
    out = pl.pallas_call(
        lambda *refs: finish_kernel(replicas, shards, *refs),
        out_shape=jax.ShapeDtypeStruct((2, half, wide + SMALL), f32),
        in_specs=[vmem, vmem],
        out_specs=vmem,
        scratch_shapes=[
            pltpu.VMEM((shards - 1, 2, half, SMALL), bf16),
            pltpu.VMEM((steps, 2, half, wide + SMALL), bf16),
            pltpu.VMEM((steps, 2, half, wide + SMALL), bf16),
            pltpu.SemaphoreType.DMA((shards - 1,)),
            pltpu.SemaphoreType.DMA((shards - 1,)),
            pltpu.SemaphoreType.DMA((steps, 2)),
            pltpu.SemaphoreType.DMA((steps, 2)),
        ],
        compiler_params=pltpu.CompilerParams(
            collective_id=2, has_side_effects=True, vmem_limit_bytes=VMEM_LIMIT),
        cost_estimate=cost(20, 4),
        name="finish_sums",
    )(piece.reshape(2, half, wide), small.reshape(shards, 2, half, SMALL))
    return out.reshape(rows, wide + SMALL)


def wanted_slots(target, seqs):
    replicas, shards = lax.axis_size("rep"), lax.axis_size("shard")
    dest_rep = target // seqs // shards
    rows = jnp.where(dest_rep[None, :] == jnp.arange(replicas)[:, None], (target % seqs)[None, :] + 1, 0).sum(axis=1)
    return dest_rep, jnp.broadcast_to(jnp.pad(rows, (0, 128 - replicas))[None], (8, 128)).astype(jnp.int32)


def gather_small(embed, conv_w, score_w, gain_attn, gain_ffn, rel_table, wanted):
    replicas, shards = lax.axis_size("rep"), lax.axis_size("shard")
    width = embed.shape[1]
    table_row = jnp.pad(rel_table.reshape(1, -1), ((0, 0), (0, width - rel_table.size)))
    packed = jnp.concatenate(
        [embed, conv_w, score_w[None], gain_attn[None], gain_ffn[None], table_row], axis=0
    )
    own = jnp.pad(packed, ((0, SMALL - packed.shape[0]), (0, 0))).T
    full, slots = gather_columns(own, wanted, replicas, shards)
    taps = full[VOCAB : VOCAB + 4].astype(f32)
    vecs = full[VOCAB + 4 : VOCAB + 7].astype(f32)
    rel = full[VOCAB + 7].reshape(shards, width)[:, : rel_table.size].reshape(BUCKETS, HEADS)
    return full, taps, vecs, rel, slots


def send_cotangent(slots, cotangent):
    replicas = lax.axis_size("rep")
    rep = lax.axis_index("rep")
    asked = jnp.where(jnp.arange(replicas)[None, :] == rep, slots, 0).sum(axis=1) - 1
    pieces = []
    for shift in range(replicas):
        slot = jnp.where(jnp.arange(replicas) == (rep + shift) % replicas, asked, 0).sum()
        sent = cotangent[0]
        for k in range(1, cotangent.shape[0]):
            sent = jnp.where(slot == k, cotangent[k], sent)
        if shift:
            sent = lax.ppermute(sent, "rep", [(r, (r + shift) % replicas) for r in range(replicas)])
        pieces.append(sent)
    return pieces


def own_order(pieces, dest_rep, lengths):
    replicas = lax.axis_size("rep")
    rep = lax.axis_index("rep")
    rows = []
    for k in range(lengths.shape[0]):
        shift = (rep - dest_rep[k]) % replicas
        row = pieces[0]
        for j in range(1, replicas):
            row = jnp.where(shift == j, pieces[j], row)
        live = 2 * jnp.arange(TOK) < lengths[k]
        rows.append(jnp.where(live[:, None], row, jnp.zeros((), bf16)))
    return jnp.concatenate(rows, axis=0)


def butterfly(x):
    replicas = lax.axis_size("rep")
    bits = [1 << b for b in range(replicas.bit_length() - 1)]
    half = x.shape[0] // 2
    parts = []
    for piece, order in ((x[:half], bits), (x[half:], bits[::-1])):
        for bit in order:
            other = lax.ppermute(piece, "rep", [(r, r ^ bit) for r in range(replicas)])
            piece = (piece.astype(f32) + other.astype(f32)).astype(f32 if bit == order[-1] else bf16)
        parts.append(piece)
    return jnp.concatenate(parts, axis=0)


def scatter_sum(grad):
    return lax.psum_scatter(grad, "shard", scatter_dimension=0, tiled=True)


def pack_ffn(ffn_in, ffn_out, h, shards):
    hs = FF // 2 // shards
    owners = FT // hs
    parts = []
    for f in range(FF // 2 // FT):
        for g in range(2):
            starts = [g * FF + (f * owners + o) * 2 * hs + h * hs for o in range(owners)]
            parts.append(jnp.concatenate([ffn_in[:, a : a + hs] for a in starts], axis=1))
    for i in range(3):
        parts.append(ffn_out[h * hs : (h + 1) * hs, i * FT : (i + 1) * FT])
    return jnp.concatenate(parts, axis=0)


def ffn_shard_grads(sums, shards):
    hs = FF // 2 // shards
    deep = D // shards
    tiles = FF // 2 // FT
    first, second = [], []
    for total in sums:
        cut = tiles * 2 * deep
        cols = total[:cut].reshape(tiles, 2, deep, FT).transpose(2, 1, 0, 3)
        first.append(cols.reshape(deep, 2, shards, 1, hs))
        second.append(total[cut:].reshape(3, hs, FT).transpose(1, 0, 2).reshape(hs, D))
    return jnp.concatenate(first, axis=3).reshape(deep, 2 * FF), jnp.concatenate(second, axis=0)


def body(
    byte_ids, lengths, target, rel_bucket, cotangent, embed, conv_w, score_w, gain_attn,
    attn_in, attn_out, gain_ffn, ffn_in, ffn_out, rel_table,
):
    seqs = byte_ids.shape[0]
    shards = lax.axis_size("shard")
    width = embed.shape[1]
    dest_rep, wanted = wanted_slots(target, seqs)
    small_weights = gather_small(embed, conv_w, score_w, gain_attn, gain_ffn, rel_table, wanted)
    small_weights, attn_in, attn_out = lax.optimization_barrier((small_weights, attn_in, attn_out))
    table, taps, vecs, rel, slots = small_weights
    attn_w = lax.all_gather(jnp.concatenate([attn_in, attn_out], axis=1), "shard", axis=0, tiled=True)
    packs = [lax.all_gather(pack_ffn(ffn_in, ffn_out, h, shards), "shard", axis=0) for h in range(2)]
    ids_col, ids_row = byte_columns(byte_ids, lengths)
    hits = bucket_hits(rel_bucket)
    hits_back = bucket_hits(rel_bucket[::-1])

    def spread(h):
        dims = (((0,), (0,)), ((), ()))
        return lax.dot_general(rel, h.astype(bf16), dims, preferred_element_type=f32).reshape(HEADS, 8, SPAN)

    z, z_back = spread(hits), spread(hits_back)

    hidden, normed, normed_t, convolved, weights = gbst_forward(lengths, ids_col, table, taps, vecs)
    pieces = send_cotangent(slots, cotangent)
    qkv = jnp.dot(normed, attn_w[:, : 3 * D], preferred_element_type=f32).astype(bf16)
    ctx, lse = attn_forward(lengths, qkv, z)
    ctx, pieces = lax.optimization_barrier((ctx, pieces))
    d_out = own_order(pieces, dest_rep, lengths)
    attended, low, low_t, d_out_t = post_attention(ctx, attn_w, hidden, vecs, d_out)
    g_half1, y1, dx1 = ffn_first(low, d_out, low_t, d_out_t, packs[0], shards)
    g_half2, out, d_att, d_ctx, g_attn_out, g_gain_ffn = ffn_second(
        lengths, low, d_out, low_t, d_out_t, packs[1], attended, y1, dx1, ctx, attn_w, vecs, shards
    )
    s_halves = [scatter_sum(g.reshape(-1, FT)) for g in (g_half1, g_half2)]
    d_ctx, s_halves[0] = lax.optimization_barrier((d_ctx, s_halves[0]))
    dqkv, gz = attn_backward(lengths, qkv, d_ctx, ctx, lse, z_back)
    s_halves[0] = butterfly(s_halves[0])
    dqkv, s_halves = lax.optimization_barrier((dqkv, s_halves))
    g_attn = qkv_grad(dqkv, normed_t, g_attn_out)
    p_attn = scatter_sum(g_attn)
    s_halves[1] = butterfly(s_halves[1])
    d_hidden, g_gain_attn = qkv_backward(dqkv, attn_w, hidden, d_att, vecs)
    d_hidden, s_halves = lax.optimization_barrier((d_hidden, s_halves))
    g_table = lax.dot_general(
        hits_back.astype(f32), gz.reshape(HEADS, -1), (((1,), (1,)), ((), ())),
        precision=lax.Precision.HIGHEST, preferred_element_type=f32,
    )
    per = g_table.size // shards
    table_row = jnp.pad(g_table.reshape(shards, per), ((0, 0), (0, width - per))).reshape(1, D)
    more = jnp.concatenate([g_gain_attn, g_gain_ffn, table_row], axis=0)
    s_ffn_in, s_ffn_out = ffn_shard_grads(s_halves, shards)
    d_hidden, more, s_ffn_in, s_ffn_out = lax.optimization_barrier((d_hidden, more, s_ffn_in, s_ffn_out))
    input_grad, small = gbst_backward(
        lengths, ids_col, ids_row, table, taps, vecs, d_hidden, convolved, weights, more
    )
    sums = finish(p_attn, small, lax.axis_size("rep"), shards)
    s_small = sums[:, 4 * D :].T
    return (
        out.reshape(seqs, TOK, D),
        input_grad,
        s_small[:VOCAB],
        s_small[VROWS : VROWS + 4],
        s_small[VROWS + 4],
        s_small[VROWS + 5],
        sums[:, : 3 * D],
        sums[:, 3 * D : 4 * D],
        s_small[VROWS + 6],
        s_ffn_in,
        s_ffn_out,
        s_small[VROWS + 7, :per].reshape(rel_table.shape),
    )


def solution(mesh):
    in_specs = (
        P(("rep", "shard"), None), P(("rep", "shard")), P(("rep", "shard")), P(),
        P(("rep", "shard"), None, None), P(None, "shard"), P(None, "shard"), P("shard"), P("shard"),
        P("shard", None), P("shard", None), P("shard"), P("shard", None), P("shard", None), P("shard", None),
    )
    out_specs = (
        P(("rep", "shard"), None, None), P(("rep", "shard"), None, None), P(None, "shard"), P(None, "shard"),
        P("shard"), P("shard"), P("shard", None), P("shard", None), P("shard"), P("shard", None),
        P("shard", None), P("shard", None),
    )
    return jax.shard_map(body, mesh=mesh, in_specs=in_specs, out_specs=out_specs, check_vma=False)
```

```python
import jax
import jax.numpy as jnp
from jax import lax
from jax.experimental import pallas as pl
from jax.experimental.pallas import tpu as pltpu
from jax.sharding import PartitionSpec as P

D = 768
VOCAB = 259
VROWS = 272
VMEM_LIMIT = 60 << 20
SMALL = 384
MAXLEN = 1024
TOK = 512
LANES = 128
QN = 88
R = 12
P_ROWS = QN * R
T_ROWS = 528
LT = D // LANES
epsilon = 1e-06
f32 = jnp.float32
bf16 = jnp.bfloat16


def cost(us, mib):
    return pl.CostEstimate(flops=int(us * 1e9), bytes_accessed=mib << 20, transcendentals=0)


def lane_iota(rows):
    return lax.broadcasted_iota(jnp.int32, (rows, LANES), 1)


def group_matrix(b):
    row = lax.broadcasted_iota(jnp.int32, (LANES, LANES), 0)
    col = lax.broadcasted_iota(jnp.int32, (LANES, LANES), 1)
    return jnp.where((row // b == col // b) & (row < R) & (col < R), 1.0, 0.0).astype(f32)


def exact_dot(a, b):
    return jnp.dot(a, b, precision=lax.Precision.HIGHEST, preferred_element_type=f32)


def place(columns, rows):
    lanes = lane_iota(rows)
    out = jnp.zeros((rows, LANES), f32)
    for r, column in enumerate(columns):
        out = jnp.where(lanes == r, column, out)
    return out


def gbst_masks(length):
    q = lax.broadcasted_iota(jnp.int32, (QN, LANES), 0)
    r = lax.broadcasted_iota(jnp.int32, (QN, LANES), 1)
    mask = jnp.where((q * R + r < length) & (r < R), 1.0, 0.0).astype(f32)
    inverse = [1.0 / jnp.maximum(exact_dot(mask, group_matrix(b)), 1.0) for b in (2, 3, 4)]
    pair = exact_dot(mask, group_matrix(2))
    alpha = mask / jnp.maximum(pair, 1.0)
    return mask, inverse, alpha


def gbst_weights(s1, inverse):
    sizes = [s1] + [exact_dot(s1, group_matrix(b)) * inv for b, inv in zip((2, 3, 4), inverse)]
    top = jnp.maximum(jnp.maximum(sizes[0], sizes[1]), jnp.maximum(sizes[2], sizes[3]))
    parts = [jnp.exp(s - top) for s in sizes]
    total = parts[0] + parts[1] + parts[2] + parts[3]
    return [p / total for p in parts]


def gbst_coefs(weights, inverse, alpha):
    a1 = weights[0] * alpha
    a2 = weights[1] * alpha * inverse[0]
    a3 = weights[2] * alpha * inverse[1]
    a4 = weights[3] * alpha * inverse[2]
    pair = group_matrix(2)
    a4s = exact_dot(a4, pair)
    own = a1 + exact_dot(a2, pair) + a4s
    return own, a3, a4s


def column(x, r):
    return jnp.broadcast_to(x[:, r : r + 1], (x.shape[0], LANES))


def hits_of(ids):
    lanes = lax.broadcasted_iota(jnp.int32, (P_ROWS, LANES), 1).astype(f32)
    return jnp.concatenate(
        [jnp.where(ids == lanes + float(i * LANES), 1.0, 0.0).astype(bf16) for i in range(SMALL // LANES)], axis=1)


def look_up(ids, table_ref):
    return lax.dot_general(
        hits_of(ids), table_ref[...].reshape(D, SMALL), (((1,), (1,)), ((), ())), preferred_element_type=f32)


def load_e(e_ref, r, lt):
    lanes = pl.ds(lt * LANES, LANES)
    if r < R:
        return e_ref[pl.ds(r * QN, QN), lanes]
    return e_ref[pl.ds((r - R) * QN + 1, QN), lanes]


def gbst_fwd_kernel(len_ref, ids_ref, table_ref, vec_ref, hidden_ref, normed_ref, turned_ref, c_ref, w_ref, e_ref, hid_ref, s_ref, k_ref):
    length = len_ref[pl.program_id(0)]
    e_ref[pl.ds(0, P_ROWS), :] = look_up(ids_ref[0], table_ref)
    e_ref[pl.ds(P_ROWS, 8), :] = jnp.zeros((8, D), f32)
    for lt in range(LT):
        lanes = pl.ds(lt * LANES, LANES)
        taps = [jnp.broadcast_to(vec_ref[j : j + 1, lanes], (QN, LANES)) for j in range(4)]
        sw = jnp.broadcast_to(vec_ref[4:5, lanes], (QN, LANES))
        for r in range(R):
            c = taps[0] * load_e(e_ref, r, lt)
            for j in range(1, 4):
                c = c + taps[j] * load_e(e_ref, r + j, lt)
            c_ref[0, pl.ds(r * QN, QN), lanes] = c
            part = c * sw
            rows = pl.ds(r * QN, QN)
            s_ref[rows, :] = part if lt == 0 else s_ref[rows, :] + part
    s1 = place([jnp.sum(s_ref[pl.ds(r * QN, QN), :], axis=1, keepdims=True) for r in range(R)], QN)
    mask, inverse, alpha = gbst_masks(length)
    weights = gbst_weights(s1, inverse)
    for b in range(4):
        w_ref[0, b] = weights[b]
    own, a3, a4s = gbst_coefs(weights, inverse, alpha)
    n = 0
    for r in range(R):
        k_ref[r] = column(own, r)
        k_ref[R + r] = column(a3, r)
    for k in range(6):
        k_ref[2 * R + k] = column(a4s, 2 * k)
    for lt in range(LT):
        lanes = pl.ds(lt * LANES, LANES)
        for half in range(2):
            c = [c_ref[0, pl.ds((half * 6 + r) * QN, QN), lanes] for r in range(6)]
            base = half * 6
            s3 = [c[0] + c[1] + c[2], c[3] + c[4] + c[5]]
            for k in range(3):
                tok = half * 3 + k
                other = tok ^ 1
                rows = pl.ds(2 * other * QN, QN)
                rows1 = pl.ds((2 * other + 1) * QN, QN)
                s2 = c_ref[0, rows, lanes] + c_ref[0, rows1, lanes]
                h = k_ref[2 * tok] * c[2 * k] + k_ref[2 * tok + 1] * c[2 * k + 1] + k_ref[2 * R + tok] * s2
                if k == 1:
                    h = h + k_ref[R + 2 * tok] * s3[0] + k_ref[R + 2 * tok + 1] * s3[1]
                else:
                    h = h + (k_ref[R + 2 * tok] + k_ref[R + 2 * tok + 1]) * s3[0 if k == 0 else 1]
                hid_ref[lt, pl.ds(tok, QN, stride=6), :] = h
    total = jnp.zeros((TOK, LANES), f32)
    for lt in range(LT):
        x = hid_ref[lt, 0:TOK, :]
        total = total + x * x
    scale = lax.rsqrt(jnp.sum(total, axis=1, keepdims=True) * (1.0 / D) + epsilon)
    for lt in range(LT):
        lanes = pl.ds(lt * LANES, LANES)
        x = hid_ref[lt, 0:TOK, :]
        hidden_ref[:, lanes] = x
        normed = (x * scale * vec_ref[5:6, lanes]).astype(bf16)
        normed_ref[:, lanes] = normed
        turned_ref[lanes, :] = normed.T


def gbst_forward(lengths, ids_col, table, vecs):
    seqs = ids_col.shape[0]
    grid_spec = pltpu.PrefetchScalarGridSpec(
        num_scalar_prefetch=1,
        grid=(seqs,),
        in_specs=[
            pl.BlockSpec((1, P_ROWS, LANES), lambda s, n: (s, 0, 0)),
            pl.BlockSpec(table.shape, lambda s, n: (0, 0, 0)),
            pl.BlockSpec((8, D), lambda s, n: (0, 0)),
        ],
        out_specs=[
            pl.BlockSpec((TOK, D), lambda s, n: (s, 0)),
            pl.BlockSpec((TOK, D), lambda s, n: (s, 0)),
            pl.BlockSpec((D, TOK), lambda s, n: (0, s)),
            pl.BlockSpec((1, P_ROWS, D), lambda s, n: (s, 0, 0)),
            pl.BlockSpec((1, 4, QN, LANES), lambda s, n: (s, 0, 0, 0)),
        ],
        scratch_shapes=[
            pltpu.VMEM((P_ROWS + 8, D), f32),
            pltpu.VMEM((LT, T_ROWS, LANES), f32),
            pltpu.VMEM((P_ROWS, LANES), f32),
            pltpu.VMEM((2 * R + 6, QN, LANES), f32),
        ],
    )
    return pl.pallas_call(
        gbst_fwd_kernel,
        grid_spec=grid_spec,
        out_shape=[
            jax.ShapeDtypeStruct((seqs * TOK, D), f32),
            jax.ShapeDtypeStruct((seqs * TOK, D), bf16),
            jax.ShapeDtypeStruct((D, seqs * TOK), bf16),
            jax.ShapeDtypeStruct((seqs, P_ROWS, D), f32),
            jax.ShapeDtypeStruct((seqs, 4, QN, LANES), f32),
        ],
        compiler_params=pltpu.CompilerParams(vmem_limit_bytes=VMEM_LIMIT),
        cost_estimate=cost(18, 30),
        name="gbst_forward",
    )(lengths, ids_col, table, vecs)


def gbst_bwd_kernel(len_ref, ids_ref, row_ref, table_ref, vec_ref, dh_ref, c_ref, w_ref, more_ref,
                    ig_ref, small_ref, ge_ref, e_ref, dt_ref, dc_ref, s_ref, k_ref, igs_ref):
    seq = pl.program_id(0)
    length = len_ref[seq]

    @pl.when(seq == 0)
    def _():
        ge_ref[...] = jnp.zeros_like(ge_ref)

    e_ref[pl.ds(0, P_ROWS), :] = look_up(ids_ref[0], table_ref)
    e_ref[pl.ds(P_ROWS, 8), :] = jnp.zeros((8, D), f32)
    for lt in range(LT):
        dt_ref[lt, 0:TOK, :] = dh_ref[:, pl.ds(lt * LANES, LANES)]
        dt_ref[lt, TOK:T_ROWS, :] = jnp.zeros((T_ROWS - TOK, LANES), f32)
    for lt in range(LT):
        lanes = pl.ds(lt * LANES, LANES)
        for half in range(2):
            c = [c_ref[0, pl.ds((half * 6 + r) * QN, QN), lanes] for r in range(6)]
            s3 = [c[0] + c[1] + c[2], c[3] + c[4] + c[5]]
            for k in range(3):
                tok = half * 3 + k
                other = tok ^ 1
                dh = dt_ref[lt, pl.ds(tok, QN, stride=6), :]
                s2 = c_ref[0, pl.ds(2 * other * QN, QN), lanes] + c_ref[0, pl.ds((2 * other + 1) * QN, QN), lanes]
                parts = [
                    (2 * tok, dh * c[2 * k]),
                    (2 * tok + 1, dh * c[2 * k + 1]),
                    (2 * R + tok, dh * s2),
                    (R + 2 * tok, dh * s3[0 if k < 2 else 1]),
                ]
                if k == 1:
                    parts.append((R + 2 * tok + 1, dh * s3[1]))
                for slot, part in parts:
                    s_ref[slot] = part if lt == 0 else s_ref[slot] + part

    def total(slot):
        return jnp.sum(s_ref[slot], axis=1, keepdims=True)

    d1, d3, dother = [], [], []
    for tok in range(6):
        d1 += [total(2 * tok), total(2 * tok + 1)]
        first = total(R + 2 * tok)
        d3 += [first, total(R + 2 * tok + 1) if tok % 3 == 1 else first]
        o = total(2 * R + tok)
        dother += [o, o]
    d1, d3, dother = place(d1, QN), place(d3, QN), place(dother, QN)
    mask, inverse, alpha = gbst_masks(length)
    weights = [w_ref[0, b] for b in range(4)]
    d2 = exact_dot(d1, group_matrix(2))
    g = [alpha * d1, alpha * d2 * inverse[0], alpha * d3 * inverse[1], alpha * (d2 + dother) * inverse[2]]
    mean = weights[0] * g[0] + weights[1] * g[1] + weights[2] * g[2] + weights[3] * g[3]
    d_size = [w * (x - mean) for w, x in zip(weights, g)]
    coef = d_size[0]
    for b, inv in zip((2, 3, 4), inverse):
        coef = coef + exact_dot(d_size[b - 1] * inv, group_matrix(b))
    own, a3, a4s = gbst_coefs(weights, inverse, alpha)
    for r in range(R):
        k_ref[r] = column(own, r)
        k_ref[R + r] = column(a3, r)
        k_ref[2 * R + r] = column(coef, r)
        k_ref[3 * R + r] = column(mask, r)
    for k in range(6):
        k_ref[4 * R + k] = column(a4s, 2 * k)

    for lt in range(LT):
        lanes = pl.ds(lt * LANES, LANES)
        taps = [jnp.broadcast_to(vec_ref[j : j + 1, lanes], (QN, LANES)) for j in range(4)]
        sw = jnp.broadcast_to(vec_ref[4:5, lanes], (QN, LANES))
        gs = jnp.zeros((QN, LANES), f32)
        gc = [jnp.zeros((QN, LANES), f32) for _ in range(4)]
        for half in range(2):
            dh = [dt_ref[lt, pl.ds(half * 3 + k, QN, stride=6), :] for k in range(3)]
            a = R + half * 6
            t3 = [
                (k_ref[a] + k_ref[a + 1]) * dh[0] + k_ref[a + 2] * dh[1],
                k_ref[a + 3] * dh[1] + (k_ref[a + 4] + k_ref[a + 5]) * dh[2],
            ]
            for k in range(3):
                tok = half * 3 + k
                other = tok ^ 1
                dother_h = dt_ref[lt, pl.ds(other, QN, stride=6), :]
                cross = k_ref[4 * R + other] * dother_h
                for e in range(2):
                    r = 2 * tok + e
                    cf = k_ref[2 * R + r]
                    dc = k_ref[r] * dh[k] + cross + t3[(r % 6) // 3] + cf * sw
                    gs = gs + cf * c_ref[0, pl.ds(r * QN, QN), lanes]
                    dc_ref[r, pl.ds(8, QN), :] = dc
                    for j in range(4):
                        gc[j] = gc[j] + dc * load_e(e_ref, r + j, lt)
        ge_ref[VROWS + 4 : VROWS + 5, lanes] += jnp.sum(gs, axis=0, keepdims=True)
        for j in range(4):
            ge_ref[VROWS + j : VROWS + j + 1, lanes] += jnp.sum(gc[j], axis=0, keepdims=True)
        for r in range(R):
            dc_ref[r, 0:8, :] = jnp.zeros((8, LANES), f32)
        for r in range(R):
            x = taps[0] * dc_ref[r, pl.ds(8, QN), :]
            for j in range(1, 4):
                back = dc_ref[r - j, pl.ds(8, QN), :] if r >= j else dc_ref[r - j + R, pl.ds(7, QN), :]
                x = x + taps[j] * back
            igs_ref[lt, pl.ds(r, QN, stride=R), :] = x * k_ref[3 * R + r]
    for lt in range(LT):
        lanes = pl.ds(lt * LANES, LANES)
        ig_ref[0, :, lanes] = igs_ref[lt, 0:MAXLEN, :].astype(bf16)
    vocab = lax.broadcasted_iota(jnp.int32, (VROWS, MAXLEN), 0)
    row_hits = jnp.where(vocab == row_ref[0], 1.0, 0.0).astype(bf16)
    ge_ref[0:VROWS, :] += jnp.dot(row_hits, ig_ref[0], preferred_element_type=f32)

    @pl.when(seq == pl.num_programs(0) - 1)
    def _():
        ge_ref[VROWS + 5 : VROWS + 8, :] = more_ref[...]
        for lt in range(LT):
            lanes = pl.ds(lt * LANES, LANES)
            small_ref[lanes, :] = ge_ref[:, lanes].T.astype(bf16)


def gbst_backward(lengths, ids_col, ids_row, table, vecs, d_hidden, c, w, more):
    seqs = ids_col.shape[0]
    grid_spec = pltpu.PrefetchScalarGridSpec(
        num_scalar_prefetch=1,
        grid=(seqs,),
        in_specs=[
            pl.BlockSpec((1, P_ROWS, LANES), lambda s, n: (s, 0, 0)),
            pl.BlockSpec((1, 1, MAXLEN), lambda s, n: (s, 0, 0)),
            pl.BlockSpec(table.shape, lambda s, n: (0, 0, 0)),
            pl.BlockSpec((8, D), lambda s, n: (0, 0)),
            pl.BlockSpec((TOK, D), lambda s, n: (s, 0)),
            pl.BlockSpec((1, P_ROWS, D), lambda s, n: (s, 0, 0)),
            pl.BlockSpec((1, 4, QN, LANES), lambda s, n: (s, 0, 0, 0)),
            pl.BlockSpec((3, D), lambda s, n: (0, 0)),
        ],
        out_specs=[
            pl.BlockSpec((1, MAXLEN, D), lambda s, n: (s, 0, 0)),
            pl.BlockSpec((D, SMALL), lambda s, n: (0, 0)),
        ],
        scratch_shapes=[
            pltpu.VMEM((SMALL, D), f32),
            pltpu.VMEM((P_ROWS + 8, D), f32),
            pltpu.VMEM((LT, T_ROWS, LANES), f32),
            pltpu.VMEM((R, QN + 8, LANES), f32),
            pltpu.VMEM((2 * R + 6, QN, LANES), f32),
            pltpu.VMEM((4 * R + 6, QN, LANES), f32),
            pltpu.VMEM((LT, P_ROWS, LANES), f32),
        ],
    )
    return pl.pallas_call(
        gbst_bwd_kernel,
        grid_spec=grid_spec,
        out_shape=[
            jax.ShapeDtypeStruct((seqs, MAXLEN, D), bf16),
            jax.ShapeDtypeStruct((D, SMALL), bf16),
        ],
        compiler_params=pltpu.CompilerParams(vmem_limit_bytes=VMEM_LIMIT),
        cost_estimate=cost(31, 40),
        name="gbst_backward",
    )(lengths, ids_col, ids_row, table, vecs, d_hidden, c, w, more)


HEADS = 12
HD = 64
BUCKETS = 32
SPAN = 1024
HB = 4
WIDE = HB * HD
GROUPS = HEADS // HB
dead_score = -1e9


def nt(a, b):
    return lax.dot_general(a, b, (((1,), (1,)), ((), ())), preferred_element_type=f32)


def nn(a, b):
    return jnp.dot(a, b, preferred_element_type=f32)


def bucket_rows(buckets):
    back = jnp.pad(buckets, (8, 0))
    rows = [
        jnp.concatenate([back[8 + TOK - 1 - s : 8 + 2 * TOK - 1 - s], back[7 - s : 7 - s + TOK]])
        for s in range(8)
    ]
    return jnp.concatenate(rows)


def bucket_hits(buckets):
    return jnp.arange(BUCKETS)[:, None] == bucket_rows(buckets)[None, :]


def build_bias(z_ref, bt_ref):
    for h in range(HB):
        z = z_ref[h]
        for g in range(TOK // 8):
            bt_ref[h, pl.ds(8 * g, 8), :] = (z if g == 0 else pltpu.roll(z, 8 * g, 1))[:, :TOK]


def own_lanes(h):
    return lax.broadcasted_iota(jnp.int32, (TOK, WIDE), 1) // HD == h


def head_parts(k, q, length, h):
    lanes = lax.broadcasted_iota(jnp.int32, (TOK, WIDE), 1)
    rows = lax.broadcasted_iota(jnp.int32, (TOK, WIDE), 0)
    spare = HD * (h + 1) % WIDE
    dead = jnp.where(2 * rows < length, 0.0, dead_score)
    kf = jnp.where(lanes // HD == h, k.astype(f32), jnp.where(lanes == spare, dead, 0.0)).astype(bf16)
    qf = jnp.where(lanes == spare, 1.0, q.astype(f32)).astype(bf16)
    return kf, qf


def join_heads(parts):
    out = parts[0]
    for h in range(1, HB):
        out = jnp.where(own_lanes(h), parts[h], out)
    return out.astype(bf16)


def attn_fwd_kernel(len_ref, q_ref, k_ref, v_ref, z_ref, ctx_ref, lse_ref, bias_ref):
    length = len_ref[pl.program_id(1)]

    @pl.when(pl.program_id(1) == 0)
    def _():
        build_bias(z_ref, bias_ref)

    q, k, v = q_ref[...], k_ref[...], v_ref[...]

    def score(h):
        kf, qf = head_parts(k, q, length, h)
        return nt(qf, kf) + bias_ref[h]

    outs = []
    lanes = lax.broadcasted_iota(jnp.int32, (TOK, LANES), 1)
    lse = jnp.zeros((TOK, LANES), f32)
    s = score(0)
    for h in range(HB):
        later = score(h + 1) if h + 1 < HB else None
        top = jnp.max(s, axis=1, keepdims=True)
        p = jnp.exp(s - top)
        total = jnp.sum(p, axis=1, keepdims=True)
        outs.append(nn(p.astype(bf16), v) * (1.0 / total))
        lse = jnp.where(lanes == h, top + jnp.log(total), lse)
        s = later
    ctx_ref[...] = join_heads(outs)
    lse_ref[0, 0] = lse.T[0:8]


def attn_forward(lengths, qkv, z):
    seqs = qkv.shape[0] // TOK
    spec = lambda off: pl.BlockSpec((TOK, WIDE), lambda hp, s, n: (s, off + hp))
    return pl.pallas_call(
        attn_fwd_kernel,
        grid_spec=pltpu.PrefetchScalarGridSpec(
            num_scalar_prefetch=1,
            grid=(GROUPS, seqs),
            in_specs=[spec(0), spec(GROUPS), spec(2 * GROUPS), pl.BlockSpec((HB, 8, SPAN), lambda hp, s, n: (hp, 0, 0))],
            out_specs=[spec(0), pl.BlockSpec((1, 1, 8, TOK), lambda hp, s, n: (hp, s, 0, 0))],
            scratch_shapes=[pltpu.VMEM((HB, TOK, TOK), f32)],
        ),
        out_shape=[
            jax.ShapeDtypeStruct((seqs * TOK, D), bf16),
            jax.ShapeDtypeStruct((GROUPS, seqs, 8, TOK), f32),
        ],
        compiler_params=pltpu.CompilerParams(vmem_limit_bytes=VMEM_LIMIT),
        cost_estimate=cost(27, 20),
        name="attn_forward",
    )(lengths, qkv, qkv, qkv, z)


def attn_bwd_kernel(len_ref, q_ref, k_ref, v_ref, do_ref, o_ref, lse_ref, z_ref, dqkv_ref, gz_ref, bt_ref, g_ref):
    s_id = pl.program_id(1)
    length = len_ref[s_id]

    @pl.when(s_id == 0)
    def _():
        build_bias(z_ref, bt_ref)
        g_ref[...] = jnp.zeros_like(g_ref)

    q, k, v, do = q_ref[...], k_ref[...], v_ref[...], do_ref[...]
    kt = k.astype(f32).T.astype(bf16)
    lanes8 = lax.broadcasted_iota(jnp.int32, (8, WIDE), 1)
    rows8 = lax.broadcasted_iota(jnp.int32, (8, WIDE), 0)
    pick = jnp.where(lanes8 // HD == rows8, 1.0, 0.0).astype(bf16)
    prod = do.astype(f32) * o_ref[...].astype(f32)
    upper = prod.astype(bf16)
    delta = nt(pick, upper) + nt(pick, (prod - upper.astype(f32)).astype(bf16))
    dq, dk, dv = [], [], []

    def first(h):
        kf, qf = head_parts(k, q, length, h)
        vf = jnp.where(own_lanes(h), v.astype(f32), 0.0).astype(bf16)
        return nt(kf, qf) + bt_ref[h], nt(vf, do)

    now = first(0)
    for h in range(HB):
        later = first(h + 1) if h + 1 < HB else None
        s, d_prob = now
        p = jnp.exp(s - lse_ref[0, 0, h : h + 1, :])
        ds = p * (d_prob - delta[h : h + 1, :])
        g_ref[h] += ds
        low = ds.astype(bf16)
        dv.append(nn(p.astype(bf16), do))
        dk.append(nn(low, q))
        dq.append(nn(kt[h * HD : (h + 1) * HD], low))
        now = later
    dqkv_ref[0] = jnp.concatenate(dq, axis=0).T.astype(bf16)
    dqkv_ref[1] = join_heads(dk)
    dqkv_ref[2] = join_heads(dv)

    @pl.when(s_id == pl.num_programs(1) - 1)
    def _():
        for h in range(HB):
            total = jnp.zeros((8, SPAN), f32)
            for g in range(LANES // 8):
                tiles = [jnp.zeros((8, LANES), f32) for _ in range(SPAN // LANES)]
                for j in range(TOK // LANES):
                    x = g_ref[h, pl.ds(LANES * j + 8 * g, 8), :]
                    for t in range(TOK // LANES):
                        n = (t - j) % (SPAN // LANES)
                        tiles[n] = tiles[n] + x[:, t * LANES : (t + 1) * LANES]
                piece = jnp.concatenate(tiles, axis=1)
                total = total + (piece if g == 0 else pltpu.roll(piece, SPAN - 8 * g, 1))
            gz_ref[h] = total


def attn_backward(lengths, qkv, d_ctx, ctx, lse, z):
    seqs = qkv.shape[0] // TOK
    spec = lambda off: pl.BlockSpec((TOK, WIDE), lambda hp, s, n: (s, off + hp))
    return pl.pallas_call(
        attn_bwd_kernel,
        grid_spec=pltpu.PrefetchScalarGridSpec(
            num_scalar_prefetch=1,
            grid=(GROUPS, seqs),
            in_specs=[
                spec(0), spec(GROUPS), spec(2 * GROUPS), spec(0), spec(0),
                pl.BlockSpec((1, 1, 8, TOK), lambda hp, s, n: (hp, s, 0, 0)),
                pl.BlockSpec((HB, 8, SPAN), lambda hp, s, n: (hp, 0, 0)),
            ],
            out_specs=[
                pl.BlockSpec((3, TOK, WIDE), lambda hp, s, n: (0, s, hp)),
                pl.BlockSpec((HB, 8, SPAN), lambda hp, s, n: (hp, 0, 0)),
            ],
            scratch_shapes=[pltpu.VMEM((HB, TOK, TOK), f32), pltpu.VMEM((HB, TOK, TOK), f32)],
        ),
        out_shape=[
            jax.ShapeDtypeStruct((3, seqs * TOK, D), bf16),
            jax.ShapeDtypeStruct((HEADS, 8, SPAN), f32),
        ],
        compiler_params=pltpu.CompilerParams(vmem_limit_bytes=VMEM_LIMIT),
        cost_estimate=cost(46, 30),
        name="attn_backward",
    )(lengths, qkv, qkv, qkv, d_ctx, ctx, lse, z)


FF = 2048
FT = 256
RC = 512
MT = 256


def rms_scale(x):
    return lax.rsqrt(jnp.sum(x * x, axis=1, keepdims=True) * (1.0 / D) + epsilon)


def post_kernel(ctx_ref, w_ref, hidden_ref, vec_ref, do_ref, att_ref, low_ref, low_t_ref, do_t_ref):
    att = hidden_ref[...] + nn(ctx_ref[...], out_weights(w_ref))
    att_ref[...] = att
    low = (att * rms_scale(att) * vec_ref[6:7, :]).astype(bf16)
    low_ref[...] = low
    low_t_ref[...] = low.T
    do_t_ref[...] = do_ref[...].T


def rows_spec(width=D):
    return pl.BlockSpec((TOK, width), lambda s, *n: (s, 0))


def whole(*shape):
    return pl.BlockSpec(shape, lambda s, *n: (0,) * len(shape))


def out_block(shards):
    deep = D // shards
    return pl.BlockSpec((shards, 3 * deep, FT), lambda s, *n: (0, 4, 0))


def out_weights(ref):
    deep = ref.shape[1] // 3
    return jnp.concatenate([ref[:, i * deep : (i + 1) * deep, :].reshape(D, FT) for i in range(3)], axis=1)


def post_attention(ctx, pack, hidden, vecs, d_out, shards):
    rows = ctx.shape[0]
    cols_spec = pl.BlockSpec((D, TOK), lambda s: (0, s))
    return pl.pallas_call(
        post_kernel,
        grid=(rows // TOK,),
        in_specs=[rows_spec(), out_block(shards), rows_spec(), whole(8, D), rows_spec()],
        out_specs=[rows_spec(), rows_spec(), cols_spec, cols_spec],
        out_shape=[
            jax.ShapeDtypeStruct((rows, D), f32),
            jax.ShapeDtypeStruct((rows, D), bf16),
            jax.ShapeDtypeStruct((D, rows), bf16),
            jax.ShapeDtypeStruct((D, rows), bf16),
        ],
        compiler_params=pltpu.CompilerParams(vmem_limit_bytes=VMEM_LIMIT),
        cost_estimate=cost(6, 30),
        name="post_attention",
    )(ctx, pack, hidden, vecs, d_out)


def gelu_parts(v):
    c = 0.7978845608
    v2 = v * v
    t = jnp.tanh(v * (c + (c * 0.044715) * v2))
    half = 0.5 + 0.5 * t
    gelu = v * half
    slope = half + (0.5 * v) * (1.0 - t * t) * (c + (3.0 * c * 0.044715) * v2)
    return gelu, slope


def ffn_steps(x_any, d_any, xt_any, dt_any, wgu_ref, wo_ref, grad_ref, y_any, dx_any,
              x_ref, d_ref, xt_ref, dt_ref, y_ref, dx_ref, a_ref, dg_ref, du_ref, gu_ref, go_ref, in_sem, out_sem, sems):
    f = pl.program_id(0)
    steps = FF // 2 // FT
    rows_total = x_ref.shape[0]
    chunks = rows_total // RC
    shards, part = gu_ref.shape[1], gu_ref.shape[2]
    owners, deep = go_ref.shape[1], go_ref.shape[2]
    base = steps * part

    def copies(slot, step):
        return (
            pltpu.make_async_copy(
                gu_ref.at[slot], grad_ref.at[:, pl.ds(step * part, part), :], sems.at[0, slot]),
            pltpu.make_async_copy(
                go_ref.at[slot], grad_ref.at[pl.ds(step * owners, owners), pl.ds(base, deep), :], sems.at[1, slot]),
        )

    def row_loads(i):
        rows = pl.ds(i * RC, RC)
        return (
            pltpu.make_async_copy(x_any.at[rows], x_ref.at[rows], in_sem.at[0, i]),
            pltpu.make_async_copy(d_any.at[rows], d_ref.at[rows], in_sem.at[1, i]),
        )

    def turned_loads():
        return (
            pltpu.make_async_copy(xt_any, xt_ref, in_sem.at[2, 0]),
            pltpu.make_async_copy(dt_any, dt_ref, in_sem.at[2, 1]),
        )

    def row_stores(i):
        rows = pl.ds(i * RC, RC)
        return (
            pltpu.make_async_copy(y_ref.at[rows], y_any.at[rows], out_sem.at[0, i]),
            pltpu.make_async_copy(dx_ref.at[rows], dx_any.at[rows], out_sem.at[1, i]),
        )

    @pl.when(f == 0)
    def _():
        for i in range(chunks):
            for copy in row_loads(i):
                copy.start()
        for copy in turned_loads():
            copy.start()
        y_ref[...] = jnp.zeros_like(y_ref)
        dx_ref[...] = jnp.zeros_like(dx_ref)

    d_rows = part // 2
    third = deep // 3
    wg = wgu_ref[:, 0:d_rows, :].reshape(D, FT)
    wu = wgu_ref[:, d_rows:part, :].reshape(D, FT)
    wo = jnp.concatenate(
        [wo_ref[:, i * third : (i + 1) * third, :].reshape(FT, FT) for i in range(3)], axis=1)

    @pl.when(f == 0)
    def _():
        for i in range(chunks):
            for copy in row_loads(i):
                copy.wait()

    for i in range(chunks):
        rows = pl.ds(i * RC, RC)
        x, d = x_ref[rows, :], d_ref[rows, :]
        gelu, slope = gelu_parts(nn(x, wg))
        up = nn(x, wu)
        da = nt(d, wo)
        act = (gelu * up).astype(bf16)
        dg = (da * up * slope).astype(bf16)
        du = (da * gelu).astype(bf16)
        a_ref[rows, :] = act
        dg_ref[rows, :] = dg
        du_ref[rows, :] = du
        y_ref[rows, :] += nn(act, wo)
        dx_ref[rows, :] += nt(dg, wg) + nt(du, wu)
    if y_any is not None:

        @pl.when(f == steps - 1)
        def _():
            for i in range(chunks):
                for copy in row_stores(i):
                    copy.start()

    slot = lax.rem(f, 2)

    @pl.when(f == 0)
    def _():
        for copy in turned_loads():
            copy.wait()

    @pl.when(f >= 2)
    def _():
        for copy in copies(slot, f - 2):
            copy.wait()

    gu_ref[slot, :, 0:d_rows, :] = nn(xt_ref[...], dg_ref[...]).astype(bf16).reshape(shards, d_rows, FT)
    gu_ref[slot, :, d_rows:part, :] = nn(xt_ref[...], du_ref[...]).astype(bf16).reshape(shards, d_rows, FT)
    go = nn(dt_ref[...], a_ref[...]).T.astype(bf16)
    for i in range(3):
        go_ref[slot, :, i * third : (i + 1) * third, :] = go[:, i * FT : (i + 1) * FT].reshape(owners, third, FT)
    for copy in copies(slot, f):
        copy.start()

    @pl.when(f == steps - 1)
    def _():
        for copy in copies(1 - slot, f - 1) + copies(slot, f):
            copy.wait()
        if y_any is not None:
            for i in range(chunks):
                for copy in row_stores(i):
                    copy.wait()


def first_kernel(x, d, xt, dt, wgu, wo, grad, y, dx, *scratch):
    ffn_steps(x, d, xt, dt, wgu, wo, grad, y, dx, *scratch)


def second_kernel(len_ref, x, d, xt, dt, wgu, wo, att_ref, y1_ref, dx1_ref, do_ref, ctx_ref, w_ref, vec_ref,
                  grad, out_ref, datt_ref, dctx_ref, gw_ref, gg_ref, acc_ref, flat_ref, *scratch):
    f = pl.program_id(0)
    steps = FF // 2 // FT

    @pl.when(f == 0)
    def _():
        acc_ref[...] = jnp.zeros_like(acc_ref)
        gg_ref[...] = jnp.zeros_like(gg_ref)
        flat_ref[...] = out_weights(w_ref)

    @pl.when(f < steps)
    def _():
        ffn_steps(x, d, xt, dt, wgu, wo, grad, None, None, *scratch)

    @pl.when(f >= steps)
    def _():
        tile = f - steps
        y_ref, dx_ref = scratch[4], scratch[5]
        rows = pl.ds(pl.multiple_of(tile * MT, MT), MT)
        per = TOK // MT
        length = len_ref[tile // per]
        place_in = lax.rem(tile, per) * MT + lax.broadcasted_iota(jnp.int32, (MT, 1), 0)
        live = jnp.where(2 * place_in < length, 1.0, 0.0).astype(f32)
        att = att_ref[...]
        out_ref[...] = ((att + y1_ref[...] + y_ref[rows, :]) * live).astype(bf16)
        back, gain_grad = norm_back(att, dx1_ref[...] + dx_ref[rows, :], vec_ref[6:7, :])
        gg_ref[...] += gain_grad
        d_att = do_ref[...].astype(f32) + back
        datt_ref[...] = d_att
        low = d_att.astype(bf16)
        dctx_ref[...] = nt(low, flat_ref[...]).astype(bf16)
        acc_ref[...] += nn(ctx_ref[...].T, low)

    @pl.when(f == pl.num_programs(0) - 1)
    def _():
        gw_ref[...] = acc_ref[...].astype(bf16)


def ffn_scratch(rows, shards):
    part, hs = 2 * D // shards, FF // 2 // shards
    return [
        pltpu.VMEM((rows, D), bf16),
        pltpu.VMEM((rows, D), bf16),
        pltpu.VMEM((D, rows), bf16),
        pltpu.VMEM((D, rows), bf16),
        pltpu.VMEM((rows, D), f32),
        pltpu.VMEM((rows, D), f32),
        pltpu.VMEM((rows, FT), bf16),
        pltpu.VMEM((rows, FT), bf16),
        pltpu.VMEM((rows, FT), bf16),
        pltpu.VMEM((2, shards, part, FT), bf16),
        pltpu.VMEM((2, FT // hs, 3 * hs, FT), bf16),
        pltpu.SemaphoreType.DMA((3, max(2, rows // RC))),
        pltpu.SemaphoreType.DMA((2, rows // RC)),
        pltpu.SemaphoreType.DMA((2, 2)),
    ]


def ffn_specs(tiles, shards):
    last = lambda f: jnp.minimum(f, tiles - 1)
    part, hs = 2 * D // shards, FF // 2 // shards
    return [pl.BlockSpec(memory_space=pl.ANY)] * 4 + [
        pl.BlockSpec((shards, part, FT), lambda f, *n: (0, last(f), 0)),
        pl.BlockSpec((FT // hs, 3 * hs, FT), lambda f, *n: (last(f), 2, 0)),
    ]


def grad_shape(shards):
    part, hs = 2 * D // shards, FF // 2 // shards
    return jax.ShapeDtypeStruct((shards, FF // 2 // FT * part + 3 * hs, FT), bf16)


def ffn_first(x, d_out, xt, dt, pack, shards):
    rows = x.shape[0]
    tiles = FF // 2 // FT
    anywhere = pl.BlockSpec(memory_space=pl.ANY)
    return pl.pallas_call(
        first_kernel,
        grid=(tiles,),
        in_specs=ffn_specs(tiles, shards),
        out_specs=[anywhere] * 3,
        out_shape=[
            grad_shape(shards),
            jax.ShapeDtypeStruct((rows, D), f32),
            jax.ShapeDtypeStruct((rows, D), f32),
        ],
        scratch_shapes=ffn_scratch(rows, shards),
        compiler_params=pltpu.CompilerParams(vmem_limit_bytes=VMEM_LIMIT),
        cost_estimate=cost(36, 40),
        name="ffn_first",
    )(x, d_out, xt, dt, pack, pack)


def ffn_second(lengths, x, d_out, xt, dt, pack, att, y1, dx1, ctx, pack0, vecs, shards):
    rows = x.shape[0]
    tiles = FF // 2 // FT
    tile_rows = pl.BlockSpec((MT, D), lambda f, n: (jnp.maximum(f - tiles, 0), 0))
    return pl.pallas_call(
        second_kernel,
        grid_spec=pltpu.PrefetchScalarGridSpec(
            num_scalar_prefetch=1,
            grid=(tiles + rows // MT,),
            in_specs=ffn_specs(tiles, shards) + [tile_rows] * 5 + [out_block(shards), whole(8, D)],
            out_specs=[pl.BlockSpec(memory_space=pl.ANY), tile_rows, tile_rows, tile_rows, whole(D, D), whole(1, D)],
            scratch_shapes=[pltpu.VMEM((D, D), f32), pltpu.VMEM((D, D), bf16)] + ffn_scratch(rows, shards),
        ),
        out_shape=[
            grad_shape(shards),
            jax.ShapeDtypeStruct((rows, D), bf16),
            jax.ShapeDtypeStruct((rows, D), f32),
            jax.ShapeDtypeStruct((rows, D), bf16),
            jax.ShapeDtypeStruct((D, D), bf16),
            jax.ShapeDtypeStruct((1, D), f32),
        ],
        compiler_params=pltpu.CompilerParams(vmem_limit_bytes=VMEM_LIMIT),
        cost_estimate=cost(46, 60),
        name="ffn_second",
    )(lengths, x, d_out, xt, dt, pack, pack, att, y1, dx1, d_out, ctx, pack0, vecs)


def norm_back(x, grad, gain):
    r = rms_scale(x)
    n = x * r
    u = gain * grad
    mean = jnp.sum(n * u, axis=1, keepdims=True) * (1.0 / D)
    return r * (u - n * mean), jnp.sum(n * grad, axis=0, keepdims=True)


def qkv_grad_kernel(dqkv_ref, normed_t_ref, go_ref, gw_ref):
    i = pl.program_id(0)

    @pl.when(i < 3)
    def _():
        gw_ref[...] = nn(normed_t_ref[...], dqkv_ref[0]).astype(bf16)

    @pl.when(i == 3)
    def _():
        gw_ref[...] = go_ref[...]


def qkv_grad(dqkv, normed_t, g_attn_out):
    rows = normed_t.shape[1]
    return pl.pallas_call(
        qkv_grad_kernel,
        grid=(4,),
        in_specs=[
            pl.BlockSpec((1, rows, D), lambda i: (jnp.minimum(i, 2), 0, 0)),
            whole(D, rows), whole(D, D),
        ],
        out_specs=pl.BlockSpec((D, D), lambda i: (0, i)),
        out_shape=jax.ShapeDtypeStruct((D, 4 * D), bf16),
        compiler_params=pltpu.CompilerParams(vmem_limit_bytes=VMEM_LIMIT),
        cost_estimate=cost(11, 20),
        name="qkv_grad",
    )(dqkv, normed_t, g_attn_out)


def qkv_back_kernel(dqkv_ref, w_ref, hidden_ref, datt_ref, vec_ref, dh_ref, gg_ref):
    @pl.when(pl.program_id(0) == 0)
    def _():
        gg_ref[...] = jnp.zeros_like(gg_ref)

    dn = nt(dqkv_ref[0], w_ref[:, 0:D])
    for i in range(1, 3):
        dn = dn + nt(dqkv_ref[i], w_ref[:, i * D : (i + 1) * D])
    back, gain_grad = norm_back(hidden_ref[...], dn, vec_ref[5:6, :])
    gg_ref[...] += gain_grad
    dh_ref[...] = datt_ref[...] + back


def qkv_backward(dqkv, attn_w, hidden, d_att, vecs):
    rows = hidden.shape[0]
    tile = pl.BlockSpec((TOK, D), lambda s: (s, 0))
    return pl.pallas_call(
        qkv_back_kernel,
        grid=(rows // TOK,),
        in_specs=[
            pl.BlockSpec((3, TOK, D), lambda s: (0, s, 0)),
            pl.BlockSpec((D, 3 * D), lambda s: (0, 0)),
            tile, tile, whole(8, D),
        ],
        out_specs=[tile, whole(1, D)],
        out_shape=[jax.ShapeDtypeStruct((rows, D), f32), jax.ShapeDtypeStruct((1, D), f32)],
        compiler_params=pltpu.CompilerParams(vmem_limit_bytes=VMEM_LIMIT),
        cost_estimate=cost(14, 40),
        name="qkv_backward",
    )(dqkv, attn_w, hidden, d_att, vecs)


MESH = pl.DeviceIdType.MESH


def greet(peers):
    barrier = pltpu.get_barrier_semaphore()
    for peer in peers:
        pl.semaphore_signal(barrier, inc=1, device_id=peer, device_id_type=MESH)
    pl.semaphore_wait(barrier, len(peers))


def pack_half(out_ref, ffn_in_ref, ffn_out_ref, h, shards):
    hs = FF // 2 // shards
    owners = FT // hs
    deep = ffn_in_ref.shape[0]
    row = 0
    for f in range(FF // 2 // FT):
        for g in range(2):
            starts = [g * FF + (f * owners + o) * 2 * hs + h * hs for o in range(owners)]
            out_ref[row : row + deep, :] = jnp.concatenate([ffn_in_ref[:, a : a + hs] for a in starts], axis=1)
            row += deep
    for i in range(3):
        out_ref[row : row + hs, :] = ffn_out_ref[h * hs : (h + 1) * hs, i * FT : (i + 1) * FT]
        row += hs
    return row


def prepare_kernel(replicas, shards, embed_ref, conv_ref, rest_ref, wanted_ref, ids_ref, attn_out_ref, ffn_in_ref, ffn_out_ref,
                   table_ref, vec_ref, slots_ref, column_ref, pack0_ref, pack1_ref,
                   own_ref, wide_ref, turn_ref, nat_ref, send_sem, recv_sem):
    rep, me = lax.axis_index("rep"), lax.axis_index("shard")
    deep = embed_ref.shape[1]
    peers = [(rep, lax.rem(me + i, shards)) for i in range(1, shards)]
    others = [(lax.rem(rep + i, replicas), me) for i in range(1, replicas)]
    greet(peers + others)
    wide_ref[...] = jnp.zeros_like(wide_ref)
    wide_ref[0:VOCAB, 0:deep] = embed_ref[...].astype(f32)
    wide_ref[VOCAB : VOCAB + 4, 0:deep] = conv_ref[...].astype(f32)
    wide_ref[VOCAB + 4 : VOCAB + 8, 0:deep] = rest_ref[...].astype(f32)
    own_ref[...] = wide_ref[...].T[0:deep].astype(bf16)
    copies = []
    for i, peer in enumerate(peers + others):
        near = i < len(peers)
        copy = pltpu.make_async_remote_copy(
            src_ref=own_ref if near else wanted_ref, dst_ref=table_ref.at[me] if near else slots_ref.at[rep],
            send_sem=send_sem.at[i], recv_sem=recv_sem.at[i], device_id=peer, device_id_type=MESH)
        copy.start()
        copies.append(copy)
    table_ref[me] = own_ref[...]
    slots_ref[rep] = wanted_ref[...]
    row = pack_half(pack0_ref, ffn_in_ref, ffn_out_ref, 0, shards)
    for i in range(3):
        pack0_ref[row : row + deep, :] = attn_out_ref[:, i * FT : (i + 1) * FT]
        row += deep
    pack_half(pack1_ref, ffn_in_ref, ffn_out_ref, 1, shards)
    seqs = ids_ref.shape[0]
    turn_ref[...] = jnp.full(turn_ref.shape, -1.0, f32)
    turn_ref[0:seqs, 0:MAXLEN] = ids_ref[...].astype(f32)
    nat_ref[...] = turn_ref[...].T
    for r in range(R):
        rows = nat_ref[pl.ds(r, QN, stride=R), :]
        for s in range(seqs):
            column_ref[s, r * QN : (r + 1) * QN, :] = jnp.broadcast_to(rows[:, s : s + 1], (QN, 128))
    for copy in copies:
        copy.wait()
    last = table_ref[:, :, SMALL - 128 :].astype(f32).reshape(D, 128).T
    first = VOCAB - (SMALL - 128)
    vec_ref[...] = last[first : first + 8]


def prepare(embed, conv_w, rest, wanted, ids, attn_out, ffn_in, ffn_out, replicas, shards):
    deep = embed.shape[1]
    seqs = ids.shape[0]
    part, hs = 2 * D // shards, FF // 2 // shards
    rows = FF // 2 // FT * part + 3 * hs
    vmem = pl.BlockSpec(memory_space=pltpu.VMEM)
    return pl.pallas_call(
        lambda *refs: prepare_kernel(replicas, shards, *refs),
        out_shape=[
            jax.ShapeDtypeStruct((shards, deep, SMALL), bf16),
            jax.ShapeDtypeStruct((8, D), f32),
            jax.ShapeDtypeStruct((replicas, 8, 128), jnp.int32),
            jax.ShapeDtypeStruct((seqs, P_ROWS, 128), f32),
            jax.ShapeDtypeStruct((rows + 3 * deep, FT), bf16),
            jax.ShapeDtypeStruct((rows, FT), bf16),
        ],
        in_specs=[vmem] * 8,
        out_specs=[vmem] * 6,
        scratch_shapes=[
            pltpu.VMEM((deep, SMALL), bf16),
            pltpu.VMEM((SMALL, 128), f32),
            pltpu.VMEM((128, 1152), f32),
            pltpu.VMEM((1152, 128), f32),
            pltpu.SemaphoreType.DMA((shards + replicas - 2,)),
            pltpu.SemaphoreType.DMA((shards + replicas - 2,)),
        ],
        compiler_params=pltpu.CompilerParams(collective_id=1, has_side_effects=True, vmem_limit_bytes=VMEM_LIMIT),
        cost_estimate=cost(12, 8),
        name="prepare",
    )(embed, conv_w, rest, wanted, ids, attn_out, ffn_in, ffn_out)


def finish_kernel(replicas, shards, piece_ref, small_ref, in_ref, out_ref, turned_ref, got_ref, held_ref, other_ref,
                  last_ref, send_sem, recv_sem, send2_sem, recv2_sem):
    rep, me = lax.axis_index("rep"), lax.axis_index("shard")
    wide = piece_ref.shape[2]
    half = piece_ref.shape[1]
    bits = [1 << b for b in range(replicas.bit_length() - 1)]
    peers = [(rep, lax.rem(me + i, shards)) for i in range(1, shards)]
    partners = {}
    for bit in bits:
        down = lax.rem(rep // bit, 2)
        partners[bit] = (rep + bit - 2 * bit * down, me)
    greet(peers + [partners[bit] for bit in bits])
    copies = []
    for i, peer in enumerate(peers):
        copy = pltpu.make_async_remote_copy(
            src_ref=small_ref.at[peer[1]], dst_ref=got_ref.at[i], send_sem=send_sem.at[i],
            recv_sem=recv_sem.at[i], device_id=peer, device_id_type=MESH)
        copy.start()
        copies.append(copy)
    last_ref[...] = jnp.zeros_like(last_ref)
    held_ref[0, :, :, 0:wide] = piece_ref[...]
    total = small_ref[me].astype(f32)
    for i, copy in enumerate(copies):
        copy.wait()
        total = total + got_ref[i].astype(f32)
    held_ref[0, :, :, wide:] = total.astype(bf16)
    for t in range(len(bits)):
        copies = []
        for h, order in enumerate((bits, bits[::-1])):
            copy = pltpu.make_async_remote_copy(
                src_ref=held_ref.at[t, h], dst_ref=other_ref.at[t, h], send_sem=send2_sem.at[t, h],
                recv_sem=recv2_sem.at[t, h], device_id=partners[order[t]], device_id_type=MESH)
            copy.start()
            copies.append(copy)
        for h, copy in enumerate(copies):
            copy.wait()
            total = held_ref[t, h].astype(f32) + other_ref[t, h].astype(f32)
            if t == len(bits) - 1:
                rows = slice(h * half, (h + 1) * half)
                in_ref[rows, :] = total[:, 0 : 3 * D]
                out_ref[rows, :] = total[:, 3 * D : wide]
                last_ref[rows, :] = total[:, wide:]
            else:
                held_ref[t + 1, h] = total.astype(bf16)
    turned_ref[...] = last_ref[...].T


def finish(piece, small, replicas, shards):
    rows, wide = piece.shape
    half = rows // 2
    steps = replicas.bit_length() - 1
    vmem = pl.BlockSpec(memory_space=pltpu.VMEM)
    return pl.pallas_call(
        lambda *refs: finish_kernel(replicas, shards, *refs),
        out_shape=[
            jax.ShapeDtypeStruct((rows, 3 * D), f32),
            jax.ShapeDtypeStruct((rows, D), f32),
            jax.ShapeDtypeStruct((SMALL, 128), f32),
        ],
        in_specs=[vmem, vmem],
        out_specs=[vmem] * 3,
        scratch_shapes=[
            pltpu.VMEM((shards - 1, 2, half, SMALL), bf16),
            pltpu.VMEM((steps, 2, half, wide + SMALL), bf16),
            pltpu.VMEM((steps, 2, half, wide + SMALL), bf16),
            pltpu.VMEM((128, SMALL), f32),
            pltpu.SemaphoreType.DMA((shards - 1,)),
            pltpu.SemaphoreType.DMA((shards - 1,)),
            pltpu.SemaphoreType.DMA((steps, 2)),
            pltpu.SemaphoreType.DMA((steps, 2)),
        ],
        compiler_params=pltpu.CompilerParams(
            collective_id=2, has_side_effects=True, vmem_limit_bytes=VMEM_LIMIT),
        cost_estimate=cost(20, 4),
        name="finish_sums",
    )(piece.reshape(2, half, wide), small.reshape(shards, 2, half, SMALL))


def unpack_kernel(shards, first_ref, second_ref, in_ref, out_ref):
    hs = FF // 2 // shards
    deep = in_ref.shape[0]
    owners = FT // hs
    for h, ref in enumerate((first_ref, second_ref)):
        row = 0
        for f in range(FF // 2 // FT):
            for g in range(2):
                x = ref[row : row + deep, :]
                for o in range(owners):
                    start = g * FF + (f * owners + o) * 2 * hs + h * hs
                    in_ref[:, start : start + hs] = x[:, o * hs : (o + 1) * hs]
                row += deep
        for i in range(3):
            out_ref[h * hs : (h + 1) * hs, i * FT : (i + 1) * FT] = ref[row : row + hs, :]
            row += hs


def unpack(first, second, shards):
    vmem = pl.BlockSpec(memory_space=pltpu.VMEM)
    return pl.pallas_call(
        lambda *refs: unpack_kernel(shards, *refs),
        out_shape=[
            jax.ShapeDtypeStruct((D // shards, 2 * FF), f32),
            jax.ShapeDtypeStruct((FF // shards, D), f32),
        ],
        in_specs=[vmem] * 2,
        out_specs=[vmem] * 2,
        compiler_params=pltpu.CompilerParams(vmem_limit_bytes=VMEM_LIMIT),
        cost_estimate=cost(3, 5),
        name="unpack",
    )(first, second)


def wanted_slots(target, seqs):
    replicas, shards = lax.axis_size("rep"), lax.axis_size("shard")
    dest_rep = target // seqs // shards
    rows = jnp.where(dest_rep[None, :] == jnp.arange(replicas)[:, None], (target % seqs)[None, :] + 1, 0).sum(axis=1)
    return dest_rep, jnp.broadcast_to(jnp.pad(rows, (0, 128 - replicas))[None], (8, 128)).astype(jnp.int32)


def send_cotangent(slots, cotangent):
    replicas = lax.axis_size("rep")
    rep = lax.axis_index("rep")
    asked = jnp.where(jnp.arange(replicas)[None, :] == rep, slots, 0).sum(axis=1) - 1
    pieces = []
    for shift in range(replicas):
        slot = jnp.where(jnp.arange(replicas) == (rep + shift) % replicas, asked, 0).sum()
        sent = cotangent[0]
        for k in range(1, cotangent.shape[0]):
            sent = jnp.where(slot == k, cotangent[k], sent)
        if shift:
            sent = lax.ppermute(sent, "rep", [(r, (r + shift) % replicas) for r in range(replicas)])
        pieces.append(sent)
    return pieces


def own_order(pieces, dest_rep, lengths):
    replicas = lax.axis_size("rep")
    rep = lax.axis_index("rep")
    rows = []
    for k in range(lengths.shape[0]):
        shift = (rep - dest_rep[k]) % replicas
        row = pieces[0]
        for j in range(1, replicas):
            row = jnp.where(shift == j, pieces[j], row)
        live = 2 * jnp.arange(TOK) < lengths[k]
        rows.append(jnp.where(live[:, None], row, jnp.zeros((), bf16)))
    return jnp.concatenate(rows, axis=0)


def swap(x, bit):
    replicas = lax.axis_size("rep")
    return lax.ppermute(x, "rep", [(r, r ^ bit) for r in range(replicas)])


def rep_bits(turn):
    bits = [1 << b for b in range(lax.axis_size("rep").bit_length() - 1)]
    return bits[turn:] + bits[:turn]


def add_low(a, b):
    return (a.astype(f32) + b.astype(f32)).astype(bf16)


def scatter_sum(grad):
    return lax.psum_scatter(grad, "shard", scatter_dimension=0, tiled=True)


def body(
    byte_ids, lengths, target, rel_bucket, cotangent, embed, conv_w, score_w, gain_attn,
    attn_in, attn_out, gain_ffn, ffn_in, ffn_out, rel_table,
):
    seqs = byte_ids.shape[0]
    replicas, shards = lax.axis_size("rep"), lax.axis_size("shard")
    width = embed.shape[1]
    attn_w = lax.all_gather(attn_in, "shard", axis=0, tiled=True)
    dest_rep, wanted = wanted_slots(target, seqs)
    rest = jnp.concatenate(
        [score_w, gain_attn, gain_ffn, rel_table.reshape(-1), jnp.zeros((width - rel_table.size,), bf16)]
    ).reshape(4, width)
    ids = jnp.where(jnp.arange(MAXLEN)[None, :] < lengths[:, None], byte_ids, -1)
    table, vecs, slots, ids_col, pack0, pack1 = prepare(
        embed, conv_w, rest, wanted, ids, attn_out, ffn_in, ffn_out, replicas, shards
    )
    slots = slots[:, 0, :replicas]
    packs = [lax.all_gather(pack, "shard", axis=0) for pack in (pack0, pack1)]
    rel = vecs[7].astype(bf16).reshape(shards, width)[:, : rel_table.size].reshape(BUCKETS, HEADS)
    hits = bucket_hits(rel_bucket)
    hits_back = bucket_hits(rel_bucket[::-1])

    def spread(h):
        dims = (((0,), (0,)), ((), ()))
        return lax.dot_general(rel, h.astype(bf16), dims, preferred_element_type=f32).reshape(HEADS, 8, SPAN)

    z, z_back = spread(hits), spread(hits_back)

    hidden, normed, normed_t, convolved, weights = gbst_forward(lengths, ids_col, table, vecs)
    pieces = send_cotangent(slots, cotangent)
    qkv = jnp.dot(normed, attn_w, preferred_element_type=f32).astype(bf16)
    ctx, lse = attn_forward(lengths, qkv, z)
    ctx, pieces = lax.optimization_barrier((ctx, pieces))
    d_out = own_order(pieces, dest_rep, lengths)
    attended, low, low_t, d_out_t = post_attention(ctx, packs[0], hidden, vecs, d_out, shards)
    g_half1, y1, dx1 = ffn_first(low, d_out, low_t, d_out_t, packs[0], shards)
    g_half2, out, d_att, d_ctx, g_attn_out, g_gain_ffn = ffn_second(
        lengths, low, d_out, low_t, d_out_t, packs[1], attended, y1, dx1, ctx, packs[0], vecs, shards
    )
    one, two = [scatter_sum(g.reshape(-1, FT)) for g in (g_half1, g_half2)]
    bits1, bits2 = rep_bits(0), rep_bits(1)
    d_ctx, one = lax.optimization_barrier((d_ctx, one))
    other = swap(one, bits1[0])
    dqkv, gz = attn_backward(lengths, qkv, d_ctx, ctx, lse, z_back)
    dqkv, other, two = lax.optimization_barrier((dqkv, other, two))
    one = add_low(one, other)
    g_attn = qkv_grad(dqkv, normed_t, g_attn_out)
    p_attn = scatter_sum(g_attn)
    others = swap(one, bits1[1]), swap(two, bits2[0])
    d_hidden, g_gain_attn = qkv_backward(dqkv, attn_w, hidden, d_att, vecs)
    d_hidden, others = lax.optimization_barrier((d_hidden, others))
    one, two = add_low(one, others[0]), add_low(two, others[1])
    for bit in bits1[2:]:
        one = add_low(one, swap(one, bit))
    g_table = lax.dot_general(
        hits_back.astype(f32), gz.reshape(HEADS, -1), (((1,), (1,)), ((), ())),
        precision=lax.Precision.HIGHEST, preferred_element_type=f32,
    )
    per = g_table.size // shards
    table_row = jnp.pad(g_table.reshape(shards, per), ((0, 0), (0, width - per))).reshape(1, D)
    more = jnp.concatenate([g_gain_attn, g_gain_ffn, table_row], axis=0)
    d_hidden, more, one, two = lax.optimization_barrier((d_hidden, more, one, two))
    other = swap(two, bits2[1])
    input_grad, small = gbst_backward(
        lengths, ids_col, ids.reshape(seqs, 1, MAXLEN), table, vecs, d_hidden, convolved, weights, more
    )
    small, other = lax.optimization_barrier((small, other))
    two = add_low(two, other)
    for bit in bits2[2:]:
        two = add_low(two, swap(two, bit))
    s_attn_in, s_attn_out, turned = finish(p_attn, small, replicas, shards)
    s_small = turned[:, :width]
    s_ffn_in, s_ffn_out = unpack(one.astype(f32), two.astype(f32), shards)
    return (
        out.reshape(seqs, TOK, D),
        input_grad,
        s_small[:VOCAB],
        s_small[VROWS : VROWS + 4],
        s_small[VROWS + 4],
        s_small[VROWS + 5],
        s_attn_in,
        s_attn_out,
        s_small[VROWS + 6],
        s_ffn_in,
        s_ffn_out,
        s_small[VROWS + 7, :per].reshape(rel_table.shape),
    )


def solution(mesh):
    in_specs = (
        P(("rep", "shard"), None), P(("rep", "shard")), P(("rep", "shard")), P(),
        P(("rep", "shard"), None, None), P(None, "shard"), P(None, "shard"), P("shard"), P("shard"),
        P("shard", None), P("shard", None), P("shard"), P("shard", None), P("shard", None), P("shard", None),
    )
    out_specs = (
        P(("rep", "shard"), None, None), P(("rep", "shard"), None, None), P(None, "shard"), P(None, "shard"),
        P("shard"), P("shard"), P("shard", None), P("shard", None), P("shard"), P("shard", None),
        P("shard", None), P("shard", None),
    )
    return jax.shard_map(body, mesh=mesh, in_specs=in_specs, out_specs=out_specs, check_vma=False)
```

```python
import jax
import jax.numpy as jnp
from jax import lax
from jax.experimental import pallas as pl
from jax.experimental.pallas import tpu as pltpu
from jax.sharding import PartitionSpec as P

D = 768
VOCAB = 259
VROWS = 272
VMEM_LIMIT = 60 << 20
SMALL = 384
MAXLEN = 1024
TOK = 512
LANES = 128
QN = 88
R = 12
P_ROWS = QN * R
T_ROWS = 528
LT = D // LANES
epsilon = 1e-06
f32 = jnp.float32
bf16 = jnp.bfloat16


def cost(us, mib):
    return pl.CostEstimate(flops=int(us * 1e9), bytes_accessed=mib << 20, transcendentals=0)


def lane_iota(rows):
    return lax.broadcasted_iota(jnp.int32, (rows, LANES), 1)


def group_matrix(b):
    row = lax.broadcasted_iota(jnp.int32, (LANES, LANES), 0)
    col = lax.broadcasted_iota(jnp.int32, (LANES, LANES), 1)
    return jnp.where((row // b == col // b) & (row < R) & (col < R), 1.0, 0.0).astype(f32)


def exact_dot(a, b):
    return jnp.dot(a, b, precision=lax.Precision.HIGHEST, preferred_element_type=f32)


def place(columns, rows):
    lanes = lane_iota(rows)
    out = jnp.zeros((rows, LANES), f32)
    for r, column in enumerate(columns):
        out = jnp.where(lanes == r, column, out)
    return out


def gbst_masks(length):
    q = lax.broadcasted_iota(jnp.int32, (QN, LANES), 0)
    r = lax.broadcasted_iota(jnp.int32, (QN, LANES), 1)
    mask = jnp.where((q * R + r < length) & (r < R), 1.0, 0.0).astype(f32)
    inverse = [1.0 / jnp.maximum(exact_dot(mask, group_matrix(b)), 1.0) for b in (2, 3, 4)]
    pair = exact_dot(mask, group_matrix(2))
    alpha = mask / jnp.maximum(pair, 1.0)
    return mask, inverse, alpha


def gbst_weights(s1, inverse):
    sizes = [s1] + [exact_dot(s1, group_matrix(b)) * inv for b, inv in zip((2, 3, 4), inverse)]
    top = jnp.maximum(jnp.maximum(sizes[0], sizes[1]), jnp.maximum(sizes[2], sizes[3]))
    parts = [jnp.exp(s - top) for s in sizes]
    total = parts[0] + parts[1] + parts[2] + parts[3]
    return [p / total for p in parts]


def gbst_coefs(weights, inverse, alpha):
    a1 = weights[0] * alpha
    a2 = weights[1] * alpha * inverse[0]
    a3 = weights[2] * alpha * inverse[1]
    a4 = weights[3] * alpha * inverse[2]
    pair = group_matrix(2)
    a4s = exact_dot(a4, pair)
    own = a1 + exact_dot(a2, pair) + a4s
    return own, a3, a4s


def column(x, r):
    return jnp.broadcast_to(x[:, r : r + 1], (x.shape[0], LANES))


def hits_of(ids):
    lanes = lax.broadcasted_iota(jnp.int32, (P_ROWS, LANES), 1).astype(f32)
    return jnp.concatenate(
        [jnp.where(ids == lanes + float(i * LANES), 1.0, 0.0).astype(bf16) for i in range(SMALL // LANES)], axis=1)


def look_up(ids, table_ref):
    return lax.dot_general(
        hits_of(ids), table_ref[...].reshape(D, SMALL), (((1,), (1,)), ((), ())), preferred_element_type=f32)


def load_e(e_ref, r, lt):
    lanes = pl.ds(lt * LANES, LANES)
    if r < R:
        return e_ref[pl.ds(r * QN, QN), lanes]
    return e_ref[pl.ds((r - R) * QN + 1, QN), lanes]


def gbst_fwd_kernel(len_ref, ids_ref, table_ref, vec_ref, hidden_ref, normed_ref, turned_ref, c_ref, w_ref, e_ref, hid_ref, s_ref, k_ref):
    length = len_ref[pl.program_id(0)]
    e_ref[pl.ds(0, P_ROWS), :] = look_up(ids_ref[0], table_ref)
    e_ref[pl.ds(P_ROWS, 8), :] = jnp.zeros((8, D), f32)
    for lt in range(LT):
        lanes = pl.ds(lt * LANES, LANES)
        taps = [jnp.broadcast_to(vec_ref[j : j + 1, lanes], (QN, LANES)) for j in range(4)]
        sw = jnp.broadcast_to(vec_ref[4:5, lanes], (QN, LANES))
        for r in range(R):
            c = taps[0] * load_e(e_ref, r, lt)
            for j in range(1, 4):
                c = c + taps[j] * load_e(e_ref, r + j, lt)
            c_ref[0, pl.ds(r * QN, QN), lanes] = c
            part = c * sw
            rows = pl.ds(r * QN, QN)
            s_ref[rows, :] = part if lt == 0 else s_ref[rows, :] + part
    s1 = place([jnp.sum(s_ref[pl.ds(r * QN, QN), :], axis=1, keepdims=True) for r in range(R)], QN)
    mask, inverse, alpha = gbst_masks(length)
    weights = gbst_weights(s1, inverse)
    for b in range(4):
        w_ref[0, b] = weights[b]
    own, a3, a4s = gbst_coefs(weights, inverse, alpha)
    n = 0
    for r in range(R):
        k_ref[r] = column(own, r)
        k_ref[R + r] = column(a3, r)
    for k in range(6):
        k_ref[2 * R + k] = column(a4s, 2 * k)
    for lt in range(LT):
        lanes = pl.ds(lt * LANES, LANES)
        for half in range(2):
            c = [c_ref[0, pl.ds((half * 6 + r) * QN, QN), lanes] for r in range(6)]
            base = half * 6
            s3 = [c[0] + c[1] + c[2], c[3] + c[4] + c[5]]
            for k in range(3):
                tok = half * 3 + k
                other = tok ^ 1
                rows = pl.ds(2 * other * QN, QN)
                rows1 = pl.ds((2 * other + 1) * QN, QN)
                s2 = c_ref[0, rows, lanes] + c_ref[0, rows1, lanes]
                h = k_ref[2 * tok] * c[2 * k] + k_ref[2 * tok + 1] * c[2 * k + 1] + k_ref[2 * R + tok] * s2
                if k == 1:
                    h = h + k_ref[R + 2 * tok] * s3[0] + k_ref[R + 2 * tok + 1] * s3[1]
                else:
                    h = h + (k_ref[R + 2 * tok] + k_ref[R + 2 * tok + 1]) * s3[0 if k == 0 else 1]
                hid_ref[lt, pl.ds(tok, QN, stride=6), :] = h
    total = jnp.zeros((TOK, LANES), f32)
    for lt in range(LT):
        x = hid_ref[lt, 0:TOK, :]
        total = total + x * x
    scale = lax.rsqrt(jnp.sum(total, axis=1, keepdims=True) * (1.0 / D) + epsilon)
    for lt in range(LT):
        lanes = pl.ds(lt * LANES, LANES)
        x = hid_ref[lt, 0:TOK, :]
        hidden_ref[:, lanes] = x
        normed = (x * scale * vec_ref[5:6, lanes]).astype(bf16)
        normed_ref[:, lanes] = normed
        turned_ref[lanes, :] = normed.T


def gbst_forward(lengths, ids_col, table, vecs):
    seqs = ids_col.shape[0]
    grid_spec = pltpu.PrefetchScalarGridSpec(
        num_scalar_prefetch=1,
        grid=(seqs,),
        in_specs=[
            pl.BlockSpec((1, P_ROWS, LANES), lambda s, n: (s, 0, 0)),
            pl.BlockSpec(table.shape, lambda s, n: (0, 0, 0)),
            pl.BlockSpec((16, D), lambda s, n: (0, 0)),
        ],
        out_specs=[
            pl.BlockSpec((TOK, D), lambda s, n: (s, 0)),
            pl.BlockSpec((TOK, D), lambda s, n: (s, 0)),
            pl.BlockSpec((D, TOK), lambda s, n: (0, s)),
            pl.BlockSpec((1, P_ROWS, D), lambda s, n: (s, 0, 0)),
            pl.BlockSpec((1, 4, QN, LANES), lambda s, n: (s, 0, 0, 0)),
        ],
        scratch_shapes=[
            pltpu.VMEM((P_ROWS + 8, D), f32),
            pltpu.VMEM((LT, T_ROWS, LANES), f32),
            pltpu.VMEM((P_ROWS, LANES), f32),
            pltpu.VMEM((2 * R + 6, QN, LANES), f32),
        ],
    )
    return pl.pallas_call(
        gbst_fwd_kernel,
        grid_spec=grid_spec,
        out_shape=[
            jax.ShapeDtypeStruct((seqs * TOK, D), f32),
            jax.ShapeDtypeStruct((seqs * TOK, D), bf16),
            jax.ShapeDtypeStruct((D, seqs * TOK), bf16),
            jax.ShapeDtypeStruct((seqs, P_ROWS, D), f32),
            jax.ShapeDtypeStruct((seqs, 4, QN, LANES), f32),
        ],
        compiler_params=pltpu.CompilerParams(vmem_limit_bytes=VMEM_LIMIT),
        cost_estimate=cost(18, 30),
        name="gbst_forward",
    )(lengths, ids_col, table, vecs)


def gbst_bwd_kernel(len_ref, ids_ref, row_ref, table_ref, vec_ref, dh_ref, c_ref, w_ref, more_ref,
                    ig_ref, small_ref, ge_ref, e_ref, dt_ref, dc_ref, s_ref, k_ref, igs_ref):
    seq = pl.program_id(0)
    length = len_ref[seq]

    @pl.when(seq == 0)
    def _():
        ge_ref[...] = jnp.zeros_like(ge_ref)

    e_ref[pl.ds(0, P_ROWS), :] = look_up(ids_ref[0], table_ref)
    e_ref[pl.ds(P_ROWS, 8), :] = jnp.zeros((8, D), f32)
    for lt in range(LT):
        dt_ref[lt, 0:TOK, :] = dh_ref[:, pl.ds(lt * LANES, LANES)]
        dt_ref[lt, TOK:T_ROWS, :] = jnp.zeros((T_ROWS - TOK, LANES), f32)
    for lt in range(LT):
        lanes = pl.ds(lt * LANES, LANES)
        for half in range(2):
            c = [c_ref[0, pl.ds((half * 6 + r) * QN, QN), lanes] for r in range(6)]
            s3 = [c[0] + c[1] + c[2], c[3] + c[4] + c[5]]
            for k in range(3):
                tok = half * 3 + k
                other = tok ^ 1
                dh = dt_ref[lt, pl.ds(tok, QN, stride=6), :]
                s2 = c_ref[0, pl.ds(2 * other * QN, QN), lanes] + c_ref[0, pl.ds((2 * other + 1) * QN, QN), lanes]
                parts = [
                    (2 * tok, dh * c[2 * k]),
                    (2 * tok + 1, dh * c[2 * k + 1]),
                    (2 * R + tok, dh * s2),
                    (R + 2 * tok, dh * s3[0 if k < 2 else 1]),
                ]
                if k == 1:
                    parts.append((R + 2 * tok + 1, dh * s3[1]))
                for slot, part in parts:
                    s_ref[slot] = part if lt == 0 else s_ref[slot] + part

    def total(slot):
        return jnp.sum(s_ref[slot], axis=1, keepdims=True)

    d1, d3, dother = [], [], []
    for tok in range(6):
        d1 += [total(2 * tok), total(2 * tok + 1)]
        first = total(R + 2 * tok)
        d3 += [first, total(R + 2 * tok + 1) if tok % 3 == 1 else first]
        o = total(2 * R + tok)
        dother += [o, o]
    d1, d3, dother = place(d1, QN), place(d3, QN), place(dother, QN)
    mask, inverse, alpha = gbst_masks(length)
    weights = [w_ref[0, b] for b in range(4)]
    d2 = exact_dot(d1, group_matrix(2))
    g = [alpha * d1, alpha * d2 * inverse[0], alpha * d3 * inverse[1], alpha * (d2 + dother) * inverse[2]]
    mean = weights[0] * g[0] + weights[1] * g[1] + weights[2] * g[2] + weights[3] * g[3]
    d_size = [w * (x - mean) for w, x in zip(weights, g)]
    coef = d_size[0]
    for b, inv in zip((2, 3, 4), inverse):
        coef = coef + exact_dot(d_size[b - 1] * inv, group_matrix(b))
    own, a3, a4s = gbst_coefs(weights, inverse, alpha)
    for r in range(R):
        k_ref[r] = column(own, r)
        k_ref[R + r] = column(a3, r)
        k_ref[2 * R + r] = column(coef, r)
        k_ref[3 * R + r] = column(mask, r)
    for k in range(6):
        k_ref[4 * R + k] = column(a4s, 2 * k)

    for lt in range(LT):
        lanes = pl.ds(lt * LANES, LANES)
        taps = [jnp.broadcast_to(vec_ref[j : j + 1, lanes], (QN, LANES)) for j in range(4)]
        sw = jnp.broadcast_to(vec_ref[4:5, lanes], (QN, LANES))
        gs = jnp.zeros((QN, LANES), f32)
        gc = [jnp.zeros((QN, LANES), f32) for _ in range(4)]
        for half in range(2):
            dh = [dt_ref[lt, pl.ds(half * 3 + k, QN, stride=6), :] for k in range(3)]
            a = R + half * 6
            t3 = [
                (k_ref[a] + k_ref[a + 1]) * dh[0] + k_ref[a + 2] * dh[1],
                k_ref[a + 3] * dh[1] + (k_ref[a + 4] + k_ref[a + 5]) * dh[2],
            ]
            for k in range(3):
                tok = half * 3 + k
                other = tok ^ 1
                dother_h = dt_ref[lt, pl.ds(other, QN, stride=6), :]
                cross = k_ref[4 * R + other] * dother_h
                for e in range(2):
                    r = 2 * tok + e
                    cf = k_ref[2 * R + r]
                    dc = k_ref[r] * dh[k] + cross + t3[(r % 6) // 3] + cf * sw
                    gs = gs + cf * c_ref[0, pl.ds(r * QN, QN), lanes]
                    dc_ref[r, pl.ds(8, QN), :] = dc
                    for j in range(4):
                        gc[j] = gc[j] + dc * load_e(e_ref, r + j, lt)
        ge_ref[VROWS + 4 : VROWS + 5, lanes] += jnp.sum(gs, axis=0, keepdims=True)
        for j in range(4):
            ge_ref[VROWS + j : VROWS + j + 1, lanes] += jnp.sum(gc[j], axis=0, keepdims=True)
        for r in range(R):
            dc_ref[r, 0:8, :] = jnp.zeros((8, LANES), f32)
        for r in range(R):
            x = taps[0] * dc_ref[r, pl.ds(8, QN), :]
            for j in range(1, 4):
                back = dc_ref[r - j, pl.ds(8, QN), :] if r >= j else dc_ref[r - j + R, pl.ds(7, QN), :]
                x = x + taps[j] * back
            igs_ref[lt, pl.ds(r, QN, stride=R), :] = x * k_ref[3 * R + r]
    for lt in range(LT):
        lanes = pl.ds(lt * LANES, LANES)
        ig_ref[0, :, lanes] = igs_ref[lt, 0:MAXLEN, :].astype(bf16)
    vocab = lax.broadcasted_iota(jnp.int32, (VROWS, MAXLEN), 0)
    row_hits = jnp.where(vocab == row_ref[0], 1.0, 0.0).astype(bf16)
    ge_ref[0:VROWS, :] += jnp.dot(row_hits, ig_ref[0], preferred_element_type=f32)

    @pl.when(seq == pl.num_programs(0) - 1)
    def _():
        ge_ref[VROWS + 5 : VROWS + 8, :] = more_ref[...]
        for lt in range(LT):
            lanes = pl.ds(lt * LANES, LANES)
            small_ref[lanes, :] = ge_ref[:, lanes].T.astype(bf16)


def gbst_backward(lengths, ids_col, ids_row, table, vecs, d_hidden, c, w, more):
    seqs = ids_col.shape[0]
    grid_spec = pltpu.PrefetchScalarGridSpec(
        num_scalar_prefetch=1,
        grid=(seqs,),
        in_specs=[
            pl.BlockSpec((1, P_ROWS, LANES), lambda s, n: (s, 0, 0)),
            pl.BlockSpec((1, 1, MAXLEN), lambda s, n: (s, 0, 0)),
            pl.BlockSpec(table.shape, lambda s, n: (0, 0, 0)),
            pl.BlockSpec((16, D), lambda s, n: (0, 0)),
            pl.BlockSpec((TOK, D), lambda s, n: (s, 0)),
            pl.BlockSpec((1, P_ROWS, D), lambda s, n: (s, 0, 0)),
            pl.BlockSpec((1, 4, QN, LANES), lambda s, n: (s, 0, 0, 0)),
            pl.BlockSpec((3, D), lambda s, n: (0, 0)),
        ],
        out_specs=[
            pl.BlockSpec((1, MAXLEN, D), lambda s, n: (s, 0, 0)),
            pl.BlockSpec((D, SMALL), lambda s, n: (0, 0)),
        ],
        scratch_shapes=[
            pltpu.VMEM((SMALL, D), f32),
            pltpu.VMEM((P_ROWS + 8, D), f32),
            pltpu.VMEM((LT, T_ROWS, LANES), f32),
            pltpu.VMEM((R, QN + 8, LANES), f32),
            pltpu.VMEM((2 * R + 6, QN, LANES), f32),
            pltpu.VMEM((4 * R + 6, QN, LANES), f32),
            pltpu.VMEM((LT, P_ROWS, LANES), f32),
        ],
    )
    return pl.pallas_call(
        gbst_bwd_kernel,
        grid_spec=grid_spec,
        out_shape=[
            jax.ShapeDtypeStruct((seqs, MAXLEN, D), bf16),
            jax.ShapeDtypeStruct((D, SMALL), bf16),
        ],
        compiler_params=pltpu.CompilerParams(vmem_limit_bytes=VMEM_LIMIT),
        cost_estimate=cost(31, 40),
        name="gbst_backward",
    )(lengths, ids_col, ids_row, table, vecs, d_hidden, c, w, more)


HEADS = 12
HD = 64
BUCKETS = 32
SPAN = 1024
HB = 4
WIDE = HB * HD
GROUPS = HEADS // HB
dead_score = -1e9


def nt(a, b):
    return lax.dot_general(a, b, (((1,), (1,)), ((), ())), preferred_element_type=f32)


def nn(a, b):
    return jnp.dot(a, b, preferred_element_type=f32)


def bucket_hits(buckets):
    row = jnp.concatenate([buckets[TOK - 1 :], buckets[:1], buckets[: TOK - 1]])
    return jnp.arange(BUCKETS)[:, None] == row[None, :]


def build_bias(z_ref, bt_ref):
    for h in range(HB):
        row = jnp.broadcast_to(z_ref[h], (8, SPAN))
        sub = lax.broadcasted_iota(jnp.int32, (8, SPAN), 0)
        z = row
        for s in range(1, 8):
            z = jnp.where(sub == s, pltpu.roll(row, s, 1), z)
        for g in range(TOK // 8):
            bt_ref[h, pl.ds(8 * g, 8), :] = (z if g == 0 else pltpu.roll(z, 8 * g, 1))[:, :TOK]


def own_lanes(h):
    return lax.broadcasted_iota(jnp.int32, (TOK, WIDE), 1) // HD == h


def head_parts(k, q, length, h):
    lanes = lax.broadcasted_iota(jnp.int32, (TOK, WIDE), 1)
    rows = lax.broadcasted_iota(jnp.int32, (TOK, WIDE), 0)
    spare = HD * (h + 1) % WIDE
    dead = jnp.where(2 * rows < length, 0.0, dead_score)
    kf = jnp.where(lanes // HD == h, k.astype(f32), jnp.where(lanes == spare, dead, 0.0)).astype(bf16)
    qf = jnp.where(lanes == spare, 1.0, q.astype(f32)).astype(bf16)
    return kf, qf


def join_heads(parts):
    out = parts[0]
    for h in range(1, HB):
        out = jnp.where(own_lanes(h), parts[h], out)
    return out.astype(bf16)


def attn_fwd_kernel(len_ref, q_ref, k_ref, v_ref, z_ref, ctx_ref, lse_ref, bias_ref):
    length = len_ref[pl.program_id(1)]

    @pl.when(pl.program_id(1) == 0)
    def _():
        build_bias(z_ref, bias_ref)

    q, k, v = q_ref[...], k_ref[...], v_ref[...]

    def score(h):
        kf, qf = head_parts(k, q, length, h)
        return nt(qf, kf) + bias_ref[h]

    outs = []
    lanes = lax.broadcasted_iota(jnp.int32, (TOK, LANES), 1)
    lse = jnp.zeros((TOK, LANES), f32)
    s = score(0)
    for h in range(HB):
        later = score(h + 1) if h + 1 < HB else None
        top = jnp.max(s, axis=1, keepdims=True)
        p = jnp.exp(s - top)
        total = jnp.sum(p, axis=1, keepdims=True)
        outs.append(nn(p.astype(bf16), v) * (1.0 / total))
        lse = jnp.where(lanes == h, top + jnp.log(total), lse)
        s = later
    ctx_ref[...] = join_heads(outs)
    lse_ref[0, 0] = lse.T[0:8]


def attn_forward(lengths, qkv, z):
    seqs = qkv.shape[0] // TOK
    spec = lambda off: pl.BlockSpec((TOK, WIDE), lambda hp, s, n: (s, off + hp))
    return pl.pallas_call(
        attn_fwd_kernel,
        grid_spec=pltpu.PrefetchScalarGridSpec(
            num_scalar_prefetch=1,
            grid=(GROUPS, seqs),
            in_specs=[spec(0), spec(GROUPS), spec(2 * GROUPS), pl.BlockSpec((HB, 1, SPAN), lambda hp, s, n: (hp, 0, 0))],
            out_specs=[spec(0), pl.BlockSpec((1, 1, 8, TOK), lambda hp, s, n: (hp, s, 0, 0))],
            scratch_shapes=[pltpu.VMEM((HB, TOK, TOK), f32)],
        ),
        out_shape=[
            jax.ShapeDtypeStruct((seqs * TOK, D), bf16),
            jax.ShapeDtypeStruct((GROUPS, seqs, 8, TOK), f32),
        ],
        compiler_params=pltpu.CompilerParams(vmem_limit_bytes=VMEM_LIMIT),
        cost_estimate=cost(27, 20),
        name="attn_forward",
    )(lengths, qkv, qkv, qkv, z)


def attn_bwd_kernel(len_ref, q_ref, k_ref, v_ref, do_ref, o_ref, lse_ref, z_ref, dqkv_ref, gz_ref, bt_ref, g_ref):
    s_id = pl.program_id(1)
    length = len_ref[s_id]

    @pl.when(s_id == 0)
    def _():
        build_bias(z_ref, bt_ref)
        g_ref[...] = jnp.zeros_like(g_ref)

    q, k, v, do = q_ref[...], k_ref[...], v_ref[...], do_ref[...]
    kt = k.astype(f32).T.astype(bf16)
    lanes8 = lax.broadcasted_iota(jnp.int32, (8, WIDE), 1)
    rows8 = lax.broadcasted_iota(jnp.int32, (8, WIDE), 0)
    pick = jnp.where(lanes8 // HD == rows8, 1.0, 0.0).astype(bf16)
    prod = do.astype(f32) * o_ref[...].astype(f32)
    upper = prod.astype(bf16)
    delta = nt(pick, upper) + nt(pick, (prod - upper.astype(f32)).astype(bf16))
    dq, dk, dv = [], [], []

    def first(h):
        kf, qf = head_parts(k, q, length, h)
        vf = jnp.where(own_lanes(h), v.astype(f32), 0.0).astype(bf16)
        return nt(kf, qf) + bt_ref[h], nt(vf, do)

    now = first(0)
    for h in range(HB):
        later = first(h + 1) if h + 1 < HB else None
        s, d_prob = now
        p = jnp.exp(s - lse_ref[0, 0, h : h + 1, :])
        ds = p * (d_prob - delta[h : h + 1, :])
        g_ref[h] += ds
        low = ds.astype(bf16)
        dv.append(nn(p.astype(bf16), do))
        dk.append(nn(low, q))
        dq.append(nn(kt[h * HD : (h + 1) * HD], low))
        now = later
    dqkv_ref[0] = jnp.concatenate(dq, axis=0).T.astype(bf16)
    dqkv_ref[1] = join_heads(dk)
    dqkv_ref[2] = join_heads(dv)

    @pl.when(s_id == pl.num_programs(1) - 1)
    def _():
        for h in range(HB):
            total = jnp.zeros((8, SPAN), f32)
            for g in range(LANES // 8):
                tiles = [jnp.zeros((8, LANES), f32) for _ in range(SPAN // LANES)]
                for j in range(TOK // LANES):
                    x = g_ref[h, pl.ds(LANES * j + 8 * g, 8), :]
                    for t in range(TOK // LANES):
                        n = (t - j) % (SPAN // LANES)
                        tiles[n] = tiles[n] + x[:, t * LANES : (t + 1) * LANES]
                piece = jnp.concatenate(tiles, axis=1)
                total = total + (piece if g == 0 else pltpu.roll(piece, SPAN - 8 * g, 1))
            out = total[0:1]
            for s in range(1, 8):
                out = out + pltpu.roll(jnp.broadcast_to(total[s : s + 1], (8, SPAN)), SPAN - s, 1)[0:1]
            gz_ref[h] = out


def attn_backward(lengths, qkv, d_ctx, ctx, lse, z):
    seqs = qkv.shape[0] // TOK
    spec = lambda off: pl.BlockSpec((TOK, WIDE), lambda hp, s, n: (s, off + hp))
    return pl.pallas_call(
        attn_bwd_kernel,
        grid_spec=pltpu.PrefetchScalarGridSpec(
            num_scalar_prefetch=1,
            grid=(GROUPS, seqs),
            in_specs=[
                spec(0), spec(GROUPS), spec(2 * GROUPS), spec(0), spec(0),
                pl.BlockSpec((1, 1, 8, TOK), lambda hp, s, n: (hp, s, 0, 0)),
                pl.BlockSpec((HB, 1, SPAN), lambda hp, s, n: (hp, 0, 0)),
            ],
            out_specs=[
                pl.BlockSpec((3, TOK, WIDE), lambda hp, s, n: (0, s, hp)),
                pl.BlockSpec((HB, 1, SPAN), lambda hp, s, n: (hp, 0, 0)),
            ],
            scratch_shapes=[pltpu.VMEM((HB, TOK, TOK), f32), pltpu.VMEM((HB, TOK, TOK), f32)],
        ),
        out_shape=[
            jax.ShapeDtypeStruct((3, seqs * TOK, D), bf16),
            jax.ShapeDtypeStruct((HEADS, 1, SPAN), f32),
        ],
        compiler_params=pltpu.CompilerParams(vmem_limit_bytes=VMEM_LIMIT),
        cost_estimate=cost(46, 30),
        name="attn_backward",
    )(lengths, qkv, qkv, qkv, d_ctx, ctx, lse, z)


FF = 2048
FT = 256
RC = 512
MT = 256


def rms_scale(x):
    return lax.rsqrt(jnp.sum(x * x, axis=1, keepdims=True) * (1.0 / D) + epsilon)


def post_kernel(len_ref, shift_ref, ctx_ref, w_ref, hidden_ref, vec_ref, *refs):
    pieces, (att_ref, low_ref, low_t_ref, do_ref, do_t_ref) = refs[:-5], refs[-5:]
    s = pl.program_id(0)
    for i, piece in enumerate(pieces):
        @pl.when(shift_ref[s] == i)
        def _():
            do_ref[...] = piece[...]

    live = 2 * lax.broadcasted_iota(jnp.int32, (TOK, D), 0) < len_ref[s]
    d_out = jnp.where(live, do_ref[...].astype(f32), 0.0).astype(bf16)
    do_ref[...] = d_out
    do_t_ref[...] = d_out.T
    att = hidden_ref[...] + nn(ctx_ref[...], out_weights(w_ref))
    att_ref[...] = att
    low = (att * rms_scale(att) * vec_ref[6:7, :]).astype(bf16)
    low_ref[...] = low
    low_t_ref[...] = low.T


def rows_spec(width=D):
    return pl.BlockSpec((TOK, width), lambda s, *n: (s, 0))


def whole(*shape):
    return pl.BlockSpec(shape, lambda s, *n: (0,) * len(shape))


def out_block(shards):
    deep = D // shards
    return pl.BlockSpec((shards, 3 * deep, FT), lambda s, *n: (0, 4, 0))


def out_weights(ref):
    deep = ref.shape[1] // 3
    return jnp.concatenate([ref[:, i * deep : (i + 1) * deep, :].reshape(D, FT) for i in range(3)], axis=1)


def post_attention(lengths, shifts, ctx, pack, hidden, vecs, pieces, shards):
    rows = ctx.shape[0]
    cols_spec = pl.BlockSpec((D, TOK), lambda s, *n: (0, s))
    return pl.pallas_call(
        post_kernel,
        grid_spec=pltpu.PrefetchScalarGridSpec(
            num_scalar_prefetch=2,
            grid=(rows // TOK,),
            in_specs=[rows_spec(), out_block(shards), rows_spec(), whole(16, D)] + [whole(TOK, D)] * len(pieces),
            out_specs=[rows_spec(), rows_spec(), cols_spec, rows_spec(), cols_spec],
        ),
        out_shape=[
            jax.ShapeDtypeStruct((rows, D), f32),
            jax.ShapeDtypeStruct((rows, D), bf16),
            jax.ShapeDtypeStruct((D, rows), bf16),
            jax.ShapeDtypeStruct((rows, D), bf16),
            jax.ShapeDtypeStruct((D, rows), bf16),
        ],
        compiler_params=pltpu.CompilerParams(vmem_limit_bytes=VMEM_LIMIT),
        cost_estimate=cost(10, 30),
        name="post_attention",
    )(lengths, shifts, ctx, pack, hidden, vecs, *pieces)


def gelu_parts(v):
    c = 0.7978845608
    v2 = v * v
    t = jnp.tanh(v * (c + (c * 0.044715) * v2))
    half = 0.5 + 0.5 * t
    gelu = v * half
    slope = half + (0.5 * v) * (1.0 - t * t) * (c + (3.0 * c * 0.044715) * v2)
    return gelu, slope


def ffn_steps(x_any, d_any, xt_any, dt_any, wgu_ref, wo_ref, grad_ref, y_any, dx_any,
              x_ref, d_ref, xt_ref, dt_ref, y_ref, dx_ref, a_ref, dg_ref, du_ref, gu_ref, go_ref, in_sem, out_sem, sems):
    f = pl.program_id(0)
    steps = FF // 2 // FT
    rows_total = x_ref.shape[0]
    chunks = rows_total // RC
    shards, part = gu_ref.shape[1], gu_ref.shape[2]
    owners, deep = go_ref.shape[1], go_ref.shape[2]
    base = steps * part

    def copies(slot, step):
        return (
            pltpu.make_async_copy(
                gu_ref.at[slot], grad_ref.at[:, pl.ds(step * part, part), :], sems.at[0, slot]),
            pltpu.make_async_copy(
                go_ref.at[slot], grad_ref.at[pl.ds(step * owners, owners), pl.ds(base, deep), :], sems.at[1, slot]),
        )

    def row_loads(i):
        rows = pl.ds(i * RC, RC)
        return (
            pltpu.make_async_copy(x_any.at[rows], x_ref.at[rows], in_sem.at[0, i]),
            pltpu.make_async_copy(d_any.at[rows], d_ref.at[rows], in_sem.at[1, i]),
        )

    def turned_loads():
        return (
            pltpu.make_async_copy(xt_any, xt_ref, in_sem.at[2, 0]),
            pltpu.make_async_copy(dt_any, dt_ref, in_sem.at[2, 1]),
        )

    def row_stores(i):
        rows = pl.ds(i * RC, RC)
        return (
            pltpu.make_async_copy(y_ref.at[rows], y_any.at[rows], out_sem.at[0, i]),
            pltpu.make_async_copy(dx_ref.at[rows], dx_any.at[rows], out_sem.at[1, i]),
        )

    @pl.when(f == 0)
    def _():
        for i in range(chunks):
            for copy in row_loads(i):
                copy.start()
        for copy in turned_loads():
            copy.start()
        y_ref[...] = jnp.zeros_like(y_ref)
        dx_ref[...] = jnp.zeros_like(dx_ref)

    d_rows = part // 2
    third = deep // 3
    wg = wgu_ref[:, 0:d_rows, :].reshape(D, FT)
    wu = wgu_ref[:, d_rows:part, :].reshape(D, FT)
    wo = jnp.concatenate(
        [wo_ref[:, i * third : (i + 1) * third, :].reshape(FT, FT) for i in range(3)], axis=1)

    @pl.when(f == 0)
    def _():
        for i in range(chunks):
            for copy in row_loads(i):
                copy.wait()

    for i in range(chunks):
        rows = pl.ds(i * RC, RC)
        x, d = x_ref[rows, :], d_ref[rows, :]
        gelu, slope = gelu_parts(nn(x, wg))
        up = nn(x, wu)
        da = nt(d, wo)
        act = (gelu * up).astype(bf16)
        dg = (da * up * slope).astype(bf16)
        du = (da * gelu).astype(bf16)
        a_ref[rows, :] = act
        dg_ref[rows, :] = dg
        du_ref[rows, :] = du
        y_ref[rows, :] += nn(act, wo)
        dx_ref[rows, :] += nt(dg, wg) + nt(du, wu)
    if y_any is not None:

        @pl.when(f == steps - 1)
        def _():
            for i in range(chunks):
                for copy in row_stores(i):
                    copy.start()

    slot = lax.rem(f, 2)

    @pl.when(f == 0)
    def _():
        for copy in turned_loads():
            copy.wait()

    @pl.when(f >= 2)
    def _():
        for copy in copies(slot, f - 2):
            copy.wait()

    gu_ref[slot, :, 0:d_rows, :] = nn(xt_ref[...], dg_ref[...]).astype(bf16).reshape(shards, d_rows, FT)
    gu_ref[slot, :, d_rows:part, :] = nn(xt_ref[...], du_ref[...]).astype(bf16).reshape(shards, d_rows, FT)
    go = nn(dt_ref[...], a_ref[...]).T.astype(bf16)
    for i in range(3):
        go_ref[slot, :, i * third : (i + 1) * third, :] = go[:, i * FT : (i + 1) * FT].reshape(owners, third, FT)
    for copy in copies(slot, f):
        copy.start()

    @pl.when(f == steps - 1)
    def _():
        for copy in copies(1 - slot, f - 1) + copies(slot, f):
            copy.wait()
        if y_any is not None:
            for i in range(chunks):
                for copy in row_stores(i):
                    copy.wait()


def first_kernel(x, d, xt, dt, wgu, wo, grad, y, dx, *scratch):
    ffn_steps(x, d, xt, dt, wgu, wo, grad, y, dx, *scratch)


def second_kernel(len_ref, x, d, xt, dt, wgu, wo, att_ref, y1_ref, dx1_ref, do_ref, ctx_ref, w_ref, vec_ref,
                  grad, out_ref, datt_ref, dctx_ref, gw_ref, gg_ref, acc_ref, flat_ref, *scratch):
    f = pl.program_id(0)
    steps = FF // 2 // FT

    @pl.when(f == 0)
    def _():
        acc_ref[...] = jnp.zeros_like(acc_ref)
        gg_ref[...] = jnp.zeros_like(gg_ref)
        flat_ref[...] = out_weights(w_ref)

    @pl.when(f < steps)
    def _():
        ffn_steps(x, d, xt, dt, wgu, wo, grad, None, None, *scratch)

    @pl.when(f >= steps)
    def _():
        tile = f - steps
        y_ref, dx_ref = scratch[4], scratch[5]
        rows = pl.ds(pl.multiple_of(tile * MT, MT), MT)
        per = TOK // MT
        length = len_ref[tile // per]
        place_in = lax.rem(tile, per) * MT + lax.broadcasted_iota(jnp.int32, (MT, 1), 0)
        live = jnp.where(2 * place_in < length, 1.0, 0.0).astype(f32)
        att = att_ref[...]
        out_ref[...] = ((att + y1_ref[...] + y_ref[rows, :]) * live).astype(bf16)
        back, gain_grad = norm_back(att, dx1_ref[...] + dx_ref[rows, :], vec_ref[6:7, :])
        gg_ref[...] += gain_grad
        d_att = do_ref[...].astype(f32) + back
        datt_ref[...] = d_att
        low = d_att.astype(bf16)
        dctx_ref[...] = nt(low, flat_ref[...]).astype(bf16)
        acc_ref[...] += nn(ctx_ref[...].T, low)

    @pl.when(f == pl.num_programs(0) - 1)
    def _():
        gw_ref[...] = acc_ref[...].astype(bf16)


def ffn_scratch(rows, shards):
    part, hs = 2 * D // shards, FF // 2 // shards
    return [
        pltpu.VMEM((rows, D), bf16),
        pltpu.VMEM((rows, D), bf16),
        pltpu.VMEM((D, rows), bf16),
        pltpu.VMEM((D, rows), bf16),
        pltpu.VMEM((rows, D), f32),
        pltpu.VMEM((rows, D), f32),
        pltpu.VMEM((rows, FT), bf16),
        pltpu.VMEM((rows, FT), bf16),
        pltpu.VMEM((rows, FT), bf16),
        pltpu.VMEM((2, shards, part, FT), bf16),
        pltpu.VMEM((2, FT // hs, 3 * hs, FT), bf16),
        pltpu.SemaphoreType.DMA((3, max(2, rows // RC))),
        pltpu.SemaphoreType.DMA((2, rows // RC)),
        pltpu.SemaphoreType.DMA((2, 2)),
    ]


def ffn_specs(tiles, shards):
    last = lambda f: jnp.minimum(f, tiles - 1)
    part, hs = 2 * D // shards, FF // 2 // shards
    return [pl.BlockSpec(memory_space=pl.ANY)] * 4 + [
        pl.BlockSpec((shards, part, FT), lambda f, *n: (0, last(f), 0)),
        pl.BlockSpec((FT // hs, 3 * hs, FT), lambda f, *n: (last(f), 2, 0)),
    ]


def grad_shape(shards):
    part, hs = 2 * D // shards, FF // 2 // shards
    return jax.ShapeDtypeStruct((shards, FF // 2 // FT * part + 3 * hs, FT), bf16)


def ffn_first(x, d_out, xt, dt, pack, shards):
    rows = x.shape[0]
    tiles = FF // 2 // FT
    anywhere = pl.BlockSpec(memory_space=pl.ANY)
    return pl.pallas_call(
        first_kernel,
        grid=(tiles,),
        in_specs=ffn_specs(tiles, shards),
        out_specs=[anywhere] * 3,
        out_shape=[
            grad_shape(shards),
            jax.ShapeDtypeStruct((rows, D), f32),
            jax.ShapeDtypeStruct((rows, D), f32),
        ],
        scratch_shapes=ffn_scratch(rows, shards),
        compiler_params=pltpu.CompilerParams(vmem_limit_bytes=VMEM_LIMIT),
        cost_estimate=cost(36, 40),
        name="ffn_first",
    )(x, d_out, xt, dt, pack, pack)


def ffn_second(lengths, x, d_out, xt, dt, pack, att, y1, dx1, ctx, pack0, vecs, shards):
    rows = x.shape[0]
    tiles = FF // 2 // FT
    tile_rows = pl.BlockSpec((MT, D), lambda f, n: (jnp.maximum(f - tiles, 0), 0))
    return pl.pallas_call(
        second_kernel,
        grid_spec=pltpu.PrefetchScalarGridSpec(
            num_scalar_prefetch=1,
            grid=(tiles + rows // MT,),
            in_specs=ffn_specs(tiles, shards) + [tile_rows] * 5 + [out_block(shards), whole(16, D)],
            out_specs=[pl.BlockSpec(memory_space=pl.ANY), tile_rows, tile_rows, tile_rows, whole(D, D), whole(1, D)],
            scratch_shapes=[pltpu.VMEM((D, D), f32), pltpu.VMEM((D, D), bf16)] + ffn_scratch(rows, shards),
        ),
        out_shape=[
            grad_shape(shards),
            jax.ShapeDtypeStruct((rows, D), bf16),
            jax.ShapeDtypeStruct((rows, D), f32),
            jax.ShapeDtypeStruct((rows, D), bf16),
            jax.ShapeDtypeStruct((D, D), bf16),
            jax.ShapeDtypeStruct((1, D), f32),
        ],
        compiler_params=pltpu.CompilerParams(vmem_limit_bytes=VMEM_LIMIT),
        cost_estimate=cost(46, 60),
        name="ffn_second",
    )(lengths, x, d_out, xt, dt, pack, pack, att, y1, dx1, d_out, ctx, pack0, vecs)


def norm_back(x, grad, gain):
    r = rms_scale(x)
    n = x * r
    u = gain * grad
    mean = jnp.sum(n * u, axis=1, keepdims=True) * (1.0 / D)
    return r * (u - n * mean), jnp.sum(n * grad, axis=0, keepdims=True)


def qkv_grad_kernel(dqkv_ref, normed_t_ref, go_ref, gw_ref):
    i = pl.program_id(0)

    @pl.when(i < 3)
    def _():
        gw_ref[...] = nn(normed_t_ref[...], dqkv_ref[0]).astype(bf16)

    @pl.when(i == 3)
    def _():
        gw_ref[...] = go_ref[...]


def qkv_grad(dqkv, normed_t, g_attn_out):
    rows = normed_t.shape[1]
    return pl.pallas_call(
        qkv_grad_kernel,
        grid=(4,),
        in_specs=[
            pl.BlockSpec((1, rows, D), lambda i: (jnp.minimum(i, 2), 0, 0)),
            whole(D, rows), whole(D, D),
        ],
        out_specs=pl.BlockSpec((D, D), lambda i: (0, i)),
        out_shape=jax.ShapeDtypeStruct((D, 4 * D), bf16),
        compiler_params=pltpu.CompilerParams(vmem_limit_bytes=VMEM_LIMIT),
        cost_estimate=cost(11, 20),
        name="qkv_grad",
    )(dqkv, normed_t, g_attn_out)


def qkv_back_kernel(dqkv_ref, w_ref, hidden_ref, datt_ref, vec_ref, dh_ref, gg_ref):
    @pl.when(pl.program_id(0) == 0)
    def _():
        gg_ref[...] = jnp.zeros_like(gg_ref)

    dn = nt(dqkv_ref[0], w_ref[:, 0:D])
    for i in range(1, 3):
        dn = dn + nt(dqkv_ref[i], w_ref[:, i * D : (i + 1) * D])
    back, gain_grad = norm_back(hidden_ref[...], dn, vec_ref[5:6, :])
    gg_ref[...] += gain_grad
    dh_ref[...] = datt_ref[...] + back


def qkv_backward(dqkv, attn_w, hidden, d_att, vecs):
    rows = hidden.shape[0]
    tile = pl.BlockSpec((TOK, D), lambda s: (s, 0))
    return pl.pallas_call(
        qkv_back_kernel,
        grid=(rows // TOK,),
        in_specs=[
            pl.BlockSpec((3, TOK, D), lambda s: (0, s, 0)),
            pl.BlockSpec((D, 3 * D), lambda s: (0, 0)),
            tile, tile, whole(16, D),
        ],
        out_specs=[tile, whole(1, D)],
        out_shape=[jax.ShapeDtypeStruct((rows, D), f32), jax.ShapeDtypeStruct((1, D), f32)],
        compiler_params=pltpu.CompilerParams(vmem_limit_bytes=VMEM_LIMIT),
        cost_estimate=cost(14, 40),
        name="qkv_backward",
    )(dqkv, attn_w, hidden, d_att, vecs)


MESH = pl.DeviceIdType.MESH


def greet(peers):
    barrier = pltpu.get_barrier_semaphore()
    for peer in peers:
        pl.semaphore_signal(barrier, inc=1, device_id=peer, device_id_type=MESH)
    pl.semaphore_wait(barrier, len(peers))


def pack_half(out_ref, ffn_in_ref, ffn_out_ref, h, shards):
    hs = FF // 2 // shards
    owners = FT // hs
    deep = ffn_in_ref.shape[0]
    row = 0
    for f in range(FF // 2 // FT):
        for g in range(2):
            starts = [g * FF + (f * owners + o) * 2 * hs + h * hs for o in range(owners)]
            out_ref[row : row + deep, :] = jnp.concatenate([ffn_in_ref[:, a : a + hs] for a in starts], axis=1)
            row += deep
    for i in range(3):
        out_ref[row : row + hs, :] = ffn_out_ref[h * hs : (h + 1) * hs, i * FT : (i + 1) * FT]
        row += hs
    return row


def prepare_kernel(replicas, shards, length_ref, target_ref, embed_ref, conv_ref, score_ref, gain1_ref, gain2_ref, rel_ref,
                   ids_ref, attn_out_ref, ffn_in_ref, ffn_out_ref,
                   table_ref, vec_ref, slots_ref, column_ref, pack0_ref, pack1_ref,
                   own_ref, wide_ref, turn_ref, nat_ref, wanted_ref, send_sem, recv_sem):
    rep, me = lax.axis_index("rep"), lax.axis_index("shard")
    deep = embed_ref.shape[1]
    seqs = ids_ref.shape[0]
    twin = me + 1 - 2 * lax.rem(me, 2)
    far = [lax.rem(me + 2 * i, shards) for i in range(1, shards // 2)]
    others = [lax.rem(rep + i, replicas) for i in range(1, replicas)]
    greet([(rep, twin)] + [(rep, p) for p in far] + [(p, me) for p in others])

    def send(i, src, dst, device):
        copy = pltpu.make_async_remote_copy(
            src_ref=src, dst_ref=dst, send_sem=send_sem.at[i], recv_sem=recv_sem.at[i],
            device_id=device, device_id_type=MESH)
        copy.start()
        return copy

    wide_ref[...] = jnp.zeros_like(wide_ref)
    wide_ref[0:VOCAB, 0:deep] = embed_ref[...].astype(f32)
    wide_ref[VOCAB : VOCAB + 4, 0:deep] = conv_ref[...].astype(f32)
    for i, ref in enumerate((score_ref, gain1_ref, gain2_ref)):
        wide_ref[VOCAB + 4 + i : VOCAB + 5 + i, 0:deep] = ref[...].astype(f32).reshape(1, deep)
    rel_rows, heads = rel_ref.shape
    wide_ref[VOCAB + 7 : VOCAB + 7 + rel_rows, 0:heads] = rel_ref[...].astype(f32)
    own_ref[...] = wide_ref[...].T[0:deep].astype(bf16)
    near = [send(0, own_ref, table_ref.at[me], (rep, twin))]
    direct = [send(1 + i, own_ref, table_ref.at[me], (rep, p)) for i, p in enumerate(far)]
    lanes = lax.broadcasted_iota(jnp.int32, (8, 128), 1)
    wanted = jnp.zeros((8, 128), jnp.int32)
    for k in range(seqs):
        slot = target_ref[k] % seqs
        wanted = wanted + jnp.where(lanes == target_ref[k] // seqs // shards, slot + 1, 0)
    wanted_ref[...] = wanted
    base = shards
    asks = [send(base + i, wanted_ref, slots_ref.at[rep], (p, me)) for i, p in enumerate(others)]
    table_ref[me] = own_ref[...]
    slots_ref[rep] = wanted_ref[...]
    row = pack_half(pack0_ref, ffn_in_ref, ffn_out_ref, 0, shards)
    for i in range(3):
        pack0_ref[row : row + deep, :] = attn_out_ref[:, i * FT : (i + 1) * FT]
        row += deep
    pack_half(pack1_ref, ffn_in_ref, ffn_out_ref, 1, shards)
    base = base + replicas - 1
    for i, copy in enumerate(direct):
        copy.wait()
        source = lax.rem(me - 2 * (i + 1) + shards, shards)
        near.append(send(base + i, table_ref.at[source], table_ref.at[source], (rep, twin)))
    turn_ref[...] = jnp.full(turn_ref.shape, -1.0, f32)
    place = lax.broadcasted_iota(jnp.int32, (1, MAXLEN), 1)
    for s in range(seqs):
        turn_ref[s : s + 1, 0:MAXLEN] = jnp.where(place < length_ref[s], ids_ref[s : s + 1, :], -1).astype(f32)
    nat_ref[...] = turn_ref[...].T
    for r in range(R):
        rows = nat_ref[pl.ds(r, QN, stride=R), :]
        for s in range(seqs):
            column_ref[s, r * QN : (r + 1) * QN, :] = jnp.broadcast_to(rows[:, s : s + 1], (QN, 128))
    for copy in near + asks:
        copy.wait()
    last = table_ref[:, :, SMALL - 128 :].astype(f32).reshape(D, 128).T
    first = VOCAB - (SMALL - 128)
    vec_ref[...] = last[first : first + 16]


def prepare(lengths, target, embed, conv_w, score_w, gain_attn, gain_ffn, rel_table, ids, attn_out, ffn_in, ffn_out,
            replicas, shards):
    deep = embed.shape[1]
    seqs = ids.shape[0]
    part, hs = 2 * D // shards, FF // 2 // shards
    rows = FF // 2 // FT * part + 3 * hs
    sems = shards + replicas - 1 + shards // 2 - 1
    vmem = pl.BlockSpec(memory_space=pltpu.VMEM)
    smem = pl.BlockSpec(memory_space=pltpu.SMEM)
    return pl.pallas_call(
        lambda *refs: prepare_kernel(replicas, shards, *refs),
        out_shape=[
            jax.ShapeDtypeStruct((shards, deep, SMALL), bf16),
            jax.ShapeDtypeStruct((16, D), f32),
            jax.ShapeDtypeStruct((replicas, 8, 128), jnp.int32),
            jax.ShapeDtypeStruct((seqs, P_ROWS, 128), f32),
            jax.ShapeDtypeStruct((rows + 3 * deep, FT), bf16),
            jax.ShapeDtypeStruct((rows, FT), bf16),
        ],
        in_specs=[smem] * 2 + [vmem] * 10,
        out_specs=[vmem] * 6,
        scratch_shapes=[
            pltpu.VMEM((deep, SMALL), bf16),
            pltpu.VMEM((SMALL, 128), f32),
            pltpu.VMEM((128, 1152), f32),
            pltpu.VMEM((1152, 128), f32),
            pltpu.VMEM((8, 128), jnp.int32),
            pltpu.SemaphoreType.DMA((sems,)),
            pltpu.SemaphoreType.DMA((sems,)),
        ],
        compiler_params=pltpu.CompilerParams(collective_id=1, has_side_effects=True, vmem_limit_bytes=VMEM_LIMIT),
        cost_estimate=cost(12, 8),
        name="prepare",
    )(lengths, target, embed, conv_w, score_w, gain_attn, gain_ffn, rel_table, ids, attn_out, ffn_in, ffn_out)


def pick_kernel(order_ref, in_ref, *out_refs):
    for i, ref in enumerate(out_refs):
        @pl.when(pl.program_id(0) == i)
        def _():
            ref[...] = in_ref[0]


def pick(order, rows):
    count = order.shape[0]
    block = (rows.shape[1], rows.shape[2])
    return pl.pallas_call(
        pick_kernel,
        grid_spec=pltpu.PrefetchScalarGridSpec(
            num_scalar_prefetch=1,
            grid=(count,),
            in_specs=[pl.BlockSpec((1,) + block, lambda i, order: (order[i], 0, 0))],
            out_specs=[pl.BlockSpec(block, lambda i, order: (0, 0))] * count,
        ),
        out_shape=[jax.ShapeDtypeStruct(block, rows.dtype)] * count,
        compiler_params=pltpu.CompilerParams(vmem_limit_bytes=VMEM_LIMIT),
        cost_estimate=cost(4, 6),
        name="pick",
    )(order, rows)


def finish_kernel(replicas, shards, piece_ref, small_ref, in_ref, out_ref, embed_ref, conv_ref, rest_ref, got_ref, held_ref, other_ref,
                  last_ref, send_sem, recv_sem, send2_sem, recv2_sem):
    rep, me = lax.axis_index("rep"), lax.axis_index("shard")
    wide = piece_ref.shape[2]
    half = piece_ref.shape[1]
    bits = [1 << b for b in range(replicas.bit_length() - 1)]
    peers = [(rep, lax.rem(me + i, shards)) for i in range(1, shards)]
    partners = {}
    for bit in bits:
        down = lax.rem(rep // bit, 2)
        partners[bit] = (rep + bit - 2 * bit * down, me)
    greet(peers + [partners[bit] for bit in bits])
    copies = []
    for i, peer in enumerate(peers):
        copy = pltpu.make_async_remote_copy(
            src_ref=small_ref.at[peer[1]], dst_ref=got_ref.at[i], send_sem=send_sem.at[i],
            recv_sem=recv_sem.at[i], device_id=peer, device_id_type=MESH)
        copy.start()
        copies.append(copy)
    last_ref[...] = jnp.zeros_like(last_ref)
    held_ref[0, :, :, 0:wide] = piece_ref[...]
    total = small_ref[me].astype(f32)
    for i, copy in enumerate(copies):
        copy.wait()
        total = total + got_ref[i].astype(f32)
    held_ref[0, :, :, wide:] = total.astype(bf16)
    for t in range(len(bits)):
        copies = []
        for h, order in enumerate((bits, bits[::-1])):
            copy = pltpu.make_async_remote_copy(
                src_ref=held_ref.at[t, h], dst_ref=other_ref.at[t, h], send_sem=send2_sem.at[t, h],
                recv_sem=recv2_sem.at[t, h], device_id=partners[order[t]], device_id_type=MESH)
            copy.start()
            copies.append(copy)
        for h, copy in enumerate(copies):
            copy.wait()
            total = held_ref[t, h].astype(f32) + other_ref[t, h].astype(f32)
            if t == len(bits) - 1:
                rows = slice(h * half, (h + 1) * half)
                in_ref[rows, :] = total[:, 0 : 3 * D]
                out_ref[rows, :] = total[:, 3 * D : wide]
                last_ref[rows, :] = total[:, wide:]
            else:
                held_ref[t + 1, h] = total.astype(bf16)
    turned = last_ref[...].T
    deep = embed_ref.shape[1]
    embed_ref[...] = turned[0:VOCAB, 0:deep]
    conv_ref[...] = turned[VROWS : VROWS + 4, 0:deep]
    rest_ref[...] = turned[VROWS + 4 : VROWS + 8, 0:deep]


def finish(piece, small, replicas, shards):
    rows, wide = piece.shape
    half = rows // 2
    steps = replicas.bit_length() - 1
    vmem = pl.BlockSpec(memory_space=pltpu.VMEM)
    return pl.pallas_call(
        lambda *refs: finish_kernel(replicas, shards, *refs),
        out_shape=[
            jax.ShapeDtypeStruct((rows, 3 * D), f32),
            jax.ShapeDtypeStruct((rows, D), f32),
            jax.ShapeDtypeStruct((VOCAB, rows), f32),
            jax.ShapeDtypeStruct((4, rows), f32),
            jax.ShapeDtypeStruct((4, rows), f32),
        ],
        in_specs=[vmem, vmem],
        out_specs=[vmem] * 5,
        scratch_shapes=[
            pltpu.VMEM((shards - 1, 2, half, SMALL), bf16),
            pltpu.VMEM((steps, 2, half, wide + SMALL), bf16),
            pltpu.VMEM((steps, 2, half, wide + SMALL), bf16),
            pltpu.VMEM((128, SMALL), f32),
            pltpu.SemaphoreType.DMA((shards - 1,)),
            pltpu.SemaphoreType.DMA((shards - 1,)),
            pltpu.SemaphoreType.DMA((steps, 2)),
            pltpu.SemaphoreType.DMA((steps, 2)),
        ],
        compiler_params=pltpu.CompilerParams(
            collective_id=2, has_side_effects=True, vmem_limit_bytes=VMEM_LIMIT),
        cost_estimate=cost(20, 4),
        name="finish_sums",
    )(piece.reshape(2, half, wide), small.reshape(shards, 2, half, SMALL))


def unpack_kernel(shards, first_ref, second_ref, other_ref, in_ref, out_ref):
    hs = FF // 2 // shards
    deep = in_ref.shape[0]
    owners = FT // hs
    for h in range(2):
        def load(start, count):
            rows = slice(start, start + count)
            if h == 0:
                return first_ref[rows, :].astype(f32)
            return second_ref[rows, :].astype(f32) + other_ref[rows, :].astype(f32)

        row = 0
        for f in range(FF // 2 // FT):
            for g in range(2):
                x = load(row, deep)
                for o in range(owners):
                    start = g * FF + (f * owners + o) * 2 * hs + h * hs
                    in_ref[:, start : start + hs] = x[:, o * hs : (o + 1) * hs]
                row += deep
        for i in range(3):
            out_ref[h * hs : (h + 1) * hs, i * FT : (i + 1) * FT] = load(row, hs)
            row += hs


def unpack(first, second, other, shards):
    vmem = pl.BlockSpec(memory_space=pltpu.VMEM)
    return pl.pallas_call(
        lambda *refs: unpack_kernel(shards, *refs),
        out_shape=[
            jax.ShapeDtypeStruct((D // shards, 2 * FF), f32),
            jax.ShapeDtypeStruct((FF // shards, D), f32),
        ],
        in_specs=[vmem] * 3,
        out_specs=[vmem] * 2,
        compiler_params=pltpu.CompilerParams(vmem_limit_bytes=VMEM_LIMIT),
        cost_estimate=cost(3, 5),
        name="unpack",
    )(first, second, other)


def send_cotangent(slots, cotangent):
    replicas = lax.axis_size("rep")
    places = jnp.arange(replicas)
    rep = lax.axis_index("rep")
    asked = jnp.where(places[None, :] == rep, slots, 0).sum(axis=1) - 1
    turned = (places[None, :] == (rep + places[:, None]) % replicas) * asked[None, :]
    pieces = list(pick(jnp.maximum(turned.sum(axis=1), 0), cotangent))
    for shift in range(1, replicas):
        pieces[shift] = lax.ppermute(pieces[shift], "rep", [(r, (r + shift) % replicas) for r in range(replicas)])
    return pieces


def swap(x, bit):
    replicas = lax.axis_size("rep")
    return lax.ppermute(x, "rep", [(r, r ^ bit) for r in range(replicas)])


def add_low(a, b):
    return (a.astype(f32) + b.astype(f32)).astype(bf16)


def scatter_sum(grad):
    return lax.psum_scatter(grad, "shard", scatter_dimension=0, tiled=True)


def body(
    byte_ids, lengths, target, rel_bucket, cotangent, embed, conv_w, score_w, gain_attn,
    attn_in, attn_out, gain_ffn, ffn_in, ffn_out, rel_table,
):
    seqs = byte_ids.shape[0]
    replicas, shards = lax.axis_size("rep"), lax.axis_size("shard")
    width = embed.shape[1]
    attn_w = lax.all_gather(attn_in, "shard", axis=0, tiled=True)
    table, vecs, slots, ids_col, pack0, pack1 = prepare(
        lengths, target, embed, conv_w, score_w, gain_attn, gain_ffn, rel_table, byte_ids,
        attn_out, ffn_in, ffn_out, replicas, shards,
    )
    packs = [lax.all_gather(pack, "shard", axis=0) for pack in (pack0, pack1)]
    rel_rows = rel_table.shape[0]
    rel = vecs[7 : 7 + rel_rows].astype(bf16).reshape(rel_rows, shards, width)[:, :, :HEADS]
    rel = rel.transpose(1, 0, 2).reshape(BUCKETS, HEADS)
    hits = bucket_hits(rel_bucket)
    hits_back = bucket_hits(rel_bucket[::-1])

    def spread(h):
        dims = (((0,), (0,)), ((), ()))
        return lax.dot_general(rel, h.astype(bf16), dims, preferred_element_type=f32).reshape(HEADS, 1, SPAN)

    z, z_back = spread(hits), spread(hits_back)

    hidden, normed, normed_t, convolved, weights = gbst_forward(lengths, ids_col, table, vecs)
    qkv = jnp.dot(normed, attn_w, preferred_element_type=f32).astype(bf16)
    qkv, slots = lax.optimization_barrier((qkv, slots))
    pieces = send_cotangent(slots[:, 0, :replicas], cotangent)
    ctx, lse = attn_forward(lengths, qkv, z)
    ctx, pieces = lax.optimization_barrier((ctx, pieces))
    shifts = (lax.axis_index("rep") - target // seqs // shards) % replicas
    attended, low, low_t, d_out, d_out_t = post_attention(
        lengths, shifts, ctx, packs[0], hidden, vecs, pieces, shards
    )
    g_half1, y1, dx1 = ffn_first(low, d_out, low_t, d_out_t, packs[0], shards)
    g_half2, out, d_att, d_ctx, g_attn_out, g_gain_ffn = ffn_second(
        lengths, low, d_out, low_t, d_out_t, packs[1], attended, y1, dx1, ctx, packs[0], vecs, shards
    )
    one, two = [scatter_sum(g.reshape(-1, FT)) for g in (g_half1, g_half2)]
    bits = [1 << b for b in range(replicas.bit_length() - 1)]
    d_ctx, one = lax.optimization_barrier((d_ctx, one))
    other = swap(one, bits[0])
    dqkv, gz = attn_backward(lengths, qkv, d_ctx, ctx, lse, z_back)
    dqkv, other = lax.optimization_barrier((dqkv, other))
    one = add_low(one, other)
    g_attn = qkv_grad(dqkv, normed_t, g_attn_out)
    g_attn, two = lax.optimization_barrier((g_attn, two))
    p_attn = scatter_sum(g_attn)
    others = swap(one, bits[1]), swap(two, bits[0])
    d_hidden, g_gain_attn = qkv_backward(dqkv, attn_w, hidden, d_att, vecs)
    d_hidden, others = lax.optimization_barrier((d_hidden, others))
    one, two = add_low(one, others[0]), add_low(two, others[1])
    for bit in bits[2:]:
        one, two = add_low(one, swap(one, bit)), add_low(two, swap(two, bit))
    g_table = lax.dot_general(
        hits_back.astype(f32), gz.reshape(HEADS, SPAN), (((1,), (1,)), ((), ())),
        precision=lax.Precision.HIGHEST, preferred_element_type=f32,
    )
    per = g_table.size // shards
    table_row = jnp.pad(g_table.reshape(shards, per), ((0, 0), (0, width - per))).reshape(1, D)
    more = jnp.concatenate([g_gain_attn, g_gain_ffn, table_row], axis=0)
    d_hidden, more, one, two = lax.optimization_barrier((d_hidden, more, one, two))
    other = swap(two, bits[1])
    ids = jnp.where(jnp.arange(MAXLEN)[None, :] < lengths[:, None], byte_ids, -1)
    input_grad, small = gbst_backward(
        lengths, ids_col, ids.reshape(seqs, 1, MAXLEN), table, vecs, d_hidden, convolved, weights, more
    )
    small, other = lax.optimization_barrier((small, other))
    s_attn_in, s_attn_out, s_embed, s_conv, s_rest = finish(p_attn, small, replicas, shards)
    s_ffn_in, s_ffn_out = unpack(one, two, other, shards)
    return (
        out.reshape(seqs, TOK, D),
        input_grad,
        s_embed,
        s_conv,
        s_rest[0],
        s_rest[1],
        s_attn_in,
        s_attn_out,
        s_rest[2],
        s_ffn_in,
        s_ffn_out,
        s_rest[3, :per].reshape(rel_table.shape),
    )


def solution(mesh):
    in_specs = (
        P(("rep", "shard"), None), P(("rep", "shard")), P(("rep", "shard")), P(),
        P(("rep", "shard"), None, None), P(None, "shard"), P(None, "shard"), P("shard"), P("shard"),
        P("shard", None), P("shard", None), P("shard"), P("shard", None), P("shard", None), P("shard", None),
    )
    out_specs = (
        P(("rep", "shard"), None, None), P(("rep", "shard"), None, None), P(None, "shard"), P(None, "shard"),
        P("shard"), P("shard"), P("shard", None), P("shard", None), P("shard"), P("shard", None),
        P("shard", None), P("shard", None),
    )
    return jax.shard_map(body, mesh=mesh, in_specs=in_specs, out_specs=out_specs, check_vma=False)
```

```python
import jax
import jax.numpy as jnp
from jax import lax
from jax.experimental import pallas as pl
from jax.experimental.pallas import tpu as pltpu
from jax.sharding import PartitionSpec as P

D = 768
VOCAB = 259
VROWS = 272
VMEM_LIMIT = 60 << 20
SMALL = 384
MAXLEN = 1024
TOK = 512
LANES = 128
QN = 88
R = 12
P_ROWS = QN * R
T_ROWS = 528
LT = D // LANES
epsilon = 1e-06
f32 = jnp.float32
bf16 = jnp.bfloat16


def cost(us, mib):
    return pl.CostEstimate(flops=int(us * 1e9), bytes_accessed=mib << 20, transcendentals=0)


def lane_iota(rows):
    return lax.broadcasted_iota(jnp.int32, (rows, LANES), 1)


def group_matrix(b):
    row = lax.broadcasted_iota(jnp.int32, (LANES, LANES), 0)
    col = lax.broadcasted_iota(jnp.int32, (LANES, LANES), 1)
    return jnp.where((row // b == col // b) & (row < R) & (col < R), 1.0, 0.0).astype(f32)


def exact_dot(a, b):
    return jnp.dot(a, b, precision=lax.Precision.HIGHEST, preferred_element_type=f32)


def place(columns, rows):
    lanes = lane_iota(rows)
    out = jnp.zeros((rows, LANES), f32)
    for r, column in enumerate(columns):
        out = jnp.where(lanes == r, column, out)
    return out


def gbst_masks(length):
    q = lax.broadcasted_iota(jnp.int32, (QN, LANES), 0)
    r = lax.broadcasted_iota(jnp.int32, (QN, LANES), 1)
    mask = jnp.where((q * R + r < length) & (r < R), 1.0, 0.0).astype(f32)
    inverse = [1.0 / jnp.maximum(exact_dot(mask, group_matrix(b)), 1.0) for b in (2, 3, 4)]
    pair = exact_dot(mask, group_matrix(2))
    alpha = mask / jnp.maximum(pair, 1.0)
    return mask, inverse, alpha


def gbst_weights(s1, inverse):
    sizes = [s1] + [exact_dot(s1, group_matrix(b)) * inv for b, inv in zip((2, 3, 4), inverse)]
    top = jnp.maximum(jnp.maximum(sizes[0], sizes[1]), jnp.maximum(sizes[2], sizes[3]))
    parts = [jnp.exp(s - top) for s in sizes]
    total = parts[0] + parts[1] + parts[2] + parts[3]
    return [p / total for p in parts]


def gbst_coefs(weights, inverse, alpha):
    a1 = weights[0] * alpha
    a2 = weights[1] * alpha * inverse[0]
    a3 = weights[2] * alpha * inverse[1]
    a4 = weights[3] * alpha * inverse[2]
    pair = group_matrix(2)
    a4s = exact_dot(a4, pair)
    own = a1 + exact_dot(a2, pair) + a4s
    return own, a3, a4s


def column(x, r):
    return jnp.broadcast_to(x[:, r : r + 1], (x.shape[0], LANES))


def hits_of(ids):
    lanes = lax.broadcasted_iota(jnp.int32, (P_ROWS, LANES), 1).astype(f32)
    return jnp.concatenate(
        [jnp.where(ids == lanes + float(i * LANES), 1.0, 0.0).astype(bf16) for i in range(SMALL // LANES)], axis=1)


def look_up(ids, table_ref):
    return lax.dot_general(
        hits_of(ids), table_ref[...].reshape(D, SMALL), (((1,), (1,)), ((), ())), preferred_element_type=f32)


def load_e(e_ref, r, lt):
    lanes = pl.ds(lt * LANES, LANES)
    if r < R:
        return e_ref[pl.ds(r * QN, QN), lanes]
    return e_ref[pl.ds((r - R) * QN + 1, QN), lanes]


def gbst_fwd_kernel(len_ref, ids_ref, table_ref, vec_ref, hidden_ref, normed_ref, turned_ref, c_ref, w_ref, e_ref, hid_ref, s_ref, k_ref):
    length = len_ref[pl.program_id(0)]
    e_ref[pl.ds(0, P_ROWS), :] = look_up(ids_ref[0], table_ref)
    e_ref[pl.ds(P_ROWS, 8), :] = jnp.zeros((8, D), f32)
    for lt in range(LT):
        lanes = pl.ds(lt * LANES, LANES)
        taps = [jnp.broadcast_to(vec_ref[j : j + 1, lanes], (QN, LANES)) for j in range(4)]
        sw = jnp.broadcast_to(vec_ref[4:5, lanes], (QN, LANES))
        for r in range(R):
            c = taps[0] * load_e(e_ref, r, lt)
            for j in range(1, 4):
                c = c + taps[j] * load_e(e_ref, r + j, lt)
            c_ref[0, pl.ds(r * QN, QN), lanes] = c
            part = c * sw
            rows = pl.ds(r * QN, QN)
            s_ref[rows, :] = part if lt == 0 else s_ref[rows, :] + part
    s1 = place([jnp.sum(s_ref[pl.ds(r * QN, QN), :], axis=1, keepdims=True) for r in range(R)], QN)
    mask, inverse, alpha = gbst_masks(length)
    weights = gbst_weights(s1, inverse)
    for b in range(4):
        w_ref[0, b] = weights[b]
    own, a3, a4s = gbst_coefs(weights, inverse, alpha)
    n = 0
    for r in range(R):
        k_ref[r] = column(own, r)
        k_ref[R + r] = column(a3, r)
    for k in range(6):
        k_ref[2 * R + k] = column(a4s, 2 * k)
    for lt in range(LT):
        lanes = pl.ds(lt * LANES, LANES)
        for half in range(2):
            c = [c_ref[0, pl.ds((half * 6 + r) * QN, QN), lanes] for r in range(6)]
            base = half * 6
            s3 = [c[0] + c[1] + c[2], c[3] + c[4] + c[5]]
            for k in range(3):
                tok = half * 3 + k
                other = tok ^ 1
                rows = pl.ds(2 * other * QN, QN)
                rows1 = pl.ds((2 * other + 1) * QN, QN)
                s2 = c_ref[0, rows, lanes] + c_ref[0, rows1, lanes]
                h = k_ref[2 * tok] * c[2 * k] + k_ref[2 * tok + 1] * c[2 * k + 1] + k_ref[2 * R + tok] * s2
                if k == 1:
                    h = h + k_ref[R + 2 * tok] * s3[0] + k_ref[R + 2 * tok + 1] * s3[1]
                else:
                    h = h + (k_ref[R + 2 * tok] + k_ref[R + 2 * tok + 1]) * s3[0 if k == 0 else 1]
                hid_ref[lt, pl.ds(tok, QN, stride=6), :] = h
    total = jnp.zeros((TOK, LANES), f32)
    for lt in range(LT):
        x = hid_ref[lt, 0:TOK, :]
        total = total + x * x
    scale = lax.rsqrt(jnp.sum(total, axis=1, keepdims=True) * (1.0 / D) + epsilon)
    for lt in range(LT):
        lanes = pl.ds(lt * LANES, LANES)
        x = hid_ref[lt, 0:TOK, :]
        hidden_ref[:, lanes] = x
        normed = (x * scale * vec_ref[5:6, lanes]).astype(bf16)
        normed_ref[:, lanes] = normed
        turned_ref[lanes, :] = normed.T


def gbst_forward(lengths, ids_col, table, vecs):
    seqs = ids_col.shape[0]
    grid_spec = pltpu.PrefetchScalarGridSpec(
        num_scalar_prefetch=1,
        grid=(seqs,),
        in_specs=[
            pl.BlockSpec((1, P_ROWS, LANES), lambda s, n: (s, 0, 0)),
            pl.BlockSpec(table.shape, lambda s, n: (0, 0, 0)),
            pl.BlockSpec((8, D), lambda s, n: (0, 0)),
        ],
        out_specs=[
            pl.BlockSpec((TOK, D), lambda s, n: (s, 0)),
            pl.BlockSpec((TOK, D), lambda s, n: (s, 0)),
            pl.BlockSpec((D, TOK), lambda s, n: (0, s)),
            pl.BlockSpec((1, P_ROWS, D), lambda s, n: (s, 0, 0)),
            pl.BlockSpec((1, 4, QN, LANES), lambda s, n: (s, 0, 0, 0)),
        ],
        scratch_shapes=[
            pltpu.VMEM((P_ROWS + 8, D), f32),
            pltpu.VMEM((LT, T_ROWS, LANES), f32),
            pltpu.VMEM((P_ROWS, LANES), f32),
            pltpu.VMEM((2 * R + 6, QN, LANES), f32),
        ],
    )
    return pl.pallas_call(
        gbst_fwd_kernel,
        grid_spec=grid_spec,
        out_shape=[
            jax.ShapeDtypeStruct((seqs * TOK, D), f32),
            jax.ShapeDtypeStruct((seqs * TOK, D), bf16),
            jax.ShapeDtypeStruct((D, seqs * TOK), bf16),
            jax.ShapeDtypeStruct((seqs, P_ROWS, D), f32),
            jax.ShapeDtypeStruct((seqs, 4, QN, LANES), f32),
        ],
        compiler_params=pltpu.CompilerParams(vmem_limit_bytes=VMEM_LIMIT),
        cost_estimate=cost(18, 30),
        name="gbst_forward",
    )(lengths, ids_col, table, vecs)


def gbst_bwd_kernel(len_ref, ids_ref, row_ref, table_ref, vec_ref, dh_ref, c_ref, w_ref, gain1_ref, gain2_ref, rel_ref,
                    ig_ref, small_ref, ge_ref, e_ref, dt_ref, dc_ref, s_ref, k_ref, igs_ref):
    seq = pl.program_id(0)
    length = len_ref[seq]

    @pl.when(seq == 0)
    def _():
        ge_ref[...] = jnp.zeros_like(ge_ref)

    e_ref[pl.ds(0, P_ROWS), :] = look_up(ids_ref[0], table_ref)
    e_ref[pl.ds(P_ROWS, 8), :] = jnp.zeros((8, D), f32)
    for lt in range(LT):
        dt_ref[lt, 0:TOK, :] = dh_ref[:, pl.ds(lt * LANES, LANES)]
        dt_ref[lt, TOK:T_ROWS, :] = jnp.zeros((T_ROWS - TOK, LANES), f32)
    for lt in range(LT):
        lanes = pl.ds(lt * LANES, LANES)
        for half in range(2):
            c = [c_ref[0, pl.ds((half * 6 + r) * QN, QN), lanes] for r in range(6)]
            s3 = [c[0] + c[1] + c[2], c[3] + c[4] + c[5]]
            for k in range(3):
                tok = half * 3 + k
                other = tok ^ 1
                dh = dt_ref[lt, pl.ds(tok, QN, stride=6), :]
                s2 = c_ref[0, pl.ds(2 * other * QN, QN), lanes] + c_ref[0, pl.ds((2 * other + 1) * QN, QN), lanes]
                parts = [
                    (2 * tok, dh * c[2 * k]),
                    (2 * tok + 1, dh * c[2 * k + 1]),
                    (2 * R + tok, dh * s2),
                    (R + 2 * tok, dh * s3[0 if k < 2 else 1]),
                ]
                if k == 1:
                    parts.append((R + 2 * tok + 1, dh * s3[1]))
                for slot, part in parts:
                    s_ref[slot] = part if lt == 0 else s_ref[slot] + part

    def total(slot):
        return jnp.sum(s_ref[slot], axis=1, keepdims=True)

    d1, d3, dother = [], [], []
    for tok in range(6):
        d1 += [total(2 * tok), total(2 * tok + 1)]
        first = total(R + 2 * tok)
        d3 += [first, total(R + 2 * tok + 1) if tok % 3 == 1 else first]
        o = total(2 * R + tok)
        dother += [o, o]
    d1, d3, dother = place(d1, QN), place(d3, QN), place(dother, QN)
    mask, inverse, alpha = gbst_masks(length)
    weights = [w_ref[0, b] for b in range(4)]
    d2 = exact_dot(d1, group_matrix(2))
    g = [alpha * d1, alpha * d2 * inverse[0], alpha * d3 * inverse[1], alpha * (d2 + dother) * inverse[2]]
    mean = weights[0] * g[0] + weights[1] * g[1] + weights[2] * g[2] + weights[3] * g[3]
    d_size = [w * (x - mean) for w, x in zip(weights, g)]
    coef = d_size[0]
    for b, inv in zip((2, 3, 4), inverse):
        coef = coef + exact_dot(d_size[b - 1] * inv, group_matrix(b))
    own, a3, a4s = gbst_coefs(weights, inverse, alpha)
    for r in range(R):
        k_ref[r] = column(own, r)
        k_ref[R + r] = column(a3, r)
        k_ref[2 * R + r] = column(coef, r)
        k_ref[3 * R + r] = column(mask, r)
    for k in range(6):
        k_ref[4 * R + k] = column(a4s, 2 * k)

    for lt in range(LT):
        lanes = pl.ds(lt * LANES, LANES)
        taps = [jnp.broadcast_to(vec_ref[j : j + 1, lanes], (QN, LANES)) for j in range(4)]
        sw = jnp.broadcast_to(vec_ref[4:5, lanes], (QN, LANES))
        gs = jnp.zeros((QN, LANES), f32)
        gc = [jnp.zeros((QN, LANES), f32) for _ in range(4)]
        for half in range(2):
            dh = [dt_ref[lt, pl.ds(half * 3 + k, QN, stride=6), :] for k in range(3)]
            a = R + half * 6
            t3 = [
                (k_ref[a] + k_ref[a + 1]) * dh[0] + k_ref[a + 2] * dh[1],
                k_ref[a + 3] * dh[1] + (k_ref[a + 4] + k_ref[a + 5]) * dh[2],
            ]
            for k in range(3):
                tok = half * 3 + k
                other = tok ^ 1
                dother_h = dt_ref[lt, pl.ds(other, QN, stride=6), :]
                cross = k_ref[4 * R + other] * dother_h
                for e in range(2):
                    r = 2 * tok + e
                    cf = k_ref[2 * R + r]
                    dc = k_ref[r] * dh[k] + cross + t3[(r % 6) // 3] + cf * sw
                    gs = gs + cf * c_ref[0, pl.ds(r * QN, QN), lanes]
                    dc_ref[r, pl.ds(8, QN), :] = dc
                    for j in range(4):
                        gc[j] = gc[j] + dc * load_e(e_ref, r + j, lt)
        ge_ref[VROWS + 4 : VROWS + 5, lanes] += jnp.sum(gs, axis=0, keepdims=True)
        for j in range(4):
            ge_ref[VROWS + j : VROWS + j + 1, lanes] += jnp.sum(gc[j], axis=0, keepdims=True)
        for r in range(R):
            dc_ref[r, 0:8, :] = jnp.zeros((8, LANES), f32)
        for r in range(R):
            x = taps[0] * dc_ref[r, pl.ds(8, QN), :]
            for j in range(1, 4):
                back = dc_ref[r - j, pl.ds(8, QN), :] if r >= j else dc_ref[r - j + R, pl.ds(7, QN), :]
                x = x + taps[j] * back
            igs_ref[lt, pl.ds(r, QN, stride=R), :] = x * k_ref[3 * R + r]
    for lt in range(LT):
        lanes = pl.ds(lt * LANES, LANES)
        ig_ref[0, :, lanes] = igs_ref[lt, 0:MAXLEN, :].astype(bf16)
    vocab = lax.broadcasted_iota(jnp.int32, (VROWS, MAXLEN), 0)
    row_hits = jnp.where(vocab == row_ref[0], 1.0, 0.0).astype(bf16)
    ge_ref[0:VROWS, :] += jnp.dot(row_hits, ig_ref[0], preferred_element_type=f32)

    @pl.when(seq == pl.num_programs(0) - 1)
    def _():
        ge_ref[VROWS + 5 : VROWS + 6, :] = gain1_ref[...]
        ge_ref[VROWS + 6 : VROWS + 7, :] = gain2_ref[...]
        ge_ref[VROWS + 7 : VROWS + 15, :] = rel_ref[...]
        for lt in range(LT):
            lanes = pl.ds(lt * LANES, LANES)
            small_ref[lanes, :] = ge_ref[:, lanes].T.astype(bf16)


def gbst_backward(lengths, ids_col, ids_row, table, vecs, d_hidden, c, w, gain1, gain2, rel):
    seqs = ids_col.shape[0]
    grid_spec = pltpu.PrefetchScalarGridSpec(
        num_scalar_prefetch=1,
        grid=(seqs,),
        in_specs=[
            pl.BlockSpec((1, P_ROWS, LANES), lambda s, n: (s, 0, 0)),
            pl.BlockSpec((1, 1, MAXLEN), lambda s, n: (s, 0, 0)),
            pl.BlockSpec(table.shape, lambda s, n: (0, 0, 0)),
            pl.BlockSpec((8, D), lambda s, n: (0, 0)),
            pl.BlockSpec((TOK, D), lambda s, n: (s, 0)),
            pl.BlockSpec((1, P_ROWS, D), lambda s, n: (s, 0, 0)),
            pl.BlockSpec((1, 4, QN, LANES), lambda s, n: (s, 0, 0, 0)),
            pl.BlockSpec((1, D), lambda s, n: (0, 0)),
            pl.BlockSpec((1, D), lambda s, n: (0, 0)),
            pl.BlockSpec((8, D), lambda s, n: (0, 0)),
        ],
        out_specs=[
            pl.BlockSpec((1, MAXLEN, D), lambda s, n: (s, 0, 0)),
            pl.BlockSpec((D, SMALL), lambda s, n: (0, 0)),
        ],
        scratch_shapes=[
            pltpu.VMEM((SMALL, D), f32),
            pltpu.VMEM((P_ROWS + 8, D), f32),
            pltpu.VMEM((LT, T_ROWS, LANES), f32),
            pltpu.VMEM((R, QN + 8, LANES), f32),
            pltpu.VMEM((2 * R + 6, QN, LANES), f32),
            pltpu.VMEM((4 * R + 6, QN, LANES), f32),
            pltpu.VMEM((LT, P_ROWS, LANES), f32),
        ],
    )
    return pl.pallas_call(
        gbst_bwd_kernel,
        grid_spec=grid_spec,
        out_shape=[
            jax.ShapeDtypeStruct((seqs, MAXLEN, D), bf16),
            jax.ShapeDtypeStruct((D, SMALL), bf16),
        ],
        compiler_params=pltpu.CompilerParams(vmem_limit_bytes=VMEM_LIMIT),
        cost_estimate=cost(31, 40),
        name="gbst_backward",
    )(lengths, ids_col, ids_row, table, vecs, d_hidden, c, w, gain1, gain2, rel)


HEADS = 12
HD = 64
BUCKETS = 32
SPAN = 1024
HB = 4
WIDE = HB * HD
GROUPS = HEADS // HB
dead_score = -1e9


def nt(a, b):
    return lax.dot_general(a, b, (((1,), (1,)), ((), ())), preferred_element_type=f32)


def nn(a, b):
    return jnp.dot(a, b, preferred_element_type=f32)


def bucket_row(buckets):
    return jnp.concatenate([buckets[TOK - 1 :], buckets[:1], buckets[: TOK - 1]]).reshape(1, SPAN)


def bucket_hits(row_ref):
    return jnp.where(lax.broadcasted_iota(jnp.int32, (BUCKETS, SPAN), 0) == row_ref[...], 1.0, 0.0).astype(f32)


def spread_table(rel_ref, row_ref, z_ref):
    dims = (((0,), (0,)), ((), ()))
    z_ref[...] = lax.dot_general(
        rel_ref[...].astype(bf16), bucket_hits(row_ref).astype(bf16), dims, preferred_element_type=f32)


def build_bias(z_ref, bt_ref, group):
    for h in range(HB):
        row = jnp.broadcast_to(z_ref[pl.ds(group * HB + h, 1), :], (8, SPAN))
        sub = lax.broadcasted_iota(jnp.int32, (8, SPAN), 0)
        z = row
        for s in range(1, 8):
            z = jnp.where(sub == s, pltpu.roll(row, s, 1), z)
        for g in range(TOK // 8):
            bt_ref[h, pl.ds(8 * g, 8), :] = (z if g == 0 else pltpu.roll(z, 8 * g, 1))[:, :TOK]


def own_lanes(h):
    return lax.broadcasted_iota(jnp.int32, (TOK, WIDE), 1) // HD == h


def head_parts(k, q, length, h):
    lanes = lax.broadcasted_iota(jnp.int32, (TOK, WIDE), 1)
    rows = lax.broadcasted_iota(jnp.int32, (TOK, WIDE), 0)
    spare = HD * (h + 1) % WIDE
    dead = jnp.where(2 * rows < length, 0.0, dead_score)
    kf = jnp.where(lanes // HD == h, k.astype(f32), jnp.where(lanes == spare, dead, 0.0)).astype(bf16)
    qf = jnp.where(lanes == spare, 1.0, q.astype(f32)).astype(bf16)
    return kf, qf


def join_heads(parts):
    out = parts[0]
    for h in range(1, HB):
        out = jnp.where(own_lanes(h), parts[h], out)
    return out.astype(bf16)


def attn_fwd_kernel(len_ref, q_ref, k_ref, v_ref, rel_ref, row_ref, ctx_ref, lse_ref, bias_ref, z_ref):
    length = len_ref[pl.program_id(1)]

    @pl.when((pl.program_id(0) == 0) & (pl.program_id(1) == 0))
    def _():
        spread_table(rel_ref, row_ref, z_ref)

    @pl.when(pl.program_id(1) == 0)
    def _():
        build_bias(z_ref, bias_ref, pl.program_id(0))

    q, k, v = q_ref[...], k_ref[...], v_ref[...]

    def score(h):
        kf, qf = head_parts(k, q, length, h)
        return nt(qf, kf) + bias_ref[h]

    outs = []
    lanes = lax.broadcasted_iota(jnp.int32, (TOK, LANES), 1)
    lse = jnp.zeros((TOK, LANES), f32)
    s = score(0)
    for h in range(HB):
        later = score(h + 1) if h + 1 < HB else None
        top = jnp.max(s, axis=1, keepdims=True)
        p = jnp.exp(s - top)
        total = jnp.sum(p, axis=1, keepdims=True)
        outs.append(nn(p.astype(bf16), v) * (1.0 / total))
        lse = jnp.where(lanes == h, top + jnp.log(total), lse)
        s = later
    ctx_ref[...] = join_heads(outs)
    lse_ref[0, 0] = lse.T[0:8]


def table_specs():
    return [
        pl.BlockSpec((BUCKETS, LANES), lambda hp, s, n: (0, 0)),
        pl.BlockSpec((1, SPAN), lambda hp, s, n: (0, 0)),
    ]


def attn_forward(lengths, qkv, rel, row):
    seqs = qkv.shape[0] // TOK
    spec = lambda off: pl.BlockSpec((TOK, WIDE), lambda hp, s, n: (s, off + hp))
    return pl.pallas_call(
        attn_fwd_kernel,
        grid_spec=pltpu.PrefetchScalarGridSpec(
            num_scalar_prefetch=1,
            grid=(GROUPS, seqs),
            in_specs=[spec(0), spec(GROUPS), spec(2 * GROUPS)] + table_specs(),
            out_specs=[spec(0), pl.BlockSpec((1, 1, 8, TOK), lambda hp, s, n: (hp, s, 0, 0))],
            scratch_shapes=[pltpu.VMEM((HB, TOK, TOK), f32), pltpu.VMEM((LANES, SPAN), f32)],
        ),
        out_shape=[
            jax.ShapeDtypeStruct((seqs * TOK, D), bf16),
            jax.ShapeDtypeStruct((GROUPS, seqs, 8, TOK), f32),
        ],
        compiler_params=pltpu.CompilerParams(vmem_limit_bytes=VMEM_LIMIT),
        cost_estimate=cost(27, 20),
        name="attn_forward",
    )(lengths, qkv, qkv, qkv, rel, row)


def attn_bwd_kernel(shards, len_ref, q_ref, k_ref, v_ref, do_ref, o_ref, lse_ref, rel_ref, row_ref, dqkv_ref, gt_ref, bt_ref, g_ref, z_ref, gz_ref):
    s_id = pl.program_id(1)
    length = len_ref[s_id]

    @pl.when((pl.program_id(0) == 0) & (s_id == 0))
    def _():
        spread_table(rel_ref, row_ref, z_ref)
        gz_ref[...] = jnp.zeros_like(gz_ref)

    @pl.when(s_id == 0)
    def _():
        build_bias(z_ref, bt_ref, pl.program_id(0))
        g_ref[...] = jnp.zeros_like(g_ref)

    q, k, v, do = q_ref[...], k_ref[...], v_ref[...], do_ref[...]
    kt = k.astype(f32).T.astype(bf16)
    lanes8 = lax.broadcasted_iota(jnp.int32, (8, WIDE), 1)
    rows8 = lax.broadcasted_iota(jnp.int32, (8, WIDE), 0)
    pick = jnp.where(lanes8 // HD == rows8, 1.0, 0.0).astype(bf16)
    prod = do.astype(f32) * o_ref[...].astype(f32)
    upper = prod.astype(bf16)
    delta = nt(pick, upper) + nt(pick, (prod - upper.astype(f32)).astype(bf16))
    dq, dk, dv = [], [], []

    def first(h):
        kf, qf = head_parts(k, q, length, h)
        vf = jnp.where(own_lanes(h), v.astype(f32), 0.0).astype(bf16)
        return nt(kf, qf) + bt_ref[h], nt(vf, do)

    now = first(0)
    for h in range(HB):
        later = first(h + 1) if h + 1 < HB else None
        s, d_prob = now
        p = jnp.exp(s - lse_ref[0, 0, h : h + 1, :])
        ds = p * (d_prob - delta[h : h + 1, :])
        g_ref[h] += ds
        low = ds.astype(bf16)
        dv.append(nn(p.astype(bf16), do))
        dk.append(nn(low, q))
        dq.append(nn(kt[h * HD : (h + 1) * HD], low))
        now = later
    dqkv_ref[0] = jnp.concatenate(dq, axis=0).T.astype(bf16)
    dqkv_ref[1] = join_heads(dk)
    dqkv_ref[2] = join_heads(dv)

    @pl.when(s_id == pl.num_programs(1) - 1)
    def _():
        for h in range(HB):
            total = jnp.zeros((8, SPAN), f32)
            for g in range(LANES // 8):
                tiles = [jnp.zeros((8, LANES), f32) for _ in range(SPAN // LANES)]
                for j in range(TOK // LANES):
                    x = g_ref[h, pl.ds(LANES * j + 8 * g, 8), :]
                    for t in range(TOK // LANES):
                        n = (t - j) % (SPAN // LANES)
                        tiles[n] = tiles[n] + x[:, t * LANES : (t + 1) * LANES]
                piece = jnp.concatenate(tiles, axis=1)
                total = total + (piece if g == 0 else pltpu.roll(piece, SPAN - 8 * g, 1))
            out = total[0:1]
            for s in range(1, 8):
                out = out + pltpu.roll(jnp.broadcast_to(total[s : s + 1], (8, SPAN)), SPAN - s, 1)[0:1]
            gz_ref[pl.ds(pl.program_id(0) * HB + h, 1), :] = out

    @pl.when((pl.program_id(0) == GROUPS - 1) & (s_id == pl.num_programs(1) - 1))
    def _():
        total = lax.dot_general(
            bucket_hits(row_ref), gz_ref[...], (((1,), (1,)), ((), ())),
            precision=lax.Precision.HIGHEST, preferred_element_type=f32)
        gt_ref[...] = jnp.zeros_like(gt_ref)
        per = BUCKETS // shards
        for s in range(shards):
            start = s * (D // shards)
            gt_ref[0:per, start : start + HEADS] = total[s * per : (s + 1) * per, 0:HEADS]


def attn_backward(lengths, qkv, d_ctx, ctx, lse, rel, row, shards):
    seqs = qkv.shape[0] // TOK
    spec = lambda off: pl.BlockSpec((TOK, WIDE), lambda hp, s, n: (s, off + hp))
    return pl.pallas_call(
        lambda *refs: attn_bwd_kernel(shards, *refs),
        grid_spec=pltpu.PrefetchScalarGridSpec(
            num_scalar_prefetch=1,
            grid=(GROUPS, seqs),
            in_specs=[
                spec(0), spec(GROUPS), spec(2 * GROUPS), spec(0), spec(0),
                pl.BlockSpec((1, 1, 8, TOK), lambda hp, s, n: (hp, s, 0, 0)),
            ] + table_specs(),
            out_specs=[
                pl.BlockSpec((3, TOK, WIDE), lambda hp, s, n: (0, s, hp)),
                pl.BlockSpec((8, D), lambda hp, s, n: (0, 0)),
            ],
            scratch_shapes=[
                pltpu.VMEM((HB, TOK, TOK), f32), pltpu.VMEM((HB, TOK, TOK), f32),
                pltpu.VMEM((LANES, SPAN), f32), pltpu.VMEM((16, SPAN), f32),
            ],
        ),
        out_shape=[
            jax.ShapeDtypeStruct((3, seqs * TOK, D), bf16),
            jax.ShapeDtypeStruct((8, D), f32),
        ],
        compiler_params=pltpu.CompilerParams(vmem_limit_bytes=VMEM_LIMIT),
        cost_estimate=cost(46, 30),
        name="attn_backward",
    )(lengths, qkv, qkv, qkv, d_ctx, ctx, lse, rel, row)


FF = 2048
FT = 256
RC = 512
MT = 256


def rms_scale(x):
    return lax.rsqrt(jnp.sum(x * x, axis=1, keepdims=True) * (1.0 / D) + epsilon)


def post_kernel(len_ref, shift_ref, ctx_ref, w_ref, hidden_ref, vec_ref, *refs):
    pieces, (att_ref, low_ref, low_t_ref, do_ref, do_t_ref) = refs[:-5], refs[-5:]
    s = pl.program_id(0)
    for i, piece in enumerate(pieces):
        @pl.when(shift_ref[s] == i)
        def _():
            do_ref[...] = piece[...]

    live = 2 * lax.broadcasted_iota(jnp.int32, (TOK, D), 0) < len_ref[s]
    d_out = jnp.where(live, do_ref[...].astype(f32), 0.0).astype(bf16)
    do_ref[...] = d_out
    do_t_ref[...] = d_out.T
    att = hidden_ref[...] + nn(ctx_ref[...], out_weights(w_ref))
    att_ref[...] = att
    low = (att * rms_scale(att) * vec_ref[6:7, :]).astype(bf16)
    low_ref[...] = low
    low_t_ref[...] = low.T


def rows_spec(width=D):
    return pl.BlockSpec((TOK, width), lambda s, *n: (s, 0))


def whole(*shape):
    return pl.BlockSpec(shape, lambda s, *n: (0,) * len(shape))


def out_block(shards):
    deep = D // shards
    return pl.BlockSpec((shards, 3 * deep, FT), lambda s, *n: (0, 4, 0))


def out_weights(ref):
    deep = ref.shape[1] // 3
    return jnp.concatenate([ref[:, i * deep : (i + 1) * deep, :].reshape(D, FT) for i in range(3)], axis=1)


def post_attention(lengths, shifts, ctx, pack, hidden, vecs, pieces, shards):
    rows = ctx.shape[0]
    cols_spec = pl.BlockSpec((D, TOK), lambda s, *n: (0, s))
    return pl.pallas_call(
        post_kernel,
        grid_spec=pltpu.PrefetchScalarGridSpec(
            num_scalar_prefetch=2,
            grid=(rows // TOK,),
            in_specs=[rows_spec(), out_block(shards), rows_spec(), whole(8, D)] + [whole(TOK, D)] * len(pieces),
            out_specs=[rows_spec(), rows_spec(), cols_spec, rows_spec(), cols_spec],
        ),
        out_shape=[
            jax.ShapeDtypeStruct((rows, D), f32),
            jax.ShapeDtypeStruct((rows, D), bf16),
            jax.ShapeDtypeStruct((D, rows), bf16),
            jax.ShapeDtypeStruct((rows, D), bf16),
            jax.ShapeDtypeStruct((D, rows), bf16),
        ],
        compiler_params=pltpu.CompilerParams(vmem_limit_bytes=VMEM_LIMIT),
        cost_estimate=cost(10, 30),
        name="post_attention",
    )(lengths, shifts, ctx, pack, hidden, vecs, *pieces)


def gelu_parts(v):
    c = 0.7978845608
    v2 = v * v
    t = jnp.tanh(v * (c + (c * 0.044715) * v2))
    half = 0.5 + 0.5 * t
    gelu = v * half
    slope = half + (0.5 * v) * (1.0 - t * t) * (c + (3.0 * c * 0.044715) * v2)
    return gelu, slope


def ffn_steps(x_any, d_any, xt_any, dt_any, wgu_ref, wo_ref, grad_ref, y_any, dx_any,
              x_ref, d_ref, xt_ref, dt_ref, y_ref, dx_ref, a_ref, dg_ref, du_ref, gu_ref, go_ref, in_sem, out_sem, sems):
    f = pl.program_id(0)
    steps = FF // 2 // FT
    rows_total = x_ref.shape[0]
    chunks = rows_total // RC
    shards, part = gu_ref.shape[1], gu_ref.shape[2]
    owners, deep = go_ref.shape[1], go_ref.shape[2]
    base = steps * part

    def copies(slot, step):
        return (
            pltpu.make_async_copy(
                gu_ref.at[slot], grad_ref.at[:, pl.ds(step * part, part), :], sems.at[0, slot]),
            pltpu.make_async_copy(
                go_ref.at[slot], grad_ref.at[pl.ds(step * owners, owners), pl.ds(base, deep), :], sems.at[1, slot]),
        )

    def row_loads(i):
        rows = pl.ds(i * RC, RC)
        return (
            pltpu.make_async_copy(x_any.at[rows], x_ref.at[rows], in_sem.at[0, i]),
            pltpu.make_async_copy(d_any.at[rows], d_ref.at[rows], in_sem.at[1, i]),
        )

    def turned_loads():
        return (
            pltpu.make_async_copy(xt_any, xt_ref, in_sem.at[2, 0]),
            pltpu.make_async_copy(dt_any, dt_ref, in_sem.at[2, 1]),
        )

    def row_stores(i):
        rows = pl.ds(i * RC, RC)
        return (
            pltpu.make_async_copy(y_ref.at[rows], y_any.at[rows], out_sem.at[0, i]),
            pltpu.make_async_copy(dx_ref.at[rows], dx_any.at[rows], out_sem.at[1, i]),
        )

    @pl.when(f == 0)
    def _():
        for i in range(chunks):
            for copy in row_loads(i):
                copy.start()
        for copy in turned_loads():
            copy.start()
        y_ref[...] = jnp.zeros_like(y_ref)
        dx_ref[...] = jnp.zeros_like(dx_ref)

    d_rows = part // 2
    third = deep // 3
    wg = wgu_ref[:, 0:d_rows, :].reshape(D, FT)
    wu = wgu_ref[:, d_rows:part, :].reshape(D, FT)
    wo = jnp.concatenate(
        [wo_ref[:, i * third : (i + 1) * third, :].reshape(FT, FT) for i in range(3)], axis=1)

    @pl.when(f == 0)
    def _():
        for i in range(chunks):
            for copy in row_loads(i):
                copy.wait()

    for i in range(chunks):
        rows = pl.ds(i * RC, RC)
        x, d = x_ref[rows, :], d_ref[rows, :]
        gelu, slope = gelu_parts(nn(x, wg))
        up = nn(x, wu)
        da = nt(d, wo)
        act = (gelu * up).astype(bf16)
        dg = (da * up * slope).astype(bf16)
        du = (da * gelu).astype(bf16)
        a_ref[rows, :] = act
        dg_ref[rows, :] = dg
        du_ref[rows, :] = du
        y_ref[rows, :] += nn(act, wo)
        dx_ref[rows, :] += nt(dg, wg) + nt(du, wu)
    if y_any is not None:

        @pl.when(f == steps - 1)
        def _():
            for i in range(chunks):
                for copy in row_stores(i):
                    copy.start()

    slot = lax.rem(f, 2)

    @pl.when(f == 0)
    def _():
        for copy in turned_loads():
            copy.wait()

    @pl.when(f >= 2)
    def _():
        for copy in copies(slot, f - 2):
            copy.wait()

    gu_ref[slot, :, 0:d_rows, :] = nn(xt_ref[...], dg_ref[...]).astype(bf16).reshape(shards, d_rows, FT)
    gu_ref[slot, :, d_rows:part, :] = nn(xt_ref[...], du_ref[...]).astype(bf16).reshape(shards, d_rows, FT)
    go = nn(dt_ref[...], a_ref[...]).T.astype(bf16)
    for i in range(3):
        go_ref[slot, :, i * third : (i + 1) * third, :] = go[:, i * FT : (i + 1) * FT].reshape(owners, third, FT)
    for copy in copies(slot, f):
        copy.start()

    @pl.when(f == steps - 1)
    def _():
        for copy in copies(1 - slot, f - 1) + copies(slot, f):
            copy.wait()
        if y_any is not None:
            for i in range(chunks):
                for copy in row_stores(i):
                    copy.wait()


def first_kernel(x, d, xt, dt, wgu, wo, grad, y, dx, *scratch):
    ffn_steps(x, d, xt, dt, wgu, wo, grad, y, dx, *scratch)


def second_kernel(len_ref, x, d, xt, dt, wgu, wo, att_ref, y1_ref, dx1_ref, do_ref, ctx_ref, w_ref, vec_ref,
                  grad, out_ref, datt_ref, dctx_ref, gg_ref, acc_ref, flat_ref, join_ref, join_sem, *scratch):
    f = pl.program_id(0)
    steps = FF // 2 // FT

    @pl.when(f == 0)
    def _():
        acc_ref[...] = jnp.zeros_like(acc_ref)
        gg_ref[...] = jnp.zeros_like(gg_ref)
        flat_ref[...] = out_weights(w_ref)

    @pl.when(f < steps)
    def _():
        ffn_steps(x, d, xt, dt, wgu, wo, grad, None, None, *scratch)

    @pl.when(f >= steps)
    def _():
        tile = f - steps
        y_ref, dx_ref = scratch[4], scratch[5]
        rows = pl.ds(pl.multiple_of(tile * MT, MT), MT)
        per = TOK // MT
        length = len_ref[tile // per]
        place_in = lax.rem(tile, per) * MT + lax.broadcasted_iota(jnp.int32, (MT, 1), 0)
        live = jnp.where(2 * place_in < length, 1.0, 0.0).astype(f32)
        att = att_ref[...]
        out_ref[...] = ((att + y1_ref[...] + y_ref[rows, :]) * live).astype(bf16)
        back, gain_grad = norm_back(att, dx1_ref[...] + dx_ref[rows, :], vec_ref[6:7, :])
        gg_ref[...] += gain_grad
        d_att = do_ref[...].astype(f32) + back
        datt_ref[...] = d_att
        low = d_att.astype(bf16)
        dctx_ref[...] = nt(low, flat_ref[...]).astype(bf16)
        acc_ref[...] += nn(ctx_ref[...].T, low)

    @pl.when(f == pl.num_programs(0) - 1)
    def _():
        shards, deep = join_ref.shape[0], join_ref.shape[1] // 3
        for i in range(3):
            block = acc_ref[:, i * FT : (i + 1) * FT].astype(bf16).reshape(shards, deep, FT)
            join_ref[:, i * deep : (i + 1) * deep, :] = block
        copy = pltpu.make_async_copy(join_ref, grad.at[:, pl.ds(grad.shape[1] - 3 * deep, 3 * deep), :], join_sem)
        copy.start()
        copy.wait()


def ffn_scratch(rows, shards):
    part, hs = 2 * D // shards, FF // 2 // shards
    return [
        pltpu.VMEM((rows, D), bf16),
        pltpu.VMEM((rows, D), bf16),
        pltpu.VMEM((D, rows), bf16),
        pltpu.VMEM((D, rows), bf16),
        pltpu.VMEM((rows, D), f32),
        pltpu.VMEM((rows, D), f32),
        pltpu.VMEM((rows, FT), bf16),
        pltpu.VMEM((rows, FT), bf16),
        pltpu.VMEM((rows, FT), bf16),
        pltpu.VMEM((2, shards, part, FT), bf16),
        pltpu.VMEM((2, FT // hs, 3 * hs, FT), bf16),
        pltpu.SemaphoreType.DMA((3, max(2, rows // RC))),
        pltpu.SemaphoreType.DMA((2, rows // RC)),
        pltpu.SemaphoreType.DMA((2, 2)),
    ]


def ffn_specs(tiles, shards):
    last = lambda f: jnp.minimum(f, tiles - 1)
    part, hs = 2 * D // shards, FF // 2 // shards
    return [pl.BlockSpec(memory_space=pl.ANY)] * 4 + [
        pl.BlockSpec((shards, part, FT), lambda f, *n: (0, last(f), 0)),
        pl.BlockSpec((FT // hs, 3 * hs, FT), lambda f, *n: (last(f), 2, 0)),
    ]


def grad_shape(shards, more=0):
    part, hs = 2 * D // shards, FF // 2 // shards
    return jax.ShapeDtypeStruct((shards, FF // 2 // FT * part + 3 * hs + more, FT), bf16)


def ffn_first(x, d_out, xt, dt, pack, shards):
    rows = x.shape[0]
    tiles = FF // 2 // FT
    anywhere = pl.BlockSpec(memory_space=pl.ANY)
    return pl.pallas_call(
        first_kernel,
        grid=(tiles,),
        in_specs=ffn_specs(tiles, shards),
        out_specs=[anywhere] * 3,
        out_shape=[
            grad_shape(shards),
            jax.ShapeDtypeStruct((rows, D), f32),
            jax.ShapeDtypeStruct((rows, D), f32),
        ],
        scratch_shapes=ffn_scratch(rows, shards),
        compiler_params=pltpu.CompilerParams(vmem_limit_bytes=VMEM_LIMIT),
        cost_estimate=cost(36, 40),
        name="ffn_first",
    )(x, d_out, xt, dt, pack, pack)


def ffn_second(lengths, x, d_out, xt, dt, pack, att, y1, dx1, ctx, pack0, vecs, shards):
    rows = x.shape[0]
    tiles = FF // 2 // FT
    tile_rows = pl.BlockSpec((MT, D), lambda f, n: (jnp.maximum(f - tiles, 0), 0))
    return pl.pallas_call(
        second_kernel,
        grid_spec=pltpu.PrefetchScalarGridSpec(
            num_scalar_prefetch=1,
            grid=(tiles + rows // MT,),
            in_specs=ffn_specs(tiles, shards) + [tile_rows] * 5 + [out_block(shards), whole(8, D)],
            out_specs=[pl.BlockSpec(memory_space=pl.ANY), tile_rows, tile_rows, tile_rows, whole(1, D)],
            scratch_shapes=[
                pltpu.VMEM((D, D), f32), pltpu.VMEM((D, D), bf16),
                pltpu.VMEM((shards, 3 * D // shards, FT), bf16), pltpu.SemaphoreType.DMA,
            ] + ffn_scratch(rows, shards),
        ),
        out_shape=[
            grad_shape(shards, 3 * D // shards),
            jax.ShapeDtypeStruct((rows, D), bf16),
            jax.ShapeDtypeStruct((rows, D), f32),
            jax.ShapeDtypeStruct((rows, D), bf16),
            jax.ShapeDtypeStruct((1, D), f32),
        ],
        compiler_params=pltpu.CompilerParams(vmem_limit_bytes=VMEM_LIMIT),
        cost_estimate=cost(46, 60),
        name="ffn_second",
    )(lengths, x, d_out, xt, dt, pack, pack, att, y1, dx1, d_out, ctx, pack0, vecs)


def norm_back(x, grad, gain):
    r = rms_scale(x)
    n = x * r
    u = gain * grad
    mean = jnp.sum(n * u, axis=1, keepdims=True) * (1.0 / D)
    return r * (u - n * mean), jnp.sum(n * grad, axis=0, keepdims=True)


def qkv_grad_kernel(dqkv_ref, normed_t_ref, gw_ref):
    gw_ref[...] = nn(normed_t_ref[...], dqkv_ref[0]).astype(bf16)


def qkv_grad(dqkv, normed_t):
    rows = normed_t.shape[1]
    return pl.pallas_call(
        qkv_grad_kernel,
        grid=(3,),
        in_specs=[pl.BlockSpec((1, rows, D), lambda i: (i, 0, 0)), whole(D, rows)],
        out_specs=pl.BlockSpec((D, D), lambda i: (0, i)),
        out_shape=jax.ShapeDtypeStruct((D, 3 * D), bf16),
        compiler_params=pltpu.CompilerParams(vmem_limit_bytes=VMEM_LIMIT),
        cost_estimate=cost(11, 20),
        name="qkv_grad",
    )(dqkv, normed_t)


def qkv_back_kernel(dqkv_ref, w_ref, hidden_ref, datt_ref, vec_ref, dh_ref, gg_ref):
    @pl.when(pl.program_id(0) == 0)
    def _():
        gg_ref[...] = jnp.zeros_like(gg_ref)

    dn = nt(dqkv_ref[0], w_ref[:, 0:D])
    for i in range(1, 3):
        dn = dn + nt(dqkv_ref[i], w_ref[:, i * D : (i + 1) * D])
    back, gain_grad = norm_back(hidden_ref[...], dn, vec_ref[5:6, :])
    gg_ref[...] += gain_grad
    dh_ref[...] = datt_ref[...] + back


def qkv_backward(dqkv, attn_w, hidden, d_att, vecs):
    rows = hidden.shape[0]
    tile = pl.BlockSpec((TOK, D), lambda s: (s, 0))
    return pl.pallas_call(
        qkv_back_kernel,
        grid=(rows // TOK,),
        in_specs=[
            pl.BlockSpec((3, TOK, D), lambda s: (0, s, 0)),
            pl.BlockSpec((D, 3 * D), lambda s: (0, 0)),
            tile, tile, whole(8, D),
        ],
        out_specs=[tile, whole(1, D)],
        out_shape=[jax.ShapeDtypeStruct((rows, D), f32), jax.ShapeDtypeStruct((1, D), f32)],
        compiler_params=pltpu.CompilerParams(vmem_limit_bytes=VMEM_LIMIT),
        cost_estimate=cost(14, 40),
        name="qkv_backward",
    )(dqkv, attn_w, hidden, d_att, vecs)


MESH = pl.DeviceIdType.MESH


def greet(peers):
    barrier = pltpu.get_barrier_semaphore()
    for peer in peers:
        pl.semaphore_signal(barrier, inc=1, device_id=peer, device_id_type=MESH)
    pl.semaphore_wait(barrier, len(peers))


def pack_half(out_ref, ffn_in_ref, ffn_out_ref, h, shards):
    hs = FF // 2 // shards
    owners = FT // hs
    deep = ffn_in_ref.shape[0]
    row = 0
    for f in range(FF // 2 // FT):
        for g in range(2):
            starts = [g * FF + (f * owners + o) * 2 * hs + h * hs for o in range(owners)]
            out_ref[row : row + deep, :] = jnp.concatenate([ffn_in_ref[:, a : a + hs] for a in starts], axis=1)
            row += deep
    for i in range(3):
        out_ref[row : row + hs, :] = ffn_out_ref[h * hs : (h + 1) * hs, i * FT : (i + 1) * FT]
        row += hs
    return row


def prepare_kernel(replicas, shards, length_ref, target_ref, embed_ref, conv_ref, score_ref, gain1_ref, gain2_ref, rel_ref,
                   ids_ref, attn_out_ref, ffn_in_ref, ffn_out_ref,
                   table_ref, vec_ref, table_rel_ref, slots_ref, column_ref, pack0_ref, pack1_ref,
                   own_ref, wide_ref, turn_ref, nat_ref, wanted_ref, send_sem, recv_sem):
    rep, me = lax.axis_index("rep"), lax.axis_index("shard")
    deep = embed_ref.shape[1]
    seqs = ids_ref.shape[0]
    twin = me + 1 - 2 * lax.rem(me, 2)
    far = [lax.rem(me + 2 * i, shards) for i in range(1, shards // 2)]
    others = [lax.rem(rep + i, replicas) for i in range(1, replicas)]
    greet([(rep, twin)] + [(rep, p) for p in far] + [(p, me) for p in others])

    def send(i, src, dst, device):
        copy = pltpu.make_async_remote_copy(
            src_ref=src, dst_ref=dst, send_sem=send_sem.at[i], recv_sem=recv_sem.at[i],
            device_id=device, device_id_type=MESH)
        copy.start()
        return copy

    wide_ref[...] = jnp.zeros_like(wide_ref)
    wide_ref[0:VOCAB, 0:deep] = embed_ref[...].astype(f32)
    wide_ref[VOCAB : VOCAB + 4, 0:deep] = conv_ref[...].astype(f32)
    for i, ref in enumerate((score_ref, gain1_ref, gain2_ref)):
        wide_ref[VOCAB + 4 + i : VOCAB + 5 + i, 0:deep] = ref[...].astype(f32).reshape(1, deep)
    rel_rows, heads = rel_ref.shape
    wide_ref[VOCAB + 7 : VOCAB + 7 + rel_rows, 0:heads] = rel_ref[...].astype(f32)
    own_ref[...] = wide_ref[...].T[0:deep].astype(bf16)
    near = [send(0, own_ref, table_ref.at[me], (rep, twin))]
    direct = [send(1 + i, own_ref, table_ref.at[me], (rep, p)) for i, p in enumerate(far)]
    lanes = lax.broadcasted_iota(jnp.int32, (8, 128), 1)
    wanted = jnp.zeros((8, 128), jnp.int32)
    for k in range(seqs):
        slot = target_ref[k] % seqs
        wanted = wanted + jnp.where(lanes == target_ref[k] // seqs // shards, slot + 1, 0)
    wanted_ref[...] = wanted
    base = shards
    asks = [send(base + i, wanted_ref, slots_ref.at[rep], (p, me)) for i, p in enumerate(others)]
    table_ref[me] = own_ref[...]
    slots_ref[rep] = wanted_ref[...]
    row = pack_half(pack0_ref, ffn_in_ref, ffn_out_ref, 0, shards)
    for i in range(3):
        pack0_ref[row : row + deep, :] = attn_out_ref[:, i * FT : (i + 1) * FT]
        row += deep
    pack_half(pack1_ref, ffn_in_ref, ffn_out_ref, 1, shards)
    base = base + replicas - 1
    for i, copy in enumerate(direct):
        copy.wait()
        source = lax.rem(me - 2 * (i + 1) + shards, shards)
        near.append(send(base + i, table_ref.at[source], table_ref.at[source], (rep, twin)))
    turn_ref[...] = jnp.full(turn_ref.shape, -1.0, f32)
    place = lax.broadcasted_iota(jnp.int32, (1, MAXLEN), 1)
    for s in range(seqs):
        turn_ref[s : s + 1, 0:MAXLEN] = jnp.where(place < length_ref[s], ids_ref[s : s + 1, :], -1).astype(f32)
    nat_ref[...] = turn_ref[...].T
    for r in range(R):
        rows = nat_ref[pl.ds(r, QN, stride=R), :]
        for s in range(seqs):
            column_ref[s, r * QN : (r + 1) * QN, :] = jnp.broadcast_to(rows[:, s : s + 1], (QN, 128))
    for copy in near + asks:
        copy.wait()
    last = table_ref[:, :, SMALL - 128 :].astype(f32).reshape(D, 128).T
    first = VOCAB - (SMALL - 128)
    vec_ref[...] = last[first : first + 8]
    table_rel_ref[...] = jnp.zeros_like(table_rel_ref)
    for s in range(shards):
        block = last[first + 7 : first + 7 + rel_rows, s * deep : s * deep + heads]
        table_rel_ref[s * rel_rows : (s + 1) * rel_rows, 0:heads] = block


def prepare(lengths, target, embed, conv_w, score_w, gain_attn, gain_ffn, rel_table, ids, attn_out, ffn_in, ffn_out,
            replicas, shards):
    deep = embed.shape[1]
    seqs = ids.shape[0]
    part, hs = 2 * D // shards, FF // 2 // shards
    rows = FF // 2 // FT * part + 3 * hs
    sems = shards + replicas - 1 + shards // 2 - 1
    vmem = pl.BlockSpec(memory_space=pltpu.VMEM)
    smem = pl.BlockSpec(memory_space=pltpu.SMEM)
    return pl.pallas_call(
        lambda *refs: prepare_kernel(replicas, shards, *refs),
        out_shape=[
            jax.ShapeDtypeStruct((shards, deep, SMALL), bf16),
            jax.ShapeDtypeStruct((8, D), f32),
            jax.ShapeDtypeStruct((BUCKETS, 128), f32),
            jax.ShapeDtypeStruct((replicas, 8, 128), jnp.int32),
            jax.ShapeDtypeStruct((seqs, P_ROWS, 128), f32),
            jax.ShapeDtypeStruct((rows + 3 * deep, FT), bf16),
            jax.ShapeDtypeStruct((rows, FT), bf16),
        ],
        in_specs=[smem] * 2 + [vmem] * 10,
        out_specs=[vmem] * 7,
        scratch_shapes=[
            pltpu.VMEM((deep, SMALL), bf16),
            pltpu.VMEM((SMALL, 128), f32),
            pltpu.VMEM((128, 1152), f32),
            pltpu.VMEM((1152, 128), f32),
            pltpu.VMEM((8, 128), jnp.int32),
            pltpu.SemaphoreType.DMA((sems,)),
            pltpu.SemaphoreType.DMA((sems,)),
        ],
        compiler_params=pltpu.CompilerParams(collective_id=1, has_side_effects=True, vmem_limit_bytes=VMEM_LIMIT),
        cost_estimate=cost(12, 8),
        name="prepare",
    )(lengths, target, embed, conv_w, score_w, gain_attn, gain_ffn, rel_table, ids, attn_out, ffn_in, ffn_out)


def pick_kernel(order_ref, in_ref, *refs):
    out_refs, sems = refs[:-1], refs[-1]
    copies = [pltpu.make_async_copy(in_ref.at[order_ref[i]], ref, sems.at[i]) for i, ref in enumerate(out_refs)]
    for copy in copies:
        copy.start()
    for copy in copies:
        copy.wait()


def pick(order, rows):
    count = order.shape[0]
    anywhere = pl.BlockSpec(memory_space=pl.ANY)
    return pl.pallas_call(
        pick_kernel,
        in_specs=[pl.BlockSpec(memory_space=pltpu.SMEM), anywhere],
        out_specs=[anywhere] * count,
        out_shape=[jax.ShapeDtypeStruct(rows.shape[1:], rows.dtype)] * count,
        scratch_shapes=[pltpu.SemaphoreType.DMA((count,))],
        compiler_params=pltpu.CompilerParams(vmem_limit_bytes=VMEM_LIMIT),
        cost_estimate=cost(3, 6),
        name="pick",
    )(order, rows)


def finish_kernel(replicas, shards, piece_ref, small_ref, in_ref, embed_ref, conv_ref, rest_ref,
                  twin_ref, both_ref, far_ref, held_ref, other_ref, part_ref, part2_ref, last_ref,
                  twin_send, twin_recv, far_send, far_recv, send_sem, recv_sem, send2_sem, recv2_sem):
    rep, me = lax.axis_index("rep"), lax.axis_index("shard")
    half = piece_ref.shape[1]
    chips = shards // 2
    core = lax.rem(me, 2)
    twin = me + 1 - 2 * core
    bits = [1 << b for b in range(replicas.bit_length() - 1)]
    orders = (bits, bits[::-1])
    far = [lax.rem(me + 2 * i, shards) for i in range(1, chips)]
    partners = {}
    for bit in bits:
        down = lax.rem(rep // bit, 2)
        partners[bit] = (rep + bit - 2 * bit * down, me)
    greet([(rep, twin)] + [(rep, p) for p in far] + [partners[bit] for bit in bits])

    def send(src, dst, sems, i, device):
        copy = pltpu.make_async_remote_copy(
            src_ref=src, dst_ref=dst, send_sem=sems[0].at[i], recv_sem=sems[1].at[i],
            device_id=device, device_id_type=MESH)
        copy.start()
        return copy

    near = [
        send(small_ref.at[2 * z + 1 - core], twin_ref.at[z], (twin_send, twin_recv), z, (rep, twin))
        for z in range(chips)
    ]

    def exchange(t, mine, theirs, sems):
        return [send(mine.at[t, h], theirs.at[t, h], sems, (t, h), partners[orders[h][t]]) for h in range(2)]

    held_ref[0] = piece_ref[...]
    large = exchange(0, held_ref, other_ref, (send_sem, recv_sem))
    for z, copy in enumerate(near):
        copy.wait()
        both_ref[z] = (small_ref[2 * z + core].astype(f32) + twin_ref[z].astype(f32)).astype(bf16)
    away = [send(both_ref.at[p // 2], far_ref.at[i], (far_send, far_recv), i, (rep, p)) for i, p in enumerate(far)]
    last_ref[...] = jnp.zeros_like(last_ref)
    total = both_ref[me // 2].astype(f32)
    for i, copy in enumerate(away):
        copy.wait()
        total = total + far_ref[i].astype(f32)
    part_ref[0] = total.astype(bf16)
    little = exchange(0, part_ref, part2_ref, (send2_sem, recv2_sem))
    for t in range(len(bits)):
        final = t == len(bits) - 1
        for h, copy in enumerate(large):
            copy.wait()
            total = held_ref[t, h].astype(f32) + other_ref[t, h].astype(f32)
            if final:
                in_ref[h * half : (h + 1) * half, :] = total
            else:
                held_ref[t + 1, h] = total.astype(bf16)
        if not final:
            large = exchange(t + 1, held_ref, other_ref, (send_sem, recv_sem))
        for h, copy in enumerate(little):
            copy.wait()
            total = part_ref[t, h].astype(f32) + part2_ref[t, h].astype(f32)
            if final:
                last_ref[h * half : (h + 1) * half, :] = total
            else:
                part_ref[t + 1, h] = total.astype(bf16)
        if not final:
            little = exchange(t + 1, part_ref, part2_ref, (send2_sem, recv2_sem))
    turned = last_ref[...].T
    deep = embed_ref.shape[1]
    embed_ref[...] = turned[0:VOCAB, 0:deep]
    conv_ref[...] = turned[VROWS : VROWS + 4, 0:deep]
    rest_ref[...] = turned[VROWS : VROWS + 16, 0:deep]


def finish(piece, small, replicas, shards):
    rows, wide = piece.shape
    half = rows // 2
    chips = shards // 2
    steps = replicas.bit_length() - 1
    vmem = pl.BlockSpec(memory_space=pltpu.VMEM)
    sems = lambda *shape: [pltpu.SemaphoreType.DMA(shape), pltpu.SemaphoreType.DMA(shape)]
    return pl.pallas_call(
        lambda *refs: finish_kernel(replicas, shards, *refs),
        out_shape=[
            jax.ShapeDtypeStruct((rows, wide), f32),
            jax.ShapeDtypeStruct((VOCAB, rows), f32),
            jax.ShapeDtypeStruct((4, rows), f32),
            jax.ShapeDtypeStruct((16, rows), f32),
        ],
        in_specs=[vmem] * 2,
        out_specs=[vmem] * 4,
        scratch_shapes=[
            pltpu.VMEM((chips, 2, half, SMALL), bf16),
            pltpu.VMEM((chips, 2, half, SMALL), bf16),
            pltpu.VMEM((chips - 1, 2, half, SMALL), bf16),
            pltpu.VMEM((steps, 2, half, wide), bf16),
            pltpu.VMEM((steps, 2, half, wide), bf16),
            pltpu.VMEM((steps, 2, half, SMALL), bf16),
            pltpu.VMEM((steps, 2, half, SMALL), bf16),
            pltpu.VMEM((128, SMALL), f32),
        ] + sems(chips) + sems(chips - 1) + sems(steps, 2) + sems(steps, 2),
        compiler_params=pltpu.CompilerParams(
            collective_id=2, has_side_effects=True, vmem_limit_bytes=VMEM_LIMIT),
        cost_estimate=cost(20, 4),
        name="finish_sums",
    )(piece.reshape(2, half, wide), small.reshape(shards, 2, half, SMALL))


def deliver_kernel(in_ref, embed_ref, conv_ref, rest_ref, in_out, embed_out, conv_out, score_out, gain1_out, gain2_out, rel_out):
    in_out[...] = in_ref[...]
    embed_out[...] = embed_ref[...]
    conv_out[...] = conv_ref[...]
    for i, ref in enumerate((score_out, gain1_out, gain2_out)):
        ref[...] = rest_ref[4 + i : 5 + i, :].reshape(ref.shape)
    rel_out[...] = rest_ref[7 : 7 + rel_out.shape[0], 0 : rel_out.shape[1]]


def deliver(parts, rel_rows):
    deep = parts[0].shape[0]
    vmem = pl.BlockSpec(memory_space=pltpu.VMEM)
    line = jax.ShapeDtypeStruct((deep,), f32)
    return pl.pallas_call(
        deliver_kernel,
        out_shape=[jax.ShapeDtypeStruct(x.shape, f32) for x in parts[:3]]
        + [line] * 3 + [jax.ShapeDtypeStruct((rel_rows, HEADS), f32)],
        in_specs=[vmem] * 4,
        out_specs=[vmem] * 7,
        compiler_params=pltpu.CompilerParams(vmem_limit_bytes=VMEM_LIMIT),
        cost_estimate=cost(2, 2),
        name="deliver",
    )(*parts)


def unpack_kernel(shards, first_ref, second_ref, other_ref, in_ref, out_ref, attn_ref):
    hs = FF // 2 // shards
    deep = in_ref.shape[0]
    owners = FT // hs
    for h in range(2):
        def load(start, count):
            rows = slice(start, start + count)
            if h == 0:
                return first_ref[rows, :].astype(f32)
            return second_ref[rows, :].astype(f32) + other_ref[rows, :].astype(f32)

        row = 0
        for f in range(FF // 2 // FT):
            for g in range(2):
                x = load(row, deep)
                for o in range(owners):
                    start = g * FF + (f * owners + o) * 2 * hs + h * hs
                    in_ref[:, start : start + hs] = x[:, o * hs : (o + 1) * hs]
                row += deep
        for i in range(3):
            out_ref[h * hs : (h + 1) * hs, i * FT : (i + 1) * FT] = load(row, hs)
            row += hs
        if h == 1:
            for i in range(3):
                attn_ref[:, i * FT : (i + 1) * FT] = load(row + i * deep, deep)


def unpack(first, second, other, shards):
    vmem = pl.BlockSpec(memory_space=pltpu.VMEM)
    return pl.pallas_call(
        lambda *refs: unpack_kernel(shards, *refs),
        out_shape=[
            jax.ShapeDtypeStruct((D // shards, 2 * FF), f32),
            jax.ShapeDtypeStruct((FF // shards, D), f32),
            jax.ShapeDtypeStruct((D // shards, D), f32),
        ],
        in_specs=[vmem] * 3,
        out_specs=[vmem] * 3,
        compiler_params=pltpu.CompilerParams(vmem_limit_bytes=VMEM_LIMIT),
        cost_estimate=cost(3, 5),
        name="unpack",
    )(first, second, other)


def send_cotangent(slots, cotangent):
    replicas = lax.axis_size("rep")
    places = jnp.arange(replicas)
    rep = lax.axis_index("rep")
    asked = jnp.where(places[None, :] == rep, slots, 0).sum(axis=1) - 1
    turned = (places[None, :] == (rep + places[:, None]) % replicas) * asked[None, :]
    pieces = list(pick(jnp.maximum(turned.sum(axis=1), 0), cotangent))
    for shift in range(1, replicas):
        pieces[shift] = lax.ppermute(pieces[shift], "rep", [(r, (r + shift) % replicas) for r in range(replicas)])
    return pieces


def swap(x, bit):
    replicas = lax.axis_size("rep")
    return lax.ppermute(x, "rep", [(r, r ^ bit) for r in range(replicas)])


def add_low(a, b):
    return (a.astype(f32) + b.astype(f32)).astype(bf16)


def scatter_sum(grad):
    return lax.psum_scatter(grad, "shard", scatter_dimension=0, tiled=True)


def body(
    byte_ids, lengths, target, rel_bucket, cotangent, embed, conv_w, score_w, gain_attn,
    attn_in, attn_out, gain_ffn, ffn_in, ffn_out, rel_table,
):
    seqs = byte_ids.shape[0]
    replicas, shards = lax.axis_size("rep"), lax.axis_size("shard")
    attn_w = lax.all_gather(attn_in, "shard", axis=0, tiled=True)
    table, vecs, rel, slots, ids_col, pack0, pack1 = prepare(
        lengths, target, embed, conv_w, score_w, gain_attn, gain_ffn, rel_table, byte_ids,
        attn_out, ffn_in, ffn_out, replicas, shards,
    )
    packs = [lax.all_gather(pack, "shard", axis=0) for pack in (pack0, pack1)]
    row, row_back = bucket_row(rel_bucket), bucket_row(rel_bucket[::-1])

    hidden, normed, normed_t, convolved, weights = gbst_forward(lengths, ids_col, table, vecs)
    qkv = jnp.dot(normed, attn_w, preferred_element_type=f32).astype(bf16)
    qkv, slots = lax.optimization_barrier((qkv, slots))
    pieces = send_cotangent(slots[:, 0, :replicas], cotangent)
    ctx, lse = attn_forward(lengths, qkv, rel, row)
    ctx, pieces = lax.optimization_barrier((ctx, pieces))
    shifts = (lax.axis_index("rep") - target // seqs // shards) % replicas
    attended, low, low_t, d_out, d_out_t = post_attention(
        lengths, shifts, ctx, packs[0], hidden, vecs, pieces, shards
    )
    g_half1, y1, dx1 = ffn_first(low, d_out, low_t, d_out_t, packs[0], shards)
    g_half2, out, d_att, d_ctx, g_gain_ffn = ffn_second(
        lengths, low, d_out, low_t, d_out_t, packs[1], attended, y1, dx1, ctx, packs[0], vecs, shards
    )
    one, two = [scatter_sum(g.reshape(-1, FT)) for g in (g_half1, g_half2)]
    bits = [1 << b for b in range(replicas.bit_length() - 1)]
    d_ctx, one = lax.optimization_barrier((d_ctx, one))
    other = swap(one, bits[0])
    dqkv, g_rel = attn_backward(lengths, qkv, d_ctx, ctx, lse, rel, row_back, shards)
    dqkv, other = lax.optimization_barrier((dqkv, other))
    one = add_low(one, other)
    g_attn = qkv_grad(dqkv, normed_t)
    g_attn, two = lax.optimization_barrier((g_attn, two))
    p_attn = scatter_sum(g_attn)
    others = swap(one, bits[1]), swap(two, bits[0])
    d_hidden, g_gain_attn = qkv_backward(dqkv, attn_w, hidden, d_att, vecs)
    d_hidden, others = lax.optimization_barrier((d_hidden, others))
    one, two = add_low(one, others[0]), add_low(two, others[1])
    for bit in bits[2:]:
        one, two = add_low(one, swap(one, bit)), add_low(two, swap(two, bit))
    d_hidden, one, two = lax.optimization_barrier((d_hidden, one, two))
    other = swap(two, bits[1])
    ids = jnp.where(jnp.arange(MAXLEN)[None, :] < lengths[:, None], byte_ids, -1)
    input_grad, small = gbst_backward(
        lengths, ids_col, ids.reshape(seqs, 1, MAXLEN), table, vecs, d_hidden, convolved, weights,
        g_gain_attn, g_gain_ffn, g_rel,
    )
    small, other = lax.optimization_barrier((small, other))
    parts = finish(p_attn, small, replicas, shards)
    s_ffn_in, s_ffn_out, s_attn_out = unpack(one, two, other, shards)
    s_attn_in, s_embed, s_conv, s_score, s_gain_attn, s_gain_ffn, s_rel = deliver(parts, rel_table.shape[0])
    return (
        out.reshape(seqs, TOK, D), input_grad, s_embed, s_conv, s_score, s_gain_attn, s_attn_in, s_attn_out,
        s_gain_ffn, s_ffn_in, s_ffn_out, s_rel,
    )


def solution(mesh):
    in_specs = (
        P(("rep", "shard"), None), P(("rep", "shard")), P(("rep", "shard")), P(),
        P(("rep", "shard"), None, None), P(None, "shard"), P(None, "shard"), P("shard"), P("shard"),
        P("shard", None), P("shard", None), P("shard"), P("shard", None), P("shard", None), P("shard", None),
    )
    out_specs = (
        P(("rep", "shard"), None, None), P(("rep", "shard"), None, None), P(None, "shard"), P(None, "shard"),
        P("shard"), P("shard"), P("shard", None), P("shard", None), P("shard"), P("shard", None),
        P("shard", None), P("shard", None),
    )
    return jax.shard_map(body, mesh=mesh, in_specs=in_specs, out_specs=out_specs, check_vma=False)
```

```python
import jax
import jax.numpy as jnp
from jax import lax
from jax.experimental import pallas as pl
from jax.experimental.pallas import tpu as pltpu
from jax.sharding import PartitionSpec as P

D = 768
VOCAB = 259
VROWS = 272
VMEM_LIMIT = 60 << 20
SMALL = 384
MAXLEN = 1024
TOK = 512
LANES = 128
QN = 88
R = 12
P_ROWS = QN * R
T_ROWS = 528
LT = D // LANES
epsilon = 1e-06
f32 = jnp.float32
bf16 = jnp.bfloat16


def cost(us, mib):
    return pl.CostEstimate(flops=int(us * 1e9), bytes_accessed=mib << 20, transcendentals=0)


def lane_iota(rows):
    return lax.broadcasted_iota(jnp.int32, (rows, LANES), 1)


def group_matrix(b):
    row = lax.broadcasted_iota(jnp.int32, (LANES, LANES), 0)
    col = lax.broadcasted_iota(jnp.int32, (LANES, LANES), 1)
    return jnp.where((row // b == col // b) & (row < R) & (col < R), 1.0, 0.0).astype(f32)


def exact_dot(a, b):
    return jnp.dot(a, b, precision=lax.Precision.HIGHEST, preferred_element_type=f32)


def place(columns, rows):
    lanes = lane_iota(rows)
    out = jnp.zeros((rows, LANES), f32)
    for r, column in enumerate(columns):
        out = jnp.where(lanes == r, column, out)
    return out


def gbst_masks(length):
    q = lax.broadcasted_iota(jnp.int32, (QN, LANES), 0)
    r = lax.broadcasted_iota(jnp.int32, (QN, LANES), 1)
    mask = jnp.where((q * R + r < length) & (r < R), 1.0, 0.0).astype(f32)
    inverse = [1.0 / jnp.maximum(exact_dot(mask, group_matrix(b)), 1.0) for b in (2, 3, 4)]
    pair = exact_dot(mask, group_matrix(2))
    alpha = mask / jnp.maximum(pair, 1.0)
    return mask, inverse, alpha


def gbst_weights(s1, inverse):
    sizes = [s1] + [exact_dot(s1, group_matrix(b)) * inv for b, inv in zip((2, 3, 4), inverse)]
    top = jnp.maximum(jnp.maximum(sizes[0], sizes[1]), jnp.maximum(sizes[2], sizes[3]))
    parts = [jnp.exp(s - top) for s in sizes]
    total = parts[0] + parts[1] + parts[2] + parts[3]
    return [p / total for p in parts]


def gbst_coefs(weights, inverse, alpha):
    a1 = weights[0] * alpha
    a2 = weights[1] * alpha * inverse[0]
    a3 = weights[2] * alpha * inverse[1]
    a4 = weights[3] * alpha * inverse[2]
    pair = group_matrix(2)
    a4s = exact_dot(a4, pair)
    own = a1 + exact_dot(a2, pair) + a4s
    return own, a3, a4s


def column(x, r):
    return jnp.broadcast_to(x[:, r : r + 1], (x.shape[0], LANES))


def hits_of(ids):
    lanes = lax.broadcasted_iota(jnp.int32, (P_ROWS, LANES), 1).astype(f32)
    return jnp.concatenate(
        [jnp.where(ids == lanes + float(i * LANES), 1.0, 0.0).astype(bf16) for i in range(SMALL // LANES)], axis=1)


def look_up(ids, table_ref):
    return lax.dot_general(
        hits_of(ids), table_ref[...].reshape(D, SMALL), (((1,), (1,)), ((), ())), preferred_element_type=f32)


def load_e(e_ref, r, lt):
    lanes = pl.ds(lt * LANES, LANES)
    if r < R:
        return e_ref[pl.ds(r * QN, QN), lanes]
    return e_ref[pl.ds((r - R) * QN + 1, QN), lanes]


def gbst_fwd_kernel(len_ref, ids_ref, table_ref, vec_ref, hidden_ref, normed_ref, turned_ref, c_ref, w_ref, e_ref, hid_ref, s_ref, k_ref):
    length = len_ref[pl.program_id(0)]
    e_ref[pl.ds(0, P_ROWS), :] = look_up(ids_ref[0], table_ref)
    e_ref[pl.ds(P_ROWS, 8), :] = jnp.zeros((8, D), f32)
    for lt in range(LT):
        lanes = pl.ds(lt * LANES, LANES)
        taps = [jnp.broadcast_to(vec_ref[j : j + 1, lanes], (QN, LANES)) for j in range(4)]
        sw = jnp.broadcast_to(vec_ref[4:5, lanes], (QN, LANES))
        for r in range(R):
            c = taps[0] * load_e(e_ref, r, lt)
            for j in range(1, 4):
                c = c + taps[j] * load_e(e_ref, r + j, lt)
            c_ref[0, pl.ds(r * QN, QN), lanes] = c
            part = c * sw
            rows = pl.ds(r * QN, QN)
            s_ref[rows, :] = part if lt == 0 else s_ref[rows, :] + part
    s1 = place([jnp.sum(s_ref[pl.ds(r * QN, QN), :], axis=1, keepdims=True) for r in range(R)], QN)
    mask, inverse, alpha = gbst_masks(length)
    weights = gbst_weights(s1, inverse)
    for b in range(4):
        w_ref[0, b] = weights[b]
    own, a3, a4s = gbst_coefs(weights, inverse, alpha)
    n = 0
    for r in range(R):
        k_ref[r] = column(own, r)
        k_ref[R + r] = column(a3, r)
    for k in range(6):
        k_ref[2 * R + k] = column(a4s, 2 * k)
    for lt in range(LT):
        lanes = pl.ds(lt * LANES, LANES)
        for half in range(2):
            c = [c_ref[0, pl.ds((half * 6 + r) * QN, QN), lanes] for r in range(6)]
            base = half * 6
            s3 = [c[0] + c[1] + c[2], c[3] + c[4] + c[5]]
            for k in range(3):
                tok = half * 3 + k
                other = tok ^ 1
                rows = pl.ds(2 * other * QN, QN)
                rows1 = pl.ds((2 * other + 1) * QN, QN)
                s2 = c_ref[0, rows, lanes] + c_ref[0, rows1, lanes]
                h = k_ref[2 * tok] * c[2 * k] + k_ref[2 * tok + 1] * c[2 * k + 1] + k_ref[2 * R + tok] * s2
                if k == 1:
                    h = h + k_ref[R + 2 * tok] * s3[0] + k_ref[R + 2 * tok + 1] * s3[1]
                else:
                    h = h + (k_ref[R + 2 * tok] + k_ref[R + 2 * tok + 1]) * s3[0 if k == 0 else 1]
                hid_ref[lt, pl.ds(tok, QN, stride=6), :] = h
    total = jnp.zeros((TOK, LANES), f32)
    for lt in range(LT):
        x = hid_ref[lt, 0:TOK, :]
        total = total + x * x
    scale = lax.rsqrt(jnp.sum(total, axis=1, keepdims=True) * (1.0 / D) + epsilon)
    for lt in range(LT):
        lanes = pl.ds(lt * LANES, LANES)
        x = hid_ref[lt, 0:TOK, :]
        hidden_ref[:, lanes] = x
        normed = (x * scale * vec_ref[5:6, lanes]).astype(bf16)
        normed_ref[:, lanes] = normed
        turned_ref[lanes, :] = normed.T


def gbst_forward(lengths, ids_col, table, vecs):
    seqs = ids_col.shape[0]
    grid_spec = pltpu.PrefetchScalarGridSpec(
        num_scalar_prefetch=1,
        grid=(seqs,),
        in_specs=[
            pl.BlockSpec((1, P_ROWS, LANES), lambda s, n: (s, 0, 0)),
            pl.BlockSpec(table.shape, lambda s, n: (0, 0, 0)),
            pl.BlockSpec((8, D), lambda s, n: (0, 0)),
        ],
        out_specs=[
            pl.BlockSpec((TOK, D), lambda s, n: (s, 0)),
            pl.BlockSpec((TOK, D), lambda s, n: (s, 0)),
            pl.BlockSpec((D, TOK), lambda s, n: (0, s)),
            pl.BlockSpec((1, P_ROWS, D), lambda s, n: (s, 0, 0)),
            pl.BlockSpec((1, 4, QN, LANES), lambda s, n: (s, 0, 0, 0)),
        ],
        scratch_shapes=[
            pltpu.VMEM((P_ROWS + 8, D), f32),
            pltpu.VMEM((LT, T_ROWS, LANES), f32),
            pltpu.VMEM((P_ROWS, LANES), f32),
            pltpu.VMEM((2 * R + 6, QN, LANES), f32),
        ],
    )
    return pl.pallas_call(
        gbst_fwd_kernel,
        grid_spec=grid_spec,
        out_shape=[
            jax.ShapeDtypeStruct((seqs * TOK, D), f32),
            jax.ShapeDtypeStruct((seqs * TOK, D), bf16),
            jax.ShapeDtypeStruct((D, seqs * TOK), bf16),
            jax.ShapeDtypeStruct((seqs, P_ROWS, D), f32),
            jax.ShapeDtypeStruct((seqs, 4, QN, LANES), f32),
        ],
        compiler_params=pltpu.CompilerParams(vmem_limit_bytes=VMEM_LIMIT),
        cost_estimate=cost(18, 30),
        name="gbst_forward",
    )(lengths, ids_col, table, vecs)


def gbst_bwd_kernel(len_ref, ids_ref, row_ref, table_ref, vec_ref, dh_ref, c_ref, w_ref, gain1_ref, gain2_ref, rel_ref,
                    ig_ref, small_ref, ge_ref, e_ref, dt_ref, dc_ref, s_ref, k_ref, igs_ref):
    seq = pl.program_id(0)
    length = len_ref[seq]

    @pl.when(seq == 0)
    def _():
        ge_ref[...] = jnp.zeros_like(ge_ref)

    e_ref[pl.ds(0, P_ROWS), :] = look_up(ids_ref[0], table_ref)
    e_ref[pl.ds(P_ROWS, 8), :] = jnp.zeros((8, D), f32)
    for lt in range(LT):
        dt_ref[lt, 0:TOK, :] = dh_ref[:, pl.ds(lt * LANES, LANES)]
        dt_ref[lt, TOK:T_ROWS, :] = jnp.zeros((T_ROWS - TOK, LANES), f32)
    for lt in range(LT):
        lanes = pl.ds(lt * LANES, LANES)
        for half in range(2):
            c = [c_ref[0, pl.ds((half * 6 + r) * QN, QN), lanes] for r in range(6)]
            s3 = [c[0] + c[1] + c[2], c[3] + c[4] + c[5]]
            for k in range(3):
                tok = half * 3 + k
                other = tok ^ 1
                dh = dt_ref[lt, pl.ds(tok, QN, stride=6), :]
                s2 = c_ref[0, pl.ds(2 * other * QN, QN), lanes] + c_ref[0, pl.ds((2 * other + 1) * QN, QN), lanes]
                parts = [
                    (2 * tok, dh * c[2 * k]),
                    (2 * tok + 1, dh * c[2 * k + 1]),
                    (2 * R + tok, dh * s2),
                    (R + 2 * tok, dh * s3[0 if k < 2 else 1]),
                ]
                if k == 1:
                    parts.append((R + 2 * tok + 1, dh * s3[1]))
                for slot, part in parts:
                    s_ref[slot] = part if lt == 0 else s_ref[slot] + part

    def total(slot):
        return jnp.sum(s_ref[slot], axis=1, keepdims=True)

    d1, d3, dother = [], [], []
    for tok in range(6):
        d1 += [total(2 * tok), total(2 * tok + 1)]
        first = total(R + 2 * tok)
        d3 += [first, total(R + 2 * tok + 1) if tok % 3 == 1 else first]
        o = total(2 * R + tok)
        dother += [o, o]
    d1, d3, dother = place(d1, QN), place(d3, QN), place(dother, QN)
    mask, inverse, alpha = gbst_masks(length)
    weights = [w_ref[0, b] for b in range(4)]
    d2 = exact_dot(d1, group_matrix(2))
    g = [alpha * d1, alpha * d2 * inverse[0], alpha * d3 * inverse[1], alpha * (d2 + dother) * inverse[2]]
    mean = weights[0] * g[0] + weights[1] * g[1] + weights[2] * g[2] + weights[3] * g[3]
    d_size = [w * (x - mean) for w, x in zip(weights, g)]
    coef = d_size[0]
    for b, inv in zip((2, 3, 4), inverse):
        coef = coef + exact_dot(d_size[b - 1] * inv, group_matrix(b))
    own, a3, a4s = gbst_coefs(weights, inverse, alpha)
    for r in range(R):
        k_ref[r] = column(own, r)
        k_ref[R + r] = column(a3, r)
        k_ref[2 * R + r] = column(coef, r)
        k_ref[3 * R + r] = column(mask, r)
    for k in range(6):
        k_ref[4 * R + k] = column(a4s, 2 * k)

    for lt in range(LT):
        lanes = pl.ds(lt * LANES, LANES)
        taps = [jnp.broadcast_to(vec_ref[j : j + 1, lanes], (QN, LANES)) for j in range(4)]
        sw = jnp.broadcast_to(vec_ref[4:5, lanes], (QN, LANES))
        gs = jnp.zeros((QN, LANES), f32)
        gc = [jnp.zeros((QN, LANES), f32) for _ in range(4)]
        for half in range(2):
            dh = [dt_ref[lt, pl.ds(half * 3 + k, QN, stride=6), :] for k in range(3)]
            a = R + half * 6
            t3 = [
                (k_ref[a] + k_ref[a + 1]) * dh[0] + k_ref[a + 2] * dh[1],
                k_ref[a + 3] * dh[1] + (k_ref[a + 4] + k_ref[a + 5]) * dh[2],
            ]
            for k in range(3):
                tok = half * 3 + k
                other = tok ^ 1
                dother_h = dt_ref[lt, pl.ds(other, QN, stride=6), :]
                cross = k_ref[4 * R + other] * dother_h
                for e in range(2):
                    r = 2 * tok + e
                    cf = k_ref[2 * R + r]
                    dc = k_ref[r] * dh[k] + cross + t3[(r % 6) // 3] + cf * sw
                    gs = gs + cf * c_ref[0, pl.ds(r * QN, QN), lanes]
                    dc_ref[r, pl.ds(8, QN), :] = dc
                    for j in range(4):
                        gc[j] = gc[j] + dc * load_e(e_ref, r + j, lt)
        ge_ref[VROWS + 4 : VROWS + 5, lanes] += jnp.sum(gs, axis=0, keepdims=True)
        for j in range(4):
            ge_ref[VROWS + j : VROWS + j + 1, lanes] += jnp.sum(gc[j], axis=0, keepdims=True)
        for r in range(R):
            dc_ref[r, 0:8, :] = jnp.zeros((8, LANES), f32)
        for r in range(R):
            x = taps[0] * dc_ref[r, pl.ds(8, QN), :]
            for j in range(1, 4):
                back = dc_ref[r - j, pl.ds(8, QN), :] if r >= j else dc_ref[r - j + R, pl.ds(7, QN), :]
                x = x + taps[j] * back
            igs_ref[lt, pl.ds(r, QN, stride=R), :] = x * k_ref[3 * R + r]
    for lt in range(LT):
        lanes = pl.ds(lt * LANES, LANES)
        ig_ref[0, :, lanes] = igs_ref[lt, 0:MAXLEN, :].astype(bf16)
    vocab = lax.broadcasted_iota(jnp.int32, (VROWS, MAXLEN), 0)
    row_hits = jnp.where(vocab == row_ref[0], 1.0, 0.0).astype(bf16)
    ge_ref[0:VROWS, :] += jnp.dot(row_hits, ig_ref[0], preferred_element_type=f32)

    @pl.when(seq == pl.num_programs(0) - 1)
    def _():
        ge_ref[VROWS + 5 : VROWS + 6, :] = gain1_ref[...]
        ge_ref[VROWS + 6 : VROWS + 7, :] = gain2_ref[...]
        ge_ref[VROWS + 7 : VROWS + 15, :] = rel_ref[...]
        for lt in range(LT):
            lanes = pl.ds(lt * LANES, LANES)
            small_ref[lanes, :] = ge_ref[:, lanes].T.astype(bf16)


def gbst_backward(lengths, ids_col, ids_row, table, vecs, d_hidden, c, w, gain1, gain2, rel):
    seqs = ids_col.shape[0]
    grid_spec = pltpu.PrefetchScalarGridSpec(
        num_scalar_prefetch=1,
        grid=(seqs,),
        in_specs=[
            pl.BlockSpec((1, P_ROWS, LANES), lambda s, n: (s, 0, 0)),
            pl.BlockSpec((1, 1, MAXLEN), lambda s, n: (s, 0, 0)),
            pl.BlockSpec(table.shape, lambda s, n: (0, 0, 0)),
            pl.BlockSpec((8, D), lambda s, n: (0, 0)),
            pl.BlockSpec((TOK, D), lambda s, n: (s, 0)),
            pl.BlockSpec((1, P_ROWS, D), lambda s, n: (s, 0, 0)),
            pl.BlockSpec((1, 4, QN, LANES), lambda s, n: (s, 0, 0, 0)),
            pl.BlockSpec((1, D), lambda s, n: (0, 0)),
            pl.BlockSpec((1, D), lambda s, n: (0, 0)),
            pl.BlockSpec((8, D), lambda s, n: (0, 0)),
        ],
        out_specs=[
            pl.BlockSpec((1, MAXLEN, D), lambda s, n: (s, 0, 0)),
            pl.BlockSpec((D, SMALL), lambda s, n: (0, 0)),
        ],
        scratch_shapes=[
            pltpu.VMEM((SMALL, D), f32),
            pltpu.VMEM((P_ROWS + 8, D), f32),
            pltpu.VMEM((LT, T_ROWS, LANES), f32),
            pltpu.VMEM((R, QN + 8, LANES), f32),
            pltpu.VMEM((2 * R + 6, QN, LANES), f32),
            pltpu.VMEM((4 * R + 6, QN, LANES), f32),
            pltpu.VMEM((LT, P_ROWS, LANES), f32),
        ],
    )
    return pl.pallas_call(
        gbst_bwd_kernel,
        grid_spec=grid_spec,
        out_shape=[
            jax.ShapeDtypeStruct((seqs, MAXLEN, D), bf16),
            jax.ShapeDtypeStruct((D, SMALL), bf16),
        ],
        compiler_params=pltpu.CompilerParams(vmem_limit_bytes=VMEM_LIMIT),
        cost_estimate=cost(31, 40),
        name="gbst_backward",
    )(lengths, ids_col, ids_row, table, vecs, d_hidden, c, w, gain1, gain2, rel)


HEADS = 12
HD = 64
BUCKETS = 32
SPAN = 1024
HB = 4
WIDE = HB * HD
GROUPS = HEADS // HB
dead_score = -1e9


def nt(a, b):
    return lax.dot_general(a, b, (((1,), (1,)), ((), ())), preferred_element_type=f32)


def nn(a, b):
    return jnp.dot(a, b, preferred_element_type=f32)


def bucket_rows(buckets):
    def row(x):
        return jnp.concatenate([x[TOK - 1 :], x[:1], x[: TOK - 1]])

    return jnp.stack([row(buckets), row(buckets[::-1])])


def bucket_hits(row_ref, way):
    return jnp.where(lax.broadcasted_iota(jnp.int32, (BUCKETS, SPAN), 0) == row_ref[way : way + 1, :], 1.0, 0.0).astype(f32)


def spread_table(rel_ref, row_ref, z_ref, way):
    dims = (((0,), (0,)), ((), ()))
    z_ref[...] = lax.dot_general(
        rel_ref[...].astype(bf16), bucket_hits(row_ref, way).astype(bf16), dims, preferred_element_type=f32)


def build_bias(z_ref, bt_ref, group):
    for h in range(HB):
        row = jnp.broadcast_to(z_ref[pl.ds(group * HB + h, 1), :], (8, SPAN))
        z = pltpu.roll(row, 0, 1, stride=1, stride_axis=0)
        for g in range(TOK // 8):
            bt_ref[h, pl.ds(8 * g, 8), :] = (z if g == 0 else pltpu.roll(z, 8 * g, 1))[:, :TOK]


def own_lanes(h):
    return lax.broadcasted_iota(jnp.int32, (TOK, WIDE), 1) // HD == h


def head_parts(k, q, length, h):
    lanes = lax.broadcasted_iota(jnp.int32, (TOK, WIDE), 1)
    rows = lax.broadcasted_iota(jnp.int32, (TOK, WIDE), 0)
    spare = HD * (h + 1) % WIDE
    dead = jnp.where(2 * rows < length, 0.0, dead_score)
    kf = jnp.where(lanes // HD == h, k.astype(f32), jnp.where(lanes == spare, dead, 0.0)).astype(bf16)
    qf = jnp.where(lanes == spare, 1.0, q.astype(f32)).astype(bf16)
    return kf, qf


def join_heads(parts):
    out = parts[0]
    for h in range(1, HB):
        out = jnp.where(own_lanes(h), parts[h], out)
    return out.astype(bf16)


def attn_fwd_kernel(len_ref, q_ref, k_ref, v_ref, rel_ref, row_ref, ctx_ref, lse_ref, bias_ref, z_ref):
    length = len_ref[pl.program_id(1)]

    @pl.when((pl.program_id(0) == 0) & (pl.program_id(1) == 0))
    def _():
        spread_table(rel_ref, row_ref, z_ref, 0)

    @pl.when(pl.program_id(1) == 0)
    def _():
        build_bias(z_ref, bias_ref, pl.program_id(0))

    q, k, v = q_ref[...], k_ref[...], v_ref[...]

    def score(h):
        kf, qf = head_parts(k, q, length, h)
        return nt(qf, kf) + bias_ref[h]

    outs = []
    lanes = lax.broadcasted_iota(jnp.int32, (TOK, LANES), 1)
    lse = jnp.zeros((TOK, LANES), f32)
    s = score(0)
    for h in range(HB):
        later = score(h + 1) if h + 1 < HB else None
        top = jnp.max(s, axis=1, keepdims=True)
        p = jnp.exp(s - top)
        total = jnp.sum(p, axis=1, keepdims=True)
        outs.append(nn(p.astype(bf16), v) * (1.0 / total))
        lse = jnp.where(lanes == h, top + jnp.log(total), lse)
        s = later
    ctx_ref[...] = join_heads(outs)
    lse_ref[0, 0] = lse.T[0:8]


def table_specs():
    return [
        pl.BlockSpec((BUCKETS, LANES), lambda hp, s, n: (0, 0)),
        pl.BlockSpec((2, SPAN), lambda hp, s, n: (0, 0)),
    ]


def attn_forward(lengths, qkv, rel, row):
    seqs = qkv.shape[0] // TOK
    spec = lambda off: pl.BlockSpec((TOK, WIDE), lambda hp, s, n: (s, off + hp))
    return pl.pallas_call(
        attn_fwd_kernel,
        grid_spec=pltpu.PrefetchScalarGridSpec(
            num_scalar_prefetch=1,
            grid=(GROUPS, seqs),
            in_specs=[spec(0), spec(GROUPS), spec(2 * GROUPS)] + table_specs(),
            out_specs=[spec(0), pl.BlockSpec((1, 1, 8, TOK), lambda hp, s, n: (hp, s, 0, 0))],
            scratch_shapes=[pltpu.VMEM((HB, TOK, TOK), f32), pltpu.VMEM((LANES, SPAN), f32)],
        ),
        out_shape=[
            jax.ShapeDtypeStruct((seqs * TOK, D), bf16),
            jax.ShapeDtypeStruct((GROUPS, seqs, 8, TOK), f32),
        ],
        compiler_params=pltpu.CompilerParams(vmem_limit_bytes=VMEM_LIMIT),
        cost_estimate=cost(27, 20),
        name="attn_forward",
    )(lengths, qkv, qkv, qkv, rel, row)


def attn_bwd_kernel(shards, len_ref, q_ref, k_ref, v_ref, do_ref, o_ref, lse_ref, rel_ref, row_ref, dqkv_ref, gt_ref, bt_ref, g_ref, z_ref, gz_ref):
    s_id = pl.program_id(1)
    length = len_ref[s_id]

    @pl.when((pl.program_id(0) == 0) & (s_id == 0))
    def _():
        spread_table(rel_ref, row_ref, z_ref, 1)
        gz_ref[...] = jnp.zeros_like(gz_ref)

    @pl.when(s_id == 0)
    def _():
        build_bias(z_ref, bt_ref, pl.program_id(0))
        g_ref[...] = jnp.zeros_like(g_ref)

    q, k, v, do = q_ref[...], k_ref[...], v_ref[...], do_ref[...]
    kt = k.astype(f32).T.astype(bf16)
    lanes8 = lax.broadcasted_iota(jnp.int32, (8, WIDE), 1)
    rows8 = lax.broadcasted_iota(jnp.int32, (8, WIDE), 0)
    pick = jnp.where(lanes8 // HD == rows8, 1.0, 0.0).astype(bf16)
    prod = do.astype(f32) * o_ref[...].astype(f32)
    upper = prod.astype(bf16)
    delta = nt(pick, upper) + nt(pick, (prod - upper.astype(f32)).astype(bf16))
    dq, dk, dv = [], [], []

    def first(h):
        kf, qf = head_parts(k, q, length, h)
        vf = jnp.where(own_lanes(h), v.astype(f32), 0.0).astype(bf16)
        return nt(kf, qf) + bt_ref[h], nt(vf, do)

    now = first(0)
    for h in range(HB):
        later = first(h + 1) if h + 1 < HB else None
        s, d_prob = now
        p = jnp.exp(s - lse_ref[0, 0, h : h + 1, :])
        ds = p * (d_prob - delta[h : h + 1, :])
        g_ref[h] += ds
        low = ds.astype(bf16)
        dv.append(nn(p.astype(bf16), do))
        dk.append(nn(low, q))
        dq.append(nn(kt[h * HD : (h + 1) * HD], low))
        now = later
    dqkv_ref[0] = jnp.concatenate(dq, axis=0).T.astype(bf16)
    dqkv_ref[1] = join_heads(dk)
    dqkv_ref[2] = join_heads(dv)

    @pl.when(s_id == pl.num_programs(1) - 1)
    def _():
        for h in range(HB):
            total = jnp.zeros((8, SPAN), f32)
            for g in range(LANES // 8):
                tiles = [jnp.zeros((8, LANES), f32) for _ in range(SPAN // LANES)]
                for j in range(TOK // LANES):
                    x = g_ref[h, pl.ds(LANES * j + 8 * g, 8), :]
                    for t in range(TOK // LANES):
                        n = (t - j) % (SPAN // LANES)
                        tiles[n] = tiles[n] + x[:, t * LANES : (t + 1) * LANES]
                piece = jnp.concatenate(tiles, axis=1)
                total = total + (piece if g == 0 else pltpu.roll(piece, SPAN - 8 * g, 1))
            out = total[0:1]
            for s in range(1, 8):
                out = out + pltpu.roll(jnp.broadcast_to(total[s : s + 1], (8, SPAN)), SPAN - s, 1)[0:1]
            gz_ref[pl.ds(pl.program_id(0) * HB + h, 1), :] = out

    @pl.when((pl.program_id(0) == GROUPS - 1) & (s_id == pl.num_programs(1) - 1))
    def _():
        total = lax.dot_general(
            bucket_hits(row_ref, 1), gz_ref[...], (((1,), (1,)), ((), ())),
            precision=lax.Precision.HIGHEST, preferred_element_type=f32)
        gt_ref[...] = jnp.zeros_like(gt_ref)
        per = BUCKETS // shards
        for s in range(shards):
            start = s * (D // shards)
            gt_ref[0:per, start : start + HEADS] = total[s * per : (s + 1) * per, 0:HEADS]


def attn_backward(lengths, qkv, d_ctx, ctx, lse, rel, row, shards):
    seqs = qkv.shape[0] // TOK
    spec = lambda off: pl.BlockSpec((TOK, WIDE), lambda hp, s, n: (s, off + hp))
    return pl.pallas_call(
        lambda *refs: attn_bwd_kernel(shards, *refs),
        grid_spec=pltpu.PrefetchScalarGridSpec(
            num_scalar_prefetch=1,
            grid=(GROUPS, seqs),
            in_specs=[
                spec(0), spec(GROUPS), spec(2 * GROUPS), spec(0), spec(0),
                pl.BlockSpec((1, 1, 8, TOK), lambda hp, s, n: (hp, s, 0, 0)),
            ] + table_specs(),
            out_specs=[
                pl.BlockSpec((3, TOK, WIDE), lambda hp, s, n: (0, s, hp)),
                pl.BlockSpec((8, D), lambda hp, s, n: (0, 0)),
            ],
            scratch_shapes=[
                pltpu.VMEM((HB, TOK, TOK), f32), pltpu.VMEM((HB, TOK, TOK), f32),
                pltpu.VMEM((LANES, SPAN), f32), pltpu.VMEM((16, SPAN), f32),
            ],
        ),
        out_shape=[
            jax.ShapeDtypeStruct((3, seqs * TOK, D), bf16),
            jax.ShapeDtypeStruct((8, D), f32),
        ],
        compiler_params=pltpu.CompilerParams(vmem_limit_bytes=VMEM_LIMIT),
        cost_estimate=cost(46, 30),
        name="attn_backward",
    )(lengths, qkv, qkv, qkv, d_ctx, ctx, lse, rel, row)


FF = 2048
FT = 256
RC = 512
MT = 512


def rms_scale(x):
    return lax.rsqrt(jnp.sum(x * x, axis=1, keepdims=True) * (1.0 / D) + epsilon)


def post_kernel(len_ref, shift_ref, ctx_ref, w_ref, hidden_ref, vec_ref, *refs):
    pieces, (att_ref, low_ref, low_t_ref, do_ref, do_t_ref) = refs[:-5], refs[-5:]
    s = pl.program_id(0)
    for i, piece in enumerate(pieces):
        @pl.when(shift_ref[s] == i)
        def _():
            do_ref[...] = piece[...]

    live = 2 * lax.broadcasted_iota(jnp.int32, (TOK, D), 0) < len_ref[s]
    d_out = jnp.where(live, do_ref[...].astype(f32), 0.0).astype(bf16)
    do_ref[...] = d_out
    do_t_ref[...] = d_out.T
    att = hidden_ref[...] + nn(ctx_ref[...], out_weights(w_ref))
    att_ref[...] = att
    low = (att * rms_scale(att) * vec_ref[6:7, :]).astype(bf16)
    low_ref[...] = low
    low_t_ref[...] = low.T


def rows_spec(width=D):
    return pl.BlockSpec((TOK, width), lambda s, *n: (s, 0))


def whole(*shape):
    return pl.BlockSpec(shape, lambda s, *n: (0,) * len(shape))


def out_block(shards):
    deep = D // shards
    return pl.BlockSpec((shards, 3 * deep, FT), lambda s, *n: (0, 4, 0))


def out_weights(ref):
    deep = ref.shape[1] // 3
    return jnp.concatenate([ref[:, i * deep : (i + 1) * deep, :].reshape(D, FT) for i in range(3)], axis=1)


def post_attention(lengths, shifts, ctx, pack, hidden, vecs, pieces, shards):
    rows = ctx.shape[0]
    cols_spec = pl.BlockSpec((D, TOK), lambda s, *n: (0, s))
    return pl.pallas_call(
        post_kernel,
        grid_spec=pltpu.PrefetchScalarGridSpec(
            num_scalar_prefetch=2,
            grid=(rows // TOK,),
            in_specs=[rows_spec(), out_block(shards), rows_spec(), whole(8, D)] + [whole(TOK, D)] * len(pieces),
            out_specs=[rows_spec(), rows_spec(), cols_spec, rows_spec(), cols_spec],
        ),
        out_shape=[
            jax.ShapeDtypeStruct((rows, D), f32),
            jax.ShapeDtypeStruct((rows, D), bf16),
            jax.ShapeDtypeStruct((D, rows), bf16),
            jax.ShapeDtypeStruct((rows, D), bf16),
            jax.ShapeDtypeStruct((D, rows), bf16),
        ],
        compiler_params=pltpu.CompilerParams(vmem_limit_bytes=VMEM_LIMIT),
        cost_estimate=cost(10, 30),
        name="post_attention",
    )(lengths, shifts, ctx, pack, hidden, vecs, *pieces)


def gelu_parts(v):
    c = 0.7978845608
    v2 = v * v
    t = jnp.tanh(v * (c + (c * 0.044715) * v2))
    half = 0.5 + 0.5 * t
    gelu = v * half
    slope = half + (0.5 * v) * (1.0 - t * t) * (c + (3.0 * c * 0.044715) * v2)
    return gelu, slope


def ffn_steps(x_any, d_any, xt_any, dt_any, wgu_ref, wo_ref, grad_ref, y_any, dx_any,
              x_ref, d_ref, xt_ref, dt_ref, y_ref, dx_ref, a_ref, dg_ref, du_ref, gu_ref, go_ref, in_sem, out_sem, sems,
              low_ref=None):
    f = pl.program_id(0)
    steps = FF // 2 // FT
    rows_total = x_ref.shape[0]
    chunks = rows_total // RC
    shards, part = gu_ref.shape[1], gu_ref.shape[2]
    owners, deep = go_ref.shape[1], go_ref.shape[2]
    base = steps * part

    def copies(slot, step):
        return (
            pltpu.make_async_copy(
                gu_ref.at[slot], grad_ref.at[:, pl.ds(step * part, part), :], sems.at[0, slot]),
            pltpu.make_async_copy(
                go_ref.at[slot], grad_ref.at[pl.ds(step * owners, owners), pl.ds(base, deep), :], sems.at[1, slot]),
        )

    def row_loads(i):
        rows = pl.ds(i * RC, RC)
        return (
            pltpu.make_async_copy(x_any.at[rows], x_ref.at[rows], in_sem.at[0, i]),
            pltpu.make_async_copy(d_any.at[rows], d_ref.at[rows], in_sem.at[1, i]),
        )

    def turned_loads():
        return (
            pltpu.make_async_copy(xt_any, xt_ref, in_sem.at[2, 0]),
            pltpu.make_async_copy(dt_any, dt_ref, in_sem.at[2, 1]),
        )

    def row_stores(i):
        rows = pl.ds(i * RC, RC)
        return (
            pltpu.make_async_copy(low_ref.at[0, rows], y_any.at[rows], out_sem.at[0, i]),
            pltpu.make_async_copy(low_ref.at[1, rows], dx_any.at[rows], out_sem.at[1, i]),
        )

    d_rows = part // 2
    third = deep // 3

    def rows_pass(first):
        wg = wgu_ref[:, 0:d_rows, :].reshape(D, FT)
        wu = wgu_ref[:, d_rows:part, :].reshape(D, FT)
        wo = jnp.concatenate(
            [wo_ref[:, i * third : (i + 1) * third, :].reshape(FT, FT) for i in range(3)], axis=1)
        for i in range(chunks):
            rows = pl.ds(i * RC, RC)
            if first:
                for copy in row_loads(i):
                    copy.wait()
            x, d = x_ref[rows, :], d_ref[rows, :]
            gelu, slope = gelu_parts(nn(x, wg))
            up = nn(x, wu)
            da = nt(d, wo)
            act = (gelu * up).astype(bf16)
            dg = (da * up * slope).astype(bf16)
            du = (da * gelu).astype(bf16)
            a_ref[rows, :] = act
            dg_ref[rows, :] = dg
            du_ref[rows, :] = du
            y = nn(act, wo)
            dx = nt(dg, wg) + nt(du, wu)
            y_ref[rows, :] = y if first else y_ref[rows, :] + y
            dx_ref[rows, :] = dx if first else dx_ref[rows, :] + dx

    @pl.when(f == 0)
    def _():
        for i in range(chunks):
            for copy in row_loads(i):
                copy.start()
        for copy in turned_loads():
            copy.start()
        rows_pass(True)

    @pl.when(f > 0)
    def _():
        rows_pass(False)

    if y_any is not None:

        @pl.when(f == steps - 1)
        def _():
            for i in range(chunks):
                rows = pl.ds(i * RC, RC)
                low_ref[0, rows, :] = y_ref[rows, :].astype(bf16)
                low_ref[1, rows, :] = dx_ref[rows, :].astype(bf16)
                for copy in row_stores(i):
                    copy.start()

    slot = lax.rem(f, 2)

    @pl.when(f == 0)
    def _():
        for copy in turned_loads():
            copy.wait()

    @pl.when(f >= 2)
    def _():
        for copy in copies(slot, f - 2):
            copy.wait()

    gu_ref[slot, :, 0:d_rows, :] = nn(xt_ref[...], dg_ref[...]).astype(bf16).reshape(shards, d_rows, FT)
    gu_ref[slot, :, d_rows:part, :] = nn(xt_ref[...], du_ref[...]).astype(bf16).reshape(shards, d_rows, FT)
    go = nn(dt_ref[...], a_ref[...]).T.astype(bf16)
    for i in range(3):
        go_ref[slot, :, i * third : (i + 1) * third, :] = go[:, i * FT : (i + 1) * FT].reshape(owners, third, FT)
    for copy in copies(slot, f):
        copy.start()

    @pl.when(f == steps - 1)
    def _():
        for copy in copies(1 - slot, f - 1) + copies(slot, f):
            copy.wait()
        if y_any is not None:
            for i in range(chunks):
                for copy in row_stores(i):
                    copy.wait()


def first_kernel(x, d, xt, dt, wgu, wo, grad, y, dx, *scratch):
    ffn_steps(x, d, xt, dt, wgu, wo, grad, y, dx, *scratch)


def second_kernel(len_ref, x, d, xt, dt, wgu, wo, att_ref, y1_ref, dx1_ref, do_ref, ctx_ref, w_ref, vec_ref,
                  grad, out_ref, datt_ref, dctx_ref, gg_ref, acc_ref, flat_ref, join_ref, join_sem, *scratch):
    f = pl.program_id(0)
    steps = FF // 2 // FT

    @pl.when(f == 0)
    def _():
        acc_ref[...] = jnp.zeros_like(acc_ref)
        gg_ref[...] = jnp.zeros_like(gg_ref)
        flat_ref[...] = out_weights(w_ref)

    @pl.when(f < steps)
    def _():
        ffn_steps(x, d, xt, dt, wgu, wo, grad, None, None, *scratch)

    @pl.when(f >= steps)
    def _():
        tile = f - steps
        y_ref, dx_ref = scratch[4], scratch[5]
        rows = pl.ds(pl.multiple_of(tile * MT, MT), MT)
        per = TOK // MT
        length = len_ref[tile // per]
        place_in = lax.rem(tile, per) * MT + lax.broadcasted_iota(jnp.int32, (MT, 1), 0)
        live = jnp.where(2 * place_in < length, 1.0, 0.0).astype(f32)
        att = att_ref[...]
        out_ref[...] = ((att + y1_ref[...].astype(f32) + y_ref[rows, :]) * live).astype(bf16)
        back, gain_grad = norm_back(att, dx1_ref[...].astype(f32) + dx_ref[rows, :], vec_ref[6:7, :])
        gg_ref[...] += gain_grad
        d_att = do_ref[...].astype(f32) + back
        low = d_att.astype(bf16)
        datt_ref[...] = low
        dctx_ref[...] = nt(low, flat_ref[...]).astype(bf16)
        acc_ref[...] += nn(ctx_ref[...].T, low)

    @pl.when(f == pl.num_programs(0) - 1)
    def _():
        shards, deep = join_ref.shape[0], join_ref.shape[1] // 3
        for i in range(3):
            block = acc_ref[:, i * FT : (i + 1) * FT].astype(bf16).reshape(shards, deep, FT)
            join_ref[:, i * deep : (i + 1) * deep, :] = block
        copy = pltpu.make_async_copy(join_ref, grad.at[:, pl.ds(grad.shape[1] - 3 * deep, 3 * deep), :], join_sem)
        copy.start()
        copy.wait()


def ffn_scratch(rows, shards):
    part, hs = 2 * D // shards, FF // 2 // shards
    return [
        pltpu.VMEM((rows, D), bf16),
        pltpu.VMEM((rows, D), bf16),
        pltpu.VMEM((D, rows), bf16),
        pltpu.VMEM((D, rows), bf16),
        pltpu.VMEM((rows, D), f32),
        pltpu.VMEM((rows, D), f32),
        pltpu.VMEM((rows, FT), bf16),
        pltpu.VMEM((rows, FT), bf16),
        pltpu.VMEM((rows, FT), bf16),
        pltpu.VMEM((2, shards, part, FT), bf16),
        pltpu.VMEM((2, FT // hs, 3 * hs, FT), bf16),
        pltpu.SemaphoreType.DMA((3, max(2, rows // RC))),
        pltpu.SemaphoreType.DMA((2, rows // RC)),
        pltpu.SemaphoreType.DMA((2, 2)),
    ]


def ffn_specs(tiles, shards):
    last = lambda f: jnp.minimum(f, tiles - 1)
    part, hs = 2 * D // shards, FF // 2 // shards
    return [pl.BlockSpec(memory_space=pl.ANY)] * 4 + [
        pl.BlockSpec((shards, part, FT), lambda f, *n: (0, last(f), 0)),
        pl.BlockSpec((FT // hs, 3 * hs, FT), lambda f, *n: (last(f), 2, 0)),
    ]


def grad_shape(shards, more=0):
    part, hs = 2 * D // shards, FF // 2 // shards
    return jax.ShapeDtypeStruct((shards, FF // 2 // FT * part + 3 * hs + more, FT), bf16)


def ffn_first(x, d_out, xt, dt, pack, shards):
    rows = x.shape[0]
    tiles = FF // 2 // FT
    anywhere = pl.BlockSpec(memory_space=pl.ANY)
    return pl.pallas_call(
        first_kernel,
        grid=(tiles,),
        in_specs=ffn_specs(tiles, shards),
        out_specs=[anywhere] * 3,
        out_shape=[
            grad_shape(shards),
            jax.ShapeDtypeStruct((rows, D), bf16),
            jax.ShapeDtypeStruct((rows, D), bf16),
        ],
        scratch_shapes=ffn_scratch(rows, shards) + [pltpu.VMEM((2, rows, D), bf16)],
        compiler_params=pltpu.CompilerParams(vmem_limit_bytes=VMEM_LIMIT),
        cost_estimate=cost(36, 40),
        name="ffn_first",
    )(x, d_out, xt, dt, pack, pack)


def ffn_second(lengths, x, d_out, xt, dt, pack, att, y1, dx1, ctx, pack0, vecs, shards):
    rows = x.shape[0]
    tiles = FF // 2 // FT
    tile_rows = pl.BlockSpec((MT, D), lambda f, n: (jnp.maximum(f - tiles, 0), 0))
    return pl.pallas_call(
        second_kernel,
        grid_spec=pltpu.PrefetchScalarGridSpec(
            num_scalar_prefetch=1,
            grid=(tiles + rows // MT,),
            in_specs=ffn_specs(tiles, shards) + [tile_rows] * 5 + [out_block(shards), whole(8, D)],
            out_specs=[pl.BlockSpec(memory_space=pl.ANY), tile_rows, tile_rows, tile_rows, whole(1, D)],
            scratch_shapes=[
                pltpu.VMEM((D, D), f32), pltpu.VMEM((D, D), bf16),
                pltpu.VMEM((shards, 3 * D // shards, FT), bf16), pltpu.SemaphoreType.DMA,
            ] + ffn_scratch(rows, shards),
        ),
        out_shape=[
            grad_shape(shards, 3 * D // shards),
            jax.ShapeDtypeStruct((rows, D), bf16),
            jax.ShapeDtypeStruct((rows, D), bf16),
            jax.ShapeDtypeStruct((rows, D), bf16),
            jax.ShapeDtypeStruct((1, D), f32),
        ],
        compiler_params=pltpu.CompilerParams(vmem_limit_bytes=VMEM_LIMIT),
        cost_estimate=cost(46, 60),
        name="ffn_second",
    )(lengths, x, d_out, xt, dt, pack, pack, att, y1, dx1, d_out, ctx, pack0, vecs)


def norm_back(x, grad, gain):
    r = rms_scale(x)
    n = x * r
    u = gain * grad
    mean = jnp.sum(n * u, axis=1, keepdims=True) * (1.0 / D)
    return r * (u - n * mean), jnp.sum(n * grad, axis=0, keepdims=True)


def qkv_grad_kernel(dqkv_ref, normed_t_ref, gw_ref):
    gw_ref[...] = nn(normed_t_ref[...], dqkv_ref[0]).astype(bf16)


def qkv_grad(dqkv, normed_t):
    rows = normed_t.shape[1]
    return pl.pallas_call(
        qkv_grad_kernel,
        grid=(3,),
        in_specs=[pl.BlockSpec((1, rows, D), lambda i: (i, 0, 0)), whole(D, rows)],
        out_specs=pl.BlockSpec((D, D), lambda i: (0, i)),
        out_shape=jax.ShapeDtypeStruct((D, 3 * D), bf16),
        compiler_params=pltpu.CompilerParams(vmem_limit_bytes=VMEM_LIMIT),
        cost_estimate=cost(11, 20),
        name="qkv_grad",
    )(dqkv, normed_t)


def qkv_back_kernel(dqkv_ref, w_ref, hidden_ref, datt_ref, vec_ref, dh_ref, gg_ref):
    @pl.when(pl.program_id(0) == 0)
    def _():
        gg_ref[...] = jnp.zeros_like(gg_ref)

    dn = nt(dqkv_ref[0], w_ref[:, 0:D])
    for i in range(1, 3):
        dn = dn + nt(dqkv_ref[i], w_ref[:, i * D : (i + 1) * D])
    back, gain_grad = norm_back(hidden_ref[...], dn, vec_ref[5:6, :])
    gg_ref[...] += gain_grad
    dh_ref[...] = datt_ref[...].astype(f32) + back


def qkv_backward(dqkv, attn_w, hidden, d_att, vecs):
    rows = hidden.shape[0]
    tile = pl.BlockSpec((TOK, D), lambda s: (s, 0))
    return pl.pallas_call(
        qkv_back_kernel,
        grid=(rows // TOK,),
        in_specs=[
            pl.BlockSpec((3, TOK, D), lambda s: (0, s, 0)),
            pl.BlockSpec((D, 3 * D), lambda s: (0, 0)),
            tile, tile, whole(8, D),
        ],
        out_specs=[tile, whole(1, D)],
        out_shape=[jax.ShapeDtypeStruct((rows, D), f32), jax.ShapeDtypeStruct((1, D), f32)],
        compiler_params=pltpu.CompilerParams(vmem_limit_bytes=VMEM_LIMIT),
        cost_estimate=cost(14, 40),
        name="qkv_backward",
    )(dqkv, attn_w, hidden, d_att, vecs)


MESH = pl.DeviceIdType.MESH


def greet(peers):
    barrier = pltpu.get_barrier_semaphore()
    for peer in peers:
        pl.semaphore_signal(barrier, inc=1, device_id=peer, device_id_type=MESH)
    pl.semaphore_wait(barrier, len(peers))


def pack_half(out_ref, ffn_in_ref, ffn_out_ref, h, shards):
    hs = FF // 2 // shards
    owners = FT // hs
    deep = ffn_in_ref.shape[0]
    row = 0
    for f in range(FF // 2 // FT):
        for g in range(2):
            starts = [g * FF + (f * owners + o) * 2 * hs + h * hs for o in range(owners)]
            out_ref[row : row + deep, :] = jnp.concatenate([ffn_in_ref[:, a : a + hs] for a in starts], axis=1)
            row += deep
    for i in range(3):
        out_ref[row : row + hs, :] = ffn_out_ref[h * hs : (h + 1) * hs, i * FT : (i + 1) * FT]
        row += hs
    return row


def prepare_kernel(replicas, shards, length_ref, target_ref, embed_ref, conv_ref, score_ref, gain1_ref, gain2_ref, rel_ref,
                   ids_ref, attn_out_ref, ffn_in_ref, ffn_out_ref,
                   table_ref, vec_ref, table_rel_ref, slots_ref, column_ref, pack0_ref, pack1_ref,
                   own_ref, wide_ref, turn_ref, nat_ref, wanted_ref, send_sem, recv_sem):
    rep, me = lax.axis_index("rep"), lax.axis_index("shard")
    deep = embed_ref.shape[1]
    seqs = ids_ref.shape[0]
    twin = me + 1 - 2 * lax.rem(me, 2)
    far = [lax.rem(me + 2 * i, shards) for i in range(1, shards // 2)]
    others = [lax.rem(rep + i, replicas) for i in range(1, replicas)]
    greet([(rep, twin)] + [(rep, p) for p in far] + [(p, me) for p in others])

    def send(i, src, dst, device):
        copy = pltpu.make_async_remote_copy(
            src_ref=src, dst_ref=dst, send_sem=send_sem.at[i], recv_sem=recv_sem.at[i],
            device_id=device, device_id_type=MESH)
        copy.start()
        return copy

    wide_ref[...] = jnp.zeros_like(wide_ref)
    wide_ref[0:VOCAB, 0:deep] = embed_ref[...].astype(f32)
    wide_ref[VOCAB : VOCAB + 4, 0:deep] = conv_ref[...].astype(f32)
    for i, ref in enumerate((score_ref, gain1_ref, gain2_ref)):
        wide_ref[VOCAB + 4 + i : VOCAB + 5 + i, 0:deep] = ref[...].astype(f32).reshape(1, deep)
    rel_rows, heads = rel_ref.shape
    wide_ref[VOCAB + 7 : VOCAB + 7 + rel_rows, 0:heads] = rel_ref[...].astype(f32)
    own_ref[...] = wide_ref[...].T[0:deep].astype(bf16)
    near = [send(0, own_ref, table_ref.at[me], (rep, twin))]
    direct = [send(1 + i, own_ref, table_ref.at[me], (rep, p)) for i, p in enumerate(far)]
    lanes = lax.broadcasted_iota(jnp.int32, (8, 128), 1)
    wanted = jnp.zeros((8, 128), jnp.int32)
    for k in range(seqs):
        slot = target_ref[k] % seqs
        wanted = wanted + jnp.where(lanes == target_ref[k] // seqs // shards, slot + 1, 0)
    wanted_ref[...] = wanted
    base = shards
    asks = [send(base + i, wanted_ref, slots_ref.at[rep], (p, me)) for i, p in enumerate(others)]
    table_ref[me] = own_ref[...]
    slots_ref[rep] = wanted_ref[...]
    row = pack_half(pack0_ref, ffn_in_ref, ffn_out_ref, 0, shards)
    for i in range(3):
        pack0_ref[row : row + deep, :] = attn_out_ref[:, i * FT : (i + 1) * FT]
        row += deep
    pack_half(pack1_ref, ffn_in_ref, ffn_out_ref, 1, shards)
    base = base + replicas - 1
    for i, copy in enumerate(direct):
        copy.wait()
        source = lax.rem(me - 2 * (i + 1) + shards, shards)
        near.append(send(base + i, table_ref.at[source], table_ref.at[source], (rep, twin)))
    turn_ref[...] = jnp.full(turn_ref.shape, -1.0, f32)
    place = lax.broadcasted_iota(jnp.int32, (1, MAXLEN), 1)
    for s in range(seqs):
        turn_ref[s : s + 1, 0:MAXLEN] = jnp.where(place < length_ref[s], ids_ref[s : s + 1, :], -1).astype(f32)
    nat_ref[...] = turn_ref[...].T
    for r in range(R):
        rows = nat_ref[pl.ds(r, QN, stride=R), :]
        for s in range(seqs):
            column_ref[s, r * QN : (r + 1) * QN, :] = jnp.broadcast_to(rows[:, s : s + 1], (QN, 128))
    for copy in near + asks:
        copy.wait()
    last = table_ref[:, :, SMALL - 128 :].astype(f32).reshape(D, 128).T
    first = VOCAB - (SMALL - 128)
    vec_ref[...] = last[first : first + 8]
    table_rel_ref[...] = jnp.zeros_like(table_rel_ref)
    for s in range(shards):
        block = last[first + 7 : first + 7 + rel_rows, s * deep : s * deep + heads]
        table_rel_ref[s * rel_rows : (s + 1) * rel_rows, 0:heads] = block


def prepare(lengths, target, embed, conv_w, score_w, gain_attn, gain_ffn, rel_table, ids, attn_out, ffn_in, ffn_out,
            replicas, shards):
    deep = embed.shape[1]
    seqs = ids.shape[0]
    part, hs = 2 * D // shards, FF // 2 // shards
    rows = FF // 2 // FT * part + 3 * hs
    sems = shards + replicas - 1 + shards // 2 - 1
    vmem = pl.BlockSpec(memory_space=pltpu.VMEM)
    smem = pl.BlockSpec(memory_space=pltpu.SMEM)
    return pl.pallas_call(
        lambda *refs: prepare_kernel(replicas, shards, *refs),
        out_shape=[
            jax.ShapeDtypeStruct((shards, deep, SMALL), bf16),
            jax.ShapeDtypeStruct((8, D), f32),
            jax.ShapeDtypeStruct((BUCKETS, 128), f32),
            jax.ShapeDtypeStruct((replicas, 8, 128), jnp.int32),
            jax.ShapeDtypeStruct((seqs, P_ROWS, 128), f32),
            jax.ShapeDtypeStruct((rows + 3 * deep, FT), bf16),
            jax.ShapeDtypeStruct((rows, FT), bf16),
        ],
        in_specs=[smem] * 2 + [vmem] * 10,
        out_specs=[vmem] * 7,
        scratch_shapes=[
            pltpu.VMEM((deep, SMALL), bf16),
            pltpu.VMEM((SMALL, 128), f32),
            pltpu.VMEM((128, 1152), f32),
            pltpu.VMEM((1152, 128), f32),
            pltpu.VMEM((8, 128), jnp.int32),
            pltpu.SemaphoreType.DMA((sems,)),
            pltpu.SemaphoreType.DMA((sems,)),
        ],
        compiler_params=pltpu.CompilerParams(collective_id=1, has_side_effects=True, vmem_limit_bytes=VMEM_LIMIT),
        cost_estimate=cost(12, 8),
        name="prepare",
    )(lengths, target, embed, conv_w, score_w, gain_attn, gain_ffn, rel_table, ids, attn_out, ffn_in, ffn_out)


def pick_kernel(order_ref, in_ref, *out_refs):
    for i, ref in enumerate(out_refs):
        @pl.when(pl.program_id(0) == i)
        def _():
            ref[...] = in_ref[0]


def pick(order, rows):
    count = order.shape[0]
    block = (rows.shape[1], rows.shape[2])
    return pl.pallas_call(
        pick_kernel,
        grid_spec=pltpu.PrefetchScalarGridSpec(
            num_scalar_prefetch=1,
            grid=(count,),
            in_specs=[pl.BlockSpec((1,) + block, lambda i, order: (order[i], 0, 0))],
            out_specs=[pl.BlockSpec(block, lambda i, order: (0, 0))] * count,
        ),
        out_shape=[jax.ShapeDtypeStruct(block, rows.dtype)] * count,
        compiler_params=pltpu.CompilerParams(vmem_limit_bytes=VMEM_LIMIT),
        cost_estimate=cost(4, 6),
        name="pick",
    )(order, rows)


def finish_kernel(replicas, shards, piece_ref, small_ref, in_ref, embed_ref, conv_ref, rest_ref,
                  twin_ref, both_ref, far_ref, held_ref, other_ref, part_ref, part2_ref, last_ref,
                  twin_send, twin_recv, far_send, far_recv, send_sem, recv_sem, send2_sem, recv2_sem):
    rep, me = lax.axis_index("rep"), lax.axis_index("shard")
    half = piece_ref.shape[1]
    chips = shards // 2
    core = lax.rem(me, 2)
    twin = me + 1 - 2 * core
    bits = [1 << b for b in range(replicas.bit_length() - 1)]
    orders = (bits, bits[::-1])
    far = [lax.rem(me + 2 * i, shards) for i in range(1, chips)]
    partners = {}
    for bit in bits:
        down = lax.rem(rep // bit, 2)
        partners[bit] = (rep + bit - 2 * bit * down, me)
    greet([(rep, twin)] + [(rep, p) for p in far] + [partners[bit] for bit in bits])

    def send(src, dst, sems, i, device):
        copy = pltpu.make_async_remote_copy(
            src_ref=src, dst_ref=dst, send_sem=sems[0].at[i], recv_sem=sems[1].at[i],
            device_id=device, device_id_type=MESH)
        copy.start()
        return copy

    near = [
        send(small_ref.at[2 * z + 1 - core], twin_ref.at[z], (twin_send, twin_recv), z, (rep, twin))
        for z in range(chips)
    ]

    def exchange(t, mine, theirs, sems):
        return [send(mine.at[t, h], theirs.at[t, h], sems, (t, h), partners[orders[h][t]]) for h in range(2)]

    held_ref[0] = piece_ref[...]
    large = exchange(0, held_ref, other_ref, (send_sem, recv_sem))
    for z, copy in enumerate(near):
        copy.wait()
        both_ref[z] = (small_ref[2 * z + core].astype(f32) + twin_ref[z].astype(f32)).astype(bf16)
    away = [send(both_ref.at[p // 2], far_ref.at[i], (far_send, far_recv), i, (rep, p)) for i, p in enumerate(far)]
    last_ref[...] = jnp.zeros_like(last_ref)
    total = both_ref[me // 2].astype(f32)
    for i, copy in enumerate(away):
        copy.wait()
        total = total + far_ref[i].astype(f32)
    part_ref[0] = total.astype(bf16)
    little = exchange(0, part_ref, part2_ref, (send2_sem, recv2_sem))
    for t in range(len(bits)):
        final = t == len(bits) - 1
        for h, copy in enumerate(large):
            copy.wait()
            total = held_ref[t, h].astype(f32) + other_ref[t, h].astype(f32)
            if final:
                in_ref[h * half : (h + 1) * half, :] = total
            else:
                held_ref[t + 1, h] = total.astype(bf16)
        if not final:
            large = exchange(t + 1, held_ref, other_ref, (send_sem, recv_sem))
        for h, copy in enumerate(little):
            copy.wait()
            total = part_ref[t, h].astype(f32) + part2_ref[t, h].astype(f32)
            if final:
                last_ref[h * half : (h + 1) * half, :] = total
            else:
                part_ref[t + 1, h] = total.astype(bf16)
        if not final:
            little = exchange(t + 1, part_ref, part2_ref, (send2_sem, recv2_sem))
    turned = last_ref[...].T
    deep = embed_ref.shape[1]
    embed_ref[...] = turned[0:VOCAB, 0:deep]
    conv_ref[...] = turned[VROWS : VROWS + 4, 0:deep]
    rest_ref[...] = turned[VROWS : VROWS + 16, 0:deep]


def finish(piece, small, replicas, shards):
    rows, wide = piece.shape
    half = rows // 2
    chips = shards // 2
    steps = replicas.bit_length() - 1
    vmem = pl.BlockSpec(memory_space=pltpu.VMEM)
    sems = lambda *shape: [pltpu.SemaphoreType.DMA(shape), pltpu.SemaphoreType.DMA(shape)]
    return pl.pallas_call(
        lambda *refs: finish_kernel(replicas, shards, *refs),
        out_shape=[
            jax.ShapeDtypeStruct((rows, wide), f32),
            jax.ShapeDtypeStruct((VOCAB, rows), f32),
            jax.ShapeDtypeStruct((4, rows), f32),
            jax.ShapeDtypeStruct((16, rows), f32),
        ],
        in_specs=[vmem] * 2,
        out_specs=[vmem] * 4,
        scratch_shapes=[
            pltpu.VMEM((chips, 2, half, SMALL), bf16),
            pltpu.VMEM((chips, 2, half, SMALL), bf16),
            pltpu.VMEM((chips - 1, 2, half, SMALL), bf16),
            pltpu.VMEM((steps, 2, half, wide), bf16),
            pltpu.VMEM((steps, 2, half, wide), bf16),
            pltpu.VMEM((steps, 2, half, SMALL), bf16),
            pltpu.VMEM((steps, 2, half, SMALL), bf16),
            pltpu.VMEM((128, SMALL), f32),
        ] + sems(chips) + sems(chips - 1) + sems(steps, 2) + sems(steps, 2),
        compiler_params=pltpu.CompilerParams(
            collective_id=2, has_side_effects=True, vmem_limit_bytes=VMEM_LIMIT),
        cost_estimate=cost(20, 4),
        name="finish_sums",
    )(piece.reshape(2, half, wide), small.reshape(shards, 2, half, SMALL))


def deliver_kernel(in_ref, embed_ref, conv_ref, rest_ref, in_out, embed_out, conv_out, score_out, gain1_out, gain2_out, rel_out):
    in_out[...] = in_ref[...]
    embed_out[...] = embed_ref[...]
    conv_out[...] = conv_ref[...]
    for i, ref in enumerate((score_out, gain1_out, gain2_out)):
        ref[...] = rest_ref[4 + i : 5 + i, :].reshape(ref.shape)
    rel_out[...] = rest_ref[7 : 7 + rel_out.shape[0], 0 : rel_out.shape[1]]


def deliver(parts, rel_rows):
    deep = parts[0].shape[0]
    vmem = pl.BlockSpec(memory_space=pltpu.VMEM)
    line = jax.ShapeDtypeStruct((deep,), f32)
    return pl.pallas_call(
        deliver_kernel,
        out_shape=[jax.ShapeDtypeStruct(x.shape, f32) for x in parts[:3]]
        + [line] * 3 + [jax.ShapeDtypeStruct((rel_rows, HEADS), f32)],
        in_specs=[vmem] * 4,
        out_specs=[vmem] * 7,
        compiler_params=pltpu.CompilerParams(vmem_limit_bytes=VMEM_LIMIT),
        cost_estimate=cost(2, 2),
        name="deliver",
    )(*parts)


def unpack_kernel(shards, first_ref, second_ref, other_ref, in_ref, out_ref, attn_ref):
    hs = FF // 2 // shards
    deep = in_ref.shape[0]
    owners = FT // hs
    for h in range(2):
        def load(start, count):
            rows = slice(start, start + count)
            if h == 0:
                return first_ref[rows, :].astype(f32)
            return second_ref[rows, :].astype(f32) + other_ref[rows, :].astype(f32)

        row = 0
        for f in range(FF // 2 // FT):
            for g in range(2):
                x = load(row, deep)
                for o in range(owners):
                    start = g * FF + (f * owners + o) * 2 * hs + h * hs
                    in_ref[:, start : start + hs] = x[:, o * hs : (o + 1) * hs]
                row += deep
        for i in range(3):
            out_ref[h * hs : (h + 1) * hs, i * FT : (i + 1) * FT] = load(row, hs)
            row += hs
        if h == 1:
            for i in range(3):
                attn_ref[:, i * FT : (i + 1) * FT] = load(row + i * deep, deep)


def unpack(first, second, other, shards):
    vmem = pl.BlockSpec(memory_space=pltpu.VMEM)
    return pl.pallas_call(
        lambda *refs: unpack_kernel(shards, *refs),
        out_shape=[
            jax.ShapeDtypeStruct((D // shards, 2 * FF), f32),
            jax.ShapeDtypeStruct((FF // shards, D), f32),
            jax.ShapeDtypeStruct((D // shards, D), f32),
        ],
        in_specs=[vmem] * 3,
        out_specs=[vmem] * 3,
        compiler_params=pltpu.CompilerParams(vmem_limit_bytes=VMEM_LIMIT),
        cost_estimate=cost(3, 5),
        name="unpack",
    )(first, second, other)


def send_cotangent(slots, cotangent):
    replicas = lax.axis_size("rep")
    places = jnp.arange(replicas)
    rep = lax.axis_index("rep")
    asked = jnp.where(places[None, :] == rep, slots, 0).sum(axis=1) - 1
    turned = (places[None, :] == (rep + places[:, None]) % replicas) * asked[None, :]
    pieces = list(pick(jnp.maximum(turned.sum(axis=1), 0), cotangent))
    for shift in range(1, replicas):
        pieces[shift] = lax.ppermute(pieces[shift], "rep", [(r, (r + shift) % replicas) for r in range(replicas)])
    return pieces


def swap(x, bit):
    replicas = lax.axis_size("rep")
    return lax.ppermute(x, "rep", [(r, r ^ bit) for r in range(replicas)])


def add_low(a, b):
    return (a.astype(f32) + b.astype(f32)).astype(bf16)


def scatter_sum(grad):
    return lax.psum_scatter(grad, "shard", scatter_dimension=0, tiled=True)


def body(
    byte_ids, lengths, target, rel_bucket, cotangent, embed, conv_w, score_w, gain_attn,
    attn_in, attn_out, gain_ffn, ffn_in, ffn_out, rel_table,
):
    seqs = byte_ids.shape[0]
    replicas, shards = lax.axis_size("rep"), lax.axis_size("shard")
    attn_w = lax.all_gather(attn_in, "shard", axis=0, tiled=True)
    table, vecs, rel, slots, ids_col, pack0, pack1 = prepare(
        lengths, target, embed, conv_w, score_w, gain_attn, gain_ffn, rel_table, byte_ids,
        attn_out, ffn_in, ffn_out, replicas, shards,
    )
    packs = [lax.all_gather(pack, "shard", axis=0) for pack in (pack0, pack1)]
    rows = bucket_rows(rel_bucket)

    hidden, normed, normed_t, convolved, weights = gbst_forward(lengths, ids_col, table, vecs)
    qkv = jnp.dot(normed, attn_w, preferred_element_type=f32).astype(bf16)
    qkv, slots = lax.optimization_barrier((qkv, slots))
    pieces = send_cotangent(slots[:, 0, :replicas], cotangent)
    ctx, lse = attn_forward(lengths, qkv, rel, rows)
    ctx, pieces = lax.optimization_barrier((ctx, pieces))
    shifts = (lax.axis_index("rep") - target // seqs // shards) % replicas
    attended, low, low_t, d_out, d_out_t = post_attention(
        lengths, shifts, ctx, packs[0], hidden, vecs, pieces, shards
    )
    g_half1, y1, dx1 = ffn_first(low, d_out, low_t, d_out_t, packs[0], shards)
    g_half2, out, d_att, d_ctx, g_gain_ffn = ffn_second(
        lengths, low, d_out, low_t, d_out_t, packs[1], attended, y1, dx1, ctx, packs[0], vecs, shards
    )
    one, two = [scatter_sum(g.reshape(-1, FT)) for g in (g_half1, g_half2)]
    bits = [1 << b for b in range(replicas.bit_length() - 1)]
    d_ctx, one = lax.optimization_barrier((d_ctx, one))
    other = swap(one, bits[0])
    dqkv, g_rel = attn_backward(lengths, qkv, d_ctx, ctx, lse, rel, rows, shards)
    dqkv, other = lax.optimization_barrier((dqkv, other))
    one = add_low(one, other)
    g_attn = qkv_grad(dqkv, normed_t)
    g_attn, two = lax.optimization_barrier((g_attn, two))
    p_attn = scatter_sum(g_attn)
    others = swap(one, bits[1]), swap(two, bits[0])
    d_hidden, g_gain_attn = qkv_backward(dqkv, attn_w, hidden, d_att, vecs)
    d_hidden, others = lax.optimization_barrier((d_hidden, others))
    one, two = add_low(one, others[0]), add_low(two, others[1])
    for bit in bits[2:]:
        one, two = add_low(one, swap(one, bit)), add_low(two, swap(two, bit))
    d_hidden, one, two = lax.optimization_barrier((d_hidden, one, two))
    other = swap(two, bits[1])
    ids = jnp.where(jnp.arange(MAXLEN)[None, :] < lengths[:, None], byte_ids, -1)
    input_grad, small = gbst_backward(
        lengths, ids_col, ids.reshape(seqs, 1, MAXLEN), table, vecs, d_hidden, convolved, weights,
        g_gain_attn, g_gain_ffn, g_rel,
    )
    small, other = lax.optimization_barrier((small, other))
    parts = finish(p_attn, small, replicas, shards)
    s_ffn_in, s_ffn_out, s_attn_out = unpack(one, two, other, shards)
    s_attn_in, s_embed, s_conv, s_score, s_gain_attn, s_gain_ffn, s_rel = deliver(parts, rel_table.shape[0])
    return (
        out.reshape(seqs, TOK, D), input_grad, s_embed, s_conv, s_score, s_gain_attn, s_attn_in, s_attn_out,
        s_gain_ffn, s_ffn_in, s_ffn_out, s_rel,
    )


def solution(mesh):
    in_specs = (
        P(("rep", "shard"), None), P(("rep", "shard")), P(("rep", "shard")), P(),
        P(("rep", "shard"), None, None), P(None, "shard"), P(None, "shard"), P("shard"), P("shard"),
        P("shard", None), P("shard", None), P("shard"), P("shard", None), P("shard", None), P("shard", None),
    )
    out_specs = (
        P(("rep", "shard"), None, None), P(("rep", "shard"), None, None), P(None, "shard"), P(None, "shard"),
        P("shard"), P("shard"), P("shard", None), P("shard", None), P("shard"), P("shard", None),
        P("shard", None), P("shard", None),
    )
    return jax.shard_map(body, mesh=mesh, in_specs=in_specs, out_specs=out_specs, check_vma=False)
```

```python
import jax
import jax.numpy as jnp
from jax import lax
from jax.experimental import pallas as pl
from jax.experimental.pallas import tpu as pltpu
from jax.sharding import PartitionSpec as P

D = 768
VOCAB = 259
VROWS = 272
VMEM_LIMIT = 60 << 20
SMALL = 384
MAXLEN = 1024
TOK = 512
LANES = 128
QN = 88
R = 12
P_ROWS = QN * R
T_ROWS = 528
LT = D // LANES
epsilon = 1e-06
f32 = jnp.float32
bf16 = jnp.bfloat16


def cost(us, mib):
    return pl.CostEstimate(flops=int(us * 1e9), bytes_accessed=mib << 20, transcendentals=0)


def lane_iota(rows):
    return lax.broadcasted_iota(jnp.int32, (rows, LANES), 1)


def group_matrix(b):
    row = lax.broadcasted_iota(jnp.int32, (LANES, LANES), 0)
    col = lax.broadcasted_iota(jnp.int32, (LANES, LANES), 1)
    return jnp.where((row // b == col // b) & (row < R) & (col < R), 1.0, 0.0).astype(f32)


def exact_dot(a, b):
    return jnp.dot(a, b, precision=lax.Precision.HIGHEST, preferred_element_type=f32)


def place(columns, rows):
    lanes = lane_iota(rows)
    out = jnp.zeros((rows, LANES), f32)
    for r, column in enumerate(columns):
        out = jnp.where(lanes == r, column, out)
    return out


def gbst_masks(length):
    q = lax.broadcasted_iota(jnp.int32, (QN, LANES), 0)
    r = lax.broadcasted_iota(jnp.int32, (QN, LANES), 1)
    mask = jnp.where((q * R + r < length) & (r < R), 1.0, 0.0).astype(f32)
    inverse = [1.0 / jnp.maximum(exact_dot(mask, group_matrix(b)), 1.0) for b in (2, 3, 4)]
    pair = exact_dot(mask, group_matrix(2))
    alpha = mask / jnp.maximum(pair, 1.0)
    return mask, inverse, alpha


def gbst_weights(s1, inverse):
    sizes = [s1] + [exact_dot(s1, group_matrix(b)) * inv for b, inv in zip((2, 3, 4), inverse)]
    top = jnp.maximum(jnp.maximum(sizes[0], sizes[1]), jnp.maximum(sizes[2], sizes[3]))
    parts = [jnp.exp(s - top) for s in sizes]
    total = parts[0] + parts[1] + parts[2] + parts[3]
    return [p / total for p in parts]


def gbst_coefs(weights, inverse, alpha):
    a1 = weights[0] * alpha
    a2 = weights[1] * alpha * inverse[0]
    a3 = weights[2] * alpha * inverse[1]
    a4 = weights[3] * alpha * inverse[2]
    pair = group_matrix(2)
    a4s = exact_dot(a4, pair)
    own = a1 + exact_dot(a2, pair) + a4s
    return own, a3, a4s


def column(x, r):
    return jnp.broadcast_to(x[:, r : r + 1], (x.shape[0], LANES))


def hits_of(ids):
    lanes = lax.broadcasted_iota(jnp.int32, (P_ROWS, LANES), 1).astype(f32)
    return jnp.concatenate(
        [jnp.where(ids == lanes + float(i * LANES), 1.0, 0.0).astype(bf16) for i in range(SMALL // LANES)], axis=1)


def look_up(ids, table_ref):
    return lax.dot_general(
        hits_of(ids), table_ref[...].reshape(D, SMALL), (((1,), (1,)), ((), ())), preferred_element_type=f32)


def load_e(e_ref, r, lt):
    lanes = pl.ds(lt * LANES, LANES)
    if r < R:
        return e_ref[pl.ds(r * QN, QN), lanes]
    return e_ref[pl.ds((r - R) * QN + 1, QN), lanes]


def gbst_fwd_kernel(len_ref, ids_ref, table_ref, vec_ref, hidden_ref, normed_ref, turned_ref, c_ref, w_ref, elow_ref, kc_ref, e_ref, hid_ref, s_ref):
    k_ref = kc_ref.at[0]
    length = len_ref[pl.program_id(0)]
    rows_e = look_up(ids_ref[0], table_ref)
    e_ref[pl.ds(0, P_ROWS), :] = rows_e
    elow_ref[0] = rows_e.astype(bf16)
    e_ref[pl.ds(P_ROWS, 8), :] = jnp.zeros((8, D), f32)
    for lt in range(LT):
        lanes = pl.ds(lt * LANES, LANES)
        taps = [jnp.broadcast_to(vec_ref[j : j + 1, lanes], (QN, LANES)) for j in range(4)]
        sw = jnp.broadcast_to(vec_ref[4:5, lanes], (QN, LANES))
        for r in range(R):
            c = taps[0] * load_e(e_ref, r, lt)
            for j in range(1, 4):
                c = c + taps[j] * load_e(e_ref, r + j, lt)
            c_ref[0, pl.ds(r * QN, QN), lanes] = c
            part = c * sw
            rows = pl.ds(r * QN, QN)
            s_ref[rows, :] = part if lt == 0 else s_ref[rows, :] + part
    s1 = place([jnp.sum(s_ref[pl.ds(r * QN, QN), :], axis=1, keepdims=True) for r in range(R)], QN)
    mask, inverse, alpha = gbst_masks(length)
    weights = gbst_weights(s1, inverse)
    for b, kept in enumerate(weights + inverse + [alpha]):
        w_ref[0, b] = kept
    own, a3, a4s = gbst_coefs(weights, inverse, alpha)
    n = 0
    for r in range(R):
        k_ref[r] = column(own, r)
        k_ref[R + r] = column(a3, r)
    for k in range(6):
        k_ref[2 * R + k] = column(a4s, 2 * k)
    for r in range(R):
        k_ref[2 * R + 6 + r] = column(mask, r)
    for lt in range(LT):
        lanes = pl.ds(lt * LANES, LANES)
        for half in range(2):
            c = [c_ref[0, pl.ds((half * 6 + r) * QN, QN), lanes] for r in range(6)]
            base = half * 6
            s3 = [c[0] + c[1] + c[2], c[3] + c[4] + c[5]]
            for k in range(3):
                tok = half * 3 + k
                other = tok ^ 1
                rows = pl.ds(2 * other * QN, QN)
                rows1 = pl.ds((2 * other + 1) * QN, QN)
                s2 = c_ref[0, rows, lanes] + c_ref[0, rows1, lanes]
                h = k_ref[2 * tok] * c[2 * k] + k_ref[2 * tok + 1] * c[2 * k + 1] + k_ref[2 * R + tok] * s2
                if k == 1:
                    h = h + k_ref[R + 2 * tok] * s3[0] + k_ref[R + 2 * tok + 1] * s3[1]
                else:
                    h = h + (k_ref[R + 2 * tok] + k_ref[R + 2 * tok + 1]) * s3[0 if k == 0 else 1]
                hid_ref[lt, pl.ds(tok, QN, stride=6), :] = h
    total = jnp.zeros((TOK, LANES), f32)
    for lt in range(LT):
        x = hid_ref[lt, 0:TOK, :]
        total = total + x * x
    scale = lax.rsqrt(jnp.sum(total, axis=1, keepdims=True) * (1.0 / D) + epsilon)
    for lt in range(LT):
        lanes = pl.ds(lt * LANES, LANES)
        x = hid_ref[lt, 0:TOK, :]
        hidden_ref[:, lanes] = x
        normed = (x * scale * vec_ref[5:6, lanes]).astype(bf16)
        normed_ref[:, lanes] = normed
        turned_ref[lanes, :] = normed.T


def gbst_forward(lengths, ids_col, table, vecs):
    seqs = ids_col.shape[0]
    grid_spec = pltpu.PrefetchScalarGridSpec(
        num_scalar_prefetch=1,
        grid=(seqs,),
        in_specs=[
            pl.BlockSpec((1, P_ROWS, LANES), lambda s, n: (s, 0, 0)),
            pl.BlockSpec(table.shape, lambda s, n: (0, 0, 0)),
            pl.BlockSpec((8, D), lambda s, n: (0, 0)),
        ],
        out_specs=[
            pl.BlockSpec((TOK, D), lambda s, n: (s, 0)),
            pl.BlockSpec((TOK, D), lambda s, n: (s, 0)),
            pl.BlockSpec((D, TOK), lambda s, n: (0, s)),
            pl.BlockSpec((1, P_ROWS, D), lambda s, n: (s, 0, 0)),
            pl.BlockSpec((1, 8, QN, LANES), lambda s, n: (s, 0, 0, 0)),
            pl.BlockSpec((1, P_ROWS, D), lambda s, n: (s, 0, 0)),
            pl.BlockSpec((1, 3 * R + 6, QN, LANES), lambda s, n: (s, 0, 0, 0)),
        ],
        scratch_shapes=[
            pltpu.VMEM((P_ROWS + 8, D), f32),
            pltpu.VMEM((LT, T_ROWS, LANES), f32),
            pltpu.VMEM((P_ROWS, LANES), f32),
        ],
    )
    return pl.pallas_call(
        gbst_fwd_kernel,
        grid_spec=grid_spec,
        out_shape=[
            jax.ShapeDtypeStruct((seqs * TOK, D), f32),
            jax.ShapeDtypeStruct((seqs * TOK, D), bf16),
            jax.ShapeDtypeStruct((D, seqs * TOK), bf16),
            jax.ShapeDtypeStruct((seqs, P_ROWS, D), f32),
            jax.ShapeDtypeStruct((seqs, 8, QN, LANES), f32),
            jax.ShapeDtypeStruct((seqs, P_ROWS, D), bf16),
            jax.ShapeDtypeStruct((seqs, 3 * R + 6, QN, LANES), f32),
        ],
        compiler_params=pltpu.CompilerParams(vmem_limit_bytes=VMEM_LIMIT),
        cost_estimate=cost(18, 30),
        name="gbst_forward",
    )(lengths, ids_col, table, vecs)


def gbst_bwd_kernel(row_ref, vec_ref, dh_ref, c_ref, w_ref, elow_ref, kc_ref, gain1_ref, gain2_ref, rel_ref,
                    ig_ref, small_ref, ge_ref, e_ref, dt_ref, dc_ref, s_ref, cf_ref, igs_ref):
    seq = pl.program_id(0)
    k_ref = kc_ref.at[0]

    @pl.when(seq == 0)
    def _():
        ge_ref[...] = jnp.zeros_like(ge_ref)

    e_ref[pl.ds(0, P_ROWS), :] = elow_ref[0].astype(f32)
    e_ref[pl.ds(P_ROWS, 8), :] = jnp.zeros((8, D), f32)
    for lt in range(LT):
        dt_ref[lt, 0:TOK, :] = dh_ref[:, pl.ds(lt * LANES, LANES)].astype(f32)
        dt_ref[lt, TOK:T_ROWS, :] = jnp.zeros((T_ROWS - TOK, LANES), f32)
    for lt in range(LT):
        lanes = pl.ds(lt * LANES, LANES)
        for half in range(2):
            c = [c_ref[0, pl.ds((half * 6 + r) * QN, QN), lanes] for r in range(6)]
            s3 = [c[0] + c[1] + c[2], c[3] + c[4] + c[5]]
            for k in range(3):
                tok = half * 3 + k
                other = tok ^ 1
                dh = dt_ref[lt, pl.ds(tok, QN, stride=6), :]
                s2 = c_ref[0, pl.ds(2 * other * QN, QN), lanes] + c_ref[0, pl.ds((2 * other + 1) * QN, QN), lanes]
                parts = [
                    (2 * tok, dh * c[2 * k]),
                    (2 * tok + 1, dh * c[2 * k + 1]),
                    (2 * R + tok, dh * s2),
                    (R + 2 * tok, dh * s3[0 if k < 2 else 1]),
                ]
                if k == 1:
                    parts.append((R + 2 * tok + 1, dh * s3[1]))
                for slot, part in parts:
                    s_ref[slot] = part if lt == 0 else s_ref[slot] + part

    def total(slot):
        return jnp.sum(s_ref[slot], axis=1, keepdims=True)

    d1, d3, dother = [], [], []
    for tok in range(6):
        d1 += [total(2 * tok), total(2 * tok + 1)]
        first = total(R + 2 * tok)
        d3 += [first, total(R + 2 * tok + 1) if tok % 3 == 1 else first]
        o = total(2 * R + tok)
        dother += [o, o]
    d1, d3, dother = place(d1, QN), place(d3, QN), place(dother, QN)
    weights = [w_ref[0, b] for b in range(4)]
    inverse = [w_ref[0, 4 + b] for b in range(3)]
    alpha = w_ref[0, 7]
    d2 = exact_dot(d1, group_matrix(2))
    g = [alpha * d1, alpha * d2 * inverse[0], alpha * d3 * inverse[1], alpha * (d2 + dother) * inverse[2]]
    mean = weights[0] * g[0] + weights[1] * g[1] + weights[2] * g[2] + weights[3] * g[3]
    d_size = [w * (x - mean) for w, x in zip(weights, g)]
    coef = d_size[0]
    for b, inv in zip((2, 3, 4), inverse):
        coef = coef + exact_dot(d_size[b - 1] * inv, group_matrix(b))
    for r in range(R):
        cf_ref[r] = column(coef, r)

    for lt in range(LT):
        lanes = pl.ds(lt * LANES, LANES)
        taps = [jnp.broadcast_to(vec_ref[j : j + 1, lanes], (QN, LANES)) for j in range(4)]
        sw = jnp.broadcast_to(vec_ref[4:5, lanes], (QN, LANES))
        gs = jnp.zeros((QN, LANES), f32)
        gc = [jnp.zeros((QN, LANES), f32) for _ in range(4)]
        for half in range(2):
            dh = [dt_ref[lt, pl.ds(half * 3 + k, QN, stride=6), :] for k in range(3)]
            a = R + half * 6
            t3 = [
                (k_ref[a] + k_ref[a + 1]) * dh[0] + k_ref[a + 2] * dh[1],
                k_ref[a + 3] * dh[1] + (k_ref[a + 4] + k_ref[a + 5]) * dh[2],
            ]
            for k in range(3):
                tok = half * 3 + k
                other = tok ^ 1
                dother_h = dt_ref[lt, pl.ds(other, QN, stride=6), :]
                cross = k_ref[2 * R + other] * dother_h
                for e in range(2):
                    r = 2 * tok + e
                    cf = cf_ref[r]
                    dc = k_ref[r] * dh[k] + cross + t3[(r % 6) // 3] + cf * sw
                    gs = gs + cf * c_ref[0, pl.ds(r * QN, QN), lanes]
                    dc_ref[r, pl.ds(8, QN), :] = dc
                    for j in range(4):
                        gc[j] = gc[j] + dc * load_e(e_ref, r + j, lt)
        ge_ref[VROWS + 4 : VROWS + 5, lanes] += jnp.sum(gs, axis=0, keepdims=True)
        for j in range(4):
            ge_ref[VROWS + j : VROWS + j + 1, lanes] += jnp.sum(gc[j], axis=0, keepdims=True)
        for r in range(R):
            dc_ref[r, 0:8, :] = jnp.zeros((8, LANES), f32)
        for r in range(R):
            x = taps[0] * dc_ref[r, pl.ds(8, QN), :]
            for j in range(1, 4):
                back = dc_ref[r - j, pl.ds(8, QN), :] if r >= j else dc_ref[r - j + R, pl.ds(7, QN), :]
                x = x + taps[j] * back
            igs_ref[lt, pl.ds(r, QN, stride=R), :] = x * k_ref[2 * R + 6 + r]
    for lt in range(LT):
        lanes = pl.ds(lt * LANES, LANES)
        ig_ref[0, :, lanes] = igs_ref[lt, 0:MAXLEN, :].astype(bf16)
    vocab = lax.broadcasted_iota(jnp.int32, (VROWS, MAXLEN), 0)
    row_hits = jnp.where(vocab == row_ref[0], 1.0, 0.0).astype(bf16)
    ge_ref[0:VROWS, :] += jnp.dot(row_hits, ig_ref[0], preferred_element_type=f32)

    @pl.when(seq == pl.num_programs(0) - 1)
    def _():
        ge_ref[VROWS + 5 : VROWS + 6, :] = gain1_ref[...]
        ge_ref[VROWS + 6 : VROWS + 7, :] = gain2_ref[...]
        ge_ref[VROWS + 7 : VROWS + 15, :] = rel_ref[...]
        for lt in range(LT):
            lanes = pl.ds(lt * LANES, LANES)
            small_ref[lanes, :] = ge_ref[:, lanes].T.astype(bf16)


def gbst_backward(ids_row, vecs, d_hidden, c, w, e_low, coefs, gain1, gain2, rel):
    seqs = ids_row.shape[0]
    per_seq = lambda *shape: pl.BlockSpec((1,) + shape, lambda s: (s,) + (0,) * len(shape))
    still = lambda *shape: pl.BlockSpec(shape, lambda s: (0,) * len(shape))
    return pl.pallas_call(
        gbst_bwd_kernel,
        grid=(seqs,),
        in_specs=[
            per_seq(1, MAXLEN), still(8, D), pl.BlockSpec((TOK, D), lambda s: (s, 0)), per_seq(P_ROWS, D),
            per_seq(8, QN, LANES), per_seq(P_ROWS, D), per_seq(3 * R + 6, QN, LANES),
            still(1, D), still(1, D), still(8, D),
        ],
        out_specs=[per_seq(MAXLEN, D), still(D, SMALL)],
        scratch_shapes=[
            pltpu.VMEM((SMALL, D), f32),
            pltpu.VMEM((P_ROWS + 8, D), f32),
            pltpu.VMEM((LT, T_ROWS, LANES), f32),
            pltpu.VMEM((R, QN + 8, LANES), f32),
            pltpu.VMEM((2 * R + 6, QN, LANES), f32),
            pltpu.VMEM((R, QN, LANES), f32),
            pltpu.VMEM((LT, P_ROWS, LANES), f32),
        ],
        out_shape=[
            jax.ShapeDtypeStruct((seqs, MAXLEN, D), bf16),
            jax.ShapeDtypeStruct((D, SMALL), bf16),
        ],
        compiler_params=pltpu.CompilerParams(vmem_limit_bytes=VMEM_LIMIT),
        cost_estimate=cost(26, 40),
        name="gbst_backward",
    )(ids_row, vecs, d_hidden, c, w, e_low, coefs, gain1, gain2, rel)


HEADS = 12
HD = 64
BUCKETS = 32
SPAN = 1024
HB = 4
WIDE = HB * HD
GROUPS = HEADS // HB
dead_score = -1e9


def nt(a, b):
    return lax.dot_general(a, b, (((1,), (1,)), ((), ())), preferred_element_type=f32)


def nn(a, b):
    return jnp.dot(a, b, preferred_element_type=f32)


def bucket_rows(buckets):
    def row(x):
        return jnp.concatenate([x[TOK - 1 :], x[:1], x[: TOK - 1]])

    return jnp.stack([row(buckets), row(buckets[::-1])])


def bucket_hits(row_ref, way):
    return jnp.where(lax.broadcasted_iota(jnp.int32, (BUCKETS, SPAN), 0) == row_ref[way : way + 1, :], 1.0, 0.0).astype(f32)


def spread_table(rel_ref, row_ref, z_ref, way):
    dims = (((0,), (0,)), ((), ()))
    z_ref[...] = lax.dot_general(
        rel_ref[...].astype(bf16), bucket_hits(row_ref, way).astype(bf16), dims, preferred_element_type=f32)


def build_bias(z_ref, bt_ref, group):
    for h in range(HB):
        row = jnp.broadcast_to(z_ref[pl.ds(group * HB + h, 1), :], (8, SPAN))
        z = pltpu.roll(row, 0, 1, stride=1, stride_axis=0)
        for g in range(TOK // 8):
            bt_ref[h, pl.ds(8 * g, 8), :] = (z if g == 0 else pltpu.roll(z, 8 * g, 1))[:, :TOK]


def own_lanes(h):
    return lax.broadcasted_iota(jnp.int32, (TOK, WIDE), 1) // HD == h


def head_parts(k, q, length, h):
    lanes = lax.broadcasted_iota(jnp.int32, (TOK, WIDE), 1)
    rows = lax.broadcasted_iota(jnp.int32, (TOK, WIDE), 0)
    spare = HD * (h + 1) % WIDE
    dead = jnp.where(2 * rows < length, 0.0, dead_score)
    kf = jnp.where(lanes // HD == h, k.astype(f32), jnp.where(lanes == spare, dead, 0.0)).astype(bf16)
    qf = jnp.where(lanes == spare, 1.0, q.astype(f32)).astype(bf16)
    return kf, qf


def join_heads(parts):
    out = parts[0]
    for h in range(1, HB):
        out = jnp.where(own_lanes(h), parts[h], out)
    return out.astype(bf16)


def attn_fwd_kernel(len_ref, q_ref, k_ref, v_ref, rel_ref, row_ref, ctx_ref, lse_ref, bias_ref, z_ref):
    length = len_ref[pl.program_id(1)]

    @pl.when((pl.program_id(0) == 0) & (pl.program_id(1) == 0))
    def _():
        spread_table(rel_ref, row_ref, z_ref, 0)

    @pl.when(pl.program_id(1) == 0)
    def _():
        build_bias(z_ref, bias_ref, pl.program_id(0))

    q, k, v = q_ref[...], k_ref[...], v_ref[...]

    def score(h):
        kf, qf = head_parts(k, q, length, h)
        return nt(qf, kf) + bias_ref[h]

    outs = []
    lanes = lax.broadcasted_iota(jnp.int32, (TOK, LANES), 1)
    lse = jnp.zeros((TOK, LANES), f32)
    s = score(0)
    for h in range(HB):
        later = score(h + 1) if h + 1 < HB else None
        top = jnp.max(s, axis=1, keepdims=True)
        p = jnp.exp(s - top)
        total = jnp.sum(p, axis=1, keepdims=True)
        outs.append(nn(p.astype(bf16), v) * (1.0 / total))
        lse = jnp.where(lanes == h, top + jnp.log(total), lse)
        s = later
    ctx_ref[...] = join_heads(outs)
    lse_ref[0, 0] = lse.T[0:8]


def table_specs():
    return [
        pl.BlockSpec((BUCKETS, LANES), lambda hp, s, n: (0, 0)),
        pl.BlockSpec((2, SPAN), lambda hp, s, n: (0, 0)),
    ]


def attn_forward(lengths, qkv, rel, row):
    seqs = qkv.shape[0] // TOK
    spec = lambda off: pl.BlockSpec((TOK, WIDE), lambda hp, s, n: (s, off + hp))
    return pl.pallas_call(
        attn_fwd_kernel,
        grid_spec=pltpu.PrefetchScalarGridSpec(
            num_scalar_prefetch=1,
            grid=(GROUPS, seqs),
            in_specs=[spec(0), spec(GROUPS), spec(2 * GROUPS)] + table_specs(),
            out_specs=[spec(0), pl.BlockSpec((1, 1, 8, TOK), lambda hp, s, n: (hp, s, 0, 0))],
            scratch_shapes=[pltpu.VMEM((HB, TOK, TOK), f32), pltpu.VMEM((LANES, SPAN), f32)],
        ),
        out_shape=[
            jax.ShapeDtypeStruct((seqs * TOK, D), bf16),
            jax.ShapeDtypeStruct((GROUPS, seqs, 8, TOK), f32),
        ],
        compiler_params=pltpu.CompilerParams(vmem_limit_bytes=VMEM_LIMIT),
        cost_estimate=cost(27, 20),
        name="attn_forward",
    )(lengths, qkv, qkv, qkv, rel, row)


def attn_bwd_kernel(shards, len_ref, q_ref, k_ref, v_ref, do_ref, o_ref, lse_ref, rel_ref, row_ref, dqkv_ref, gt_ref, bt_ref, g_ref, z_ref, gz_ref):
    s_id = pl.program_id(1)
    length = len_ref[s_id]

    @pl.when((pl.program_id(0) == 0) & (s_id == 0))
    def _():
        spread_table(rel_ref, row_ref, z_ref, 1)
        gz_ref[...] = jnp.zeros_like(gz_ref)

    @pl.when(s_id == 0)
    def _():
        build_bias(z_ref, bt_ref, pl.program_id(0))
        g_ref[...] = jnp.zeros_like(g_ref)

    q, k, v, do = q_ref[...], k_ref[...], v_ref[...], do_ref[...]
    kt = k.astype(f32).T.astype(bf16)
    lanes8 = lax.broadcasted_iota(jnp.int32, (8, WIDE), 1)
    rows8 = lax.broadcasted_iota(jnp.int32, (8, WIDE), 0)
    pick = jnp.where(lanes8 // HD == rows8, 1.0, 0.0).astype(bf16)
    prod = do.astype(f32) * o_ref[...].astype(f32)
    upper = prod.astype(bf16)
    delta = nt(pick, upper) + nt(pick, (prod - upper.astype(f32)).astype(bf16))
    dq, dk, dv = [], [], []

    def first(h):
        kf, qf = head_parts(k, q, length, h)
        vf = jnp.where(own_lanes(h), v.astype(f32), 0.0).astype(bf16)
        return nt(kf, qf) + bt_ref[h], nt(vf, do)

    now = first(0)
    for h in range(HB):
        later = first(h + 1) if h + 1 < HB else None
        s, d_prob = now
        p = jnp.exp(s - lse_ref[0, 0, h : h + 1, :])
        ds = p * (d_prob - delta[h : h + 1, :])
        g_ref[h] += ds
        low = ds.astype(bf16)
        dv.append(nn(p.astype(bf16), do))
        dk.append(nn(low, q))
        dq.append(nn(kt[h * HD : (h + 1) * HD], low))
        now = later
    dqkv_ref[0] = jnp.concatenate(dq, axis=0).T.astype(bf16)
    dqkv_ref[1] = join_heads(dk)
    dqkv_ref[2] = join_heads(dv)

    @pl.when(s_id == pl.num_programs(1) - 1)
    def _():
        for h in range(HB):
            total = jnp.zeros((8, SPAN), f32)
            for g in range(LANES // 8):
                tiles = [jnp.zeros((8, LANES), f32) for _ in range(SPAN // LANES)]
                for j in range(TOK // LANES):
                    x = g_ref[h, pl.ds(LANES * j + 8 * g, 8), :]
                    for t in range(TOK // LANES):
                        n = (t - j) % (SPAN // LANES)
                        tiles[n] = tiles[n] + x[:, t * LANES : (t + 1) * LANES]
                piece = jnp.concatenate(tiles, axis=1)
                total = total + (piece if g == 0 else pltpu.roll(piece, SPAN - 8 * g, 1))
            out = total[0:1]
            for s in range(1, 8):
                out = out + pltpu.roll(jnp.broadcast_to(total[s : s + 1], (8, SPAN)), SPAN - s, 1)[0:1]
            gz_ref[pl.ds(pl.program_id(0) * HB + h, 1), :] = out

    @pl.when((pl.program_id(0) == GROUPS - 1) & (s_id == pl.num_programs(1) - 1))
    def _():
        total = lax.dot_general(
            bucket_hits(row_ref, 1), gz_ref[...], (((1,), (1,)), ((), ())),
            precision=lax.Precision.HIGHEST, preferred_element_type=f32)
        gt_ref[...] = jnp.zeros_like(gt_ref)
        per = BUCKETS // shards
        for s in range(shards):
            start = s * (D // shards)
            gt_ref[0:per, start : start + HEADS] = total[s * per : (s + 1) * per, 0:HEADS]


def attn_backward(lengths, qkv, d_ctx, ctx, lse, rel, row, shards):
    seqs = qkv.shape[0] // TOK
    spec = lambda off: pl.BlockSpec((TOK, WIDE), lambda hp, s, n: (s, off + hp))
    return pl.pallas_call(
        lambda *refs: attn_bwd_kernel(shards, *refs),
        grid_spec=pltpu.PrefetchScalarGridSpec(
            num_scalar_prefetch=1,
            grid=(GROUPS, seqs),
            in_specs=[
                spec(0), spec(GROUPS), spec(2 * GROUPS), spec(0), spec(0),
                pl.BlockSpec((1, 1, 8, TOK), lambda hp, s, n: (hp, s, 0, 0)),
            ] + table_specs(),
            out_specs=[
                pl.BlockSpec((3, TOK, WIDE), lambda hp, s, n: (0, s, hp)),
                pl.BlockSpec((8, D), lambda hp, s, n: (0, 0)),
            ],
            scratch_shapes=[
                pltpu.VMEM((HB, TOK, TOK), f32), pltpu.VMEM((HB, TOK, TOK), f32),
                pltpu.VMEM((LANES, SPAN), f32), pltpu.VMEM((16, SPAN), f32),
            ],
        ),
        out_shape=[
            jax.ShapeDtypeStruct((3, seqs * TOK, D), bf16),
            jax.ShapeDtypeStruct((8, D), f32),
        ],
        compiler_params=pltpu.CompilerParams(vmem_limit_bytes=VMEM_LIMIT),
        cost_estimate=cost(46, 30),
        name="attn_backward",
    )(lengths, qkv, qkv, qkv, d_ctx, ctx, lse, rel, row)


FF = 2048
FT = 256
RC = 1024
MT = 512


def rms_scale(x):
    return lax.rsqrt(jnp.sum(x * x, axis=1, keepdims=True) * (1.0 / D) + epsilon)


def post_kernel(len_ref, shift_ref, ctx_ref, w_ref, hidden_ref, vec_ref, *refs):
    pieces, (att_ref, low_ref, low_t_ref, do_ref, do_t_ref) = refs[:-5], refs[-5:]
    s = pl.program_id(0)
    for i, piece in enumerate(pieces):
        @pl.when(shift_ref[s] == i)
        def _():
            do_ref[...] = piece[...]

    live = 2 * lax.broadcasted_iota(jnp.int32, (TOK, D), 0) < len_ref[s]
    d_out = jnp.where(live, do_ref[...].astype(f32), 0.0).astype(bf16)
    do_ref[...] = d_out
    do_t_ref[...] = d_out.T
    att = hidden_ref[...] + nn(ctx_ref[...], out_weights(w_ref))
    att_ref[...] = att
    low = (att * rms_scale(att) * vec_ref[6:7, :]).astype(bf16)
    low_ref[...] = low
    low_t_ref[...] = low.T


def rows_spec(width=D):
    return pl.BlockSpec((TOK, width), lambda s, *n: (s, 0))


def whole(*shape):
    return pl.BlockSpec(shape, lambda s, *n: (0,) * len(shape))


def out_block(shards):
    deep = D // shards
    return pl.BlockSpec((shards, 3 * deep, FT), lambda s, *n: (0, 4, 0))


def out_weights(ref):
    deep = ref.shape[1] // 3
    return jnp.concatenate([ref[:, i * deep : (i + 1) * deep, :].reshape(D, FT) for i in range(3)], axis=1)


def post_attention(lengths, shifts, ctx, pack, hidden, vecs, pieces, shards):
    rows = ctx.shape[0]
    cols_spec = pl.BlockSpec((D, TOK), lambda s, *n: (0, s))
    return pl.pallas_call(
        post_kernel,
        grid_spec=pltpu.PrefetchScalarGridSpec(
            num_scalar_prefetch=2,
            grid=(rows // TOK,),
            in_specs=[rows_spec(), out_block(shards), rows_spec(), whole(8, D)] + [whole(TOK, D)] * len(pieces),
            out_specs=[rows_spec(), rows_spec(), cols_spec, rows_spec(), cols_spec],
        ),
        out_shape=[
            jax.ShapeDtypeStruct((rows, D), f32),
            jax.ShapeDtypeStruct((rows, D), bf16),
            jax.ShapeDtypeStruct((D, rows), bf16),
            jax.ShapeDtypeStruct((rows, D), bf16),
            jax.ShapeDtypeStruct((D, rows), bf16),
        ],
        compiler_params=pltpu.CompilerParams(vmem_limit_bytes=VMEM_LIMIT),
        cost_estimate=cost(10, 30),
        name="post_attention",
    )(lengths, shifts, ctx, pack, hidden, vecs, *pieces)


def gelu_parts(v):
    c = 0.7978845608
    v2 = v * v
    t = jnp.tanh(v * (c + (c * 0.044715) * v2))
    half = 0.5 + 0.5 * t
    gelu = v * half
    slope = half + (0.5 * v) * (1.0 - t * t) * (c + (3.0 * c * 0.044715) * v2)
    return gelu, slope


def ffn_steps(x_any, d_any, xt_any, dt_any, wgu_ref, wo_ref, grad_ref, y_any, dx_any,
              x_ref, d_ref, xt_ref, dt_ref, y_ref, dx_ref, a_ref, dg_ref, du_ref, gu_ref, go_ref, in_sem, out_sem, sems,
              low_ref=None):
    f = pl.program_id(0)
    steps = FF // 2 // FT
    rows_total = x_ref.shape[0]
    chunks = rows_total // RC
    shards, part = gu_ref.shape[1], gu_ref.shape[2]
    owners, deep = go_ref.shape[1], go_ref.shape[2]
    base = steps * part

    def copies(slot, step):
        return (
            pltpu.make_async_copy(
                gu_ref.at[slot], grad_ref.at[:, pl.ds(step * part, part), :], sems.at[0, slot]),
            pltpu.make_async_copy(
                go_ref.at[slot], grad_ref.at[pl.ds(step * owners, owners), pl.ds(base, deep), :], sems.at[1, slot]),
        )

    def row_loads(i):
        rows = pl.ds(i * RC, RC)
        return (
            pltpu.make_async_copy(x_any.at[rows], x_ref.at[rows], in_sem.at[0, i]),
            pltpu.make_async_copy(d_any.at[rows], d_ref.at[rows], in_sem.at[1, i]),
        )

    def turned_loads():
        return (
            pltpu.make_async_copy(xt_any, xt_ref, in_sem.at[2, 0]),
            pltpu.make_async_copy(dt_any, dt_ref, in_sem.at[2, 1]),
        )

    def row_stores(i):
        rows = pl.ds(i * RC, RC)
        return (
            pltpu.make_async_copy(low_ref.at[0, rows], y_any.at[rows], out_sem.at[0, i]),
            pltpu.make_async_copy(low_ref.at[1, rows], dx_any.at[rows], out_sem.at[1, i]),
        )

    @pl.when(f == 0)
    def _():
        for i in range(chunks):
            for copy in row_loads(i):
                copy.start()
        for copy in turned_loads():
            copy.start()
        y_ref[...] = jnp.zeros_like(y_ref)
        dx_ref[...] = jnp.zeros_like(dx_ref)

    d_rows = part // 2
    third = deep // 3
    wg = wgu_ref[:, 0:d_rows, :].reshape(D, FT)
    wu = wgu_ref[:, d_rows:part, :].reshape(D, FT)
    wo = jnp.concatenate(
        [wo_ref[:, i * third : (i + 1) * third, :].reshape(FT, FT) for i in range(3)], axis=1)

    @pl.when(f == 0)
    def _():
        for i in range(chunks):
            for copy in row_loads(i):
                copy.wait()

    def chunk(i, carry):
        rows = pl.ds(pl.multiple_of(i * RC, RC), RC)
        x, d = x_ref[rows, :], d_ref[rows, :]
        gelu, slope = gelu_parts(nn(x, wg))
        up = nn(x, wu)
        da = nt(d, wo)
        act = (gelu * up).astype(bf16)
        dg = (da * up * slope).astype(bf16)
        du = (da * gelu).astype(bf16)
        a_ref[rows, :] = act
        dg_ref[rows, :] = dg
        du_ref[rows, :] = du
        y_ref[rows, :] += nn(act, wo)
        dx_ref[rows, :] += nt(dg, wg) + nt(du, wu)
        return carry

    lax.fori_loop(0, chunks, chunk, 0)
    if y_any is not None:

        @pl.when(f == steps - 1)
        def _():
            for i in range(chunks):
                rows = pl.ds(i * RC, RC)
                low_ref[0, rows, :] = y_ref[rows, :].astype(bf16)
                low_ref[1, rows, :] = dx_ref[rows, :].astype(bf16)
                for copy in row_stores(i):
                    copy.start()

    slot = lax.rem(f, 2)

    @pl.when(f == 0)
    def _():
        for copy in turned_loads():
            copy.wait()

    @pl.when(f >= 2)
    def _():
        for copy in copies(slot, f - 2):
            copy.wait()

    gu_ref[slot, :, 0:d_rows, :] = nn(xt_ref[...], dg_ref[...]).astype(bf16).reshape(shards, d_rows, FT)
    gu_ref[slot, :, d_rows:part, :] = nn(xt_ref[...], du_ref[...]).astype(bf16).reshape(shards, d_rows, FT)
    go = nn(dt_ref[...], a_ref[...]).T.astype(bf16)
    for i in range(3):
        go_ref[slot, :, i * third : (i + 1) * third, :] = go[:, i * FT : (i + 1) * FT].reshape(owners, third, FT)
    for copy in copies(slot, f):
        copy.start()

    @pl.when(f == steps - 1)
    def _():
        for copy in copies(1 - slot, f - 1) + copies(slot, f):
            copy.wait()
        if y_any is not None:
            for i in range(chunks):
                for copy in row_stores(i):
                    copy.wait()


def first_kernel(x, d, xt, dt, wgu, wo, grad, y, dx, *scratch):
    ffn_steps(x, d, xt, dt, wgu, wo, grad, y, dx, *scratch)


def second_kernel(len_ref, x, d, xt, dt, wgu, wo, att_ref, y1_ref, dx1_ref, do_ref, ctx_ref, w_ref, vec_ref,
                  grad, out_ref, datt_ref, dctx_ref, gg_ref, acc_ref, flat_ref, join_ref, join_sem, *scratch):
    f = pl.program_id(0)
    steps = FF // 2 // FT

    @pl.when(f == 0)
    def _():
        acc_ref[...] = jnp.zeros_like(acc_ref)
        gg_ref[...] = jnp.zeros_like(gg_ref)
        flat_ref[...] = out_weights(w_ref)

    @pl.when(f < steps)
    def _():
        ffn_steps(x, d, xt, dt, wgu, wo, grad, None, None, *scratch)

    @pl.when(f >= steps)
    def _():
        tile = f - steps
        y_ref, dx_ref = scratch[4], scratch[5]
        rows = pl.ds(pl.multiple_of(tile * MT, MT), MT)
        per = TOK // MT
        length = len_ref[tile // per]
        place_in = lax.rem(tile, per) * MT + lax.broadcasted_iota(jnp.int32, (MT, 1), 0)
        live = jnp.where(2 * place_in < length, 1.0, 0.0).astype(f32)
        att = att_ref[...]
        out_ref[...] = ((att + y1_ref[...].astype(f32) + y_ref[rows, :]) * live).astype(bf16)
        back, gain_grad = norm_back(att, dx1_ref[...].astype(f32) + dx_ref[rows, :], vec_ref[6:7, :])
        gg_ref[...] += gain_grad
        d_att = do_ref[...].astype(f32) + back
        low = d_att.astype(bf16)
        datt_ref[...] = low
        dctx_ref[...] = nt(low, flat_ref[...]).astype(bf16)
        acc_ref[...] += nn(ctx_ref[...].T, low)

    @pl.when(f == pl.num_programs(0) - 1)
    def _():
        shards, deep = join_ref.shape[0], join_ref.shape[1] // 3
        for i in range(3):
            block = acc_ref[:, i * FT : (i + 1) * FT].astype(bf16).reshape(shards, deep, FT)
            join_ref[:, i * deep : (i + 1) * deep, :] = block
        copy = pltpu.make_async_copy(join_ref, grad.at[:, pl.ds(grad.shape[1] - 3 * deep, 3 * deep), :], join_sem)
        copy.start()
        copy.wait()


def ffn_scratch(rows, shards):
    part, hs = 2 * D // shards, FF // 2 // shards
    return [
        pltpu.VMEM((rows, D), bf16),
        pltpu.VMEM((rows, D), bf16),
        pltpu.VMEM((D, rows), bf16),
        pltpu.VMEM((D, rows), bf16),
        pltpu.VMEM((rows, D), f32),
        pltpu.VMEM((rows, D), f32),
        pltpu.VMEM((rows, FT), bf16),
        pltpu.VMEM((rows, FT), bf16),
        pltpu.VMEM((rows, FT), bf16),
        pltpu.VMEM((2, shards, part, FT), bf16),
        pltpu.VMEM((2, FT // hs, 3 * hs, FT), bf16),
        pltpu.SemaphoreType.DMA((3, max(2, rows // RC))),
        pltpu.SemaphoreType.DMA((2, rows // RC)),
        pltpu.SemaphoreType.DMA((2, 2)),
    ]


def ffn_specs(tiles, shards):
    last = lambda f: jnp.minimum(f, tiles - 1)
    part, hs = 2 * D // shards, FF // 2 // shards
    return [pl.BlockSpec(memory_space=pl.ANY)] * 4 + [
        pl.BlockSpec((shards, part, FT), lambda f, *n: (0, last(f), 0)),
        pl.BlockSpec((FT // hs, 3 * hs, FT), lambda f, *n: (last(f), 2, 0)),
    ]


def grad_shape(shards, more=0):
    part, hs = 2 * D // shards, FF // 2 // shards
    return jax.ShapeDtypeStruct((shards, FF // 2 // FT * part + 3 * hs + more, FT), bf16)


def ffn_first(x, d_out, xt, dt, pack, shards):
    rows = x.shape[0]
    tiles = FF // 2 // FT
    anywhere = pl.BlockSpec(memory_space=pl.ANY)
    return pl.pallas_call(
        first_kernel,
        grid=(tiles,),
        in_specs=ffn_specs(tiles, shards),
        out_specs=[anywhere] * 3,
        out_shape=[
            grad_shape(shards),
            jax.ShapeDtypeStruct((rows, D), bf16),
            jax.ShapeDtypeStruct((rows, D), bf16),
        ],
        scratch_shapes=ffn_scratch(rows, shards) + [pltpu.VMEM((2, rows, D), bf16)],
        compiler_params=pltpu.CompilerParams(vmem_limit_bytes=VMEM_LIMIT),
        cost_estimate=cost(36, 40),
        name="ffn_first",
    )(x, d_out, xt, dt, pack, pack)


def ffn_second(lengths, x, d_out, xt, dt, pack, att, y1, dx1, ctx, pack0, vecs, shards):
    rows = x.shape[0]
    tiles = FF // 2 // FT
    tile_rows = pl.BlockSpec((MT, D), lambda f, n: (jnp.maximum(f - tiles, 0), 0))
    return pl.pallas_call(
        second_kernel,
        grid_spec=pltpu.PrefetchScalarGridSpec(
            num_scalar_prefetch=1,
            grid=(tiles + rows // MT,),
            in_specs=ffn_specs(tiles, shards) + [tile_rows] * 5 + [out_block(shards), whole(8, D)],
            out_specs=[pl.BlockSpec(memory_space=pl.ANY), tile_rows, tile_rows, tile_rows, whole(1, D)],
            scratch_shapes=[
                pltpu.VMEM((D, D), f32), pltpu.VMEM((D, D), bf16),
                pltpu.VMEM((shards, 3 * D // shards, FT), bf16), pltpu.SemaphoreType.DMA,
            ] + ffn_scratch(rows, shards),
        ),
        out_shape=[
            grad_shape(shards, 3 * D // shards),
            jax.ShapeDtypeStruct((rows, D), bf16),
            jax.ShapeDtypeStruct((rows, D), bf16),
            jax.ShapeDtypeStruct((rows, D), bf16),
            jax.ShapeDtypeStruct((1, D), f32),
        ],
        compiler_params=pltpu.CompilerParams(vmem_limit_bytes=VMEM_LIMIT),
        cost_estimate=cost(46, 60),
        name="ffn_second",
    )(lengths, x, d_out, xt, dt, pack, pack, att, y1, dx1, d_out, ctx, pack0, vecs)


def norm_back(x, grad, gain):
    r = rms_scale(x)
    n = x * r
    u = gain * grad
    mean = jnp.sum(n * u, axis=1, keepdims=True) * (1.0 / D)
    return r * (u - n * mean), jnp.sum(n * grad, axis=0, keepdims=True)


def qkv_grad_kernel(dqkv_ref, normed_t_ref, gw_ref):
    gw_ref[...] = nn(normed_t_ref[...], dqkv_ref[0]).astype(bf16)


def qkv_grad(dqkv, normed_t):
    rows = normed_t.shape[1]
    return pl.pallas_call(
        qkv_grad_kernel,
        grid=(3,),
        in_specs=[pl.BlockSpec((1, rows, D), lambda i: (i, 0, 0)), whole(D, rows)],
        out_specs=pl.BlockSpec((D, D), lambda i: (0, i)),
        out_shape=jax.ShapeDtypeStruct((D, 3 * D), bf16),
        compiler_params=pltpu.CompilerParams(vmem_limit_bytes=VMEM_LIMIT),
        cost_estimate=cost(11, 20),
        name="qkv_grad",
    )(dqkv, normed_t)


def qkv_back_kernel(dqkv_ref, w_ref, hidden_ref, datt_ref, vec_ref, dh_ref, gg_ref):
    @pl.when(pl.program_id(0) == 0)
    def _():
        gg_ref[...] = jnp.zeros_like(gg_ref)

    dn = nt(dqkv_ref[0], w_ref[:, 0:D])
    for i in range(1, 3):
        dn = dn + nt(dqkv_ref[i], w_ref[:, i * D : (i + 1) * D])
    back, gain_grad = norm_back(hidden_ref[...], dn, vec_ref[5:6, :])
    gg_ref[...] += gain_grad
    dh_ref[...] = (datt_ref[...].astype(f32) + back).astype(bf16)


def qkv_backward(dqkv, attn_w, hidden, d_att, vecs):
    rows = hidden.shape[0]
    tile = pl.BlockSpec((TOK, D), lambda s: (s, 0))
    return pl.pallas_call(
        qkv_back_kernel,
        grid=(rows // TOK,),
        in_specs=[
            pl.BlockSpec((3, TOK, D), lambda s: (0, s, 0)),
            pl.BlockSpec((D, 3 * D), lambda s: (0, 0)),
            tile, tile, whole(8, D),
        ],
        out_specs=[tile, whole(1, D)],
        out_shape=[jax.ShapeDtypeStruct((rows, D), bf16), jax.ShapeDtypeStruct((1, D), f32)],
        compiler_params=pltpu.CompilerParams(vmem_limit_bytes=VMEM_LIMIT),
        cost_estimate=cost(14, 40),
        name="qkv_backward",
    )(dqkv, attn_w, hidden, d_att, vecs)


MESH = pl.DeviceIdType.MESH


def greet(peers):
    barrier = pltpu.get_barrier_semaphore()
    for peer in peers:
        pl.semaphore_signal(barrier, inc=1, device_id=peer, device_id_type=MESH)
    pl.semaphore_wait(barrier, len(peers))


def pack_half(out_ref, ffn_in_ref, ffn_out_ref, h, shards):
    hs = FF // 2 // shards
    owners = FT // hs
    deep = ffn_in_ref.shape[0]
    row = 0
    for f in range(FF // 2 // FT):
        for g in range(2):
            starts = [g * FF + (f * owners + o) * 2 * hs + h * hs for o in range(owners)]
            out_ref[row : row + deep, :] = jnp.concatenate([ffn_in_ref[:, a : a + hs] for a in starts], axis=1)
            row += deep
    for i in range(3):
        out_ref[row : row + hs, :] = ffn_out_ref[h * hs : (h + 1) * hs, i * FT : (i + 1) * FT]
        row += hs
    return row


def prepare_kernel(replicas, shards, length_ref, target_ref, embed_ref, conv_ref, score_ref, gain1_ref, gain2_ref, rel_ref,
                   ids_ref, attn_out_ref, ffn_in_ref, ffn_out_ref,
                   table_ref, vec_ref, table_rel_ref, slots_ref, column_ref, pack0_ref, pack1_ref,
                   own_ref, wide_ref, turn_ref, nat_ref, wanted_ref, send_sem, recv_sem):
    rep, me = lax.axis_index("rep"), lax.axis_index("shard")
    deep = embed_ref.shape[1]
    seqs = ids_ref.shape[0]
    twin = me + 1 - 2 * lax.rem(me, 2)
    far = [lax.rem(me + 2 * i, shards) for i in range(1, shards // 2)]
    others = [lax.rem(rep + i, replicas) for i in range(1, replicas)]
    greet([(rep, twin)] + [(rep, p) for p in far] + [(p, me) for p in others])

    def send(i, src, dst, device):
        copy = pltpu.make_async_remote_copy(
            src_ref=src, dst_ref=dst, send_sem=send_sem.at[i], recv_sem=recv_sem.at[i],
            device_id=device, device_id_type=MESH)
        copy.start()
        return copy

    wide_ref[...] = jnp.zeros_like(wide_ref)
    wide_ref[0:VOCAB, 0:deep] = embed_ref[...].astype(f32)
    wide_ref[VOCAB : VOCAB + 4, 0:deep] = conv_ref[...].astype(f32)
    for i, ref in enumerate((score_ref, gain1_ref, gain2_ref)):
        wide_ref[VOCAB + 4 + i : VOCAB + 5 + i, 0:deep] = ref[...].astype(f32).reshape(1, deep)
    rel_rows, heads = rel_ref.shape
    wide_ref[VOCAB + 7 : VOCAB + 7 + rel_rows, 0:heads] = rel_ref[...].astype(f32)
    own_ref[...] = wide_ref[...].T[0:deep].astype(bf16)
    near = [send(0, own_ref, table_ref.at[me], (rep, twin))]
    direct = [send(1 + i, own_ref, table_ref.at[me], (rep, p)) for i, p in enumerate(far)]
    lanes = lax.broadcasted_iota(jnp.int32, (8, 128), 1)
    wanted = jnp.zeros((8, 128), jnp.int32)
    for k in range(seqs):
        slot = target_ref[k] % seqs
        wanted = wanted + jnp.where(lanes == target_ref[k] // seqs // shards, slot + 1, 0)
    wanted_ref[...] = wanted
    base = shards
    asks = [send(base + i, wanted_ref, slots_ref.at[rep], (p, me)) for i, p in enumerate(others)]
    table_ref[me] = own_ref[...]
    slots_ref[rep] = wanted_ref[...]
    row = pack_half(pack0_ref, ffn_in_ref, ffn_out_ref, 0, shards)
    for i in range(3):
        pack0_ref[row : row + deep, :] = attn_out_ref[:, i * FT : (i + 1) * FT]
        row += deep
    pack_half(pack1_ref, ffn_in_ref, ffn_out_ref, 1, shards)
    base = base + replicas - 1
    for i, copy in enumerate(direct):
        copy.wait()
        source = lax.rem(me - 2 * (i + 1) + shards, shards)
        near.append(send(base + i, table_ref.at[source], table_ref.at[source], (rep, twin)))
    turn_ref[...] = jnp.full(turn_ref.shape, -1.0, f32)
    place = lax.broadcasted_iota(jnp.int32, (1, MAXLEN), 1)
    for s in range(seqs):
        turn_ref[s : s + 1, 0:MAXLEN] = jnp.where(place < length_ref[s], ids_ref[s : s + 1, :], -1).astype(f32)
    nat_ref[...] = turn_ref[...].T
    for r in range(R):
        rows = nat_ref[pl.ds(r, QN, stride=R), :]
        for s in range(seqs):
            column_ref[s, r * QN : (r + 1) * QN, :] = jnp.broadcast_to(rows[:, s : s + 1], (QN, 128))
    for copy in near + asks:
        copy.wait()
    last = table_ref[:, :, SMALL - 128 :].astype(f32).reshape(D, 128).T
    first = VOCAB - (SMALL - 128)
    vec_ref[...] = last[first : first + 8]
    table_rel_ref[...] = jnp.zeros_like(table_rel_ref)
    for s in range(shards):
        block = last[first + 7 : first + 7 + rel_rows, s * deep : s * deep + heads]
        table_rel_ref[s * rel_rows : (s + 1) * rel_rows, 0:heads] = block


def prepare(lengths, target, embed, conv_w, score_w, gain_attn, gain_ffn, rel_table, ids, attn_out, ffn_in, ffn_out,
            replicas, shards):
    deep = embed.shape[1]
    seqs = ids.shape[0]
    part, hs = 2 * D // shards, FF // 2 // shards
    rows = FF // 2 // FT * part + 3 * hs
    sems = shards + replicas - 1 + shards // 2 - 1
    vmem = pl.BlockSpec(memory_space=pltpu.VMEM)
    smem = pl.BlockSpec(memory_space=pltpu.SMEM)
    return pl.pallas_call(
        lambda *refs: prepare_kernel(replicas, shards, *refs),
        out_shape=[
            jax.ShapeDtypeStruct((shards, deep, SMALL), bf16),
            jax.ShapeDtypeStruct((8, D), f32),
            jax.ShapeDtypeStruct((BUCKETS, 128), f32),
            jax.ShapeDtypeStruct((replicas, 8, 128), jnp.int32),
            jax.ShapeDtypeStruct((seqs, P_ROWS, 128), f32),
            jax.ShapeDtypeStruct((rows + 3 * deep, FT), bf16),
            jax.ShapeDtypeStruct((rows, FT), bf16),
        ],
        in_specs=[smem] * 2 + [vmem] * 10,
        out_specs=[vmem] * 7,
        scratch_shapes=[
            pltpu.VMEM((deep, SMALL), bf16),
            pltpu.VMEM((SMALL, 128), f32),
            pltpu.VMEM((128, 1152), f32),
            pltpu.VMEM((1152, 128), f32),
            pltpu.VMEM((8, 128), jnp.int32),
            pltpu.SemaphoreType.DMA((sems,)),
            pltpu.SemaphoreType.DMA((sems,)),
        ],
        compiler_params=pltpu.CompilerParams(collective_id=1, has_side_effects=True, vmem_limit_bytes=VMEM_LIMIT),
        cost_estimate=cost(12, 8),
        name="prepare",
    )(lengths, target, embed, conv_w, score_w, gain_attn, gain_ffn, rel_table, ids, attn_out, ffn_in, ffn_out)


def pick_kernel(order_ref, in_ref, *out_refs):
    for i, ref in enumerate(out_refs):
        @pl.when(pl.program_id(0) == i)
        def _():
            ref[...] = in_ref[0]


def pick(order, rows):
    count = order.shape[0]
    block = (rows.shape[1], rows.shape[2])
    return pl.pallas_call(
        pick_kernel,
        grid_spec=pltpu.PrefetchScalarGridSpec(
            num_scalar_prefetch=1,
            grid=(count,),
            in_specs=[pl.BlockSpec((1,) + block, lambda i, order: (order[i], 0, 0))],
            out_specs=[pl.BlockSpec(block, lambda i, order: (0, 0))] * count,
        ),
        out_shape=[jax.ShapeDtypeStruct(block, rows.dtype)] * count,
        compiler_params=pltpu.CompilerParams(vmem_limit_bytes=VMEM_LIMIT),
        cost_estimate=cost(4, 6),
        name="pick",
    )(order, rows)


def finish_kernel(replicas, shards, piece_ref, small_ref, in_ref, embed_ref, conv_ref, rest_ref,
                  twin_ref, both_ref, far_ref, held_ref, other_ref, part_ref, part2_ref, last_ref,
                  twin_send, twin_recv, far_send, far_recv, send_sem, recv_sem, send2_sem, recv2_sem):
    rep, me = lax.axis_index("rep"), lax.axis_index("shard")
    half = piece_ref.shape[1]
    chips = shards // 2
    core = lax.rem(me, 2)
    twin = me + 1 - 2 * core
    bits = [1 << b for b in range(replicas.bit_length() - 1)]
    orders = (bits, bits[::-1])
    far = [lax.rem(me + 2 * i, shards) for i in range(1, chips)]
    partners = {}
    for bit in bits:
        down = lax.rem(rep // bit, 2)
        partners[bit] = (rep + bit - 2 * bit * down, me)
    greet([(rep, twin)] + [(rep, p) for p in far] + [partners[bit] for bit in bits])

    def send(src, dst, sems, i, device):
        copy = pltpu.make_async_remote_copy(
            src_ref=src, dst_ref=dst, send_sem=sems[0].at[i], recv_sem=sems[1].at[i],
            device_id=device, device_id_type=MESH)
        copy.start()
        return copy

    near = [
        send(small_ref.at[2 * z + 1 - core], twin_ref.at[z], (twin_send, twin_recv), z, (rep, twin))
        for z in range(chips)
    ]

    def exchange(t, mine, theirs, sems):
        return [send(mine.at[t, h], theirs.at[t, h], sems, (t, h), partners[orders[h][t]]) for h in range(2)]

    held_ref[0] = piece_ref[...]
    large = exchange(0, held_ref, other_ref, (send_sem, recv_sem))
    for z, copy in enumerate(near):
        copy.wait()
        both_ref[z] = (small_ref[2 * z + core].astype(f32) + twin_ref[z].astype(f32)).astype(bf16)
    away = [send(both_ref.at[p // 2], far_ref.at[i], (far_send, far_recv), i, (rep, p)) for i, p in enumerate(far)]
    last_ref[...] = jnp.zeros_like(last_ref)
    total = both_ref[me // 2].astype(f32)
    for i, copy in enumerate(away):
        copy.wait()
        total = total + far_ref[i].astype(f32)
    part_ref[0] = total.astype(bf16)
    little = exchange(0, part_ref, part2_ref, (send2_sem, recv2_sem))
    for t in range(len(bits)):
        final = t == len(bits) - 1
        for h, copy in enumerate(large):
            copy.wait()
            total = held_ref[t, h].astype(f32) + other_ref[t, h].astype(f32)
            if final:
                in_ref[h * half : (h + 1) * half, :] = total
            else:
                held_ref[t + 1, h] = total.astype(bf16)
        if not final:
            large = exchange(t + 1, held_ref, other_ref, (send_sem, recv_sem))
        for h, copy in enumerate(little):
            copy.wait()
            total = part_ref[t, h].astype(f32) + part2_ref[t, h].astype(f32)
            if final:
                last_ref[h * half : (h + 1) * half, :] = total
            else:
                part_ref[t + 1, h] = total.astype(bf16)
        if not final:
            little = exchange(t + 1, part_ref, part2_ref, (send2_sem, recv2_sem))
    turned = last_ref[...].T
    deep = embed_ref.shape[1]
    embed_ref[...] = turned[0:VOCAB, 0:deep]
    conv_ref[...] = turned[VROWS : VROWS + 4, 0:deep]
    rest_ref[...] = turned[VROWS : VROWS + 16, 0:deep]


def finish(piece, small, replicas, shards):
    rows, wide = piece.shape
    half = rows // 2
    chips = shards // 2
    steps = replicas.bit_length() - 1
    vmem = pl.BlockSpec(memory_space=pltpu.VMEM)
    sems = lambda *shape: [pltpu.SemaphoreType.DMA(shape), pltpu.SemaphoreType.DMA(shape)]
    return pl.pallas_call(
        lambda *refs: finish_kernel(replicas, shards, *refs),
        out_shape=[
            jax.ShapeDtypeStruct((rows, wide), f32),
            jax.ShapeDtypeStruct((VOCAB, rows), f32),
            jax.ShapeDtypeStruct((4, rows), f32),
            jax.ShapeDtypeStruct((16, rows), f32),
        ],
        in_specs=[vmem] * 2,
        out_specs=[vmem] * 4,
        scratch_shapes=[
            pltpu.VMEM((chips, 2, half, SMALL), bf16),
            pltpu.VMEM((chips, 2, half, SMALL), bf16),
            pltpu.VMEM((chips - 1, 2, half, SMALL), bf16),
            pltpu.VMEM((steps, 2, half, wide), bf16),
            pltpu.VMEM((steps, 2, half, wide), bf16),
            pltpu.VMEM((steps, 2, half, SMALL), bf16),
            pltpu.VMEM((steps, 2, half, SMALL), bf16),
            pltpu.VMEM((128, SMALL), f32),
        ] + sems(chips) + sems(chips - 1) + sems(steps, 2) + sems(steps, 2),
        compiler_params=pltpu.CompilerParams(
            collective_id=2, has_side_effects=True, vmem_limit_bytes=VMEM_LIMIT),
        cost_estimate=cost(20, 4),
        name="finish_sums",
    )(piece.reshape(2, half, wide), small.reshape(shards, 2, half, SMALL))


def deliver_kernel(in_ref, embed_ref, conv_ref, rest_ref, in_out, embed_out, conv_out, score_out, gain1_out, gain2_out, rel_out):
    in_out[...] = in_ref[...]
    embed_out[...] = embed_ref[...]
    conv_out[...] = conv_ref[...]
    for i, ref in enumerate((score_out, gain1_out, gain2_out)):
        ref[...] = rest_ref[4 + i : 5 + i, :].reshape(ref.shape)
    rel_out[...] = rest_ref[7 : 7 + rel_out.shape[0], 0 : rel_out.shape[1]]


def deliver(parts, rel_rows):
    deep = parts[0].shape[0]
    vmem = pl.BlockSpec(memory_space=pltpu.VMEM)
    line = jax.ShapeDtypeStruct((deep,), f32)
    return pl.pallas_call(
        deliver_kernel,
        out_shape=[jax.ShapeDtypeStruct(x.shape, f32) for x in parts[:3]]
        + [line] * 3 + [jax.ShapeDtypeStruct((rel_rows, HEADS), f32)],
        in_specs=[vmem] * 4,
        out_specs=[vmem] * 7,
        compiler_params=pltpu.CompilerParams(vmem_limit_bytes=VMEM_LIMIT),
        cost_estimate=cost(2, 2),
        name="deliver",
    )(*parts)


def unpack_kernel(shards, first_ref, second_ref, other_ref, in_ref, out_ref, attn_ref):
    hs = FF // 2 // shards
    deep = in_ref.shape[0]
    owners = FT // hs
    for h in range(2):
        def load(start, count):
            rows = slice(start, start + count)
            if h == 0:
                return first_ref[rows, :].astype(f32)
            return second_ref[rows, :].astype(f32) + other_ref[rows, :].astype(f32)

        row = 0
        for f in range(FF // 2 // FT):
            for g in range(2):
                x = load(row, deep)
                for o in range(owners):
                    start = g * FF + (f * owners + o) * 2 * hs + h * hs
                    in_ref[:, start : start + hs] = x[:, o * hs : (o + 1) * hs]
                row += deep
        for i in range(3):
            out_ref[h * hs : (h + 1) * hs, i * FT : (i + 1) * FT] = load(row, hs)
            row += hs
        if h == 1:
            for i in range(3):
                attn_ref[:, i * FT : (i + 1) * FT] = load(row + i * deep, deep)


def unpack(first, second, other, shards):
    vmem = pl.BlockSpec(memory_space=pltpu.VMEM)
    return pl.pallas_call(
        lambda *refs: unpack_kernel(shards, *refs),
        out_shape=[
            jax.ShapeDtypeStruct((D // shards, 2 * FF), f32),
            jax.ShapeDtypeStruct((FF // shards, D), f32),
            jax.ShapeDtypeStruct((D // shards, D), f32),
        ],
        in_specs=[vmem] * 3,
        out_specs=[vmem] * 3,
        compiler_params=pltpu.CompilerParams(vmem_limit_bytes=VMEM_LIMIT),
        cost_estimate=cost(3, 5),
        name="unpack",
    )(first, second, other)


def send_cotangent(slots, cotangent):
    replicas = lax.axis_size("rep")
    places = jnp.arange(replicas)
    rep = lax.axis_index("rep")
    asked = jnp.where(places[None, :] == rep, slots, 0).sum(axis=1) - 1
    turned = (places[None, :] == (rep + places[:, None]) % replicas) * asked[None, :]
    pieces = list(pick(jnp.maximum(turned.sum(axis=1), 0), cotangent))
    for shift in range(1, replicas):
        pieces[shift] = lax.ppermute(pieces[shift], "rep", [(r, (r + shift) % replicas) for r in range(replicas)])
    return pieces


def swap(x, bit):
    replicas = lax.axis_size("rep")
    return lax.ppermute(x, "rep", [(r, r ^ bit) for r in range(replicas)])


def add_low(a, b):
    return (a.astype(f32) + b.astype(f32)).astype(bf16)


def scatter_sum(grad):
    return lax.psum_scatter(grad, "shard", scatter_dimension=0, tiled=True)


def body(
    byte_ids, lengths, target, rel_bucket, cotangent, embed, conv_w, score_w, gain_attn,
    attn_in, attn_out, gain_ffn, ffn_in, ffn_out, rel_table,
):
    seqs = byte_ids.shape[0]
    replicas, shards = lax.axis_size("rep"), lax.axis_size("shard")
    attn_w = lax.all_gather(attn_in, "shard", axis=0, tiled=True)
    table, vecs, rel, slots, ids_col, pack0, pack1 = prepare(
        lengths, target, embed, conv_w, score_w, gain_attn, gain_ffn, rel_table, byte_ids,
        attn_out, ffn_in, ffn_out, replicas, shards,
    )
    packs = [lax.all_gather(pack, "shard", axis=0) for pack in (pack0, pack1)]
    rows = bucket_rows(rel_bucket)

    hidden, normed, normed_t, convolved, weights, e_low, coefs = gbst_forward(lengths, ids_col, table, vecs)
    qkv = jnp.dot(normed, attn_w, preferred_element_type=f32).astype(bf16)
    qkv, slots = lax.optimization_barrier((qkv, slots))
    pieces = send_cotangent(slots[:, 0, :replicas], cotangent)
    ctx, lse = attn_forward(lengths, qkv, rel, rows)
    ctx, pieces = lax.optimization_barrier((ctx, pieces))
    shifts = (lax.axis_index("rep") - target // seqs // shards) % replicas
    attended, low, low_t, d_out, d_out_t = post_attention(
        lengths, shifts, ctx, packs[0], hidden, vecs, pieces, shards
    )
    g_half1, y1, dx1 = ffn_first(low, d_out, low_t, d_out_t, packs[0], shards)
    g_half2, out, d_att, d_ctx, g_gain_ffn = ffn_second(
        lengths, low, d_out, low_t, d_out_t, packs[1], attended, y1, dx1, ctx, packs[0], vecs, shards
    )
    one, two = [scatter_sum(g.reshape(-1, FT)) for g in (g_half1, g_half2)]
    bits = [1 << b for b in range(replicas.bit_length() - 1)]
    d_ctx, one = lax.optimization_barrier((d_ctx, one))
    other = swap(one, bits[0])
    dqkv, g_rel = attn_backward(lengths, qkv, d_ctx, ctx, lse, rel, rows, shards)
    dqkv, other = lax.optimization_barrier((dqkv, other))
    one = add_low(one, other)
    g_attn = qkv_grad(dqkv, normed_t)
    g_attn, two = lax.optimization_barrier((g_attn, two))
    p_attn = scatter_sum(g_attn)
    others = swap(one, bits[1]), swap(two, bits[0])
    d_hidden, g_gain_attn = qkv_backward(dqkv, attn_w, hidden, d_att, vecs)
    d_hidden, others = lax.optimization_barrier((d_hidden, others))
    one, two = add_low(one, others[0]), add_low(two, others[1])
    for bit in bits[2:]:
        one, two = add_low(one, swap(one, bit)), add_low(two, swap(two, bit))
    d_hidden, one, two = lax.optimization_barrier((d_hidden, one, two))
    other = swap(two, bits[1])
    ids = jnp.where(jnp.arange(MAXLEN)[None, :] < lengths[:, None], byte_ids, -1)
    input_grad, small = gbst_backward(
        ids.reshape(seqs, 1, MAXLEN), vecs, d_hidden, convolved, weights, e_low, coefs,
        g_gain_attn, g_gain_ffn, g_rel,
    )
    small, other = lax.optimization_barrier((small, other))
    parts = finish(p_attn, small, replicas, shards)
    s_ffn_in, s_ffn_out, s_attn_out = unpack(one, two, other, shards)
    s_attn_in, s_embed, s_conv, s_score, s_gain_attn, s_gain_ffn, s_rel = deliver(parts, rel_table.shape[0])
    return (
        out.reshape(seqs, TOK, D), input_grad, s_embed, s_conv, s_score, s_gain_attn, s_attn_in, s_attn_out,
        s_gain_ffn, s_ffn_in, s_ffn_out, s_rel,
    )


def solution(mesh):
    in_specs = (
        P(("rep", "shard"), None), P(("rep", "shard")), P(("rep", "shard")), P(),
        P(("rep", "shard"), None, None), P(None, "shard"), P(None, "shard"), P("shard"), P("shard"),
        P("shard", None), P("shard", None), P("shard"), P("shard", None), P("shard", None), P("shard", None),
    )
    out_specs = (
        P(("rep", "shard"), None, None), P(("rep", "shard"), None, None), P(None, "shard"), P(None, "shard"),
        P("shard"), P("shard"), P("shard", None), P("shard", None), P("shard"), P("shard", None),
        P("shard", None), P("shard", None),
    )
    return jax.shard_map(body, mesh=mesh, in_specs=in_specs, out_specs=out_specs, check_vma=False)
```

```python
import jax
import jax.numpy as jnp
from jax import lax
from jax.experimental import pallas as pl
from jax.experimental.pallas import tpu as pltpu
from jax.sharding import PartitionSpec as P

D = 768
VOCAB = 259
VROWS = 272
VMEM_LIMIT = 60 << 20
SMALL = 384
MAXLEN = 1024
TOK = 512
LANES = 128
QN = 88
R = 12
P_ROWS = QN * R
T_ROWS = 528
LT = D // LANES
epsilon = 1e-06
f32 = jnp.float32
bf16 = jnp.bfloat16


def cost(us, mib):
    return pl.CostEstimate(flops=int(us * 1e9), bytes_accessed=mib << 20, transcendentals=0)


def lane_iota(rows):
    return lax.broadcasted_iota(jnp.int32, (rows, LANES), 1)


def group_matrix(b):
    row = lax.broadcasted_iota(jnp.int32, (LANES, LANES), 0)
    col = lax.broadcasted_iota(jnp.int32, (LANES, LANES), 1)
    return jnp.where((row // b == col // b) & (row < R) & (col < R), 1.0, 0.0).astype(f32)


def exact_dot(a, b):
    return jnp.dot(a, b, precision=lax.Precision.HIGHEST, preferred_element_type=f32)


def place(columns, rows):
    lanes = lane_iota(rows)
    out = jnp.zeros((rows, LANES), f32)
    for r, column in enumerate(columns):
        out = jnp.where(lanes == r, column, out)
    return out


def gbst_masks(length):
    q = lax.broadcasted_iota(jnp.int32, (QN, LANES), 0)
    r = lax.broadcasted_iota(jnp.int32, (QN, LANES), 1)
    mask = jnp.where((q * R + r < length) & (r < R), 1.0, 0.0).astype(f32)
    inverse = [1.0 / jnp.maximum(exact_dot(mask, group_matrix(b)), 1.0) for b in (2, 3, 4)]
    pair = exact_dot(mask, group_matrix(2))
    alpha = mask / jnp.maximum(pair, 1.0)
    return mask, inverse, alpha


def gbst_weights(s1, inverse):
    sizes = [s1] + [exact_dot(s1, group_matrix(b)) * inv for b, inv in zip((2, 3, 4), inverse)]
    top = jnp.maximum(jnp.maximum(sizes[0], sizes[1]), jnp.maximum(sizes[2], sizes[3]))
    parts = [jnp.exp(s - top) for s in sizes]
    total = parts[0] + parts[1] + parts[2] + parts[3]
    return [p / total for p in parts]


def gbst_coefs(weights, inverse, alpha):
    a1 = weights[0] * alpha
    a2 = weights[1] * alpha * inverse[0]
    a3 = weights[2] * alpha * inverse[1]
    a4 = weights[3] * alpha * inverse[2]
    pair = group_matrix(2)
    a4s = exact_dot(a4, pair)
    own = a1 + exact_dot(a2, pair) + a4s
    return own, a3, a4s


def column(x, r):
    return jnp.broadcast_to(x[:, r : r + 1], (x.shape[0], LANES))


def hits_of(ids):
    lanes = lax.broadcasted_iota(jnp.int32, (P_ROWS, LANES), 1).astype(f32)
    return jnp.concatenate(
        [jnp.where(ids == lanes + float(i * LANES), 1.0, 0.0).astype(bf16) for i in range(SMALL // LANES)], axis=1)


def look_up(ids, table_ref):
    return lax.dot_general(
        hits_of(ids), table_ref[...].reshape(D, SMALL), (((1,), (1,)), ((), ())), preferred_element_type=f32)


def load_e(e_ref, r, lt):
    lanes = pl.ds(lt * LANES, LANES)
    if r < R:
        return e_ref[pl.ds(r * QN, QN), lanes]
    return e_ref[pl.ds((r - R) * QN + 1, QN), lanes]


def gbst_fwd_kernel(len_ref, ids_ref, table_ref, vec_ref, hidden_ref, hlow_ref, normed_ref, turned_ref, c_ref, w_ref, elow_ref, kc_ref, e_ref, hid_ref, s_ref):
    k_ref = kc_ref.at[0]
    length = len_ref[pl.program_id(0)]
    rows_e = look_up(ids_ref[0], table_ref)
    e_ref[pl.ds(0, P_ROWS), :] = rows_e
    elow_ref[0] = rows_e.astype(bf16)
    e_ref[pl.ds(P_ROWS, 8), :] = jnp.zeros((8, D), f32)
    for lt in range(LT):
        lanes = pl.ds(lt * LANES, LANES)
        taps = [jnp.broadcast_to(vec_ref[j : j + 1, lanes], (QN, LANES)) for j in range(4)]
        sw = jnp.broadcast_to(vec_ref[4:5, lanes], (QN, LANES))
        for r in range(R):
            c = taps[0] * load_e(e_ref, r, lt)
            for j in range(1, 4):
                c = c + taps[j] * load_e(e_ref, r + j, lt)
            c_ref[0, pl.ds(r * QN, QN), lanes] = c
            part = c * sw
            rows = pl.ds(r * QN, QN)
            s_ref[rows, :] = part if lt == 0 else s_ref[rows, :] + part
    s1 = place([jnp.sum(s_ref[pl.ds(r * QN, QN), :], axis=1, keepdims=True) for r in range(R)], QN)
    mask, inverse, alpha = gbst_masks(length)
    weights = gbst_weights(s1, inverse)
    for b, kept in enumerate(weights + inverse + [alpha]):
        w_ref[0, b] = kept
    own, a3, a4s = gbst_coefs(weights, inverse, alpha)
    n = 0
    for r in range(R):
        k_ref[r] = column(own, r)
        k_ref[R + r] = column(a3, r)
    for k in range(6):
        k_ref[2 * R + k] = column(a4s, 2 * k)
    for r in range(R):
        k_ref[2 * R + 6 + r] = column(mask, r)
    for lt in range(LT):
        lanes = pl.ds(lt * LANES, LANES)
        for half in range(2):
            c = [c_ref[0, pl.ds((half * 6 + r) * QN, QN), lanes] for r in range(6)]
            base = half * 6
            s3 = [c[0] + c[1] + c[2], c[3] + c[4] + c[5]]
            for k in range(3):
                tok = half * 3 + k
                other = tok ^ 1
                rows = pl.ds(2 * other * QN, QN)
                rows1 = pl.ds((2 * other + 1) * QN, QN)
                s2 = c_ref[0, rows, lanes] + c_ref[0, rows1, lanes]
                h = k_ref[2 * tok] * c[2 * k] + k_ref[2 * tok + 1] * c[2 * k + 1] + k_ref[2 * R + tok] * s2
                if k == 1:
                    h = h + k_ref[R + 2 * tok] * s3[0] + k_ref[R + 2 * tok + 1] * s3[1]
                else:
                    h = h + (k_ref[R + 2 * tok] + k_ref[R + 2 * tok + 1]) * s3[0 if k == 0 else 1]
                hid_ref[lt, pl.ds(tok, QN, stride=6), :] = h
    total = jnp.zeros((TOK, LANES), f32)
    for lt in range(LT):
        x = hid_ref[lt, 0:TOK, :]
        total = total + x * x
    scale = lax.rsqrt(jnp.sum(total, axis=1, keepdims=True) * (1.0 / D) + epsilon)
    for lt in range(LT):
        lanes = pl.ds(lt * LANES, LANES)
        x = hid_ref[lt, 0:TOK, :]
        hidden_ref[:, lanes] = x
        hlow_ref[:, lanes] = x.astype(bf16)
        normed = (x * scale * vec_ref[5:6, lanes]).astype(bf16)
        normed_ref[:, lanes] = normed
        turned_ref[lanes, :] = normed.T


def gbst_forward(lengths, ids_col, table, vecs):
    seqs = ids_col.shape[0]
    grid_spec = pltpu.PrefetchScalarGridSpec(
        num_scalar_prefetch=1,
        grid=(seqs,),
        in_specs=[
            pl.BlockSpec((1, P_ROWS, LANES), lambda s, n: (s, 0, 0)),
            pl.BlockSpec(table.shape, lambda s, n: (0, 0, 0)),
            pl.BlockSpec((8, D), lambda s, n: (0, 0)),
        ],
        out_specs=[
            pl.BlockSpec((TOK, D), lambda s, n: (s, 0)),
            pl.BlockSpec((TOK, D), lambda s, n: (s, 0)),
            pl.BlockSpec((TOK, D), lambda s, n: (s, 0)),
            pl.BlockSpec((D, TOK), lambda s, n: (0, s)),
            pl.BlockSpec((1, P_ROWS, D), lambda s, n: (s, 0, 0)),
            pl.BlockSpec((1, 8, QN, LANES), lambda s, n: (s, 0, 0, 0)),
            pl.BlockSpec((1, P_ROWS, D), lambda s, n: (s, 0, 0)),
            pl.BlockSpec((1, 3 * R + 6, QN, LANES), lambda s, n: (s, 0, 0, 0)),
        ],
        scratch_shapes=[
            pltpu.VMEM((P_ROWS + 8, D), f32),
            pltpu.VMEM((LT, T_ROWS, LANES), f32),
            pltpu.VMEM((P_ROWS, LANES), f32),
        ],
    )
    return pl.pallas_call(
        gbst_fwd_kernel,
        grid_spec=grid_spec,
        out_shape=[
            jax.ShapeDtypeStruct((seqs * TOK, D), f32),
            jax.ShapeDtypeStruct((seqs * TOK, D), bf16),
            jax.ShapeDtypeStruct((seqs * TOK, D), bf16),
            jax.ShapeDtypeStruct((D, seqs * TOK), bf16),
            jax.ShapeDtypeStruct((seqs, P_ROWS, D), f32),
            jax.ShapeDtypeStruct((seqs, 8, QN, LANES), f32),
            jax.ShapeDtypeStruct((seqs, P_ROWS, D), bf16),
            jax.ShapeDtypeStruct((seqs, 3 * R + 6, QN, LANES), f32),
        ],
        compiler_params=pltpu.CompilerParams(vmem_limit_bytes=VMEM_LIMIT),
        cost_estimate=cost(18, 30),
        name="gbst_forward",
    )(lengths, ids_col, table, vecs)


def gbst_bwd_kernel(row_ref, vec_ref, dh_ref, c_ref, w_ref, elow_ref, kc_ref, gain1_ref, gain2_ref, rel_ref,
                    ig_ref, small_ref, ge_ref, e_ref, dt_ref, dc_ref, s_ref, cf_ref, igs_ref):
    seq = pl.program_id(0)
    k_ref = kc_ref.at[0]

    @pl.when(seq == 0)
    def _():
        ge_ref[...] = jnp.zeros_like(ge_ref)

    e_ref[pl.ds(0, P_ROWS), :] = elow_ref[0].astype(f32)
    e_ref[pl.ds(P_ROWS, 8), :] = jnp.zeros((8, D), f32)
    for lt in range(LT):
        dt_ref[lt, 0:TOK, :] = dh_ref[:, pl.ds(lt * LANES, LANES)].astype(f32)
        dt_ref[lt, TOK:T_ROWS, :] = jnp.zeros((T_ROWS - TOK, LANES), f32)
    for lt in range(LT):
        lanes = pl.ds(lt * LANES, LANES)
        for half in range(2):
            c = [c_ref[0, pl.ds((half * 6 + r) * QN, QN), lanes] for r in range(6)]
            s3 = [c[0] + c[1] + c[2], c[3] + c[4] + c[5]]
            for k in range(3):
                tok = half * 3 + k
                other = tok ^ 1
                dh = dt_ref[lt, pl.ds(tok, QN, stride=6), :]
                s2 = c_ref[0, pl.ds(2 * other * QN, QN), lanes] + c_ref[0, pl.ds((2 * other + 1) * QN, QN), lanes]
                parts = [
                    (2 * tok, dh * c[2 * k]),
                    (2 * tok + 1, dh * c[2 * k + 1]),
                    (2 * R + tok, dh * s2),
                    (R + 2 * tok, dh * s3[0 if k < 2 else 1]),
                ]
                if k == 1:
                    parts.append((R + 2 * tok + 1, dh * s3[1]))
                for slot, part in parts:
                    s_ref[slot] = part if lt == 0 else s_ref[slot] + part

    def total(slot):
        return jnp.sum(s_ref[slot], axis=1, keepdims=True)

    d1, d3, dother = [], [], []
    for tok in range(6):
        d1 += [total(2 * tok), total(2 * tok + 1)]
        first = total(R + 2 * tok)
        d3 += [first, total(R + 2 * tok + 1) if tok % 3 == 1 else first]
        o = total(2 * R + tok)
        dother += [o, o]
    d1, d3, dother = place(d1, QN), place(d3, QN), place(dother, QN)
    weights = [w_ref[0, b] for b in range(4)]
    inverse = [w_ref[0, 4 + b] for b in range(3)]
    alpha = w_ref[0, 7]
    d2 = exact_dot(d1, group_matrix(2))
    g = [alpha * d1, alpha * d2 * inverse[0], alpha * d3 * inverse[1], alpha * (d2 + dother) * inverse[2]]
    mean = weights[0] * g[0] + weights[1] * g[1] + weights[2] * g[2] + weights[3] * g[3]
    d_size = [w * (x - mean) for w, x in zip(weights, g)]
    coef = d_size[0]
    for b, inv in zip((2, 3, 4), inverse):
        coef = coef + exact_dot(d_size[b - 1] * inv, group_matrix(b))
    for r in range(R):
        cf_ref[r] = column(coef, r)

    for lt in range(LT):
        lanes = pl.ds(lt * LANES, LANES)
        taps = [jnp.broadcast_to(vec_ref[j : j + 1, lanes], (QN, LANES)) for j in range(4)]
        sw = jnp.broadcast_to(vec_ref[4:5, lanes], (QN, LANES))
        gs = jnp.zeros((QN, LANES), f32)
        gc = [jnp.zeros((QN, LANES), f32) for _ in range(4)]
        for half in range(2):
            dh = [dt_ref[lt, pl.ds(half * 3 + k, QN, stride=6), :] for k in range(3)]
            a = R + half * 6
            t3 = [
                (k_ref[a] + k_ref[a + 1]) * dh[0] + k_ref[a + 2] * dh[1],
                k_ref[a + 3] * dh[1] + (k_ref[a + 4] + k_ref[a + 5]) * dh[2],
            ]
            for k in range(3):
                tok = half * 3 + k
                other = tok ^ 1
                dother_h = dt_ref[lt, pl.ds(other, QN, stride=6), :]
                cross = k_ref[2 * R + other] * dother_h
                for e in range(2):
                    r = 2 * tok + e
                    cf = cf_ref[r]
                    dc = k_ref[r] * dh[k] + cross + t3[(r % 6) // 3] + cf * sw
                    gs = gs + cf * c_ref[0, pl.ds(r * QN, QN), lanes]
                    dc_ref[r, pl.ds(8, QN), :] = dc
                    for j in range(4):
                        gc[j] = gc[j] + dc * load_e(e_ref, r + j, lt)
        ge_ref[VROWS + 4 : VROWS + 5, lanes] += jnp.sum(gs, axis=0, keepdims=True)
        for j in range(4):
            ge_ref[VROWS + j : VROWS + j + 1, lanes] += jnp.sum(gc[j], axis=0, keepdims=True)
        for r in range(R):
            dc_ref[r, 0:8, :] = jnp.zeros((8, LANES), f32)
        for r in range(R):
            x = taps[0] * dc_ref[r, pl.ds(8, QN), :]
            for j in range(1, 4):
                back = dc_ref[r - j, pl.ds(8, QN), :] if r >= j else dc_ref[r - j + R, pl.ds(7, QN), :]
                x = x + taps[j] * back
            igs_ref[lt, pl.ds(r, QN, stride=R), :] = x * k_ref[2 * R + 6 + r]
    for lt in range(LT):
        lanes = pl.ds(lt * LANES, LANES)
        ig_ref[0, :, lanes] = igs_ref[lt, 0:MAXLEN, :].astype(bf16)
    vocab = lax.broadcasted_iota(jnp.int32, (VROWS, MAXLEN), 0)
    row_hits = jnp.where(vocab == row_ref[0], 1.0, 0.0).astype(bf16)
    ge_ref[0:VROWS, :] += jnp.dot(row_hits, ig_ref[0], preferred_element_type=f32)

    @pl.when(seq == pl.num_programs(0) - 1)
    def _():
        ge_ref[VROWS + 5 : VROWS + 6, :] = gain1_ref[...]
        ge_ref[VROWS + 6 : VROWS + 7, :] = gain2_ref[...]
        ge_ref[VROWS + 7 : VROWS + 15, :] = rel_ref[...]
        for lt in range(LT):
            lanes = pl.ds(lt * LANES, LANES)
            small_ref[lanes, :] = ge_ref[:, lanes].T.astype(bf16)


def gbst_backward(ids_row, vecs, d_hidden, c, w, e_low, coefs, gain1, gain2, rel):
    seqs = ids_row.shape[0]
    per_seq = lambda *shape: pl.BlockSpec((1,) + shape, lambda s: (s,) + (0,) * len(shape))
    still = lambda *shape: pl.BlockSpec(shape, lambda s: (0,) * len(shape))
    return pl.pallas_call(
        gbst_bwd_kernel,
        grid=(seqs,),
        in_specs=[
            per_seq(1, MAXLEN), still(8, D), pl.BlockSpec((TOK, D), lambda s: (s, 0)), per_seq(P_ROWS, D),
            per_seq(8, QN, LANES), per_seq(P_ROWS, D), per_seq(3 * R + 6, QN, LANES),
            still(1, D), still(1, D), still(8, D),
        ],
        out_specs=[per_seq(MAXLEN, D), still(D, SMALL)],
        scratch_shapes=[
            pltpu.VMEM((SMALL, D), f32),
            pltpu.VMEM((P_ROWS + 8, D), f32),
            pltpu.VMEM((LT, T_ROWS, LANES), f32),
            pltpu.VMEM((R, QN + 8, LANES), f32),
            pltpu.VMEM((2 * R + 6, QN, LANES), f32),
            pltpu.VMEM((R, QN, LANES), f32),
            pltpu.VMEM((LT, P_ROWS, LANES), f32),
        ],
        out_shape=[
            jax.ShapeDtypeStruct((seqs, MAXLEN, D), bf16),
            jax.ShapeDtypeStruct((D, SMALL), bf16),
        ],
        compiler_params=pltpu.CompilerParams(vmem_limit_bytes=VMEM_LIMIT),
        cost_estimate=cost(26, 40),
        name="gbst_backward",
    )(ids_row, vecs, d_hidden, c, w, e_low, coefs, gain1, gain2, rel)


HEADS = 12
HD = 64
BUCKETS = 32
SPAN = 1024
HB = 4
WIDE = HB * HD
GROUPS = HEADS // HB
dead_score = -1e9


def nt(a, b):
    return lax.dot_general(a, b, (((1,), (1,)), ((), ())), preferred_element_type=f32)


def nn(a, b):
    return jnp.dot(a, b, preferred_element_type=f32)


def bucket_rows(buckets):
    def row(x):
        return jnp.concatenate([x[TOK - 1 :], x[:1], x[: TOK - 1]])

    return jnp.stack([row(buckets), row(buckets[::-1])])


def bucket_hits(row_ref, way):
    return jnp.where(lax.broadcasted_iota(jnp.int32, (BUCKETS, SPAN), 0) == row_ref[way : way + 1, :], 1.0, 0.0).astype(f32)


def spread_table(rel_ref, row_ref, z_ref, way):
    dims = (((0,), (0,)), ((), ()))
    z_ref[...] = lax.dot_general(
        rel_ref[...].astype(bf16), bucket_hits(row_ref, way).astype(bf16), dims, preferred_element_type=f32)


def build_bias(z_ref, bt_ref, group):
    for h in range(HB):
        row = jnp.broadcast_to(z_ref[pl.ds(group * HB + h, 1), :], (8, SPAN))
        z = pltpu.roll(row, 0, 1, stride=1, stride_axis=0)
        for g in range(TOK // 8):
            bt_ref[h, pl.ds(8 * g, 8), :] = (z if g == 0 else pltpu.roll(z, 8 * g, 1))[:, :TOK]


def pair_lanes(h):
    return slice(h // 2 * LANES, (h // 2 + 1) * LANES)


def own_lanes(h):
    return lax.broadcasted_iota(jnp.int32, (TOK, LANES), 1) // HD == h % 2


def head_parts(k, q, length, h):
    lanes = lax.broadcasted_iota(jnp.int32, (TOK, LANES), 1)
    rows = lax.broadcasted_iota(jnp.int32, (TOK, LANES), 0)
    spare = HD * (1 - h % 2)
    dead = jnp.where(2 * rows < length, 0.0, dead_score)
    kf = jnp.where(own_lanes(h), k[:, pair_lanes(h)].astype(f32), jnp.where(lanes == spare, dead, 0.0)).astype(bf16)
    qf = jnp.where(lanes == spare, 1.0, q[:, pair_lanes(h)].astype(f32)).astype(bf16)
    return kf, qf


def join_heads(parts):
    pairs = [jnp.where(own_lanes(0), parts[h], parts[h + 1]) for h in range(0, HB, 2)]
    return jnp.concatenate(pairs, axis=1).astype(bf16)


def attn_fwd_kernel(len_ref, q_ref, k_ref, v_ref, rel_ref, row_ref, ctx_ref, lse_ref, bias_ref, z_ref):
    length = len_ref[pl.program_id(1)]

    @pl.when((pl.program_id(0) == 0) & (pl.program_id(1) == 0))
    def _():
        spread_table(rel_ref, row_ref, z_ref, 0)

    @pl.when(pl.program_id(1) == 0)
    def _():
        build_bias(z_ref, bias_ref, pl.program_id(0))

    q, k, v = q_ref[...], k_ref[...], v_ref[...]

    def score(h):
        kf, qf = head_parts(k, q, length, h)
        return nt(qf, kf) + bias_ref[h]

    outs = []
    lanes = lax.broadcasted_iota(jnp.int32, (TOK, LANES), 1)
    lse = jnp.zeros((TOK, LANES), f32)
    s = score(0)
    for h in range(HB):
        later = score(h + 1) if h + 1 < HB else None
        top = jnp.max(s, axis=1, keepdims=True)
        p = jnp.exp(s - top)
        total = jnp.sum(p, axis=1, keepdims=True)
        outs.append(nn(p.astype(bf16), v[:, pair_lanes(h)]) * (1.0 / total))
        lse = jnp.where(lanes == h, top + jnp.log(total), lse)
        s = later
    ctx_ref[...] = join_heads(outs)
    lse_ref[0, 0] = lse.T[0:8]


def table_specs():
    return [
        pl.BlockSpec((BUCKETS, LANES), lambda hp, s, n: (0, 0)),
        pl.BlockSpec((2, SPAN), lambda hp, s, n: (0, 0)),
    ]


def attn_forward(lengths, qkv, rel, row):
    seqs = qkv.shape[0] // TOK
    spec = lambda off: pl.BlockSpec((TOK, WIDE), lambda hp, s, n: (s, off + hp))
    return pl.pallas_call(
        attn_fwd_kernel,
        grid_spec=pltpu.PrefetchScalarGridSpec(
            num_scalar_prefetch=1,
            grid=(GROUPS, seqs),
            in_specs=[spec(0), spec(GROUPS), spec(2 * GROUPS)] + table_specs(),
            out_specs=[spec(0), pl.BlockSpec((1, 1, 8, TOK), lambda hp, s, n: (hp, s, 0, 0))],
            scratch_shapes=[pltpu.VMEM((HB, TOK, TOK), f32), pltpu.VMEM((LANES, SPAN), f32)],
        ),
        out_shape=[
            jax.ShapeDtypeStruct((seqs * TOK, D), bf16),
            jax.ShapeDtypeStruct((GROUPS, seqs, 8, TOK), f32),
        ],
        compiler_params=pltpu.CompilerParams(vmem_limit_bytes=VMEM_LIMIT),
        cost_estimate=cost(27, 20),
        name="attn_forward",
    )(lengths, qkv, qkv, qkv, rel, row)


def attn_bwd_kernel(shards, len_ref, q_ref, k_ref, v_ref, do_ref, o_ref, lse_ref, rel_ref, row_ref, dqkv_ref, gt_ref, bt_ref, g_ref, z_ref, gz_ref):
    s_id = pl.program_id(1)
    length = len_ref[s_id]

    @pl.when((pl.program_id(0) == 0) & (s_id == 0))
    def _():
        spread_table(rel_ref, row_ref, z_ref, 1)
        gz_ref[...] = jnp.zeros_like(gz_ref)

    @pl.when(s_id == 0)
    def _():
        build_bias(z_ref, bt_ref, pl.program_id(0))
        g_ref[...] = jnp.zeros_like(g_ref)

    q, k, v, do = q_ref[...], k_ref[...], v_ref[...], do_ref[...]
    kt = k.astype(f32).T.astype(bf16)
    lanes8 = lax.broadcasted_iota(jnp.int32, (8, WIDE), 1)
    rows8 = lax.broadcasted_iota(jnp.int32, (8, WIDE), 0)
    pick = jnp.where(lanes8 // HD == rows8, 1.0, 0.0).astype(bf16)
    prod = do.astype(f32) * o_ref[...].astype(f32)
    upper = prod.astype(bf16)
    delta = nt(pick, upper) + nt(pick, (prod - upper.astype(f32)).astype(bf16))
    dq, dk, dv = [], [], []

    def first(h):
        kf, qf = head_parts(k, q, length, h)
        vf = jnp.where(own_lanes(h), v[:, pair_lanes(h)].astype(f32), 0.0).astype(bf16)
        return nt(kf, qf) + bt_ref[h], nt(vf, do[:, pair_lanes(h)])

    for h in range(HB):
        s, d_prob = first(h)
        p = jnp.exp(s - lse_ref[0, 0, h : h + 1, :])
        ds = p * (d_prob - delta[h : h + 1, :])
        g_ref[h] += ds
        low = ds.astype(bf16)
        dv.append(nn(p.astype(bf16), do[:, pair_lanes(h)]))
        dk.append(nn(low, q[:, pair_lanes(h)]))
        start = h % 2 * HD
        dq.append(nn(kt[pair_lanes(h)], low)[start : start + HD])
    dqkv_ref[0] = jnp.concatenate(dq, axis=0).T.astype(bf16)
    dqkv_ref[1] = join_heads(dk)
    dqkv_ref[2] = join_heads(dv)

    @pl.when(s_id == pl.num_programs(1) - 1)
    def _():
        for h in range(HB):
            total = jnp.zeros((8, SPAN), f32)
            for g in range(LANES // 8):
                tiles = [jnp.zeros((8, LANES), f32) for _ in range(SPAN // LANES)]
                for j in range(TOK // LANES):
                    x = g_ref[h, pl.ds(LANES * j + 8 * g, 8), :]
                    for t in range(TOK // LANES):
                        n = (t - j) % (SPAN // LANES)
                        tiles[n] = tiles[n] + x[:, t * LANES : (t + 1) * LANES]
                piece = jnp.concatenate(tiles, axis=1)
                total = total + (piece if g == 0 else pltpu.roll(piece, SPAN - 8 * g, 1))
            out = total[0:1]
            for s in range(1, 8):
                out = out + pltpu.roll(jnp.broadcast_to(total[s : s + 1], (8, SPAN)), SPAN - s, 1)[0:1]
            gz_ref[pl.ds(pl.program_id(0) * HB + h, 1), :] = out

    @pl.when((pl.program_id(0) == GROUPS - 1) & (s_id == pl.num_programs(1) - 1))
    def _():
        total = lax.dot_general(
            bucket_hits(row_ref, 1), gz_ref[...], (((1,), (1,)), ((), ())),
            precision=lax.Precision.HIGHEST, preferred_element_type=f32)
        gt_ref[...] = jnp.zeros_like(gt_ref)
        per = BUCKETS // shards
        for s in range(shards):
            start = s * (D // shards)
            gt_ref[0:per, start : start + HEADS] = total[s * per : (s + 1) * per, 0:HEADS]


def attn_backward(lengths, qkv, d_ctx, ctx, lse, rel, row, shards):
    seqs = qkv.shape[0] // TOK
    spec = lambda off: pl.BlockSpec((TOK, WIDE), lambda hp, s, n: (s, off + hp))
    return pl.pallas_call(
        lambda *refs: attn_bwd_kernel(shards, *refs),
        grid_spec=pltpu.PrefetchScalarGridSpec(
            num_scalar_prefetch=1,
            grid=(GROUPS, seqs),
            in_specs=[
                spec(0), spec(GROUPS), spec(2 * GROUPS), spec(0), spec(0),
                pl.BlockSpec((1, 1, 8, TOK), lambda hp, s, n: (hp, s, 0, 0)),
            ] + table_specs(),
            out_specs=[
                pl.BlockSpec((3, TOK, WIDE), lambda hp, s, n: (0, s, hp)),
                pl.BlockSpec((8, D), lambda hp, s, n: (0, 0)),
            ],
            scratch_shapes=[
                pltpu.VMEM((HB, TOK, TOK), f32), pltpu.VMEM((HB, TOK, TOK), f32),
                pltpu.VMEM((LANES, SPAN), f32), pltpu.VMEM((16, SPAN), f32),
            ],
        ),
        out_shape=[
            jax.ShapeDtypeStruct((3, seqs * TOK, D), bf16),
            jax.ShapeDtypeStruct((8, D), f32),
        ],
        compiler_params=pltpu.CompilerParams(vmem_limit_bytes=VMEM_LIMIT),
        cost_estimate=cost(46, 30),
        name="attn_backward",
    )(lengths, qkv, qkv, qkv, d_ctx, ctx, lse, rel, row)


FF = 2048
FT = 256
RC = 1024
MT = 512


def rms_scale(x):
    return lax.rsqrt(jnp.sum(x * x, axis=1, keepdims=True) * (1.0 / D) + epsilon)


def post_kernel(len_ref, shift_ref, ctx_ref, w_ref, hidden_ref, vec_ref, *refs):
    pieces, (att_ref, low_ref, low_t_ref, do_ref, do_t_ref) = refs[:-5], refs[-5:]
    s = pl.program_id(0)
    for i, piece in enumerate(pieces):
        @pl.when(shift_ref[s] == i)
        def _():
            do_ref[...] = piece[...]

    live = 2 * lax.broadcasted_iota(jnp.int32, (TOK, D), 0) < len_ref[s]
    d_out = jnp.where(live, do_ref[...].astype(f32), 0.0).astype(bf16)
    do_ref[...] = d_out
    do_t_ref[...] = d_out.T
    att = hidden_ref[...] + nn(ctx_ref[...], out_weights(w_ref))
    att_ref[...] = att
    low = (att * rms_scale(att) * vec_ref[6:7, :]).astype(bf16)
    low_ref[...] = low
    low_t_ref[...] = low.T


def rows_spec(width=D):
    return pl.BlockSpec((TOK, width), lambda s, *n: (s, 0))


def whole(*shape):
    return pl.BlockSpec(shape, lambda s, *n: (0,) * len(shape))


def out_block(shards):
    deep = D // shards
    return pl.BlockSpec((shards, 3 * deep, FT), lambda s, *n: (0, 4, 0))


def out_weights(ref):
    deep = ref.shape[1] // 3
    return jnp.concatenate([ref[:, i * deep : (i + 1) * deep, :].reshape(D, FT) for i in range(3)], axis=1)


def post_attention(lengths, shifts, ctx, pack, hidden, vecs, pieces, shards):
    rows = ctx.shape[0]
    cols_spec = pl.BlockSpec((D, TOK), lambda s, *n: (0, s))
    return pl.pallas_call(
        post_kernel,
        grid_spec=pltpu.PrefetchScalarGridSpec(
            num_scalar_prefetch=2,
            grid=(rows // TOK,),
            in_specs=[rows_spec(), out_block(shards), rows_spec(), whole(8, D)] + [whole(TOK, D)] * len(pieces),
            out_specs=[rows_spec(), rows_spec(), cols_spec, rows_spec(), cols_spec],
        ),
        out_shape=[
            jax.ShapeDtypeStruct((rows, D), f32),
            jax.ShapeDtypeStruct((rows, D), bf16),
            jax.ShapeDtypeStruct((D, rows), bf16),
            jax.ShapeDtypeStruct((rows, D), bf16),
            jax.ShapeDtypeStruct((D, rows), bf16),
        ],
        compiler_params=pltpu.CompilerParams(vmem_limit_bytes=VMEM_LIMIT),
        cost_estimate=cost(10, 30),
        name="post_attention",
    )(lengths, shifts, ctx, pack, hidden, vecs, *pieces)


def gelu_parts(v):
    c = 0.7978845608
    v2 = v * v
    t = jnp.tanh(v * (c + (c * 0.044715) * v2))
    half = 0.5 + 0.5 * t
    gelu = v * half
    slope = half + (0.5 * v) * (1.0 - t * t) * (c + (3.0 * c * 0.044715) * v2)
    return gelu, slope


def ffn_steps(x_any, d_any, xt_any, dt_any, wgu_ref, wo_ref, grad_ref, y_any, dx_any,
              x_ref, d_ref, xt_ref, dt_ref, y_ref, dx_ref, a_ref, dg_ref, du_ref, gu_ref, go_ref, in_sem, out_sem, sems,
              low_ref=None):
    f = pl.program_id(0)
    steps = FF // 2 // FT
    rows_total = x_ref.shape[0]
    chunks = rows_total // RC
    shards, part = gu_ref.shape[1], gu_ref.shape[2]
    owners, deep = go_ref.shape[1], go_ref.shape[2]
    base = steps * part

    def copies(slot, step):
        return (
            pltpu.make_async_copy(
                gu_ref.at[slot], grad_ref.at[:, pl.ds(step * part, part), :], sems.at[0, slot]),
            pltpu.make_async_copy(
                go_ref.at[slot], grad_ref.at[pl.ds(step * owners, owners), pl.ds(base, deep), :], sems.at[1, slot]),
        )

    def row_loads(i):
        rows = pl.ds(i * RC, RC)
        return (
            pltpu.make_async_copy(x_any.at[rows], x_ref.at[rows], in_sem.at[0, i]),
            pltpu.make_async_copy(d_any.at[rows], d_ref.at[rows], in_sem.at[1, i]),
        )

    def turned_loads():
        return (
            pltpu.make_async_copy(xt_any, xt_ref, in_sem.at[2, 0]),
            pltpu.make_async_copy(dt_any, dt_ref, in_sem.at[2, 1]),
        )

    def row_stores(i):
        rows = pl.ds(i * RC, RC)
        return (
            pltpu.make_async_copy(low_ref.at[0, rows], y_any.at[rows], out_sem.at[0, i]),
            pltpu.make_async_copy(low_ref.at[1, rows], dx_any.at[rows], out_sem.at[1, i]),
        )

    @pl.when(f == 0)
    def _():
        for i in range(chunks):
            for copy in row_loads(i):
                copy.start()
        for copy in turned_loads():
            copy.start()

    d_rows = part // 2
    third = deep // 3
    wg = wgu_ref[:, 0:d_rows, :].reshape(D, FT)
    wu = wgu_ref[:, d_rows:part, :].reshape(D, FT)
    wo = jnp.concatenate(
        [wo_ref[:, i * third : (i + 1) * third, :].reshape(FT, FT) for i in range(3)], axis=1)

    @pl.when(f == 0)
    def _():
        for i in range(chunks):
            for copy in row_loads(i):
                copy.wait()

    def chunk(i, carry):
        rows = pl.ds(pl.multiple_of(i * RC, RC), RC)
        x, d = x_ref[rows, :], d_ref[rows, :]
        gelu, slope = gelu_parts(nn(x, wg))
        up = nn(x, wu)
        da = nt(d, wo)
        act = (gelu * up).astype(bf16)
        dg = (da * up * slope).astype(bf16)
        du = (da * gelu).astype(bf16)
        a_ref[rows, :] = act
        dg_ref[rows, :] = dg
        du_ref[rows, :] = du
        y_ref[rows, :] = nn(act, wo) + jnp.where(f == 0, 0.0, y_ref[rows, :])
        dx_ref[rows, :] = nt(dg, wg) + nt(du, wu) + jnp.where(f == 0, 0.0, dx_ref[rows, :])
        return carry

    lax.fori_loop(0, chunks, chunk, 0)
    if y_any is not None:

        @pl.when(f == steps - 1)
        def _():
            for i in range(chunks):
                rows = pl.ds(i * RC, RC)
                low_ref[0, rows, :] = y_ref[rows, :].astype(bf16)
                low_ref[1, rows, :] = dx_ref[rows, :].astype(bf16)
                for copy in row_stores(i):
                    copy.start()

    slot = lax.rem(f, 2)

    @pl.when(f == 0)
    def _():
        for copy in turned_loads():
            copy.wait()

    @pl.when(f >= 2)
    def _():
        for copy in copies(slot, f - 2):
            copy.wait()

    gu_ref[slot, :, 0:d_rows, :] = nn(xt_ref[...], dg_ref[...]).astype(bf16).reshape(shards, d_rows, FT)
    gu_ref[slot, :, d_rows:part, :] = nn(xt_ref[...], du_ref[...]).astype(bf16).reshape(shards, d_rows, FT)
    go = nn(dt_ref[...], a_ref[...]).T.astype(bf16)
    for i in range(3):
        go_ref[slot, :, i * third : (i + 1) * third, :] = go[:, i * FT : (i + 1) * FT].reshape(owners, third, FT)
    for copy in copies(slot, f):
        copy.start()

    @pl.when(f == steps - 1)
    def _():
        for copy in copies(1 - slot, f - 1) + copies(slot, f):
            copy.wait()
        if y_any is not None:
            for i in range(chunks):
                for copy in row_stores(i):
                    copy.wait()


def first_kernel(x, d, xt, dt, wgu, wo, grad, y, dx, *scratch):
    ffn_steps(x, d, xt, dt, wgu, wo, grad, y, dx, *scratch)


def second_kernel(len_ref, x, d, xt, dt, wgu, wo, att_ref, y1_ref, dx1_ref, do_ref, ctx_ref, w_ref, vec_ref,
                  grad, out_ref, datt_ref, dctx_ref, gg_ref, acc_ref, flat_ref, join_ref, join_sem, *scratch):
    f = pl.program_id(0)
    steps = FF // 2 // FT

    @pl.when(f == 0)
    def _():
        acc_ref[...] = jnp.zeros_like(acc_ref)
        gg_ref[...] = jnp.zeros_like(gg_ref)
        flat_ref[...] = out_weights(w_ref)

    @pl.when(f < steps)
    def _():
        ffn_steps(x, d, xt, dt, wgu, wo, grad, None, None, *scratch)

    @pl.when(f >= steps)
    def _():
        tile = f - steps
        y_ref, dx_ref = scratch[4], scratch[5]
        rows = pl.ds(pl.multiple_of(tile * MT, MT), MT)
        per = TOK // MT
        length = len_ref[tile // per]
        place_in = lax.rem(tile, per) * MT + lax.broadcasted_iota(jnp.int32, (MT, 1), 0)
        live = jnp.where(2 * place_in < length, 1.0, 0.0).astype(f32)
        att = att_ref[...]
        out_ref[...] = ((att + y1_ref[...].astype(f32) + y_ref[rows, :]) * live).astype(bf16)
        back, gain_grad = norm_back(att, dx1_ref[...].astype(f32) + dx_ref[rows, :], vec_ref[6:7, :])
        gg_ref[...] += gain_grad
        d_att = do_ref[...].astype(f32) + back
        low = d_att.astype(bf16)
        datt_ref[...] = low
        dctx_ref[...] = nt(low, flat_ref[...]).astype(bf16)
        acc_ref[...] += nn(ctx_ref[...].T, low)

    @pl.when(f == pl.num_programs(0) - 1)
    def _():
        shards, deep = join_ref.shape[0], join_ref.shape[1] // 3
        for i in range(3):
            block = acc_ref[:, i * FT : (i + 1) * FT].astype(bf16).reshape(shards, deep, FT)
            join_ref[:, i * deep : (i + 1) * deep, :] = block
        copy = pltpu.make_async_copy(join_ref, grad.at[:, pl.ds(grad.shape[1] - 3 * deep, 3 * deep), :], join_sem)
        copy.start()
        copy.wait()


def ffn_scratch(rows, shards):
    part, hs = 2 * D // shards, FF // 2 // shards
    return [
        pltpu.VMEM((rows, D), bf16),
        pltpu.VMEM((rows, D), bf16),
        pltpu.VMEM((D, rows), bf16),
        pltpu.VMEM((D, rows), bf16),
        pltpu.VMEM((rows, D), f32),
        pltpu.VMEM((rows, D), f32),
        pltpu.VMEM((rows, FT), bf16),
        pltpu.VMEM((rows, FT), bf16),
        pltpu.VMEM((rows, FT), bf16),
        pltpu.VMEM((2, shards, part, FT), bf16),
        pltpu.VMEM((2, FT // hs, 3 * hs, FT), bf16),
        pltpu.SemaphoreType.DMA((3, max(2, rows // RC))),
        pltpu.SemaphoreType.DMA((2, rows // RC)),
        pltpu.SemaphoreType.DMA((2, 2)),
    ]


def ffn_specs(tiles, shards):
    last = lambda f: jnp.minimum(f, tiles - 1)
    part, hs = 2 * D // shards, FF // 2 // shards
    return [pl.BlockSpec(memory_space=pl.ANY)] * 4 + [
        pl.BlockSpec((shards, part, FT), lambda f, *n: (0, last(f), 0)),
        pl.BlockSpec((FT // hs, 3 * hs, FT), lambda f, *n: (last(f), 2, 0)),
    ]


def grad_shape(shards, more=0):
    part, hs = 2 * D // shards, FF // 2 // shards
    return jax.ShapeDtypeStruct((shards, FF // 2 // FT * part + 3 * hs + more, FT), bf16)


def ffn_first(x, d_out, xt, dt, pack, shards):
    rows = x.shape[0]
    tiles = FF // 2 // FT
    anywhere = pl.BlockSpec(memory_space=pl.ANY)
    return pl.pallas_call(
        first_kernel,
        grid=(tiles,),
        in_specs=ffn_specs(tiles, shards),
        out_specs=[anywhere] * 3,
        out_shape=[
            grad_shape(shards),
            jax.ShapeDtypeStruct((rows, D), bf16),
            jax.ShapeDtypeStruct((rows, D), bf16),
        ],
        scratch_shapes=ffn_scratch(rows, shards) + [pltpu.VMEM((2, rows, D), bf16)],
        compiler_params=pltpu.CompilerParams(vmem_limit_bytes=VMEM_LIMIT),
        cost_estimate=cost(36, 40),
        name="ffn_first",
    )(x, d_out, xt, dt, pack, pack)


def ffn_second(lengths, x, d_out, xt, dt, pack, att, y1, dx1, ctx, pack0, vecs, shards):
    rows = x.shape[0]
    tiles = FF // 2 // FT
    tile_rows = pl.BlockSpec((MT, D), lambda f, n: (jnp.maximum(f - tiles, 0), 0))
    return pl.pallas_call(
        second_kernel,
        grid_spec=pltpu.PrefetchScalarGridSpec(
            num_scalar_prefetch=1,
            grid=(tiles + rows // MT,),
            in_specs=ffn_specs(tiles, shards) + [tile_rows] * 5 + [out_block(shards), whole(8, D)],
            out_specs=[pl.BlockSpec(memory_space=pl.ANY), tile_rows, tile_rows, tile_rows, whole(1, D)],
            scratch_shapes=[
                pltpu.VMEM((D, D), f32), pltpu.VMEM((D, D), bf16),
                pltpu.VMEM((shards, 3 * D // shards, FT), bf16), pltpu.SemaphoreType.DMA,
            ] + ffn_scratch(rows, shards),
        ),
        out_shape=[
            grad_shape(shards, 3 * D // shards),
            jax.ShapeDtypeStruct((rows, D), bf16),
            jax.ShapeDtypeStruct((rows, D), bf16),
            jax.ShapeDtypeStruct((rows, D), bf16),
            jax.ShapeDtypeStruct((1, D), f32),
        ],
        compiler_params=pltpu.CompilerParams(vmem_limit_bytes=VMEM_LIMIT),
        cost_estimate=cost(46, 60),
        name="ffn_second",
    )(lengths, x, d_out, xt, dt, pack, pack, att, y1, dx1, d_out, ctx, pack0, vecs)


def norm_back(x, grad, gain):
    r = rms_scale(x)
    n = x * r
    u = gain * grad
    mean = jnp.sum(n * u, axis=1, keepdims=True) * (1.0 / D)
    return r * (u - n * mean), jnp.sum(n * grad, axis=0, keepdims=True)


def qkv_grad_kernel(dqkv_ref, normed_t_ref, gw_ref):
    gw_ref[...] = nn(normed_t_ref[...], dqkv_ref[0]).astype(bf16)


def qkv_grad(dqkv, normed_t):
    rows = normed_t.shape[1]
    return pl.pallas_call(
        qkv_grad_kernel,
        grid=(3,),
        in_specs=[pl.BlockSpec((1, rows, D), lambda i: (i, 0, 0)), whole(D, rows)],
        out_specs=pl.BlockSpec((D, D), lambda i: (0, i)),
        out_shape=jax.ShapeDtypeStruct((D, 3 * D), bf16),
        compiler_params=pltpu.CompilerParams(vmem_limit_bytes=VMEM_LIMIT),
        cost_estimate=cost(11, 20),
        name="qkv_grad",
    )(dqkv, normed_t)


def qkv_back_kernel(dqkv_ref, w_ref, hidden_ref, datt_ref, vec_ref, dh_ref, gg_ref):
    @pl.when(pl.program_id(0) == 0)
    def _():
        gg_ref[...] = jnp.zeros_like(gg_ref)

    dn = nt(dqkv_ref[0], w_ref[:, 0:D])
    for i in range(1, 3):
        dn = dn + nt(dqkv_ref[i], w_ref[:, i * D : (i + 1) * D])
    back, gain_grad = norm_back(hidden_ref[...].astype(f32), dn, vec_ref[5:6, :])
    gg_ref[...] += gain_grad
    dh_ref[...] = (datt_ref[...].astype(f32) + back).astype(bf16)


def qkv_backward(dqkv, attn_w, hidden, d_att, vecs):
    rows = hidden.shape[0]
    tile = pl.BlockSpec((TOK, D), lambda s: (s, 0))
    return pl.pallas_call(
        qkv_back_kernel,
        grid=(rows // TOK,),
        in_specs=[
            pl.BlockSpec((3, TOK, D), lambda s: (0, s, 0)),
            pl.BlockSpec((D, 3 * D), lambda s: (0, 0)),
            tile, tile, whole(8, D),
        ],
        out_specs=[tile, whole(1, D)],
        out_shape=[jax.ShapeDtypeStruct((rows, D), bf16), jax.ShapeDtypeStruct((1, D), f32)],
        compiler_params=pltpu.CompilerParams(vmem_limit_bytes=VMEM_LIMIT),
        cost_estimate=cost(14, 40),
        name="qkv_backward",
    )(dqkv, attn_w, hidden, d_att, vecs)


MESH = pl.DeviceIdType.MESH


def greet(peers):
    barrier = pltpu.get_barrier_semaphore()
    for peer in peers:
        pl.semaphore_signal(barrier, inc=1, device_id=peer, device_id_type=MESH)
    pl.semaphore_wait(barrier, len(peers))


def pack_half(out_ref, ffn_in_ref, ffn_out_ref, h, shards):
    hs = FF // 2 // shards
    owners = FT // hs
    deep = ffn_in_ref.shape[0]
    row = 0
    for f in range(FF // 2 // FT):
        for g in range(2):
            starts = [g * FF + (f * owners + o) * 2 * hs + h * hs for o in range(owners)]
            out_ref[row : row + deep, :] = jnp.concatenate([ffn_in_ref[:, a : a + hs] for a in starts], axis=1)
            row += deep
    for i in range(3):
        out_ref[row : row + hs, :] = ffn_out_ref[h * hs : (h + 1) * hs, i * FT : (i + 1) * FT]
        row += hs
    return row


def prepare_kernel(replicas, shards, length_ref, target_ref, embed_ref, conv_ref, score_ref, gain1_ref, gain2_ref, rel_ref,
                   ids_ref, attn_out_ref, ffn_in_ref, ffn_out_ref,
                   table_ref, vec_ref, table_rel_ref, slots_ref, column_ref, row_ref, pack0_ref, pack1_ref,
                   own_ref, wide_ref, turn_ref, nat_ref, wanted_ref, send_sem, recv_sem):
    rep, me = lax.axis_index("rep"), lax.axis_index("shard")
    deep = embed_ref.shape[1]
    seqs = ids_ref.shape[0]
    twin = me + 1 - 2 * lax.rem(me, 2)
    far = [lax.rem(me + 2 * i, shards) for i in range(1, shards // 2)]
    others = [lax.rem(rep + i, replicas) for i in range(1, replicas)]
    greet([(rep, twin)] + [(rep, p) for p in far] + [(p, me) for p in others])

    def send(i, src, dst, device):
        copy = pltpu.make_async_remote_copy(
            src_ref=src, dst_ref=dst, send_sem=send_sem.at[i], recv_sem=recv_sem.at[i],
            device_id=device, device_id_type=MESH)
        copy.start()
        return copy

    wide_ref[...] = jnp.zeros_like(wide_ref)
    wide_ref[0:VOCAB, 0:deep] = embed_ref[...].astype(f32)
    wide_ref[VOCAB : VOCAB + 4, 0:deep] = conv_ref[...].astype(f32)
    for i, ref in enumerate((score_ref, gain1_ref, gain2_ref)):
        wide_ref[VOCAB + 4 + i : VOCAB + 5 + i, 0:deep] = ref[...].astype(f32).reshape(1, deep)
    rel_rows, heads = rel_ref.shape
    wide_ref[VOCAB + 7 : VOCAB + 7 + rel_rows, 0:heads] = rel_ref[...].astype(f32)
    own_ref[...] = wide_ref[...].T[0:deep].astype(bf16)
    near = [send(0, own_ref, table_ref.at[me], (rep, twin))]
    direct = [send(1 + i, own_ref, table_ref.at[me], (rep, p)) for i, p in enumerate(far)]
    lanes = lax.broadcasted_iota(jnp.int32, (8, 128), 1)
    wanted = jnp.zeros((8, 128), jnp.int32)
    for k in range(seqs):
        slot = target_ref[k] % seqs
        wanted = wanted + jnp.where(lanes == target_ref[k] // seqs // shards, slot + 1, 0)
    wanted_ref[...] = wanted
    base = shards
    asks = [send(base + i, wanted_ref, slots_ref.at[rep], (p, me)) for i, p in enumerate(others)]
    table_ref[me] = own_ref[...]
    slots_ref[rep] = wanted_ref[...]
    row = pack_half(pack0_ref, ffn_in_ref, ffn_out_ref, 0, shards)
    for i in range(3):
        pack0_ref[row : row + deep, :] = attn_out_ref[:, i * FT : (i + 1) * FT]
        row += deep
    pack_half(pack1_ref, ffn_in_ref, ffn_out_ref, 1, shards)
    base = base + replicas - 1
    for i, copy in enumerate(direct):
        copy.wait()
        source = lax.rem(me - 2 * (i + 1) + shards, shards)
        near.append(send(base + i, table_ref.at[source], table_ref.at[source], (rep, twin)))
    turn_ref[...] = jnp.full(turn_ref.shape, -1.0, f32)
    place = lax.broadcasted_iota(jnp.int32, (1, MAXLEN), 1)
    for s in range(seqs):
        live = jnp.where(place < length_ref[s], ids_ref[s : s + 1, :], -1)
        row_ref[s] = live
        turn_ref[s : s + 1, 0:MAXLEN] = live.astype(f32)
    nat_ref[...] = turn_ref[...].T
    for r in range(R):
        rows = nat_ref[pl.ds(r, QN, stride=R), :]
        for s in range(seqs):
            column_ref[s, r * QN : (r + 1) * QN, :] = jnp.broadcast_to(rows[:, s : s + 1], (QN, 128))
    for copy in near + asks:
        copy.wait()
    last = table_ref[:, :, SMALL - 128 :].astype(f32).reshape(D, 128).T
    first = VOCAB - (SMALL - 128)
    vec_ref[...] = last[first : first + 8]
    table_rel_ref[...] = jnp.zeros_like(table_rel_ref)
    for s in range(shards):
        block = last[first + 7 : first + 7 + rel_rows, s * deep : s * deep + heads]
        table_rel_ref[s * rel_rows : (s + 1) * rel_rows, 0:heads] = block


def prepare(lengths, target, embed, conv_w, score_w, gain_attn, gain_ffn, rel_table, ids, attn_out, ffn_in, ffn_out,
            replicas, shards):
    deep = embed.shape[1]
    seqs = ids.shape[0]
    part, hs = 2 * D // shards, FF // 2 // shards
    rows = FF // 2 // FT * part + 3 * hs
    sems = shards + replicas - 1 + shards // 2 - 1
    vmem = pl.BlockSpec(memory_space=pltpu.VMEM)
    smem = pl.BlockSpec(memory_space=pltpu.SMEM)
    return pl.pallas_call(
        lambda *refs: prepare_kernel(replicas, shards, *refs),
        out_shape=[
            jax.ShapeDtypeStruct((shards, deep, SMALL), bf16),
            jax.ShapeDtypeStruct((8, D), f32),
            jax.ShapeDtypeStruct((BUCKETS, 128), f32),
            jax.ShapeDtypeStruct((replicas, 8, 128), jnp.int32),
            jax.ShapeDtypeStruct((seqs, P_ROWS, 128), f32),
            jax.ShapeDtypeStruct((seqs, 1, MAXLEN), jnp.int32),
            jax.ShapeDtypeStruct((rows + 3 * deep, FT), bf16),
            jax.ShapeDtypeStruct((rows, FT), bf16),
        ],
        in_specs=[smem] * 2 + [vmem] * 10,
        out_specs=[vmem] * 8,
        scratch_shapes=[
            pltpu.VMEM((deep, SMALL), bf16),
            pltpu.VMEM((SMALL, 128), f32),
            pltpu.VMEM((128, 1152), f32),
            pltpu.VMEM((1152, 128), f32),
            pltpu.VMEM((8, 128), jnp.int32),
            pltpu.SemaphoreType.DMA((sems,)),
            pltpu.SemaphoreType.DMA((sems,)),
        ],
        compiler_params=pltpu.CompilerParams(collective_id=1, has_side_effects=True, vmem_limit_bytes=VMEM_LIMIT),
        cost_estimate=cost(12, 8),
        name="prepare",
    )(lengths, target, embed, conv_w, score_w, gain_attn, gain_ffn, rel_table, ids, attn_out, ffn_in, ffn_out)


def pick_kernel(order_ref, in_ref, *out_refs):
    for i, ref in enumerate(out_refs):
        @pl.when(pl.program_id(0) == i)
        def _():
            ref[...] = in_ref[0]


def pick(order, rows):
    count = order.shape[0]
    block = (rows.shape[1], rows.shape[2])
    return pl.pallas_call(
        pick_kernel,
        grid_spec=pltpu.PrefetchScalarGridSpec(
            num_scalar_prefetch=1,
            grid=(count,),
            in_specs=[pl.BlockSpec((1,) + block, lambda i, order: (order[i], 0, 0))],
            out_specs=[pl.BlockSpec(block, lambda i, order: (0, 0))] * count,
        ),
        out_shape=[jax.ShapeDtypeStruct(block, rows.dtype)] * count,
        compiler_params=pltpu.CompilerParams(vmem_limit_bytes=VMEM_LIMIT),
        cost_estimate=cost(4, 6),
        name="pick",
    )(order, rows)


def finish_kernel(replicas, shards, piece_ref, small_ref, in_ref, embed_ref, conv_ref, rest_ref,
                  twin_ref, both_ref, far_ref, held_ref, other_ref, part_ref, part2_ref, last_ref,
                  twin_send, twin_recv, far_send, far_recv, send_sem, recv_sem, send2_sem, recv2_sem):
    rep, me = lax.axis_index("rep"), lax.axis_index("shard")
    half = piece_ref.shape[1]
    chips = shards // 2
    core = lax.rem(me, 2)
    twin = me + 1 - 2 * core
    bits = [1 << b for b in range(replicas.bit_length() - 1)]
    orders = (bits, bits[::-1])
    far = [lax.rem(me + 2 * i, shards) for i in range(1, chips)]
    partners = {}
    for bit in bits:
        down = lax.rem(rep // bit, 2)
        partners[bit] = (rep + bit - 2 * bit * down, me)
    greet([(rep, twin)] + [(rep, p) for p in far] + [partners[bit] for bit in bits])

    def send(src, dst, sems, i, device):
        copy = pltpu.make_async_remote_copy(
            src_ref=src, dst_ref=dst, send_sem=sems[0].at[i], recv_sem=sems[1].at[i],
            device_id=device, device_id_type=MESH)
        copy.start()
        return copy

    near = [
        send(small_ref.at[2 * z + 1 - core], twin_ref.at[z], (twin_send, twin_recv), z, (rep, twin))
        for z in range(chips)
    ]

    def exchange(t, mine, theirs, sems):
        return [send(mine.at[t, h], theirs.at[t, h], sems, (t, h), partners[orders[h][t]]) for h in range(2)]

    held_ref[0] = piece_ref[...]
    large = exchange(0, held_ref, other_ref, (send_sem, recv_sem))
    for z, copy in enumerate(near):
        copy.wait()
        both_ref[z] = (small_ref[2 * z + core].astype(f32) + twin_ref[z].astype(f32)).astype(bf16)
    away = [send(both_ref.at[p // 2], far_ref.at[i], (far_send, far_recv), i, (rep, p)) for i, p in enumerate(far)]
    last_ref[...] = jnp.zeros_like(last_ref)

    def settle(t, copies, mine, theirs, out):
        for h, copy in enumerate(copies):
            copy.wait()
            total = mine[t, h].astype(f32) + theirs[t, h].astype(f32)
            if t == len(bits) - 1:
                out[h * half : (h + 1) * half, :] = total
            else:
                mine[t + 1, h] = total.astype(bf16)

    settle(0, large, held_ref, other_ref, in_ref)
    large = exchange(1, held_ref, other_ref, (send_sem, recv_sem))
    total = both_ref[me // 2].astype(f32)
    for i, copy in enumerate(away):
        copy.wait()
        total = total + far_ref[i].astype(f32)
    part_ref[0] = total.astype(bf16)
    for t in range(len(bits)):
        little = exchange(t, part_ref, part2_ref, (send2_sem, recv2_sem))
        if t > 0:
            settle(t, large, held_ref, other_ref, in_ref)
            if t < len(bits) - 1:
                large = exchange(t + 1, held_ref, other_ref, (send_sem, recv_sem))
        settle(t, little, part_ref, part2_ref, last_ref)
    turned = last_ref[...].T
    deep = embed_ref.shape[1]
    embed_ref[...] = turned[0:VOCAB, 0:deep]
    conv_ref[...] = turned[VROWS : VROWS + 4, 0:deep]
    rest_ref[...] = turned[VROWS : VROWS + 16, 0:deep]


def finish(piece, small, replicas, shards):
    rows, wide = piece.shape
    half = rows // 2
    chips = shards // 2
    steps = replicas.bit_length() - 1
    vmem = pl.BlockSpec(memory_space=pltpu.VMEM)
    sems = lambda *shape: [pltpu.SemaphoreType.DMA(shape), pltpu.SemaphoreType.DMA(shape)]
    return pl.pallas_call(
        lambda *refs: finish_kernel(replicas, shards, *refs),
        out_shape=[
            jax.ShapeDtypeStruct((rows, wide), f32),
            jax.ShapeDtypeStruct((VOCAB, rows), f32),
            jax.ShapeDtypeStruct((4, rows), f32),
            jax.ShapeDtypeStruct((16, rows), f32),
        ],
        in_specs=[vmem] * 2,
        out_specs=[vmem] * 4,
        scratch_shapes=[
            pltpu.VMEM((chips, 2, half, SMALL), bf16),
            pltpu.VMEM((chips, 2, half, SMALL), bf16),
            pltpu.VMEM((chips - 1, 2, half, SMALL), bf16),
            pltpu.VMEM((steps, 2, half, wide), bf16),
            pltpu.VMEM((steps, 2, half, wide), bf16),
            pltpu.VMEM((steps, 2, half, SMALL), bf16),
            pltpu.VMEM((steps, 2, half, SMALL), bf16),
            pltpu.VMEM((128, SMALL), f32),
        ] + sems(chips) + sems(chips - 1) + sems(steps, 2) + sems(steps, 2),
        compiler_params=pltpu.CompilerParams(
            collective_id=2, has_side_effects=True, vmem_limit_bytes=VMEM_LIMIT),
        cost_estimate=cost(20, 4),
        name="finish_sums",
    )(piece.reshape(2, half, wide), small.reshape(shards, 2, half, SMALL))


def deliver_kernel(in_ref, embed_ref, conv_ref, rest_ref, in_out, embed_out, conv_out, score_out, gain1_out, gain2_out, rel_out):
    in_out[...] = in_ref[...]
    embed_out[...] = embed_ref[...]
    conv_out[...] = conv_ref[...]
    for i, ref in enumerate((score_out, gain1_out, gain2_out)):
        ref[...] = rest_ref[4 + i : 5 + i, :].reshape(ref.shape)
    rel_out[...] = rest_ref[7 : 7 + rel_out.shape[0], 0 : rel_out.shape[1]]


def deliver(parts, rel_rows):
    deep = parts[0].shape[0]
    vmem = pl.BlockSpec(memory_space=pltpu.VMEM)
    line = jax.ShapeDtypeStruct((deep,), f32)
    return pl.pallas_call(
        deliver_kernel,
        out_shape=[jax.ShapeDtypeStruct(x.shape, f32) for x in parts[:3]]
        + [line] * 3 + [jax.ShapeDtypeStruct((rel_rows, HEADS), f32)],
        in_specs=[vmem] * 4,
        out_specs=[vmem] * 7,
        compiler_params=pltpu.CompilerParams(vmem_limit_bytes=VMEM_LIMIT),
        cost_estimate=cost(2, 2),
        name="deliver",
    )(*parts)


def unpack_kernel(shards, first_ref, first_other_ref, second_ref, second_other_ref, in_ref, out_ref, attn_ref):
    hs = FF // 2 // shards
    deep = in_ref.shape[0]
    owners = FT // hs
    for h in range(2):
        def load(start, count):
            rows = slice(start, start + count)
            mine, theirs = ((first_ref, first_other_ref), (second_ref, second_other_ref))[h]
            return mine[rows, :].astype(f32) + theirs[rows, :].astype(f32)

        row = 0
        for f in range(FF // 2 // FT):
            for g in range(2):
                x = load(row, deep)
                for o in range(owners):
                    start = g * FF + (f * owners + o) * 2 * hs + h * hs
                    in_ref[:, start : start + hs] = x[:, o * hs : (o + 1) * hs]
                row += deep
        for i in range(3):
            out_ref[h * hs : (h + 1) * hs, i * FT : (i + 1) * FT] = load(row, hs)
            row += hs
        if h == 1:
            for i in range(3):
                attn_ref[:, i * FT : (i + 1) * FT] = load(row + i * deep, deep)


def unpack(first, first_other, second, second_other, shards):
    vmem = pl.BlockSpec(memory_space=pltpu.VMEM)
    return pl.pallas_call(
        lambda *refs: unpack_kernel(shards, *refs),
        out_shape=[
            jax.ShapeDtypeStruct((D // shards, 2 * FF), f32),
            jax.ShapeDtypeStruct((FF // shards, D), f32),
            jax.ShapeDtypeStruct((D // shards, D), f32),
        ],
        in_specs=[vmem] * 4,
        out_specs=[vmem] * 3,
        compiler_params=pltpu.CompilerParams(vmem_limit_bytes=VMEM_LIMIT),
        cost_estimate=cost(3, 5),
        name="unpack",
    )(first, first_other, second, second_other)


def send_cotangent(slots, cotangent):
    replicas = lax.axis_size("rep")
    places = jnp.arange(replicas)
    rep = lax.axis_index("rep")
    asked = jnp.where(places[None, :] == rep, slots, 0).sum(axis=1) - 1
    turned = (places[None, :] == (rep + places[:, None]) % replicas) * asked[None, :]
    pieces = list(pick(jnp.maximum(turned.sum(axis=1), 0), cotangent))
    for shift in range(1, replicas):
        pieces[shift] = lax.ppermute(pieces[shift], "rep", [(r, (r + shift) % replicas) for r in range(replicas)])
    return pieces


def swap(x, bit):
    replicas = lax.axis_size("rep")
    return lax.ppermute(x, "rep", [(r, r ^ bit) for r in range(replicas)])


def add_low(a, b):
    return (a.astype(f32) + b.astype(f32)).astype(bf16)


def scatter_sum(grad):
    return lax.psum_scatter(grad, "shard", scatter_dimension=0, tiled=True)


def body(
    byte_ids, lengths, target, rel_bucket, cotangent, embed, conv_w, score_w, gain_attn,
    attn_in, attn_out, gain_ffn, ffn_in, ffn_out, rel_table,
):
    seqs = byte_ids.shape[0]
    replicas, shards = lax.axis_size("rep"), lax.axis_size("shard")
    attn_w = lax.all_gather(attn_in, "shard", axis=0, tiled=True)
    table, vecs, rel, slots, ids_col, ids_row, pack0, pack1 = prepare(
        lengths, target, embed, conv_w, score_w, gain_attn, gain_ffn, rel_table, byte_ids,
        attn_out, ffn_in, ffn_out, replicas, shards,
    )
    packs = [lax.all_gather(pack, "shard", axis=0) for pack in (pack0, pack1)]
    rows = bucket_rows(rel_bucket)

    hidden, hidden_low, normed, normed_t, convolved, weights, e_low, coefs = gbst_forward(lengths, ids_col, table, vecs)
    qkv = jnp.dot(normed, attn_w, preferred_element_type=f32).astype(bf16)
    qkv, slots = lax.optimization_barrier((qkv, slots))
    pieces = send_cotangent(slots[:, 0, :replicas], cotangent)
    ctx, lse = attn_forward(lengths, qkv, rel, rows)
    ctx, pieces = lax.optimization_barrier((ctx, pieces))
    shifts = (lax.axis_index("rep") - target // seqs // shards) % replicas
    attended, low, low_t, d_out, d_out_t = post_attention(
        lengths, shifts, ctx, packs[0], hidden, vecs, pieces, shards
    )
    g_half1, y1, dx1 = ffn_first(low, d_out, low_t, d_out_t, packs[0], shards)
    g_half2, out, d_att, d_ctx, g_gain_ffn = ffn_second(
        lengths, low, d_out, low_t, d_out_t, packs[1], attended, y1, dx1, ctx, packs[0], vecs, shards
    )
    one, two = [scatter_sum(g.reshape(-1, FT)) for g in (g_half1, g_half2)]
    bits = [1 << b for b in range(replicas.bit_length() - 1)]
    d_ctx, one = lax.optimization_barrier((d_ctx, one))
    other = swap(one, bits[0])
    dqkv, g_rel = attn_backward(lengths, qkv, d_ctx, ctx, lse, rel, rows, shards)
    dqkv, other = lax.optimization_barrier((dqkv, other))
    one = add_low(one, other)
    g_attn = qkv_grad(dqkv, normed_t)
    g_attn, two = lax.optimization_barrier((g_attn, two))
    p_attn = scatter_sum(g_attn)
    for bit in bits[1:-1]:
        one = add_low(one, swap(one, bit))
    others = swap(one, bits[-1]), swap(two, bits[0])
    d_hidden, g_gain_attn = qkv_backward(dqkv, attn_w, hidden_low, d_att, vecs)
    d_hidden, others = lax.optimization_barrier((d_hidden, others))
    other_one, two = others[0], add_low(two, others[1])
    for bit in bits[1:-1]:
        two = add_low(two, swap(two, bit))
    d_hidden, two = lax.optimization_barrier((d_hidden, two))
    other = swap(two, bits[-1])
    input_grad, small = gbst_backward(
        ids_row, vecs, d_hidden, convolved, weights, e_low, coefs,
        g_gain_attn, g_gain_ffn, g_rel,
    )
    small, other = lax.optimization_barrier((small, other))
    parts = finish(p_attn, small, replicas, shards)
    s_ffn_in, s_ffn_out, s_attn_out = unpack(one, other_one, two, other, shards)
    s_attn_in, s_embed, s_conv, s_score, s_gain_attn, s_gain_ffn, s_rel = deliver(parts, rel_table.shape[0])
    return (
        out.reshape(seqs, TOK, D), input_grad, s_embed, s_conv, s_score, s_gain_attn, s_attn_in, s_attn_out,
        s_gain_ffn, s_ffn_in, s_ffn_out, s_rel,
    )


def solution(mesh):
    in_specs = (
        P(("rep", "shard"), None), P(("rep", "shard")), P(("rep", "shard")), P(),
        P(("rep", "shard"), None, None), P(None, "shard"), P(None, "shard"), P("shard"), P("shard"),
        P("shard", None), P("shard", None), P("shard"), P("shard", None), P("shard", None), P("shard", None),
    )
    out_specs = (
        P(("rep", "shard"), None, None), P(("rep", "shard"), None, None), P(None, "shard"), P(None, "shard"),
        P("shard"), P("shard"), P("shard", None), P("shard", None), P("shard"), P("shard", None),
        P("shard", None), P("shard", None),
    )
    return jax.shard_map(body, mesh=mesh, in_specs=in_specs, out_specs=out_specs, check_vma=False)
```

```python
import jax
import jax.numpy as jnp
from jax import lax
from jax.experimental import pallas as pl
from jax.experimental.pallas import tpu as pltpu
from jax.sharding import PartitionSpec as P

D = 768
VOCAB = 259
VROWS = 272
VMEM_LIMIT = 60 << 20
SMALL = 384
MAXLEN = 1024
TOK = 512
LANES = 128
QN = 88
R = 12
P_ROWS = QN * R
T_ROWS = 528
LT = D // LANES
epsilon = 1e-06
f32 = jnp.float32
bf16 = jnp.bfloat16


def cost(us, mib):
    return pl.CostEstimate(flops=int(us * 1e9), bytes_accessed=mib << 20, transcendentals=0)


def lane_iota(rows):
    return lax.broadcasted_iota(jnp.int32, (rows, LANES), 1)


def group_matrix(b):
    row = lax.broadcasted_iota(jnp.int32, (LANES, LANES), 0)
    col = lax.broadcasted_iota(jnp.int32, (LANES, LANES), 1)
    return jnp.where((row // b == col // b) & (row < R) & (col < R), 1.0, 0.0).astype(f32)


def exact_dot(a, b):
    return jnp.dot(a, b, precision=lax.Precision.HIGHEST, preferred_element_type=f32)


def place(columns, rows):
    lanes = lane_iota(rows)
    out = jnp.zeros((rows, LANES), f32)
    for r, column in enumerate(columns):
        out = jnp.where(lanes == r, column, out)
    return out


def gbst_masks(length):
    q = lax.broadcasted_iota(jnp.int32, (QN, LANES), 0)
    r = lax.broadcasted_iota(jnp.int32, (QN, LANES), 1)
    mask = jnp.where((q * R + r < length) & (r < R), 1.0, 0.0).astype(f32)
    inverse = [1.0 / jnp.maximum(exact_dot(mask, group_matrix(b)), 1.0) for b in (2, 3, 4)]
    pair = exact_dot(mask, group_matrix(2))
    alpha = mask / jnp.maximum(pair, 1.0)
    return mask, inverse, alpha


def gbst_weights(s1, inverse):
    sizes = [s1] + [exact_dot(s1, group_matrix(b)) * inv for b, inv in zip((2, 3, 4), inverse)]
    top = jnp.maximum(jnp.maximum(sizes[0], sizes[1]), jnp.maximum(sizes[2], sizes[3]))
    parts = [jnp.exp(s - top) for s in sizes]
    total = parts[0] + parts[1] + parts[2] + parts[3]
    return [p / total for p in parts]


def gbst_coefs(weights, inverse, alpha):
    a1 = weights[0] * alpha
    a2 = weights[1] * alpha * inverse[0]
    a3 = weights[2] * alpha * inverse[1]
    a4 = weights[3] * alpha * inverse[2]
    pair = group_matrix(2)
    a4s = exact_dot(a4, pair)
    own = a1 + exact_dot(a2, pair) + a4s
    return own, a3, a4s


def column(x, r):
    return jnp.broadcast_to(x[:, r : r + 1], (x.shape[0], LANES))


def hits_of(ids):
    lanes = lax.broadcasted_iota(jnp.int32, (P_ROWS, LANES), 1).astype(f32)
    return jnp.concatenate(
        [jnp.where(ids == lanes + float(i * LANES), 1.0, 0.0).astype(bf16) for i in range(SMALL // LANES)], axis=1)


def look_up(ids, table_ref):
    return lax.dot_general(
        hits_of(ids), table_ref[...].reshape(D, SMALL), (((1,), (1,)), ((), ())), preferred_element_type=f32)


def load_e(e_ref, r, lt):
    lanes = pl.ds(lt * LANES, LANES)
    if r < R:
        return e_ref[pl.ds(r * QN, QN), lanes]
    return e_ref[pl.ds((r - R) * QN + 1, QN), lanes]


def gbst_fwd_kernel(len_ref, ids_ref, table_ref, vec_ref, hidden_ref, hlow_ref, normed_ref, turned_ref, c_ref, w_ref, elow_ref, kc_ref, e_ref, hid_ref, s_ref):
    k_ref = kc_ref.at[0]
    length = len_ref[pl.program_id(0)]
    rows_e = look_up(ids_ref[0], table_ref)
    e_ref[pl.ds(0, P_ROWS), :] = rows_e
    elow_ref[0] = rows_e.astype(bf16)
    e_ref[pl.ds(P_ROWS, 8), :] = jnp.zeros((8, D), f32)
    for lt in range(LT):
        lanes = pl.ds(lt * LANES, LANES)
        taps = [jnp.broadcast_to(vec_ref[j : j + 1, lanes], (QN, LANES)) for j in range(4)]
        sw = jnp.broadcast_to(vec_ref[4:5, lanes], (QN, LANES))
        for r in range(R):
            c = taps[0] * load_e(e_ref, r, lt)
            for j in range(1, 4):
                c = c + taps[j] * load_e(e_ref, r + j, lt)
            c_ref[0, pl.ds(r * QN, QN), lanes] = c
            part = c * sw
            rows = pl.ds(r * QN, QN)
            s_ref[rows, :] = part if lt == 0 else s_ref[rows, :] + part
    s1 = place([jnp.sum(s_ref[pl.ds(r * QN, QN), :], axis=1, keepdims=True) for r in range(R)], QN)
    mask, inverse, alpha = gbst_masks(length)
    weights = gbst_weights(s1, inverse)
    for b, kept in enumerate(weights + inverse + [alpha]):
        w_ref[0, b] = kept
    own, a3, a4s = gbst_coefs(weights, inverse, alpha)
    n = 0
    for r in range(R):
        k_ref[r] = column(own, r)
        k_ref[R + r] = column(a3, r)
    for k in range(6):
        k_ref[2 * R + k] = column(a4s, 2 * k)
    for r in range(R):
        k_ref[2 * R + 6 + r] = column(mask, r)
    for lt in range(LT):
        lanes = pl.ds(lt * LANES, LANES)
        for half in range(2):
            c = [c_ref[0, pl.ds((half * 6 + r) * QN, QN), lanes] for r in range(6)]
            base = half * 6
            s3 = [c[0] + c[1] + c[2], c[3] + c[4] + c[5]]
            for k in range(3):
                tok = half * 3 + k
                other = tok ^ 1
                rows = pl.ds(2 * other * QN, QN)
                rows1 = pl.ds((2 * other + 1) * QN, QN)
                s2 = c_ref[0, rows, lanes] + c_ref[0, rows1, lanes]
                h = k_ref[2 * tok] * c[2 * k] + k_ref[2 * tok + 1] * c[2 * k + 1] + k_ref[2 * R + tok] * s2
                if k == 1:
                    h = h + k_ref[R + 2 * tok] * s3[0] + k_ref[R + 2 * tok + 1] * s3[1]
                else:
                    h = h + (k_ref[R + 2 * tok] + k_ref[R + 2 * tok + 1]) * s3[0 if k == 0 else 1]
                hid_ref[lt, pl.ds(tok, QN, stride=6), :] = h
    total = jnp.zeros((TOK, LANES), f32)
    for lt in range(LT):
        x = hid_ref[lt, 0:TOK, :]
        total = total + x * x
    scale = lax.rsqrt(jnp.sum(total, axis=1, keepdims=True) * (1.0 / D) + epsilon)
    for lt in range(LT):
        lanes = pl.ds(lt * LANES, LANES)
        x = hid_ref[lt, 0:TOK, :]
        hidden_ref[:, lanes] = x
        hlow_ref[:, lanes] = x.astype(bf16)
        normed = (x * scale * vec_ref[5:6, lanes]).astype(bf16)
        normed_ref[:, lanes] = normed
        turned_ref[lanes, :] = normed.T


def gbst_forward(lengths, ids_col, table, vecs):
    seqs = ids_col.shape[0]
    grid_spec = pltpu.PrefetchScalarGridSpec(
        num_scalar_prefetch=1,
        grid=(seqs,),
        in_specs=[
            pl.BlockSpec((1, P_ROWS, LANES), lambda s, n: (s, 0, 0)),
            pl.BlockSpec(table.shape, lambda s, n: (0, 0, 0)),
            pl.BlockSpec((8, D), lambda s, n: (0, 0)),
        ],
        out_specs=[
            pl.BlockSpec((TOK, D), lambda s, n: (s, 0)),
            pl.BlockSpec((TOK, D), lambda s, n: (s, 0)),
            pl.BlockSpec((TOK, D), lambda s, n: (s, 0)),
            pl.BlockSpec((D, TOK), lambda s, n: (0, s)),
            pl.BlockSpec((1, P_ROWS, D), lambda s, n: (s, 0, 0)),
            pl.BlockSpec((1, 8, QN, LANES), lambda s, n: (s, 0, 0, 0)),
            pl.BlockSpec((1, P_ROWS, D), lambda s, n: (s, 0, 0)),
            pl.BlockSpec((1, 3 * R + 6, QN, LANES), lambda s, n: (s, 0, 0, 0)),
        ],
        scratch_shapes=[
            pltpu.VMEM((P_ROWS + 8, D), f32),
            pltpu.VMEM((LT, T_ROWS, LANES), f32),
            pltpu.VMEM((P_ROWS, LANES), f32),
        ],
    )
    return pl.pallas_call(
        gbst_fwd_kernel,
        grid_spec=grid_spec,
        out_shape=[
            jax.ShapeDtypeStruct((seqs * TOK, D), f32),
            jax.ShapeDtypeStruct((seqs * TOK, D), bf16),
            jax.ShapeDtypeStruct((seqs * TOK, D), bf16),
            jax.ShapeDtypeStruct((D, seqs * TOK), bf16),
            jax.ShapeDtypeStruct((seqs, P_ROWS, D), f32),
            jax.ShapeDtypeStruct((seqs, 8, QN, LANES), f32),
            jax.ShapeDtypeStruct((seqs, P_ROWS, D), bf16),
            jax.ShapeDtypeStruct((seqs, 3 * R + 6, QN, LANES), f32),
        ],
        compiler_params=pltpu.CompilerParams(vmem_limit_bytes=VMEM_LIMIT),
        cost_estimate=cost(18, 30),
        name="gbst_forward",
    )(lengths, ids_col, table, vecs)


def gbst_bwd_kernel(row_ref, vec_ref, dh_ref, c_ref, w_ref, elow_ref, kc_ref, gain1_ref, gain2_ref, rel_ref,
                    ig_ref, small_ref, ge_ref, e_ref, dt_ref, dc_ref, s_ref, cf_ref, igs_ref):
    seq = pl.program_id(0)
    k_ref = kc_ref.at[0]

    @pl.when(seq == 0)
    def _():
        ge_ref[...] = jnp.zeros_like(ge_ref)

    e_ref[pl.ds(0, P_ROWS), :] = elow_ref[0].astype(f32)
    e_ref[pl.ds(P_ROWS, 8), :] = jnp.zeros((8, D), f32)
    for lt in range(LT):
        dt_ref[lt, 0:TOK, :] = dh_ref[:, pl.ds(lt * LANES, LANES)].astype(f32)
        dt_ref[lt, TOK:T_ROWS, :] = jnp.zeros((T_ROWS - TOK, LANES), f32)
    for lt in range(LT):
        lanes = pl.ds(lt * LANES, LANES)
        for half in range(2):
            c = [c_ref[0, pl.ds((half * 6 + r) * QN, QN), lanes] for r in range(6)]
            s3 = [c[0] + c[1] + c[2], c[3] + c[4] + c[5]]
            for k in range(3):
                tok = half * 3 + k
                other = tok ^ 1
                dh = dt_ref[lt, pl.ds(tok, QN, stride=6), :]
                s2 = c_ref[0, pl.ds(2 * other * QN, QN), lanes] + c_ref[0, pl.ds((2 * other + 1) * QN, QN), lanes]
                parts = [
                    (2 * tok, dh * c[2 * k]),
                    (2 * tok + 1, dh * c[2 * k + 1]),
                    (2 * R + tok, dh * s2),
                    (R + 2 * tok, dh * s3[0 if k < 2 else 1]),
                ]
                if k == 1:
                    parts.append((R + 2 * tok + 1, dh * s3[1]))
                for slot, part in parts:
                    s_ref[slot] = part if lt == 0 else s_ref[slot] + part

    def total(slot):
        return jnp.sum(s_ref[slot], axis=1, keepdims=True)

    d1, d3, dother = [], [], []
    for tok in range(6):
        d1 += [total(2 * tok), total(2 * tok + 1)]
        first = total(R + 2 * tok)
        d3 += [first, total(R + 2 * tok + 1) if tok % 3 == 1 else first]
        o = total(2 * R + tok)
        dother += [o, o]
    d1, d3, dother = place(d1, QN), place(d3, QN), place(dother, QN)
    weights = [w_ref[0, b] for b in range(4)]
    inverse = [w_ref[0, 4 + b] for b in range(3)]
    alpha = w_ref[0, 7]
    d2 = exact_dot(d1, group_matrix(2))
    g = [alpha * d1, alpha * d2 * inverse[0], alpha * d3 * inverse[1], alpha * (d2 + dother) * inverse[2]]
    mean = weights[0] * g[0] + weights[1] * g[1] + weights[2] * g[2] + weights[3] * g[3]
    d_size = [w * (x - mean) for w, x in zip(weights, g)]
    coef = d_size[0]
    for b, inv in zip((2, 3, 4), inverse):
        coef = coef + exact_dot(d_size[b - 1] * inv, group_matrix(b))
    for r in range(R):
        cf_ref[r] = column(coef, r)

    for lt in range(LT):
        lanes = pl.ds(lt * LANES, LANES)
        taps = [jnp.broadcast_to(vec_ref[j : j + 1, lanes], (QN, LANES)) for j in range(4)]
        sw = jnp.broadcast_to(vec_ref[4:5, lanes], (QN, LANES))
        gs = jnp.zeros((QN, LANES), f32)
        gc = [jnp.zeros((QN, LANES), f32) for _ in range(4)]
        for half in range(2):
            dh = [dt_ref[lt, pl.ds(half * 3 + k, QN, stride=6), :] for k in range(3)]
            a = R + half * 6
            t3 = [
                (k_ref[a] + k_ref[a + 1]) * dh[0] + k_ref[a + 2] * dh[1],
                k_ref[a + 3] * dh[1] + (k_ref[a + 4] + k_ref[a + 5]) * dh[2],
            ]
            for k in range(3):
                tok = half * 3 + k
                other = tok ^ 1
                dother_h = dt_ref[lt, pl.ds(other, QN, stride=6), :]
                cross = k_ref[2 * R + other] * dother_h
                for e in range(2):
                    r = 2 * tok + e
                    cf = cf_ref[r]
                    dc = k_ref[r] * dh[k] + cross + t3[(r % 6) // 3] + cf * sw
                    gs = gs + cf * c_ref[0, pl.ds(r * QN, QN), lanes]
                    dc_ref[r, pl.ds(8, QN), :] = dc
                    for j in range(4):
                        gc[j] = gc[j] + dc * load_e(e_ref, r + j, lt)
        ge_ref[VROWS + 4 : VROWS + 5, lanes] += jnp.sum(gs, axis=0, keepdims=True)
        for j in range(4):
            ge_ref[VROWS + j : VROWS + j + 1, lanes] += jnp.sum(gc[j], axis=0, keepdims=True)
        for r in range(R):
            dc_ref[r, 0:8, :] = jnp.zeros((8, LANES), f32)
        for r in range(R):
            x = taps[0] * dc_ref[r, pl.ds(8, QN), :]
            for j in range(1, 4):
                back = dc_ref[r - j, pl.ds(8, QN), :] if r >= j else dc_ref[r - j + R, pl.ds(7, QN), :]
                x = x + taps[j] * back
            igs_ref[lt, pl.ds(r, QN, stride=R), :] = x * k_ref[2 * R + 6 + r]
    for lt in range(LT):
        lanes = pl.ds(lt * LANES, LANES)
        ig_ref[0, :, lanes] = igs_ref[lt, 0:MAXLEN, :].astype(bf16)
    vocab = lax.broadcasted_iota(jnp.int32, (VROWS, MAXLEN), 0)
    row_hits = jnp.where(vocab == row_ref[0], 1.0, 0.0).astype(bf16)
    ge_ref[0:VROWS, :] += jnp.dot(row_hits, ig_ref[0], preferred_element_type=f32)

    @pl.when(seq == pl.num_programs(0) - 1)
    def _():
        ge_ref[VROWS + 5 : VROWS + 6, :] = gain1_ref[...]
        ge_ref[VROWS + 6 : VROWS + 7, :] = gain2_ref[...]
        ge_ref[VROWS + 7 : VROWS + 15, :] = rel_ref[...]
        for lt in range(LT):
            lanes = pl.ds(lt * LANES, LANES)
            small_ref[lanes, :] = ge_ref[:, lanes].T.astype(bf16)


def gbst_backward(ids_row, vecs, d_hidden, c, w, e_low, coefs, gain1, gain2, rel):
    seqs = ids_row.shape[0]
    per_seq = lambda *shape: pl.BlockSpec((1,) + shape, lambda s: (s,) + (0,) * len(shape))
    still = lambda *shape: pl.BlockSpec(shape, lambda s: (0,) * len(shape))
    return pl.pallas_call(
        gbst_bwd_kernel,
        grid=(seqs,),
        in_specs=[
            per_seq(1, MAXLEN), still(8, D), pl.BlockSpec((TOK, D), lambda s: (s, 0)), per_seq(P_ROWS, D),
            per_seq(8, QN, LANES), per_seq(P_ROWS, D), per_seq(3 * R + 6, QN, LANES),
            still(1, D), still(1, D), still(8, D),
        ],
        out_specs=[per_seq(MAXLEN, D), still(D, SMALL)],
        scratch_shapes=[
            pltpu.VMEM((SMALL, D), f32),
            pltpu.VMEM((P_ROWS + 8, D), f32),
            pltpu.VMEM((LT, T_ROWS, LANES), f32),
            pltpu.VMEM((R, QN + 8, LANES), f32),
            pltpu.VMEM((2 * R + 6, QN, LANES), f32),
            pltpu.VMEM((R, QN, LANES), f32),
            pltpu.VMEM((LT, P_ROWS, LANES), f32),
        ],
        out_shape=[
            jax.ShapeDtypeStruct((seqs, MAXLEN, D), bf16),
            jax.ShapeDtypeStruct((D, SMALL), bf16),
        ],
        compiler_params=pltpu.CompilerParams(vmem_limit_bytes=VMEM_LIMIT),
        cost_estimate=cost(26, 40),
        name="gbst_backward",
    )(ids_row, vecs, d_hidden, c, w, e_low, coefs, gain1, gain2, rel)


HEADS = 12
HD = 64
BUCKETS = 32
SPAN = 1024
HB = 4
WIDE = HB * HD
GROUPS = HEADS // HB
dead_score = -1e9


def nt(a, b):
    return lax.dot_general(a, b, (((1,), (1,)), ((), ())), preferred_element_type=f32)


def nn(a, b):
    return jnp.dot(a, b, preferred_element_type=f32)


def bucket_rows(buckets):
    def row(x):
        return jnp.concatenate([x[TOK - 1 :], x[:1], x[: TOK - 1]])

    return jnp.stack([row(buckets), row(buckets[::-1])])


def bucket_hits(row_ref, way):
    return jnp.where(lax.broadcasted_iota(jnp.int32, (BUCKETS, SPAN), 0) == row_ref[way : way + 1, :], 1.0, 0.0).astype(f32)


def spread_table(rel_ref, row_ref, z_ref, way):
    dims = (((0,), (0,)), ((), ()))
    z_ref[...] = lax.dot_general(
        rel_ref[...].astype(bf16), bucket_hits(row_ref, way).astype(bf16), dims, preferred_element_type=f32)


def build_bias(z_ref, bt_ref, group):
    for h in range(HB):
        row = jnp.broadcast_to(z_ref[pl.ds(group * HB + h, 1), :], (8, SPAN))
        z = pltpu.roll(row, 0, 1, stride=1, stride_axis=0)
        for g in range(TOK // 8):
            bt_ref[h, pl.ds(8 * g, 8), :] = (z if g == 0 else pltpu.roll(z, 8 * g, 1))[:, :TOK]


def pair_lanes(h):
    return slice(h // 2 * LANES, (h // 2 + 1) * LANES)


def own_lanes(h):
    return lax.broadcasted_iota(jnp.int32, (TOK, LANES), 1) // HD == h % 2


def head_parts(k, q, length, h):
    lanes = lax.broadcasted_iota(jnp.int32, (TOK, LANES), 1)
    rows = lax.broadcasted_iota(jnp.int32, (TOK, LANES), 0)
    spare = HD * (1 - h % 2)
    dead = jnp.where(2 * rows < length, 0.0, dead_score)
    kf = jnp.where(own_lanes(h), k[:, pair_lanes(h)].astype(f32), jnp.where(lanes == spare, dead, 0.0)).astype(bf16)
    qf = jnp.where(lanes == spare, 1.0, q[:, pair_lanes(h)].astype(f32)).astype(bf16)
    return kf, qf


def join_heads(parts):
    pairs = [jnp.where(own_lanes(0), parts[h], parts[h + 1]) for h in range(0, HB, 2)]
    return jnp.concatenate(pairs, axis=1).astype(bf16)


def attn_fwd_kernel(len_ref, q_ref, k_ref, v_ref, rel_ref, row_ref, ctx_ref, lse_ref, bias_ref, z_ref):
    length = len_ref[pl.program_id(1)]

    @pl.when((pl.program_id(0) == 0) & (pl.program_id(1) == 0))
    def _():
        spread_table(rel_ref, row_ref, z_ref, 0)

    @pl.when(pl.program_id(1) == 0)
    def _():
        build_bias(z_ref, bias_ref, pl.program_id(0))

    q, k, v = q_ref[...], k_ref[...], v_ref[...]

    def score(h):
        kf, qf = head_parts(k, q, length, h)
        return nt(qf, kf) + bias_ref[h]

    outs = []
    lanes = lax.broadcasted_iota(jnp.int32, (TOK, LANES), 1)
    lse = jnp.zeros((TOK, LANES), f32)
    s = score(0)
    for h in range(HB):
        later = score(h + 1) if h + 1 < HB else None
        top = jnp.max(s, axis=1, keepdims=True)
        p = jnp.exp(s - top)
        total = jnp.sum(p, axis=1, keepdims=True)
        outs.append(nn(p.astype(bf16), v[:, pair_lanes(h)]) * (1.0 / total))
        lse = jnp.where(lanes == h, top + jnp.log(total), lse)
        s = later
    ctx_ref[...] = join_heads(outs)
    lse_ref[0, 0] = lse.T[0:8]


def table_specs():
    return [
        pl.BlockSpec((BUCKETS, LANES), lambda hp, s, n: (0, 0)),
        pl.BlockSpec((2, SPAN), lambda hp, s, n: (0, 0)),
    ]


def attn_forward(lengths, qkv, rel, row):
    seqs = qkv.shape[0] // TOK
    spec = lambda off: pl.BlockSpec((TOK, WIDE), lambda hp, s, n: (s, off + hp))
    return pl.pallas_call(
        attn_fwd_kernel,
        grid_spec=pltpu.PrefetchScalarGridSpec(
            num_scalar_prefetch=1,
            grid=(GROUPS, seqs),
            in_specs=[spec(0), spec(GROUPS), spec(2 * GROUPS)] + table_specs(),
            out_specs=[spec(0), pl.BlockSpec((1, 1, 8, TOK), lambda hp, s, n: (hp, s, 0, 0))],
            scratch_shapes=[pltpu.VMEM((HB, TOK, TOK), f32), pltpu.VMEM((LANES, SPAN), f32)],
        ),
        out_shape=[
            jax.ShapeDtypeStruct((seqs * TOK, D), bf16),
            jax.ShapeDtypeStruct((GROUPS, seqs, 8, TOK), f32),
        ],
        compiler_params=pltpu.CompilerParams(vmem_limit_bytes=VMEM_LIMIT),
        cost_estimate=cost(27, 20),
        name="attn_forward",
    )(lengths, qkv, qkv, qkv, rel, row)


def attn_bwd_kernel(shards, len_ref, q_ref, k_ref, v_ref, do_ref, o_ref, lse_ref, rel_ref, row_ref, dqkv_ref, gt_ref, bt_ref, g_ref, z_ref, gz_ref):
    s_id = pl.program_id(1)
    length = len_ref[s_id]

    @pl.when((pl.program_id(0) == 0) & (s_id == 0))
    def _():
        spread_table(rel_ref, row_ref, z_ref, 1)
        gz_ref[...] = jnp.zeros_like(gz_ref)

    @pl.when(s_id == 0)
    def _():
        build_bias(z_ref, bt_ref, pl.program_id(0))
        g_ref[...] = jnp.zeros_like(g_ref)

    q, k, v, do = q_ref[...], k_ref[...], v_ref[...], do_ref[...]
    kt = k.astype(f32).T.astype(bf16)
    lanes8 = lax.broadcasted_iota(jnp.int32, (8, WIDE), 1)
    rows8 = lax.broadcasted_iota(jnp.int32, (8, WIDE), 0)
    pick = jnp.where(lanes8 // HD == rows8, 1.0, 0.0).astype(bf16)
    prod = do.astype(f32) * o_ref[...].astype(f32)
    upper = prod.astype(bf16)
    delta = nt(pick, upper) + nt(pick, (prod - upper.astype(f32)).astype(bf16))
    dq, dk, dv = [], [], []

    def first(h):
        kf, qf = head_parts(k, q, length, h)
        vf = jnp.where(own_lanes(h), v[:, pair_lanes(h)].astype(f32), 0.0).astype(bf16)
        return nt(kf, qf) + bt_ref[h], nt(vf, do[:, pair_lanes(h)])

    for h in range(HB):
        s, d_prob = first(h)
        p = jnp.exp(s - lse_ref[0, 0, h : h + 1, :])
        ds = p * (d_prob - delta[h : h + 1, :])
        g_ref[h] += ds
        low = ds.astype(bf16)
        dv.append(nn(p.astype(bf16), do[:, pair_lanes(h)]))
        dk.append(nn(low, q[:, pair_lanes(h)]))
        start = h % 2 * HD
        dq.append(nn(kt[pair_lanes(h)], low)[start : start + HD])
    dqkv_ref[0] = jnp.concatenate(dq, axis=0).T.astype(bf16)
    dqkv_ref[1] = join_heads(dk)
    dqkv_ref[2] = join_heads(dv)

    @pl.when(s_id == pl.num_programs(1) - 1)
    def _():
        for h in range(HB):
            total = jnp.zeros((8, SPAN), f32)
            for g in range(LANES // 8):
                tiles = [jnp.zeros((8, LANES), f32) for _ in range(SPAN // LANES)]
                for j in range(TOK // LANES):
                    x = g_ref[h, pl.ds(LANES * j + 8 * g, 8), :]
                    for t in range(TOK // LANES):
                        n = (t - j) % (SPAN // LANES)
                        tiles[n] = tiles[n] + x[:, t * LANES : (t + 1) * LANES]
                piece = jnp.concatenate(tiles, axis=1)
                total = total + (piece if g == 0 else pltpu.roll(piece, SPAN - 8 * g, 1))
            out = total[0:1]
            for s in range(1, 8):
                out = out + pltpu.roll(jnp.broadcast_to(total[s : s + 1], (8, SPAN)), SPAN - s, 1)[0:1]
            gz_ref[pl.ds(pl.program_id(0) * HB + h, 1), :] = out

    @pl.when((pl.program_id(0) == GROUPS - 1) & (s_id == pl.num_programs(1) - 1))
    def _():
        total = lax.dot_general(
            bucket_hits(row_ref, 1), gz_ref[...], (((1,), (1,)), ((), ())),
            precision=lax.Precision.HIGHEST, preferred_element_type=f32)
        gt_ref[...] = jnp.zeros_like(gt_ref)
        per = BUCKETS // shards
        for s in range(shards):
            start = s * (D // shards)
            gt_ref[0:per, start : start + HEADS] = total[s * per : (s + 1) * per, 0:HEADS]


def attn_backward(lengths, qkv, d_ctx, ctx, lse, rel, row, shards):
    seqs = qkv.shape[0] // TOK
    spec = lambda off: pl.BlockSpec((TOK, WIDE), lambda hp, s, n: (s, off + hp))
    return pl.pallas_call(
        lambda *refs: attn_bwd_kernel(shards, *refs),
        grid_spec=pltpu.PrefetchScalarGridSpec(
            num_scalar_prefetch=1,
            grid=(GROUPS, seqs),
            in_specs=[
                spec(0), spec(GROUPS), spec(2 * GROUPS), spec(0), spec(0),
                pl.BlockSpec((1, 1, 8, TOK), lambda hp, s, n: (hp, s, 0, 0)),
            ] + table_specs(),
            out_specs=[
                pl.BlockSpec((3, TOK, WIDE), lambda hp, s, n: (0, s, hp)),
                pl.BlockSpec((8, D), lambda hp, s, n: (0, 0)),
            ],
            scratch_shapes=[
                pltpu.VMEM((HB, TOK, TOK), f32), pltpu.VMEM((HB, TOK, TOK), f32),
                pltpu.VMEM((LANES, SPAN), f32), pltpu.VMEM((16, SPAN), f32),
            ],
        ),
        out_shape=[
            jax.ShapeDtypeStruct((3, seqs * TOK, D), bf16),
            jax.ShapeDtypeStruct((8, D), f32),
        ],
        compiler_params=pltpu.CompilerParams(vmem_limit_bytes=VMEM_LIMIT),
        cost_estimate=cost(46, 30),
        name="attn_backward",
    )(lengths, qkv, qkv, qkv, d_ctx, ctx, lse, rel, row)


FF = 2048
FT = 256
RC = 1024
MT = 512


def rms_scale(x):
    return lax.rsqrt(jnp.sum(x * x, axis=1, keepdims=True) * (1.0 / D) + epsilon)


def post_kernel(len_ref, shift_ref, ctx_ref, w_ref, hidden_ref, vec_ref, *refs):
    pieces, (att_ref, low_ref, low_t_ref, do_ref, do_t_ref) = refs[:-5], refs[-5:]
    s = pl.program_id(0)
    for i, piece in enumerate(pieces):
        @pl.when(shift_ref[s] == i)
        def _():
            do_ref[...] = piece[...]

    live = 2 * lax.broadcasted_iota(jnp.int32, (TOK, D), 0) < len_ref[s]
    d_out = jnp.where(live, do_ref[...].astype(f32), 0.0).astype(bf16)
    do_ref[...] = d_out
    do_t_ref[...] = d_out.T
    att = hidden_ref[...] + nn(ctx_ref[...], out_weights(w_ref))
    att_ref[...] = att
    low = (att * rms_scale(att) * vec_ref[6:7, :]).astype(bf16)
    low_ref[...] = low
    low_t_ref[...] = low.T


def rows_spec(width=D):
    return pl.BlockSpec((TOK, width), lambda s, *n: (s, 0))


def whole(*shape):
    return pl.BlockSpec(shape, lambda s, *n: (0,) * len(shape))


def out_block(shards):
    deep = D // shards
    return pl.BlockSpec((shards, 3 * deep, FT), lambda s, *n: (0, 4, 0))


def out_weights(ref):
    deep = ref.shape[1] // 3
    return jnp.concatenate([ref[:, i * deep : (i + 1) * deep, :].reshape(D, FT) for i in range(3)], axis=1)


def post_attention(lengths, shifts, ctx, pack, hidden, vecs, pieces, shards):
    rows = ctx.shape[0]
    cols_spec = pl.BlockSpec((D, TOK), lambda s, *n: (0, s))
    return pl.pallas_call(
        post_kernel,
        grid_spec=pltpu.PrefetchScalarGridSpec(
            num_scalar_prefetch=2,
            grid=(rows // TOK,),
            in_specs=[rows_spec(), out_block(shards), rows_spec(), whole(8, D)] + [whole(TOK, D)] * len(pieces),
            out_specs=[rows_spec(), rows_spec(), cols_spec, rows_spec(), cols_spec],
        ),
        out_shape=[
            jax.ShapeDtypeStruct((rows, D), f32),
            jax.ShapeDtypeStruct((rows, D), bf16),
            jax.ShapeDtypeStruct((D, rows), bf16),
            jax.ShapeDtypeStruct((rows, D), bf16),
            jax.ShapeDtypeStruct((D, rows), bf16),
        ],
        compiler_params=pltpu.CompilerParams(vmem_limit_bytes=VMEM_LIMIT),
        cost_estimate=cost(10, 30),
        name="post_attention",
    )(lengths, shifts, ctx, pack, hidden, vecs, *pieces)


def gelu_parts(v):
    c = 0.7978845608
    v2 = v * v
    t = jnp.tanh(v * (c + (c * 0.044715) * v2))
    half = 0.5 + 0.5 * t
    gelu = v * half
    slope = half + (0.5 * v) * (1.0 - t * t) * (c + (3.0 * c * 0.044715) * v2)
    return gelu, slope


def ffn_steps(x_any, d_any, xt_any, dt_any, wgu_ref, wo_ref, grad_ref, y_any, dx_any,
              x_ref, d_ref, xt_ref, dt_ref, y_ref, dx_ref, a_ref, dg_ref, du_ref, gu_ref, go_ref, in_sem, out_sem, sems,
              low_ref=None):
    f = pl.program_id(0)
    steps = FF // 2 // FT
    rows_total = x_ref.shape[0]
    chunks = rows_total // RC
    shards, part = gu_ref.shape[1], gu_ref.shape[2]
    owners, deep = go_ref.shape[1], go_ref.shape[2]
    base = steps * part

    def copies(slot, step):
        return (
            pltpu.make_async_copy(
                gu_ref.at[slot], grad_ref.at[:, pl.ds(step * part, part), :], sems.at[0, slot]),
            pltpu.make_async_copy(
                go_ref.at[slot], grad_ref.at[pl.ds(step * owners, owners), pl.ds(base, deep), :], sems.at[1, slot]),
        )

    def row_loads(i):
        rows = pl.ds(i * RC, RC)
        return (
            pltpu.make_async_copy(x_any.at[rows], x_ref.at[rows], in_sem.at[0, i]),
            pltpu.make_async_copy(d_any.at[rows], d_ref.at[rows], in_sem.at[1, i]),
        )

    def turned_loads():
        return (
            pltpu.make_async_copy(xt_any, xt_ref, in_sem.at[2, 0]),
            pltpu.make_async_copy(dt_any, dt_ref, in_sem.at[2, 1]),
        )

    def row_stores(i):
        rows = pl.ds(i * RC, RC)
        return (
            pltpu.make_async_copy(low_ref.at[0, rows], y_any.at[rows], out_sem.at[0, i]),
            pltpu.make_async_copy(low_ref.at[1, rows], dx_any.at[rows], out_sem.at[1, i]),
        )

    @pl.when(f == 0)
    def _():
        for i in range(chunks):
            for copy in row_loads(i):
                copy.start()
        for copy in turned_loads():
            copy.start()

    d_rows = part // 2
    third = deep // 3
    wg = wgu_ref[:, 0:d_rows, :].reshape(D, FT)
    wu = wgu_ref[:, d_rows:part, :].reshape(D, FT)
    wo = jnp.concatenate(
        [wo_ref[:, i * third : (i + 1) * third, :].reshape(FT, FT) for i in range(3)], axis=1)

    @pl.when(f == 0)
    def _():
        for i in range(chunks):
            for copy in row_loads(i):
                copy.wait()

    def chunk(i, carry):
        rows = pl.ds(pl.multiple_of(i * RC, RC), RC)
        x, d = x_ref[rows, :], d_ref[rows, :]
        gelu, slope = gelu_parts(nn(x, wg))
        up = nn(x, wu)
        da = nt(d, wo)
        act = (gelu * up).astype(bf16)
        dg = (da * up * slope).astype(bf16)
        du = (da * gelu).astype(bf16)
        a_ref[rows, :] = act
        dg_ref[rows, :] = dg
        du_ref[rows, :] = du
        y_ref[rows, :] = nn(act, wo) + jnp.where(f == 0, 0.0, y_ref[rows, :])
        dx_ref[rows, :] = nt(dg, wg) + nt(du, wu) + jnp.where(f == 0, 0.0, dx_ref[rows, :])
        return carry

    lax.fori_loop(0, chunks, chunk, 0)
    if y_any is not None:

        @pl.when(f == steps - 1)
        def _():
            for i in range(chunks):
                rows = pl.ds(i * RC, RC)
                low_ref[0, rows, :] = y_ref[rows, :].astype(bf16)
                low_ref[1, rows, :] = dx_ref[rows, :].astype(bf16)
                for copy in row_stores(i):
                    copy.start()

    slot = lax.rem(f, 2)

    @pl.when(f == 0)
    def _():
        for copy in turned_loads():
            copy.wait()

    @pl.when(f >= 2)
    def _():
        for copy in copies(slot, f - 2):
            copy.wait()

    gu_ref[slot, :, 0:d_rows, :] = nn(xt_ref[...], dg_ref[...]).astype(bf16).reshape(shards, d_rows, FT)
    gu_ref[slot, :, d_rows:part, :] = nn(xt_ref[...], du_ref[...]).astype(bf16).reshape(shards, d_rows, FT)
    go = nn(dt_ref[...], a_ref[...]).T.astype(bf16)
    for i in range(3):
        go_ref[slot, :, i * third : (i + 1) * third, :] = go[:, i * FT : (i + 1) * FT].reshape(owners, third, FT)
    for copy in copies(slot, f):
        copy.start()

    @pl.when(f == steps - 1)
    def _():
        for copy in copies(1 - slot, f - 1) + copies(slot, f):
            copy.wait()
        if y_any is not None:
            for i in range(chunks):
                for copy in row_stores(i):
                    copy.wait()


def first_kernel(x, d, xt, dt, wgu, wo, grad, y, dx, *scratch):
    ffn_steps(x, d, xt, dt, wgu, wo, grad, y, dx, *scratch)


def second_kernel(len_ref, x, d, xt, dt, wgu, wo, att_ref, y1_ref, dx1_ref, do_ref, ctx_ref, w_ref, vec_ref,
                  grad, out_ref, datt_ref, dctx_ref, gw_ref, gg_ref, acc_ref, flat_ref, *scratch):
    f = pl.program_id(0)
    steps = FF // 2 // FT

    @pl.when(f == 0)
    def _():
        acc_ref[...] = jnp.zeros_like(acc_ref)
        gg_ref[...] = jnp.zeros_like(gg_ref)
        flat_ref[...] = out_weights(w_ref)

    @pl.when(f < steps)
    def _():
        ffn_steps(x, d, xt, dt, wgu, wo, grad, None, None, *scratch)

    @pl.when(f >= steps)
    def _():
        tile = f - steps
        y_ref, dx_ref = scratch[4], scratch[5]
        rows = pl.ds(pl.multiple_of(tile * MT, MT), MT)
        per = TOK // MT
        length = len_ref[tile // per]
        place_in = lax.rem(tile, per) * MT + lax.broadcasted_iota(jnp.int32, (MT, 1), 0)
        live = jnp.where(2 * place_in < length, 1.0, 0.0).astype(f32)
        att = att_ref[...]
        out_ref[...] = ((att + y1_ref[...].astype(f32) + y_ref[rows, :]) * live).astype(bf16)
        back, gain_grad = norm_back(att, dx1_ref[...].astype(f32) + dx_ref[rows, :], vec_ref[6:7, :])
        gg_ref[...] += gain_grad
        d_att = do_ref[...].astype(f32) + back
        low = d_att.astype(bf16)
        datt_ref[...] = low
        dctx_ref[...] = nt(low, flat_ref[...]).astype(bf16)
        acc_ref[...] += nn(ctx_ref[...].T, low)

    @pl.when(f == pl.num_programs(0) - 1)
    def _():
        gw_ref[...] = acc_ref[...].astype(bf16)


def ffn_scratch(rows, shards):
    part, hs = 2 * D // shards, FF // 2 // shards
    return [
        pltpu.VMEM((rows, D), bf16),
        pltpu.VMEM((rows, D), bf16),
        pltpu.VMEM((D, rows), bf16),
        pltpu.VMEM((D, rows), bf16),
        pltpu.VMEM((rows, D), f32),
        pltpu.VMEM((rows, D), f32),
        pltpu.VMEM((rows, FT), bf16),
        pltpu.VMEM((rows, FT), bf16),
        pltpu.VMEM((rows, FT), bf16),
        pltpu.VMEM((2, shards, part, FT), bf16),
        pltpu.VMEM((2, FT // hs, 3 * hs, FT), bf16),
        pltpu.SemaphoreType.DMA((3, max(2, rows // RC))),
        pltpu.SemaphoreType.DMA((2, rows // RC)),
        pltpu.SemaphoreType.DMA((2, 2)),
    ]


def ffn_specs(tiles, shards):
    last = lambda f: jnp.minimum(f, tiles - 1)
    part, hs = 2 * D // shards, FF // 2 // shards
    return [pl.BlockSpec(memory_space=pl.ANY)] * 4 + [
        pl.BlockSpec((shards, part, FT), lambda f, *n: (0, last(f), 0)),
        pl.BlockSpec((FT // hs, 3 * hs, FT), lambda f, *n: (last(f), 2, 0)),
    ]


def grad_shape(shards):
    part, hs = 2 * D // shards, FF // 2 // shards
    return jax.ShapeDtypeStruct((shards, FF // 2 // FT * part + 3 * hs, FT), bf16)


def ffn_first(x, d_out, xt, dt, pack, shards):
    rows = x.shape[0]
    tiles = FF // 2 // FT
    anywhere = pl.BlockSpec(memory_space=pl.ANY)
    return pl.pallas_call(
        first_kernel,
        grid=(tiles,),
        in_specs=ffn_specs(tiles, shards),
        out_specs=[anywhere] * 3,
        out_shape=[
            grad_shape(shards),
            jax.ShapeDtypeStruct((rows, D), bf16),
            jax.ShapeDtypeStruct((rows, D), bf16),
        ],
        scratch_shapes=ffn_scratch(rows, shards) + [pltpu.VMEM((2, rows, D), bf16)],
        compiler_params=pltpu.CompilerParams(vmem_limit_bytes=VMEM_LIMIT),
        cost_estimate=cost(36, 40),
        name="ffn_first",
    )(x, d_out, xt, dt, pack, pack)


def ffn_second(lengths, x, d_out, xt, dt, pack, att, y1, dx1, ctx, pack0, vecs, shards):
    rows = x.shape[0]
    tiles = FF // 2 // FT
    tile_rows = pl.BlockSpec((MT, D), lambda f, n: (jnp.maximum(f - tiles, 0), 0))
    return pl.pallas_call(
        second_kernel,
        grid_spec=pltpu.PrefetchScalarGridSpec(
            num_scalar_prefetch=1,
            grid=(tiles + rows // MT,),
            in_specs=ffn_specs(tiles, shards) + [tile_rows] * 5 + [out_block(shards), whole(8, D)],
            out_specs=[pl.BlockSpec(memory_space=pl.ANY), tile_rows, tile_rows, tile_rows, whole(D, D), whole(1, D)],
            scratch_shapes=[
                pltpu.VMEM((D, D), f32), pltpu.VMEM((D, D), bf16),
            ] + ffn_scratch(rows, shards),
        ),
        out_shape=[
            grad_shape(shards),
            jax.ShapeDtypeStruct((rows, D), bf16),
            jax.ShapeDtypeStruct((rows, D), bf16),
            jax.ShapeDtypeStruct((rows, D), bf16),
            jax.ShapeDtypeStruct((D, D), bf16),
            jax.ShapeDtypeStruct((1, D), f32),
        ],
        compiler_params=pltpu.CompilerParams(vmem_limit_bytes=VMEM_LIMIT),
        cost_estimate=cost(46, 60),
        name="ffn_second",
    )(lengths, x, d_out, xt, dt, pack, pack, att, y1, dx1, d_out, ctx, pack0, vecs)


def norm_back(x, grad, gain):
    r = rms_scale(x)
    n = x * r
    u = gain * grad
    mean = jnp.sum(n * u, axis=1, keepdims=True) * (1.0 / D)
    return r * (u - n * mean), jnp.sum(n * grad, axis=0, keepdims=True)


def qkv_grad_kernel(dqkv_ref, normed_t_ref, go_ref, gw_ref):
    i = pl.program_id(0)

    @pl.when(i < 3)
    def _():
        gw_ref[...] = nn(normed_t_ref[...], dqkv_ref[0]).astype(bf16)

    @pl.when(i == 3)
    def _():
        gw_ref[...] = go_ref[...]


def qkv_grad(dqkv, normed_t, g_attn_out):
    rows = normed_t.shape[1]
    return pl.pallas_call(
        qkv_grad_kernel,
        grid=(4,),
        in_specs=[
            pl.BlockSpec((1, rows, D), lambda i: (jnp.minimum(i, 2), 0, 0)),
            whole(D, rows), whole(D, D),
        ],
        out_specs=pl.BlockSpec((D, D), lambda i: (0, i)),
        out_shape=jax.ShapeDtypeStruct((D, 4 * D), bf16),
        compiler_params=pltpu.CompilerParams(vmem_limit_bytes=VMEM_LIMIT),
        cost_estimate=cost(11, 20),
        name="qkv_grad",
    )(dqkv, normed_t, g_attn_out)


def qkv_back_kernel(dqkv_ref, w_ref, hidden_ref, datt_ref, vec_ref, dh_ref, gg_ref):
    @pl.when(pl.program_id(0) == 0)
    def _():
        gg_ref[...] = jnp.zeros_like(gg_ref)

    dn = nt(dqkv_ref[0], w_ref[:, 0:D])
    for i in range(1, 3):
        dn = dn + nt(dqkv_ref[i], w_ref[:, i * D : (i + 1) * D])
    back, gain_grad = norm_back(hidden_ref[...].astype(f32), dn, vec_ref[5:6, :])
    gg_ref[...] += gain_grad
    dh_ref[...] = (datt_ref[...].astype(f32) + back).astype(bf16)


def qkv_backward(dqkv, attn_w, hidden, d_att, vecs):
    rows = hidden.shape[0]
    tile = pl.BlockSpec((TOK, D), lambda s: (s, 0))
    return pl.pallas_call(
        qkv_back_kernel,
        grid=(rows // TOK,),
        in_specs=[
            pl.BlockSpec((3, TOK, D), lambda s: (0, s, 0)),
            pl.BlockSpec((D, 3 * D), lambda s: (0, 0)),
            tile, tile, whole(8, D),
        ],
        out_specs=[tile, whole(1, D)],
        out_shape=[jax.ShapeDtypeStruct((rows, D), bf16), jax.ShapeDtypeStruct((1, D), f32)],
        compiler_params=pltpu.CompilerParams(vmem_limit_bytes=VMEM_LIMIT),
        cost_estimate=cost(14, 40),
        name="qkv_backward",
    )(dqkv, attn_w, hidden, d_att, vecs)


MESH = pl.DeviceIdType.MESH


def greet(peers):
    barrier = pltpu.get_barrier_semaphore()
    for peer in peers:
        pl.semaphore_signal(barrier, inc=1, device_id=peer, device_id_type=MESH)
    pl.semaphore_wait(barrier, len(peers))


def pack_half(out_ref, ffn_in_ref, ffn_out_ref, h, shards):
    hs = FF // 2 // shards
    owners = FT // hs
    deep = ffn_in_ref.shape[0]
    row = 0
    for f in range(FF // 2 // FT):
        for g in range(2):
            starts = [g * FF + (f * owners + o) * 2 * hs + h * hs for o in range(owners)]
            out_ref[row : row + deep, :] = jnp.concatenate([ffn_in_ref[:, a : a + hs] for a in starts], axis=1)
            row += deep
    for i in range(3):
        out_ref[row : row + hs, :] = ffn_out_ref[h * hs : (h + 1) * hs, i * FT : (i + 1) * FT]
        row += hs
    return row


def prepare_kernel(replicas, shards, length_ref, target_ref, embed_ref, conv_ref, score_ref, gain1_ref, gain2_ref, rel_ref,
                   ids_ref, attn_out_ref, ffn_in_ref, ffn_out_ref,
                   table_ref, vec_ref, table_rel_ref, slots_ref, column_ref, row_ref, pack0_ref, pack1_ref,
                   own_ref, wide_ref, turn_ref, nat_ref, wanted_ref, send_sem, recv_sem):
    rep, me = lax.axis_index("rep"), lax.axis_index("shard")
    deep = embed_ref.shape[1]
    seqs = ids_ref.shape[0]
    twin = me + 1 - 2 * lax.rem(me, 2)
    far = [lax.rem(me + 2 * i, shards) for i in range(1, shards // 2)]
    others = [lax.rem(rep + i, replicas) for i in range(1, replicas)]
    greet([(rep, twin)] + [(rep, p) for p in far] + [(p, me) for p in others])

    def send(i, src, dst, device):
        copy = pltpu.make_async_remote_copy(
            src_ref=src, dst_ref=dst, send_sem=send_sem.at[i], recv_sem=recv_sem.at[i],
            device_id=device, device_id_type=MESH)
        copy.start()
        return copy

    wide_ref[...] = jnp.zeros_like(wide_ref)
    wide_ref[0:VOCAB, 0:deep] = embed_ref[...].astype(f32)
    wide_ref[VOCAB : VOCAB + 4, 0:deep] = conv_ref[...].astype(f32)
    for i, ref in enumerate((score_ref, gain1_ref, gain2_ref)):
        wide_ref[VOCAB + 4 + i : VOCAB + 5 + i, 0:deep] = ref[...].astype(f32).reshape(1, deep)
    rel_rows, heads = rel_ref.shape
    wide_ref[VOCAB + 7 : VOCAB + 7 + rel_rows, 0:heads] = rel_ref[...].astype(f32)
    own_ref[...] = wide_ref[...].T[0:deep].astype(bf16)
    near = [send(0, own_ref, table_ref.at[me], (rep, twin))]
    direct = [send(1 + i, own_ref, table_ref.at[me], (rep, p)) for i, p in enumerate(far)]
    lanes = lax.broadcasted_iota(jnp.int32, (8, 128), 1)
    wanted = jnp.zeros((8, 128), jnp.int32)
    for k in range(seqs):
        slot = target_ref[k] % seqs
        wanted = wanted + jnp.where(lanes == target_ref[k] // seqs // shards, slot + 1, 0)
    wanted_ref[...] = wanted
    base = shards
    asks = [send(base + i, wanted_ref, slots_ref.at[rep], (p, me)) for i, p in enumerate(others)]
    table_ref[me] = own_ref[...]
    slots_ref[rep] = wanted_ref[...]
    row = pack_half(pack0_ref, ffn_in_ref, ffn_out_ref, 0, shards)
    for i in range(3):
        pack0_ref[row : row + deep, :] = attn_out_ref[:, i * FT : (i + 1) * FT]
        row += deep
    pack_half(pack1_ref, ffn_in_ref, ffn_out_ref, 1, shards)
    base = base + replicas - 1
    for i, copy in enumerate(direct):
        copy.wait()
        source = lax.rem(me - 2 * (i + 1) + shards, shards)
        near.append(send(base + i, table_ref.at[source], table_ref.at[source], (rep, twin)))
    turn_ref[...] = jnp.full(turn_ref.shape, -1.0, f32)
    place = lax.broadcasted_iota(jnp.int32, (1, MAXLEN), 1)
    for s in range(seqs):
        live = jnp.where(place < length_ref[s], ids_ref[s : s + 1, :], -1)
        row_ref[s] = live
        turn_ref[s : s + 1, 0:MAXLEN] = live.astype(f32)
    nat_ref[...] = turn_ref[...].T
    for r in range(R):
        rows = nat_ref[pl.ds(r, QN, stride=R), :]
        for s in range(seqs):
            column_ref[s, r * QN : (r + 1) * QN, :] = jnp.broadcast_to(rows[:, s : s + 1], (QN, 128))
    for copy in near + asks:
        copy.wait()
    last = table_ref[:, :, SMALL - 128 :].astype(f32).reshape(D, 128).T
    first = VOCAB - (SMALL - 128)
    vec_ref[...] = last[first : first + 8]
    table_rel_ref[...] = jnp.zeros_like(table_rel_ref)
    for s in range(shards):
        block = last[first + 7 : first + 7 + rel_rows, s * deep : s * deep + heads]
        table_rel_ref[s * rel_rows : (s + 1) * rel_rows, 0:heads] = block


def prepare(lengths, target, embed, conv_w, score_w, gain_attn, gain_ffn, rel_table, ids, attn_out, ffn_in, ffn_out,
            replicas, shards):
    deep = embed.shape[1]
    seqs = ids.shape[0]
    part, hs = 2 * D // shards, FF // 2 // shards
    rows = FF // 2 // FT * part + 3 * hs
    sems = shards + replicas - 1 + shards // 2 - 1
    vmem = pl.BlockSpec(memory_space=pltpu.VMEM)
    smem = pl.BlockSpec(memory_space=pltpu.SMEM)
    return pl.pallas_call(
        lambda *refs: prepare_kernel(replicas, shards, *refs),
        out_shape=[
            jax.ShapeDtypeStruct((shards, deep, SMALL), bf16),
            jax.ShapeDtypeStruct((8, D), f32),
            jax.ShapeDtypeStruct((BUCKETS, 128), f32),
            jax.ShapeDtypeStruct((replicas, 8, 128), jnp.int32),
            jax.ShapeDtypeStruct((seqs, P_ROWS, 128), f32),
            jax.ShapeDtypeStruct((seqs, 1, MAXLEN), jnp.int32),
            jax.ShapeDtypeStruct((rows + 3 * deep, FT), bf16),
            jax.ShapeDtypeStruct((rows, FT), bf16),
        ],
        in_specs=[smem] * 2 + [vmem] * 10,
        out_specs=[vmem] * 8,
        scratch_shapes=[
            pltpu.VMEM((deep, SMALL), bf16),
            pltpu.VMEM((SMALL, 128), f32),
            pltpu.VMEM((128, 1152), f32),
            pltpu.VMEM((1152, 128), f32),
            pltpu.VMEM((8, 128), jnp.int32),
            pltpu.SemaphoreType.DMA((sems,)),
            pltpu.SemaphoreType.DMA((sems,)),
        ],
        compiler_params=pltpu.CompilerParams(collective_id=1, has_side_effects=True, vmem_limit_bytes=VMEM_LIMIT),
        cost_estimate=cost(12, 8),
        name="prepare",
    )(lengths, target, embed, conv_w, score_w, gain_attn, gain_ffn, rel_table, ids, attn_out, ffn_in, ffn_out)


def pick_kernel(order_ref, in_ref, *out_refs):
    for i, ref in enumerate(out_refs):
        @pl.when(pl.program_id(0) == i)
        def _():
            ref[...] = in_ref[0]


def pick(order, rows):
    count = order.shape[0]
    block = (rows.shape[1], rows.shape[2])
    return pl.pallas_call(
        pick_kernel,
        grid_spec=pltpu.PrefetchScalarGridSpec(
            num_scalar_prefetch=1,
            grid=(count,),
            in_specs=[pl.BlockSpec((1,) + block, lambda i, order: (order[i], 0, 0))],
            out_specs=[pl.BlockSpec(block, lambda i, order: (0, 0))] * count,
        ),
        out_shape=[jax.ShapeDtypeStruct(block, rows.dtype)] * count,
        compiler_params=pltpu.CompilerParams(vmem_limit_bytes=VMEM_LIMIT),
        cost_estimate=cost(4, 6),
        name="pick",
    )(order, rows)


def finish_kernel(replicas, shards, piece_ref, small_ref, in_ref, attn_ref, embed_ref, conv_ref, rest_ref,
                  twin_ref, both_ref, far_ref, held_ref, other_ref, part_ref, part2_ref, last_ref,
                  twin_send, twin_recv, far_send, far_recv, send_sem, recv_sem, send2_sem, recv2_sem):
    rep, me = lax.axis_index("rep"), lax.axis_index("shard")
    half = piece_ref.shape[1]
    chips = shards // 2
    core = lax.rem(me, 2)
    twin = me + 1 - 2 * core
    bits = [1 << b for b in range(replicas.bit_length() - 1)]
    orders = (bits, bits[::-1])
    far = [lax.rem(me + 2 * i, shards) for i in range(1, chips)]
    partners = {}
    for bit in bits:
        down = lax.rem(rep // bit, 2)
        partners[bit] = (rep + bit - 2 * bit * down, me)
    greet([(rep, twin)] + [(rep, p) for p in far] + [partners[bit] for bit in bits])

    def send(src, dst, sems, i, device):
        copy = pltpu.make_async_remote_copy(
            src_ref=src, dst_ref=dst, send_sem=sems[0].at[i], recv_sem=sems[1].at[i],
            device_id=device, device_id_type=MESH)
        copy.start()
        return copy

    near = [
        send(small_ref.at[2 * z + 1 - core], twin_ref.at[z], (twin_send, twin_recv), z, (rep, twin))
        for z in range(chips)
    ]

    def exchange(t, mine, theirs, sems):
        return [send(mine.at[t, h], theirs.at[t, h], sems, (t, h), partners[orders[h][t]]) for h in range(2)]

    held_ref[0] = piece_ref[...]
    large = exchange(0, held_ref, other_ref, (send_sem, recv_sem))
    for z, copy in enumerate(near):
        copy.wait()
        both_ref[z] = (small_ref[2 * z + core].astype(f32) + twin_ref[z].astype(f32)).astype(bf16)
    away = [send(both_ref.at[p // 2], far_ref.at[i], (far_send, far_recv), i, (rep, p)) for i, p in enumerate(far)]
    last_ref[...] = jnp.zeros_like(last_ref)

    def settle(t, copies, mine, theirs, outs):
        for h, copy in enumerate(copies):
            copy.wait()
            total = mine[t, h].astype(f32) + theirs[t, h].astype(f32)
            if t == len(bits) - 1:
                start = 0
                for out in outs:
                    width = out.shape[1]
                    out[h * half : (h + 1) * half, :] = total[:, start : start + width]
                    start += width
            else:
                mine[t + 1, h] = total.astype(bf16)

    settle(0, large, held_ref, other_ref, (in_ref, attn_ref))
    large = exchange(1, held_ref, other_ref, (send_sem, recv_sem))
    total = both_ref[me // 2].astype(f32)
    for i, copy in enumerate(away):
        copy.wait()
        total = total + far_ref[i].astype(f32)
    part_ref[0] = total.astype(bf16)
    for t in range(len(bits)):
        little = exchange(t, part_ref, part2_ref, (send2_sem, recv2_sem))
        if t > 0:
            settle(t, large, held_ref, other_ref, (in_ref, attn_ref))
            if t < len(bits) - 1:
                large = exchange(t + 1, held_ref, other_ref, (send_sem, recv_sem))
        settle(t, little, part_ref, part2_ref, (last_ref,))
    turned = last_ref[...].T
    deep = embed_ref.shape[1]
    embed_ref[...] = turned[0:VOCAB, 0:deep]
    conv_ref[...] = turned[VROWS : VROWS + 4, 0:deep]
    rest_ref[...] = turned[VROWS : VROWS + 16, 0:deep]


def finish(piece, small, replicas, shards):
    rows, wide = piece.shape
    half = rows // 2
    chips = shards // 2
    steps = replicas.bit_length() - 1
    vmem = pl.BlockSpec(memory_space=pltpu.VMEM)
    sems = lambda *shape: [pltpu.SemaphoreType.DMA(shape), pltpu.SemaphoreType.DMA(shape)]
    return pl.pallas_call(
        lambda *refs: finish_kernel(replicas, shards, *refs),
        out_shape=[
            jax.ShapeDtypeStruct((rows, 3 * D), f32),
            jax.ShapeDtypeStruct((rows, D), f32),
            jax.ShapeDtypeStruct((VOCAB, rows), f32),
            jax.ShapeDtypeStruct((4, rows), f32),
            jax.ShapeDtypeStruct((16, rows), f32),
        ],
        in_specs=[vmem] * 2,
        out_specs=[vmem] * 5,
        scratch_shapes=[
            pltpu.VMEM((chips, 2, half, SMALL), bf16),
            pltpu.VMEM((chips, 2, half, SMALL), bf16),
            pltpu.VMEM((chips - 1, 2, half, SMALL), bf16),
            pltpu.VMEM((steps, 2, half, wide), bf16),
            pltpu.VMEM((steps, 2, half, wide), bf16),
            pltpu.VMEM((steps, 2, half, SMALL), bf16),
            pltpu.VMEM((steps, 2, half, SMALL), bf16),
            pltpu.VMEM((128, SMALL), f32),
        ] + sems(chips) + sems(chips - 1) + sems(steps, 2) + sems(steps, 2),
        compiler_params=pltpu.CompilerParams(
            collective_id=2, has_side_effects=True, vmem_limit_bytes=VMEM_LIMIT),
        cost_estimate=cost(20, 4),
        name="finish_sums",
    )(piece.reshape(2, half, wide), small.reshape(shards, 2, half, SMALL))


def deliver_kernel(in_ref, attn_ref, embed_ref, conv_ref, rest_ref, in_out, attn_out, embed_out, conv_out, score_out, gain1_out, gain2_out, rel_out):
    in_out[...] = in_ref[...]
    attn_out[...] = attn_ref[...]
    embed_out[...] = embed_ref[...]
    conv_out[...] = conv_ref[...]
    for i, ref in enumerate((score_out, gain1_out, gain2_out)):
        ref[...] = rest_ref[4 + i : 5 + i, :].reshape(ref.shape)
    rel_out[...] = rest_ref[7 : 7 + rel_out.shape[0], 0 : rel_out.shape[1]]


def deliver(parts, rel_rows):
    deep = parts[0].shape[0]
    vmem = pl.BlockSpec(memory_space=pltpu.VMEM)
    line = jax.ShapeDtypeStruct((deep,), f32)
    return pl.pallas_call(
        deliver_kernel,
        out_shape=[jax.ShapeDtypeStruct(x.shape, f32) for x in parts[:4]]
        + [line] * 3 + [jax.ShapeDtypeStruct((rel_rows, HEADS), f32)],
        in_specs=[vmem] * 5,
        out_specs=[vmem] * 8,
        compiler_params=pltpu.CompilerParams(vmem_limit_bytes=VMEM_LIMIT),
        cost_estimate=cost(2, 2),
        name="deliver",
    )(*parts)


def unpack_kernel(shards, first_ref, first_other_ref, second_ref, second_other_ref, in_ref, out_ref):
    hs = FF // 2 // shards
    deep = in_ref.shape[0]
    owners = FT // hs
    for h in range(2):
        def load(start, count):
            rows = slice(start, start + count)
            mine, theirs = ((first_ref, first_other_ref), (second_ref, second_other_ref))[h]
            return mine[rows, :].astype(f32) + theirs[rows, :].astype(f32)

        row = 0
        for f in range(FF // 2 // FT):
            for g in range(2):
                x = load(row, deep)
                for o in range(owners):
                    start = g * FF + (f * owners + o) * 2 * hs + h * hs
                    in_ref[:, start : start + hs] = x[:, o * hs : (o + 1) * hs]
                row += deep
        for i in range(3):
            out_ref[h * hs : (h + 1) * hs, i * FT : (i + 1) * FT] = load(row, hs)
            row += hs


def unpack(first, first_other, second, second_other, shards):
    vmem = pl.BlockSpec(memory_space=pltpu.VMEM)
    return pl.pallas_call(
        lambda *refs: unpack_kernel(shards, *refs),
        out_shape=[
            jax.ShapeDtypeStruct((D // shards, 2 * FF), f32),
            jax.ShapeDtypeStruct((FF // shards, D), f32),
        ],
        in_specs=[vmem] * 4,
        out_specs=[vmem] * 2,
        compiler_params=pltpu.CompilerParams(vmem_limit_bytes=VMEM_LIMIT),
        cost_estimate=cost(3, 5),
        name="unpack",
    )(first, first_other, second, second_other)


def send_cotangent(slots, cotangent):
    replicas = lax.axis_size("rep")
    places = jnp.arange(replicas)
    rep = lax.axis_index("rep")
    asked = jnp.where(places[None, :] == rep, slots, 0).sum(axis=1) - 1
    turned = (places[None, :] == (rep + places[:, None]) % replicas) * asked[None, :]
    pieces = list(pick(jnp.maximum(turned.sum(axis=1), 0), cotangent))
    for shift in range(1, replicas):
        pieces[shift] = lax.ppermute(pieces[shift], "rep", [(r, (r + shift) % replicas) for r in range(replicas)])
    return pieces


def swap(x, bit):
    replicas = lax.axis_size("rep")
    return lax.ppermute(x, "rep", [(r, r ^ bit) for r in range(replicas)])


def add_low(a, b):
    return (a.astype(f32) + b.astype(f32)).astype(bf16)


def scatter_sum(grad):
    return lax.psum_scatter(grad, "shard", scatter_dimension=0, tiled=True)


def body(
    byte_ids, lengths, target, rel_bucket, cotangent, embed, conv_w, score_w, gain_attn,
    attn_in, attn_out, gain_ffn, ffn_in, ffn_out, rel_table,
):
    seqs = byte_ids.shape[0]
    replicas, shards = lax.axis_size("rep"), lax.axis_size("shard")
    attn_w = lax.all_gather(attn_in, "shard", axis=0, tiled=True)
    table, vecs, rel, slots, ids_col, ids_row, pack0, pack1 = prepare(
        lengths, target, embed, conv_w, score_w, gain_attn, gain_ffn, rel_table, byte_ids,
        attn_out, ffn_in, ffn_out, replicas, shards,
    )
    packs = [lax.all_gather(pack, "shard", axis=0) for pack in (pack0, pack1)]
    rows = bucket_rows(rel_bucket)

    hidden, hidden_low, normed, normed_t, convolved, weights, e_low, coefs = gbst_forward(lengths, ids_col, table, vecs)
    qkv = jnp.dot(normed, attn_w, preferred_element_type=f32).astype(bf16)
    qkv, slots = lax.optimization_barrier((qkv, slots))
    pieces = send_cotangent(slots[:, 0, :replicas], cotangent)
    ctx, lse = attn_forward(lengths, qkv, rel, rows)
    ctx, pieces = lax.optimization_barrier((ctx, pieces))
    shifts = (lax.axis_index("rep") - target // seqs // shards) % replicas
    attended, low, low_t, d_out, d_out_t = post_attention(
        lengths, shifts, ctx, packs[0], hidden, vecs, pieces, shards
    )
    g_half1, y1, dx1 = ffn_first(low, d_out, low_t, d_out_t, packs[0], shards)
    g_half2, out, d_att, d_ctx, g_attn_out, g_gain_ffn = ffn_second(
        lengths, low, d_out, low_t, d_out_t, packs[1], attended, y1, dx1, ctx, packs[0], vecs, shards
    )
    one, two = [scatter_sum(g.reshape(-1, FT)) for g in (g_half1, g_half2)]
    bits = [1 << b for b in range(replicas.bit_length() - 1)]
    d_ctx, one = lax.optimization_barrier((d_ctx, one))
    other = swap(one, bits[0])
    dqkv, g_rel = attn_backward(lengths, qkv, d_ctx, ctx, lse, rel, rows, shards)
    dqkv, other = lax.optimization_barrier((dqkv, other))
    one = add_low(one, other)
    g_attn = qkv_grad(dqkv, normed_t, g_attn_out)
    g_attn, two = lax.optimization_barrier((g_attn, two))
    p_attn = scatter_sum(g_attn)
    for bit in bits[1:-1]:
        one = add_low(one, swap(one, bit))
    others = swap(one, bits[-1]), swap(two, bits[0])
    d_hidden, g_gain_attn = qkv_backward(dqkv, attn_w, hidden_low, d_att, vecs)
    d_hidden, others = lax.optimization_barrier((d_hidden, others))
    other_one, two = others[0], add_low(two, others[1])
    for bit in bits[1:-1]:
        two = add_low(two, swap(two, bit))
    d_hidden, two = lax.optimization_barrier((d_hidden, two))
    other = swap(two, bits[-1])
    input_grad, small = gbst_backward(
        ids_row, vecs, d_hidden, convolved, weights, e_low, coefs,
        g_gain_attn, g_gain_ffn, g_rel,
    )
    small, other = lax.optimization_barrier((small, other))
    parts = finish(p_attn, small, replicas, shards)
    s_ffn_in, s_ffn_out = unpack(one, other_one, two, other, shards)
    s_attn_in, s_attn_out, s_embed, s_conv, s_score, s_gain_attn, s_gain_ffn, s_rel = deliver(parts, rel_table.shape[0])
    return (
        out.reshape(seqs, TOK, D), input_grad, s_embed, s_conv, s_score, s_gain_attn, s_attn_in, s_attn_out,
        s_gain_ffn, s_ffn_in, s_ffn_out, s_rel,
    )


def solution(mesh):
    in_specs = (
        P(("rep", "shard"), None), P(("rep", "shard")), P(("rep", "shard")), P(),
        P(("rep", "shard"), None, None), P(None, "shard"), P(None, "shard"), P("shard"), P("shard"),
        P("shard", None), P("shard", None), P("shard"), P("shard", None), P("shard", None), P("shard", None),
    )
    out_specs = (
        P(("rep", "shard"), None, None), P(("rep", "shard"), None, None), P(None, "shard"), P(None, "shard"),
        P("shard"), P("shard"), P("shard", None), P("shard", None), P("shard"), P("shard", None),
        P("shard", None), P("shard", None),
    )
    return jax.shard_map(body, mesh=mesh, in_specs=in_specs, out_specs=out_specs, check_vma=False)
```

```python
import jax
import jax.numpy as jnp
from jax import lax
from jax.experimental import pallas as pl
from jax.experimental.pallas import tpu as pltpu
from jax.sharding import PartitionSpec as P

D = 768
VOCAB = 259
VROWS = 272
VMEM_LIMIT = 60 << 20
SMALL = 384
MAXLEN = 1024
TOK = 512
LANES = 128
QN = 88
R = 12
P_ROWS = QN * R
T_ROWS = 528
LT = D // LANES
epsilon = 1e-06
f32 = jnp.float32
bf16 = jnp.bfloat16


def cost(us, mib):
    return pl.CostEstimate(flops=int(us * 1e9), bytes_accessed=mib << 20, transcendentals=0)


def lane_iota(rows):
    return lax.broadcasted_iota(jnp.int32, (rows, LANES), 1)


def group_matrix(b):
    row = lax.broadcasted_iota(jnp.int32, (LANES, LANES), 0)
    col = lax.broadcasted_iota(jnp.int32, (LANES, LANES), 1)
    return jnp.where((row // b == col // b) & (row < R) & (col < R), 1.0, 0.0).astype(f32)


def exact_dot(a, b):
    return jnp.dot(a, b, precision=lax.Precision.HIGHEST, preferred_element_type=f32)


def place(columns, rows):
    lanes = lane_iota(rows)
    out = jnp.zeros((rows, LANES), f32)
    for r, column in enumerate(columns):
        out = jnp.where(lanes == r, column, out)
    return out


def gbst_masks(length):
    q = lax.broadcasted_iota(jnp.int32, (QN, LANES), 0)
    r = lax.broadcasted_iota(jnp.int32, (QN, LANES), 1)
    mask = jnp.where((q * R + r < length) & (r < R), 1.0, 0.0).astype(f32)
    inverse = [1.0 / jnp.maximum(exact_dot(mask, group_matrix(b)), 1.0) for b in (2, 3, 4)]
    pair = exact_dot(mask, group_matrix(2))
    alpha = mask / jnp.maximum(pair, 1.0)
    return mask, inverse, alpha


def gbst_weights(s1, inverse):
    sizes = [s1] + [exact_dot(s1, group_matrix(b)) * inv for b, inv in zip((2, 3, 4), inverse)]
    top = jnp.maximum(jnp.maximum(sizes[0], sizes[1]), jnp.maximum(sizes[2], sizes[3]))
    parts = [jnp.exp(s - top) for s in sizes]
    total = parts[0] + parts[1] + parts[2] + parts[3]
    return [p / total for p in parts]


def gbst_coefs(weights, inverse, alpha):
    a1 = weights[0] * alpha
    a2 = weights[1] * alpha * inverse[0]
    a3 = weights[2] * alpha * inverse[1]
    a4 = weights[3] * alpha * inverse[2]
    pair = group_matrix(2)
    a4s = exact_dot(a4, pair)
    own = a1 + exact_dot(a2, pair) + a4s
    return own, a3, a4s


def column(x, r):
    return jnp.broadcast_to(x[:, r : r + 1], (x.shape[0], LANES))


def hits_of(ids):
    lanes = lax.broadcasted_iota(jnp.int32, (P_ROWS, LANES), 1).astype(f32)
    return jnp.concatenate(
        [jnp.where(ids == lanes + float(i * LANES), 1.0, 0.0).astype(bf16) for i in range(SMALL // LANES)], axis=1)


def look_up(ids, table_ref):
    return lax.dot_general(
        hits_of(ids), table_ref[...].reshape(D, SMALL), (((1,), (1,)), ((), ())), preferred_element_type=f32)


def load_e(e_ref, r, lt):
    lanes = pl.ds(lt * LANES, LANES)
    if r < R:
        return e_ref[pl.ds(r * QN, QN), lanes]
    return e_ref[pl.ds((r - R) * QN + 1, QN), lanes]


def gbst_fwd_kernel(len_ref, ids_ref, table_ref, vec_ref, hlow_ref, normed_ref, turned_ref, c_ref, w_ref, elow_ref, kc_ref, e_ref, hid_ref, s_ref):
    k_ref = kc_ref.at[0]
    length = len_ref[pl.program_id(0)]
    rows_e = look_up(ids_ref[0], table_ref)
    e_ref[pl.ds(0, P_ROWS), :] = rows_e
    elow_ref[0] = rows_e.astype(bf16)
    e_ref[pl.ds(P_ROWS, 8), :] = jnp.zeros((8, D), f32)
    for lt in range(LT):
        lanes = pl.ds(lt * LANES, LANES)
        taps = [jnp.broadcast_to(vec_ref[j : j + 1, lanes], (QN, LANES)) for j in range(4)]
        sw = jnp.broadcast_to(vec_ref[4:5, lanes], (QN, LANES))
        for r in range(R):
            c = taps[0] * load_e(e_ref, r, lt)
            for j in range(1, 4):
                c = c + taps[j] * load_e(e_ref, r + j, lt)
            c_ref[0, pl.ds(r * QN, QN), lanes] = c
            part = c * sw
            rows = pl.ds(r * QN, QN)
            s_ref[rows, :] = part if lt == 0 else s_ref[rows, :] + part
    s1 = place([jnp.sum(s_ref[pl.ds(r * QN, QN), :], axis=1, keepdims=True) for r in range(R)], QN)
    mask, inverse, alpha = gbst_masks(length)
    weights = gbst_weights(s1, inverse)
    for b, kept in enumerate(weights + inverse + [alpha]):
        w_ref[0, b] = kept
    own, a3, a4s = gbst_coefs(weights, inverse, alpha)
    n = 0
    for r in range(R):
        k_ref[r] = column(own, r)
        k_ref[R + r] = column(a3, r)
    for k in range(6):
        k_ref[2 * R + k] = column(a4s, 2 * k)
    for r in range(R):
        k_ref[2 * R + 6 + r] = column(mask, r)
    for lt in range(LT):
        lanes = pl.ds(lt * LANES, LANES)
        for half in range(2):
            c = [c_ref[0, pl.ds((half * 6 + r) * QN, QN), lanes] for r in range(6)]
            base = half * 6
            s3 = [c[0] + c[1] + c[2], c[3] + c[4] + c[5]]
            for k in range(3):
                tok = half * 3 + k
                other = tok ^ 1
                rows = pl.ds(2 * other * QN, QN)
                rows1 = pl.ds((2 * other + 1) * QN, QN)
                s2 = c_ref[0, rows, lanes] + c_ref[0, rows1, lanes]
                h = k_ref[2 * tok] * c[2 * k] + k_ref[2 * tok + 1] * c[2 * k + 1] + k_ref[2 * R + tok] * s2
                if k == 1:
                    h = h + k_ref[R + 2 * tok] * s3[0] + k_ref[R + 2 * tok + 1] * s3[1]
                else:
                    h = h + (k_ref[R + 2 * tok] + k_ref[R + 2 * tok + 1]) * s3[0 if k == 0 else 1]
                hid_ref[lt, pl.ds(tok, QN, stride=6), :] = h
    total = jnp.zeros((TOK, LANES), f32)
    for lt in range(LT):
        x = hid_ref[lt, 0:TOK, :]
        total = total + x * x
    scale = lax.rsqrt(jnp.sum(total, axis=1, keepdims=True) * (1.0 / D) + epsilon)
    for lt in range(LT):
        lanes = pl.ds(lt * LANES, LANES)
        x = hid_ref[lt, 0:TOK, :]
        hlow_ref[:, lanes] = x.astype(bf16)
        normed = (x * scale * vec_ref[5:6, lanes]).astype(bf16)
        normed_ref[:, lanes] = normed
        turned_ref[lanes, :] = normed.T


def gbst_forward(lengths, ids_col, table, vecs):
    seqs = ids_col.shape[0]
    grid_spec = pltpu.PrefetchScalarGridSpec(
        num_scalar_prefetch=1,
        grid=(seqs,),
        in_specs=[
            pl.BlockSpec((1, P_ROWS, LANES), lambda s, n: (s, 0, 0)),
            pl.BlockSpec(table.shape, lambda s, n: (0, 0, 0)),
            pl.BlockSpec((8, D), lambda s, n: (0, 0)),
        ],
        out_specs=[
            pl.BlockSpec((TOK, D), lambda s, n: (s, 0)),
            pl.BlockSpec((TOK, D), lambda s, n: (s, 0)),
            pl.BlockSpec((D, TOK), lambda s, n: (0, s)),
            pl.BlockSpec((1, P_ROWS, D), lambda s, n: (s, 0, 0)),
            pl.BlockSpec((1, 8, QN, LANES), lambda s, n: (s, 0, 0, 0)),
            pl.BlockSpec((1, P_ROWS, D), lambda s, n: (s, 0, 0)),
            pl.BlockSpec((1, 3 * R + 6, QN, LANES), lambda s, n: (s, 0, 0, 0)),
        ],
        scratch_shapes=[
            pltpu.VMEM((P_ROWS + 8, D), f32),
            pltpu.VMEM((LT, T_ROWS, LANES), f32),
            pltpu.VMEM((P_ROWS, LANES), f32),
        ],
    )
    return pl.pallas_call(
        gbst_fwd_kernel,
        grid_spec=grid_spec,
        out_shape=[
            jax.ShapeDtypeStruct((seqs * TOK, D), bf16),
            jax.ShapeDtypeStruct((seqs * TOK, D), bf16),
            jax.ShapeDtypeStruct((D, seqs * TOK), bf16),
            jax.ShapeDtypeStruct((seqs, P_ROWS, D), f32),
            jax.ShapeDtypeStruct((seqs, 8, QN, LANES), f32),
            jax.ShapeDtypeStruct((seqs, P_ROWS, D), bf16),
            jax.ShapeDtypeStruct((seqs, 3 * R + 6, QN, LANES), f32),
        ],
        compiler_params=pltpu.CompilerParams(vmem_limit_bytes=VMEM_LIMIT),
        cost_estimate=cost(18, 30),
        name="gbst_forward",
    )(lengths, ids_col, table, vecs)


def gbst_bwd_kernel(row_ref, vec_ref, dh_ref, c_ref, w_ref, elow_ref, kc_ref, gain1_ref, gain2_ref, rel_ref,
                    ig_ref, small_ref, ge_ref, e_ref, dt_ref, dc_ref, s_ref, cf_ref, igs_ref):
    seq = pl.program_id(0)
    k_ref = kc_ref.at[0]

    @pl.when(seq == 0)
    def _():
        ge_ref[...] = jnp.zeros_like(ge_ref)

    e_ref[pl.ds(0, P_ROWS), :] = elow_ref[0].astype(f32)
    e_ref[pl.ds(P_ROWS, 8), :] = jnp.zeros((8, D), f32)
    for lt in range(LT):
        dt_ref[lt, 0:TOK, :] = dh_ref[:, pl.ds(lt * LANES, LANES)].astype(f32)
        dt_ref[lt, TOK:T_ROWS, :] = jnp.zeros((T_ROWS - TOK, LANES), f32)
    for lt in range(LT):
        lanes = pl.ds(lt * LANES, LANES)
        for half in range(2):
            c = [c_ref[0, pl.ds((half * 6 + r) * QN, QN), lanes] for r in range(6)]
            s3 = [c[0] + c[1] + c[2], c[3] + c[4] + c[5]]
            for k in range(3):
                tok = half * 3 + k
                other = tok ^ 1
                dh = dt_ref[lt, pl.ds(tok, QN, stride=6), :]
                s2 = c_ref[0, pl.ds(2 * other * QN, QN), lanes] + c_ref[0, pl.ds((2 * other + 1) * QN, QN), lanes]
                parts = [
                    (2 * tok, dh * c[2 * k]),
                    (2 * tok + 1, dh * c[2 * k + 1]),
                    (2 * R + tok, dh * s2),
                    (R + 2 * tok, dh * s3[0 if k < 2 else 1]),
                ]
                if k == 1:
                    parts.append((R + 2 * tok + 1, dh * s3[1]))
                for slot, part in parts:
                    s_ref[slot] = part if lt == 0 else s_ref[slot] + part

    def total(slot):
        return jnp.sum(s_ref[slot], axis=1, keepdims=True)

    d1, d3, dother = [], [], []
    for tok in range(6):
        d1 += [total(2 * tok), total(2 * tok + 1)]
        first = total(R + 2 * tok)
        d3 += [first, total(R + 2 * tok + 1) if tok % 3 == 1 else first]
        o = total(2 * R + tok)
        dother += [o, o]
    d1, d3, dother = place(d1, QN), place(d3, QN), place(dother, QN)
    weights = [w_ref[0, b] for b in range(4)]
    inverse = [w_ref[0, 4 + b] for b in range(3)]
    alpha = w_ref[0, 7]
    d2 = exact_dot(d1, group_matrix(2))
    g = [alpha * d1, alpha * d2 * inverse[0], alpha * d3 * inverse[1], alpha * (d2 + dother) * inverse[2]]
    mean = weights[0] * g[0] + weights[1] * g[1] + weights[2] * g[2] + weights[3] * g[3]
    d_size = [w * (x - mean) for w, x in zip(weights, g)]
    coef = d_size[0]
    for b, inv in zip((2, 3, 4), inverse):
        coef = coef + exact_dot(d_size[b - 1] * inv, group_matrix(b))
    for r in range(R):
        cf_ref[r] = column(coef, r)

    for lt in range(LT):
        lanes = pl.ds(lt * LANES, LANES)
        taps = [jnp.broadcast_to(vec_ref[j : j + 1, lanes], (QN, LANES)) for j in range(4)]
        sw = jnp.broadcast_to(vec_ref[4:5, lanes], (QN, LANES))
        gs = jnp.zeros((QN, LANES), f32)
        gc = [jnp.zeros((QN, LANES), f32) for _ in range(4)]
        for half in range(2):
            dh = [dt_ref[lt, pl.ds(half * 3 + k, QN, stride=6), :] for k in range(3)]
            a = R + half * 6
            t3 = [
                (k_ref[a] + k_ref[a + 1]) * dh[0] + k_ref[a + 2] * dh[1],
                k_ref[a + 3] * dh[1] + (k_ref[a + 4] + k_ref[a + 5]) * dh[2],
            ]
            for k in range(3):
                tok = half * 3 + k
                other = tok ^ 1
                dother_h = dt_ref[lt, pl.ds(other, QN, stride=6), :]
                cross = k_ref[2 * R + other] * dother_h
                for e in range(2):
                    r = 2 * tok + e
                    cf = cf_ref[r]
                    dc = k_ref[r] * dh[k] + cross + t3[(r % 6) // 3] + cf * sw
                    gs = gs + cf * c_ref[0, pl.ds(r * QN, QN), lanes]
                    dc_ref[r, pl.ds(8, QN), :] = dc
                    for j in range(4):
                        gc[j] = gc[j] + dc * load_e(e_ref, r + j, lt)
        ge_ref[VROWS + 4 : VROWS + 5, lanes] += jnp.sum(gs, axis=0, keepdims=True)
        for j in range(4):
            ge_ref[VROWS + j : VROWS + j + 1, lanes] += jnp.sum(gc[j], axis=0, keepdims=True)
        for r in range(R):
            dc_ref[r, 0:8, :] = jnp.zeros((8, LANES), f32)
        for r in range(R):
            x = taps[0] * dc_ref[r, pl.ds(8, QN), :]
            for j in range(1, 4):
                back = dc_ref[r - j, pl.ds(8, QN), :] if r >= j else dc_ref[r - j + R, pl.ds(7, QN), :]
                x = x + taps[j] * back
            igs_ref[lt, pl.ds(r, QN, stride=R), :] = x * k_ref[2 * R + 6 + r]
    for lt in range(LT):
        lanes = pl.ds(lt * LANES, LANES)
        ig_ref[0, :, lanes] = igs_ref[lt, 0:MAXLEN, :].astype(bf16)
    vocab = lax.broadcasted_iota(jnp.int32, (VROWS, MAXLEN), 0)
    row_hits = jnp.where(vocab == row_ref[0], 1.0, 0.0).astype(bf16)
    ge_ref[0:VROWS, :] += jnp.dot(row_hits, ig_ref[0], preferred_element_type=f32)

    @pl.when(seq == pl.num_programs(0) - 1)
    def _():
        ge_ref[VROWS + 5 : VROWS + 6, :] = gain1_ref[...]
        ge_ref[VROWS + 6 : VROWS + 7, :] = gain2_ref[...]
        ge_ref[VROWS + 7 : VROWS + 15, :] = rel_ref[...]
        for lt in range(LT):
            lanes = pl.ds(lt * LANES, LANES)
            small_ref[lanes, :] = ge_ref[:, lanes].T.astype(bf16)


def gbst_backward(ids_row, vecs, d_hidden, c, w, e_low, coefs, gain1, gain2, rel):
    seqs = ids_row.shape[0]
    per_seq = lambda *shape: pl.BlockSpec((1,) + shape, lambda s: (s,) + (0,) * len(shape))
    still = lambda *shape: pl.BlockSpec(shape, lambda s: (0,) * len(shape))
    return pl.pallas_call(
        gbst_bwd_kernel,
        grid=(seqs,),
        in_specs=[
            per_seq(1, MAXLEN), still(8, D), pl.BlockSpec((TOK, D), lambda s: (s, 0)), per_seq(P_ROWS, D),
            per_seq(8, QN, LANES), per_seq(P_ROWS, D), per_seq(3 * R + 6, QN, LANES),
            still(1, D), still(1, D), still(8, D),
        ],
        out_specs=[per_seq(MAXLEN, D), still(D, SMALL)],
        scratch_shapes=[
            pltpu.VMEM((SMALL, D), f32),
            pltpu.VMEM((P_ROWS + 8, D), f32),
            pltpu.VMEM((LT, T_ROWS, LANES), f32),
            pltpu.VMEM((R, QN + 8, LANES), f32),
            pltpu.VMEM((2 * R + 6, QN, LANES), f32),
            pltpu.VMEM((R, QN, LANES), f32),
            pltpu.VMEM((LT, P_ROWS, LANES), f32),
        ],
        out_shape=[
            jax.ShapeDtypeStruct((seqs, MAXLEN, D), bf16),
            jax.ShapeDtypeStruct((D, SMALL), bf16),
        ],
        compiler_params=pltpu.CompilerParams(vmem_limit_bytes=VMEM_LIMIT),
        cost_estimate=cost(26, 40),
        name="gbst_backward",
    )(ids_row, vecs, d_hidden, c, w, e_low, coefs, gain1, gain2, rel)


HEADS = 12
HD = 64
BUCKETS = 32
SPAN = 1024
HB = 4
WIDE = HB * HD
GROUPS = HEADS // HB
dead_score = -1e9


def nt(a, b):
    return lax.dot_general(a, b, (((1,), (1,)), ((), ())), preferred_element_type=f32)


def nn(a, b):
    return jnp.dot(a, b, preferred_element_type=f32)


def bucket_rows(buckets):
    def row(x):
        return jnp.concatenate([x[TOK - 1 :], x[:1], x[: TOK - 1]])

    return jnp.stack([row(buckets), row(buckets[::-1])])


def bucket_hits(row_ref, way):
    return jnp.where(lax.broadcasted_iota(jnp.int32, (BUCKETS, SPAN), 0) == row_ref[way : way + 1, :], 1.0, 0.0).astype(f32)


def spread_table(rel_ref, row_ref, z_ref, way):
    dims = (((0,), (0,)), ((), ()))
    z_ref[...] = lax.dot_general(
        rel_ref[...].astype(bf16), bucket_hits(row_ref, way).astype(bf16), dims, preferred_element_type=f32)


def build_bias(z_ref, bt_ref, group):
    for h in range(HB):
        row = jnp.broadcast_to(z_ref[pl.ds(group * HB + h, 1), :], (8, SPAN))
        z = pltpu.roll(row, 0, 1, stride=1, stride_axis=0)
        for g in range(TOK // 8):
            bt_ref[h, pl.ds(8 * g, 8), :] = (z if g == 0 else pltpu.roll(z, 8 * g, 1))[:, :TOK]


def pair_lanes(h):
    return slice(h // 2 * LANES, (h // 2 + 1) * LANES)


def own_lanes(h):
    return lax.broadcasted_iota(jnp.int32, (TOK, LANES), 1) // HD == h % 2


def head_parts(k, q, length, h):
    lanes = lax.broadcasted_iota(jnp.int32, (TOK, LANES), 1)
    rows = lax.broadcasted_iota(jnp.int32, (TOK, LANES), 0)
    spare = HD * (1 - h % 2)
    dead = jnp.where(2 * rows < length, 0.0, dead_score)
    kf = jnp.where(own_lanes(h), k[:, pair_lanes(h)].astype(f32), jnp.where(lanes == spare, dead, 0.0)).astype(bf16)
    qf = jnp.where(lanes == spare, 1.0, q[:, pair_lanes(h)].astype(f32)).astype(bf16)
    return kf, qf


def join_heads(parts):
    pairs = [jnp.where(own_lanes(0), parts[h], parts[h + 1]) for h in range(0, HB, 2)]
    return jnp.concatenate(pairs, axis=1).astype(bf16)


def attn_fwd_kernel(len_ref, q_ref, k_ref, v_ref, rel_ref, row_ref, ctx_ref, lse_ref, bias_ref, z_ref):
    length = len_ref[pl.program_id(1)]

    @pl.when((pl.program_id(0) == 0) & (pl.program_id(1) == 0))
    def _():
        spread_table(rel_ref, row_ref, z_ref, 0)

    @pl.when(pl.program_id(1) == 0)
    def _():
        build_bias(z_ref, bias_ref, pl.program_id(0))

    q, k, v = q_ref[...], k_ref[...], v_ref[...]

    def score(h):
        kf, qf = head_parts(k, q, length, h)
        return nt(qf, kf) + bias_ref[h]

    outs = []
    lanes = lax.broadcasted_iota(jnp.int32, (TOK, LANES), 1)
    lse = jnp.zeros((TOK, LANES), f32)
    s = score(0)
    for h in range(HB):
        later = score(h + 1) if h + 1 < HB else None
        top = jnp.max(s, axis=1, keepdims=True)
        p = jnp.exp(s - top)
        total = jnp.sum(p, axis=1, keepdims=True)
        outs.append(nn(p.astype(bf16), v[:, pair_lanes(h)]) * (1.0 / total))
        lse = jnp.where(lanes == h, top + jnp.log(total), lse)
        s = later
    ctx_ref[...] = join_heads(outs)
    lse_ref[0, 0] = lse.T[0:8]


def table_specs():
    return [
        pl.BlockSpec((BUCKETS, LANES), lambda hp, s, n: (0, 0)),
        pl.BlockSpec((2, SPAN), lambda hp, s, n: (0, 0)),
    ]


def attn_forward(lengths, qkv, rel, row):
    seqs = qkv.shape[0] // TOK
    spec = lambda off: pl.BlockSpec((TOK, WIDE), lambda hp, s, n: (s, off + hp))
    return pl.pallas_call(
        attn_fwd_kernel,
        grid_spec=pltpu.PrefetchScalarGridSpec(
            num_scalar_prefetch=1,
            grid=(GROUPS, seqs),
            in_specs=[spec(0), spec(GROUPS), spec(2 * GROUPS)] + table_specs(),
            out_specs=[spec(0), pl.BlockSpec((1, 1, 8, TOK), lambda hp, s, n: (hp, s, 0, 0))],
            scratch_shapes=[pltpu.VMEM((HB, TOK, TOK), f32), pltpu.VMEM((LANES, SPAN), f32)],
        ),
        out_shape=[
            jax.ShapeDtypeStruct((seqs * TOK, D), bf16),
            jax.ShapeDtypeStruct((GROUPS, seqs, 8, TOK), f32),
        ],
        compiler_params=pltpu.CompilerParams(vmem_limit_bytes=VMEM_LIMIT),
        cost_estimate=cost(27, 20),
        name="attn_forward",
    )(lengths, qkv, qkv, qkv, rel, row)


def attn_bwd_kernel(shards, len_ref, q_ref, k_ref, v_ref, do_ref, o_ref, lse_ref, rel_ref, row_ref, dqkv_ref, gt_ref, bt_ref, g_ref, z_ref, gz_ref):
    s_id = pl.program_id(1)
    length = len_ref[s_id]

    @pl.when((pl.program_id(0) == 0) & (s_id == 0))
    def _():
        spread_table(rel_ref, row_ref, z_ref, 1)
        gz_ref[...] = jnp.zeros_like(gz_ref)

    @pl.when(s_id == 0)
    def _():
        build_bias(z_ref, bt_ref, pl.program_id(0))
        g_ref[...] = jnp.zeros_like(g_ref)

    q, k, v, do = q_ref[...], k_ref[...], v_ref[...], do_ref[...]
    kt = k.astype(f32).T.astype(bf16)
    lanes8 = lax.broadcasted_iota(jnp.int32, (8, WIDE), 1)
    rows8 = lax.broadcasted_iota(jnp.int32, (8, WIDE), 0)
    pick = jnp.where(lanes8 // HD == rows8, 1.0, 0.0).astype(bf16)
    prod = do.astype(f32) * o_ref[...].astype(f32)
    upper = prod.astype(bf16)
    delta = nt(pick, upper) + nt(pick, (prod - upper.astype(f32)).astype(bf16))
    dq, dk, dv = [], [], []

    def first(h):
        kf, qf = head_parts(k, q, length, h)
        vf = jnp.where(own_lanes(h), v[:, pair_lanes(h)].astype(f32), 0.0).astype(bf16)
        return nt(kf, qf) + bt_ref[h], nt(vf, do[:, pair_lanes(h)])

    for h in range(HB):
        s, d_prob = first(h)
        p = jnp.exp(s - lse_ref[0, 0, h : h + 1, :])
        ds = p * (d_prob - delta[h : h + 1, :])
        g_ref[h] += ds
        low = ds.astype(bf16)
        dv.append(nn(p.astype(bf16), do[:, pair_lanes(h)]))
        dk.append(nn(low, q[:, pair_lanes(h)]))
        start = h % 2 * HD
        dq.append(nn(kt[pair_lanes(h)], low)[start : start + HD])
    dqkv_ref[0] = jnp.concatenate(dq, axis=0).T.astype(bf16)
    dqkv_ref[1] = join_heads(dk)
    dqkv_ref[2] = join_heads(dv)

    @pl.when(s_id == pl.num_programs(1) - 1)
    def _():
        for h in range(HB):
            total = jnp.zeros((8, SPAN), f32)
            for g in range(LANES // 8):
                tiles = [jnp.zeros((8, LANES), f32) for _ in range(SPAN // LANES)]
                for j in range(TOK // LANES):
                    x = g_ref[h, pl.ds(LANES * j + 8 * g, 8), :]
                    for t in range(TOK // LANES):
                        n = (t - j) % (SPAN // LANES)
                        tiles[n] = tiles[n] + x[:, t * LANES : (t + 1) * LANES]
                piece = jnp.concatenate(tiles, axis=1)
                total = total + (piece if g == 0 else pltpu.roll(piece, SPAN - 8 * g, 1))
            out = total[0:1]
            for s in range(1, 8):
                out = out + pltpu.roll(jnp.broadcast_to(total[s : s + 1], (8, SPAN)), SPAN - s, 1)[0:1]
            gz_ref[pl.ds(pl.program_id(0) * HB + h, 1), :] = out

    @pl.when((pl.program_id(0) == GROUPS - 1) & (s_id == pl.num_programs(1) - 1))
    def _():
        total = lax.dot_general(
            bucket_hits(row_ref, 1), gz_ref[...], (((1,), (1,)), ((), ())),
            precision=lax.Precision.HIGHEST, preferred_element_type=f32)
        gt_ref[...] = jnp.zeros_like(gt_ref)
        per = BUCKETS // shards
        for s in range(shards):
            start = s * (D // shards)
            gt_ref[0:per, start : start + HEADS] = total[s * per : (s + 1) * per, 0:HEADS]


def attn_backward(lengths, qkv, d_ctx, ctx, lse, rel, row, shards):
    seqs = qkv.shape[0] // TOK
    spec = lambda off: pl.BlockSpec((TOK, WIDE), lambda hp, s, n: (s, off + hp))
    return pl.pallas_call(
        lambda *refs: attn_bwd_kernel(shards, *refs),
        grid_spec=pltpu.PrefetchScalarGridSpec(
            num_scalar_prefetch=1,
            grid=(GROUPS, seqs),
            in_specs=[
                spec(0), spec(GROUPS), spec(2 * GROUPS), spec(0), spec(0),
                pl.BlockSpec((1, 1, 8, TOK), lambda hp, s, n: (hp, s, 0, 0)),
            ] + table_specs(),
            out_specs=[
                pl.BlockSpec((3, TOK, WIDE), lambda hp, s, n: (0, s, hp)),
                pl.BlockSpec((8, D), lambda hp, s, n: (0, 0)),
            ],
            scratch_shapes=[
                pltpu.VMEM((HB, TOK, TOK), f32), pltpu.VMEM((HB, TOK, TOK), f32),
                pltpu.VMEM((LANES, SPAN), f32), pltpu.VMEM((16, SPAN), f32),
            ],
        ),
        out_shape=[
            jax.ShapeDtypeStruct((3, seqs * TOK, D), bf16),
            jax.ShapeDtypeStruct((8, D), f32),
        ],
        compiler_params=pltpu.CompilerParams(vmem_limit_bytes=VMEM_LIMIT),
        cost_estimate=cost(46, 30),
        name="attn_backward",
    )(lengths, qkv, qkv, qkv, d_ctx, ctx, lse, rel, row)


FF = 2048
FT = 256
RC = 1024
MT = 512


def rms_scale(x):
    return lax.rsqrt(jnp.sum(x * x, axis=1, keepdims=True) * (1.0 / D) + epsilon)


def post_kernel(len_ref, shift_ref, ctx_ref, w_ref, hidden_ref, vec_ref, *refs):
    pieces, (att_ref, low_ref, low_t_ref, do_ref, do_t_ref) = refs[:-5], refs[-5:]
    s = pl.program_id(0)
    for i, piece in enumerate(pieces):
        @pl.when(shift_ref[s] == i)
        def _():
            do_ref[...] = piece[...]

    live = 2 * lax.broadcasted_iota(jnp.int32, (TOK, D), 0) < len_ref[s]
    d_out = jnp.where(live, do_ref[...].astype(f32), 0.0).astype(bf16)
    do_ref[...] = d_out
    do_t_ref[...] = d_out.T
    att = hidden_ref[...].astype(f32) + nn(ctx_ref[...], out_weights(w_ref))
    att_ref[...] = att.astype(bf16)
    low = (att * rms_scale(att) * vec_ref[6:7, :]).astype(bf16)
    low_ref[...] = low
    low_t_ref[...] = low.T


def rows_spec(width=D):
    return pl.BlockSpec((TOK, width), lambda s, *n: (s, 0))


def whole(*shape):
    return pl.BlockSpec(shape, lambda s, *n: (0,) * len(shape))


def out_block(shards):
    deep = D // shards
    return pl.BlockSpec((shards, 3 * deep, FT), lambda s, *n: (0, 4, 0))


def out_weights(ref):
    deep = ref.shape[1] // 3
    return jnp.concatenate([ref[:, i * deep : (i + 1) * deep, :].reshape(D, FT) for i in range(3)], axis=1)


def post_attention(lengths, shifts, ctx, pack, hidden, vecs, pieces, shards):
    rows = ctx.shape[0]
    cols_spec = pl.BlockSpec((D, TOK), lambda s, *n: (0, s))
    return pl.pallas_call(
        post_kernel,
        grid_spec=pltpu.PrefetchScalarGridSpec(
            num_scalar_prefetch=2,
            grid=(rows // TOK,),
            in_specs=[rows_spec(), out_block(shards), rows_spec(), whole(8, D)] + [whole(TOK, D)] * len(pieces),
            out_specs=[rows_spec(), rows_spec(), cols_spec, rows_spec(), cols_spec],
        ),
        out_shape=[
            jax.ShapeDtypeStruct((rows, D), bf16),
            jax.ShapeDtypeStruct((rows, D), bf16),
            jax.ShapeDtypeStruct((D, rows), bf16),
            jax.ShapeDtypeStruct((rows, D), bf16),
            jax.ShapeDtypeStruct((D, rows), bf16),
        ],
        compiler_params=pltpu.CompilerParams(vmem_limit_bytes=VMEM_LIMIT),
        cost_estimate=cost(10, 30),
        name="post_attention",
    )(lengths, shifts, ctx, pack, hidden, vecs, *pieces)


def gelu_parts(v):
    c = 0.7978845608
    v2 = v * v
    t = jnp.tanh(v * (c + (c * 0.044715) * v2))
    half = 0.5 + 0.5 * t
    gelu = v * half
    slope = half + (0.5 * v) * (1.0 - t * t) * (c + (3.0 * c * 0.044715) * v2)
    return gelu, slope


def ffn_steps(x_any, d_any, xt_any, dt_any, wgu_ref, wo_ref, grad_ref, y_any, dx_any,
              x_ref, d_ref, xt_ref, dt_ref, y_ref, dx_ref, a_ref, dg_ref, du_ref, gu_ref, go_ref, in_sem, out_sem, sems,
              low_ref=None):
    f = pl.program_id(0)
    steps = FF // 2 // FT
    rows_total = x_ref.shape[0]
    chunks = rows_total // RC
    shards, part = gu_ref.shape[1], gu_ref.shape[2]
    owners, deep = go_ref.shape[1], go_ref.shape[2]
    base = steps * part

    def copies(slot, step):
        return (
            pltpu.make_async_copy(
                gu_ref.at[slot], grad_ref.at[:, pl.ds(step * part, part), :], sems.at[0, slot]),
            pltpu.make_async_copy(
                go_ref.at[slot], grad_ref.at[pl.ds(step * owners, owners), pl.ds(base, deep), :], sems.at[1, slot]),
        )

    def row_loads(i):
        rows = pl.ds(i * RC, RC)
        return (
            pltpu.make_async_copy(x_any.at[rows], x_ref.at[rows], in_sem.at[0, i]),
            pltpu.make_async_copy(d_any.at[rows], d_ref.at[rows], in_sem.at[1, i]),
        )

    def turned_loads():
        return (
            pltpu.make_async_copy(xt_any, xt_ref, in_sem.at[2, 0]),
            pltpu.make_async_copy(dt_any, dt_ref, in_sem.at[2, 1]),
        )

    def row_stores(i):
        rows = pl.ds(i * RC, RC)
        return (
            pltpu.make_async_copy(low_ref.at[0, rows], y_any.at[rows], out_sem.at[0, i]),
            pltpu.make_async_copy(low_ref.at[1, rows], dx_any.at[rows], out_sem.at[1, i]),
        )

    @pl.when(f == 0)
    def _():
        for i in range(chunks):
            for copy in row_loads(i):
                copy.start()
        for copy in turned_loads():
            copy.start()

    d_rows = part // 2
    third = deep // 3
    wg = wgu_ref[:, 0:d_rows, :].reshape(D, FT)
    wu = wgu_ref[:, d_rows:part, :].reshape(D, FT)
    wgu = jnp.concatenate([wg, wu], axis=1)
    wo = jnp.concatenate(
        [wo_ref[:, i * third : (i + 1) * third, :].reshape(FT, FT) for i in range(3)], axis=1)

    @pl.when(f == 0)
    def _():
        for i in range(chunks):
            for copy in row_loads(i):
                copy.wait()

    def chunk(i, carry):
        rows = pl.ds(pl.multiple_of(i * RC, RC), RC)
        x, d = x_ref[rows, :], d_ref[rows, :]
        gelu, slope = gelu_parts(nn(x, wg))
        up = nn(x, wu)
        da = nt(d, wo)
        act = (gelu * up).astype(bf16)
        dg = (da * up * slope).astype(bf16)
        du = (da * gelu).astype(bf16)
        a_ref[rows, :] = act
        dg_ref[rows, :] = dg
        du_ref[rows, :] = du
        y_ref[rows, :] = nn(act, wo) + jnp.where(f == 0, 0.0, y_ref[rows, :])
        dx_ref[rows, :] = nt(jnp.concatenate([dg, du], axis=1), wgu) + jnp.where(
            f == 0, 0.0, dx_ref[rows, :])
        return carry

    lax.fori_loop(0, chunks, chunk, 0)
    if y_any is not None:

        @pl.when(f == steps - 1)
        def _():
            for i in range(chunks):
                rows = pl.ds(i * RC, RC)
                low_ref[0, rows, :] = y_ref[rows, :].astype(bf16)
                low_ref[1, rows, :] = dx_ref[rows, :].astype(bf16)
                for copy in row_stores(i):
                    copy.start()

    slot = lax.rem(f, 2)

    @pl.when(f == 0)
    def _():
        for copy in turned_loads():
            copy.wait()

    @pl.when(f >= 2)
    def _():
        for copy in copies(slot, f - 2):
            copy.wait()

    gu_ref[slot, :, 0:d_rows, :] = nn(xt_ref[...], dg_ref[...]).astype(bf16).reshape(shards, d_rows, FT)
    gu_ref[slot, :, d_rows:part, :] = nn(xt_ref[...], du_ref[...]).astype(bf16).reshape(shards, d_rows, FT)
    go = nn(dt_ref[...], a_ref[...]).T.astype(bf16)
    for i in range(3):
        go_ref[slot, :, i * third : (i + 1) * third, :] = go[:, i * FT : (i + 1) * FT].reshape(owners, third, FT)
    for copy in copies(slot, f):
        copy.start()

    @pl.when(f == steps - 1)
    def _():
        for copy in copies(1 - slot, f - 1) + copies(slot, f):
            copy.wait()
        if y_any is not None:
            for i in range(chunks):
                for copy in row_stores(i):
                    copy.wait()


def first_kernel(x, d, xt, dt, wgu, wo, grad, y, dx, *scratch):
    ffn_steps(x, d, xt, dt, wgu, wo, grad, y, dx, *scratch)


def second_kernel(len_ref, x, d, xt, dt, wgu, wo, att_ref, y1_ref, dx1_ref, do_ref, ctx_ref, w_ref, vec_ref,
                  grad, out_ref, datt_ref, dctx_ref, gw_ref, gg_ref, acc_ref, flat_ref, *scratch):
    f = pl.program_id(0)
    steps = FF // 2 // FT

    @pl.when(f == 0)
    def _():
        acc_ref[...] = jnp.zeros_like(acc_ref)
        gg_ref[...] = jnp.zeros_like(gg_ref)
        flat_ref[...] = out_weights(w_ref)

    @pl.when(f < steps)
    def _():
        ffn_steps(x, d, xt, dt, wgu, wo, grad, None, None, *scratch)

    @pl.when(f >= steps)
    def _():
        tile = f - steps
        y_ref, dx_ref = scratch[4], scratch[5]
        rows = pl.ds(pl.multiple_of(tile * MT, MT), MT)
        per = TOK // MT
        length = len_ref[tile // per]
        place_in = lax.rem(tile, per) * MT + lax.broadcasted_iota(jnp.int32, (MT, 1), 0)
        live = jnp.where(2 * place_in < length, 1.0, 0.0).astype(f32)
        att = att_ref[...].astype(f32)
        out_ref[...] = ((att + y1_ref[...].astype(f32) + y_ref[rows, :]) * live).astype(bf16)
        back, gain_grad = norm_back(att, dx1_ref[...].astype(f32) + dx_ref[rows, :], vec_ref[6:7, :])
        gg_ref[...] += gain_grad
        d_att = do_ref[...].astype(f32) + back
        low = d_att.astype(bf16)
        datt_ref[...] = low
        dctx_ref[...] = nt(low, flat_ref[...]).astype(bf16)
        acc_ref[...] += nn(ctx_ref[...].T, low)

    @pl.when(f == pl.num_programs(0) - 1)
    def _():
        gw_ref[...] = acc_ref[...].astype(bf16)


def ffn_scratch(rows, shards):
    part, hs = 2 * D // shards, FF // 2 // shards
    return [
        pltpu.VMEM((rows, D), bf16),
        pltpu.VMEM((rows, D), bf16),
        pltpu.VMEM((D, rows), bf16),
        pltpu.VMEM((D, rows), bf16),
        pltpu.VMEM((rows, D), f32),
        pltpu.VMEM((rows, D), f32),
        pltpu.VMEM((rows, FT), bf16),
        pltpu.VMEM((rows, FT), bf16),
        pltpu.VMEM((rows, FT), bf16),
        pltpu.VMEM((2, shards, part, FT), bf16),
        pltpu.VMEM((2, FT // hs, 3 * hs, FT), bf16),
        pltpu.SemaphoreType.DMA((3, max(2, rows // RC))),
        pltpu.SemaphoreType.DMA((2, rows // RC)),
        pltpu.SemaphoreType.DMA((2, 2)),
    ]


def ffn_specs(tiles, shards):
    last = lambda f: jnp.minimum(f, tiles - 1)
    part, hs = 2 * D // shards, FF // 2 // shards
    return [pl.BlockSpec(memory_space=pl.ANY)] * 4 + [
        pl.BlockSpec((shards, part, FT), lambda f, *n: (0, last(f), 0)),
        pl.BlockSpec((FT // hs, 3 * hs, FT), lambda f, *n: (last(f), 2, 0)),
    ]


def grad_shape(shards):
    part, hs = 2 * D // shards, FF // 2 // shards
    return jax.ShapeDtypeStruct((shards, FF // 2 // FT * part + 3 * hs, FT), bf16)


def ffn_first(x, d_out, xt, dt, pack, shards):
    rows = x.shape[0]
    tiles = FF // 2 // FT
    anywhere = pl.BlockSpec(memory_space=pl.ANY)
    return pl.pallas_call(
        first_kernel,
        grid=(tiles,),
        in_specs=ffn_specs(tiles, shards),
        out_specs=[anywhere] * 3,
        out_shape=[
            grad_shape(shards),
            jax.ShapeDtypeStruct((rows, D), bf16),
            jax.ShapeDtypeStruct((rows, D), bf16),
        ],
        scratch_shapes=ffn_scratch(rows, shards) + [pltpu.VMEM((2, rows, D), bf16)],
        compiler_params=pltpu.CompilerParams(vmem_limit_bytes=VMEM_LIMIT),
        cost_estimate=cost(36, 40),
        name="ffn_first",
    )(x, d_out, xt, dt, pack, pack)


def ffn_second(lengths, x, d_out, xt, dt, pack, att, y1, dx1, ctx, pack0, vecs, shards):
    rows = x.shape[0]
    tiles = FF // 2 // FT
    tile_rows = pl.BlockSpec((MT, D), lambda f, n: (jnp.maximum(f - tiles, 0), 0))
    return pl.pallas_call(
        second_kernel,
        grid_spec=pltpu.PrefetchScalarGridSpec(
            num_scalar_prefetch=1,
            grid=(tiles + rows // MT,),
            in_specs=ffn_specs(tiles, shards) + [tile_rows] * 5 + [out_block(shards), whole(8, D)],
            out_specs=[pl.BlockSpec(memory_space=pl.ANY), tile_rows, tile_rows, tile_rows, whole(D, D), whole(1, D)],
            scratch_shapes=[
                pltpu.VMEM((D, D), f32), pltpu.VMEM((D, D), bf16),
            ] + ffn_scratch(rows, shards),
        ),
        out_shape=[
            grad_shape(shards),
            jax.ShapeDtypeStruct((rows, D), bf16),
            jax.ShapeDtypeStruct((rows, D), bf16),
            jax.ShapeDtypeStruct((rows, D), bf16),
            jax.ShapeDtypeStruct((D, D), bf16),
            jax.ShapeDtypeStruct((1, D), f32),
        ],
        compiler_params=pltpu.CompilerParams(vmem_limit_bytes=VMEM_LIMIT),
        cost_estimate=cost(46, 60),
        name="ffn_second",
    )(lengths, x, d_out, xt, dt, pack, pack, att, y1, dx1, d_out, ctx, pack0, vecs)


def norm_back(x, grad, gain):
    r = rms_scale(x)
    n = x * r
    u = gain * grad
    mean = jnp.sum(n * u, axis=1, keepdims=True) * (1.0 / D)
    return r * (u - n * mean), jnp.sum(n * grad, axis=0, keepdims=True)


def qkv_grad_kernel(dqkv_ref, normed_t_ref, go_ref, gw_ref):
    i = pl.program_id(0)

    @pl.when(i < 3)
    def _():
        gw_ref[...] = nn(normed_t_ref[...], dqkv_ref[0]).astype(bf16)

    @pl.when(i == 3)
    def _():
        gw_ref[...] = go_ref[...]


def qkv_grad(dqkv, normed_t, g_attn_out):
    rows = normed_t.shape[1]
    return pl.pallas_call(
        qkv_grad_kernel,
        grid=(4,),
        in_specs=[
            pl.BlockSpec((1, rows, D), lambda i: (jnp.minimum(i, 2), 0, 0)),
            whole(D, rows), whole(D, D),
        ],
        out_specs=pl.BlockSpec((D, D), lambda i: (0, i)),
        out_shape=jax.ShapeDtypeStruct((D, 4 * D), bf16),
        compiler_params=pltpu.CompilerParams(vmem_limit_bytes=VMEM_LIMIT),
        cost_estimate=cost(11, 20),
        name="qkv_grad",
    )(dqkv, normed_t, g_attn_out)


def qkv_back_kernel(dqkv_ref, w_ref, hidden_ref, datt_ref, vec_ref, dh_ref, gg_ref):
    @pl.when(pl.program_id(0) == 0)
    def _():
        gg_ref[...] = jnp.zeros_like(gg_ref)

    dn = nt(dqkv_ref[0], w_ref[:, 0:D])
    for i in range(1, 3):
        dn = dn + nt(dqkv_ref[i], w_ref[:, i * D : (i + 1) * D])
    back, gain_grad = norm_back(hidden_ref[...].astype(f32), dn, vec_ref[5:6, :])
    gg_ref[...] += gain_grad
    dh_ref[...] = (datt_ref[...].astype(f32) + back).astype(bf16)


def qkv_backward(dqkv, attn_w, hidden, d_att, vecs):
    rows = hidden.shape[0]
    tile = pl.BlockSpec((TOK, D), lambda s: (s, 0))
    return pl.pallas_call(
        qkv_back_kernel,
        grid=(rows // TOK,),
        in_specs=[
            pl.BlockSpec((3, TOK, D), lambda s: (0, s, 0)),
            pl.BlockSpec((D, 3 * D), lambda s: (0, 0)),
            tile, tile, whole(8, D),
        ],
        out_specs=[tile, whole(1, D)],
        out_shape=[jax.ShapeDtypeStruct((rows, D), bf16), jax.ShapeDtypeStruct((1, D), f32)],
        compiler_params=pltpu.CompilerParams(vmem_limit_bytes=VMEM_LIMIT),
        cost_estimate=cost(14, 40),
        name="qkv_backward",
    )(dqkv, attn_w, hidden, d_att, vecs)


MESH = pl.DeviceIdType.MESH


def greet(peers):
    barrier = pltpu.get_barrier_semaphore()
    for peer in peers:
        pl.semaphore_signal(barrier, inc=1, device_id=peer, device_id_type=MESH)
    pl.semaphore_wait(barrier, len(peers))


def pack_half(out_ref, ffn_in_ref, ffn_out_ref, h, shards):
    hs = FF // 2 // shards
    owners = FT // hs
    deep = ffn_in_ref.shape[0]
    row = 0
    for f in range(FF // 2 // FT):
        for g in range(2):
            starts = [g * FF + (f * owners + o) * 2 * hs + h * hs for o in range(owners)]
            out_ref[row : row + deep, :] = jnp.concatenate([ffn_in_ref[:, a : a + hs] for a in starts], axis=1)
            row += deep
    for i in range(3):
        out_ref[row : row + hs, :] = ffn_out_ref[h * hs : (h + 1) * hs, i * FT : (i + 1) * FT]
        row += hs
    return row


def prepare_kernel(replicas, shards, length_ref, target_ref, embed_ref, conv_ref, score_ref, gain1_ref, gain2_ref, rel_ref,
                   ids_ref, attn_out_ref, ffn_in_ref, ffn_out_ref,
                   table_ref, vec_ref, table_rel_ref, slots_ref, column_ref, row_ref, pack0_ref, pack1_ref,
                   own_ref, wide_ref, turn_ref, nat_ref, wanted_ref, send_sem, recv_sem):
    rep, me = lax.axis_index("rep"), lax.axis_index("shard")
    deep = embed_ref.shape[1]
    seqs = ids_ref.shape[0]
    twin = me + 1 - 2 * lax.rem(me, 2)
    far = [lax.rem(me + 2 * i, shards) for i in range(1, shards // 2)]
    others = [lax.rem(rep + i, replicas) for i in range(1, replicas)]
    greet([(rep, twin)] + [(rep, p) for p in far] + [(p, me) for p in others])

    def send(i, src, dst, device):
        copy = pltpu.make_async_remote_copy(
            src_ref=src, dst_ref=dst, send_sem=send_sem.at[i], recv_sem=recv_sem.at[i],
            device_id=device, device_id_type=MESH)
        copy.start()
        return copy

    wide_ref[...] = jnp.zeros_like(wide_ref)
    wide_ref[0:VOCAB, 0:deep] = embed_ref[...].astype(f32)
    wide_ref[VOCAB : VOCAB + 4, 0:deep] = conv_ref[...].astype(f32)
    for i, ref in enumerate((score_ref, gain1_ref, gain2_ref)):
        wide_ref[VOCAB + 4 + i : VOCAB + 5 + i, 0:deep] = ref[...].astype(f32).reshape(1, deep)
    rel_rows, heads = rel_ref.shape
    wide_ref[VOCAB + 7 : VOCAB + 7 + rel_rows, 0:heads] = rel_ref[...].astype(f32)
    own_ref[...] = wide_ref[...].T[0:deep].astype(bf16)
    near = [send(0, own_ref, table_ref.at[me], (rep, twin))]
    direct = [send(1 + i, own_ref, table_ref.at[me], (rep, p)) for i, p in enumerate(far)]
    lanes = lax.broadcasted_iota(jnp.int32, (8, 128), 1)
    wanted = jnp.zeros((8, 128), jnp.int32)
    for k in range(seqs):
        slot = target_ref[k] % seqs
        wanted = wanted + jnp.where(lanes == target_ref[k] // seqs // shards, slot + 1, 0)
    wanted_ref[...] = wanted
    base = shards
    asks = [send(base + i, wanted_ref, slots_ref.at[rep], (p, me)) for i, p in enumerate(others)]
    table_ref[me] = own_ref[...]
    slots_ref[rep] = wanted_ref[...]
    row = pack_half(pack0_ref, ffn_in_ref, ffn_out_ref, 0, shards)
    for i in range(3):
        pack0_ref[row : row + deep, :] = attn_out_ref[:, i * FT : (i + 1) * FT]
        row += deep
    pack_half(pack1_ref, ffn_in_ref, ffn_out_ref, 1, shards)
    base = base + replicas - 1
    for i, copy in enumerate(direct):
        copy.wait()
        source = lax.rem(me - 2 * (i + 1) + shards, shards)
        near.append(send(base + i, table_ref.at[source], table_ref.at[source], (rep, twin)))
    turn_ref[...] = jnp.full(turn_ref.shape, -1.0, f32)
    place = lax.broadcasted_iota(jnp.int32, (1, MAXLEN), 1)
    for s in range(seqs):
        live = jnp.where(place < length_ref[s], ids_ref[s : s + 1, :], -1)
        row_ref[s] = live
        turn_ref[s : s + 1, 0:MAXLEN] = live.astype(f32)
    nat_ref[...] = turn_ref[...].T
    for r in range(R):
        rows = nat_ref[pl.ds(r, QN, stride=R), :]
        for s in range(seqs):
            column_ref[s, r * QN : (r + 1) * QN, :] = jnp.broadcast_to(rows[:, s : s + 1], (QN, 128))
    for copy in near + asks:
        copy.wait()
    last = table_ref[:, :, SMALL - 128 :].astype(f32).reshape(D, 128).T
    first = VOCAB - (SMALL - 128)
    vec_ref[...] = last[first : first + 8]
    table_rel_ref[...] = jnp.zeros_like(table_rel_ref)
    for s in range(shards):
        block = last[first + 7 : first + 7 + rel_rows, s * deep : s * deep + heads]
        table_rel_ref[s * rel_rows : (s + 1) * rel_rows, 0:heads] = block


def prepare(lengths, target, embed, conv_w, score_w, gain_attn, gain_ffn, rel_table, ids, attn_out, ffn_in, ffn_out,
            replicas, shards):
    deep = embed.shape[1]
    seqs = ids.shape[0]
    part, hs = 2 * D // shards, FF // 2 // shards
    rows = FF // 2 // FT * part + 3 * hs
    sems = shards + replicas - 1 + shards // 2 - 1
    vmem = pl.BlockSpec(memory_space=pltpu.VMEM)
    smem = pl.BlockSpec(memory_space=pltpu.SMEM)
    return pl.pallas_call(
        lambda *refs: prepare_kernel(replicas, shards, *refs),
        out_shape=[
            jax.ShapeDtypeStruct((shards, deep, SMALL), bf16),
            jax.ShapeDtypeStruct((8, D), f32),
            jax.ShapeDtypeStruct((BUCKETS, 128), f32),
            jax.ShapeDtypeStruct((replicas, 8, 128), jnp.int32),
            jax.ShapeDtypeStruct((seqs, P_ROWS, 128), f32),
            jax.ShapeDtypeStruct((seqs, 1, MAXLEN), jnp.int32),
            jax.ShapeDtypeStruct((rows + 3 * deep, FT), bf16),
            jax.ShapeDtypeStruct((rows, FT), bf16),
        ],
        in_specs=[smem] * 2 + [vmem] * 10,
        out_specs=[vmem] * 8,
        scratch_shapes=[
            pltpu.VMEM((deep, SMALL), bf16),
            pltpu.VMEM((SMALL, 128), f32),
            pltpu.VMEM((128, 1152), f32),
            pltpu.VMEM((1152, 128), f32),
            pltpu.VMEM((8, 128), jnp.int32),
            pltpu.SemaphoreType.DMA((sems,)),
            pltpu.SemaphoreType.DMA((sems,)),
        ],
        compiler_params=pltpu.CompilerParams(collective_id=1, has_side_effects=True, vmem_limit_bytes=VMEM_LIMIT),
        cost_estimate=cost(12, 8),
        name="prepare",
    )(lengths, target, embed, conv_w, score_w, gain_attn, gain_ffn, rel_table, ids, attn_out, ffn_in, ffn_out)


def pick_kernel(order_ref, in_ref, *out_refs):
    for i, ref in enumerate(out_refs):
        @pl.when(pl.program_id(0) == i)
        def _():
            ref[...] = in_ref[0]


def pick(order, rows):
    count = order.shape[0]
    block = (rows.shape[1], rows.shape[2])
    return pl.pallas_call(
        pick_kernel,
        grid_spec=pltpu.PrefetchScalarGridSpec(
            num_scalar_prefetch=1,
            grid=(count,),
            in_specs=[pl.BlockSpec((1,) + block, lambda i, order: (order[i], 0, 0))],
            out_specs=[pl.BlockSpec(block, lambda i, order: (0, 0))] * count,
        ),
        out_shape=[jax.ShapeDtypeStruct(block, rows.dtype)] * count,
        compiler_params=pltpu.CompilerParams(vmem_limit_bytes=VMEM_LIMIT),
        cost_estimate=cost(4, 6),
        name="pick",
    )(order, rows)


def finish_kernel(replicas, shards, piece_ref, small_ref, in_ref, attn_ref, embed_ref, conv_ref, rest_ref,
                  twin_ref, both_ref, far_ref, held_ref, other_ref, part_ref, part2_ref, last_ref,
                  twin_send, twin_recv, far_send, far_recv, send_sem, recv_sem, send2_sem, recv2_sem):
    rep, me = lax.axis_index("rep"), lax.axis_index("shard")
    half = piece_ref.shape[1]
    chips = shards // 2
    core = lax.rem(me, 2)
    twin = me + 1 - 2 * core
    bits = [1 << b for b in range(replicas.bit_length() - 1)]
    orders = (bits, bits[::-1])
    far = [lax.rem(me + 2 * i, shards) for i in range(1, chips)]
    partners = {}
    for bit in bits:
        down = lax.rem(rep // bit, 2)
        partners[bit] = (rep + bit - 2 * bit * down, me)
    greet([(rep, twin)] + [(rep, p) for p in far] + [partners[bit] for bit in bits])

    def send(src, dst, sems, i, device):
        copy = pltpu.make_async_remote_copy(
            src_ref=src, dst_ref=dst, send_sem=sems[0].at[i], recv_sem=sems[1].at[i],
            device_id=device, device_id_type=MESH)
        copy.start()
        return copy

    near = [
        send(small_ref.at[2 * z + 1 - core], twin_ref.at[z], (twin_send, twin_recv), z, (rep, twin))
        for z in range(chips)
    ]

    def exchange(t, mine, theirs, sems):
        return [send(mine.at[t, h], theirs.at[t, h], sems, (t, h), partners[orders[h][t]]) for h in range(2)]

    held_ref[0] = piece_ref[...]
    large = exchange(0, held_ref, other_ref, (send_sem, recv_sem))
    for z, copy in enumerate(near):
        copy.wait()
        both_ref[z] = (small_ref[2 * z + core].astype(f32) + twin_ref[z].astype(f32)).astype(bf16)
    away = [send(both_ref.at[p // 2], far_ref.at[i], (far_send, far_recv), i, (rep, p)) for i, p in enumerate(far)]
    last_ref[...] = jnp.zeros_like(last_ref)

    def settle(t, copies, mine, theirs, outs):
        for h, copy in enumerate(copies):
            copy.wait()
            total = mine[t, h].astype(f32) + theirs[t, h].astype(f32)
            if t == len(bits) - 1:
                start = 0
                for out in outs:
                    width = out.shape[1]
                    out[h * half : (h + 1) * half, :] = total[:, start : start + width]
                    start += width
            else:
                mine[t + 1, h] = total.astype(bf16)

    settle(0, large, held_ref, other_ref, (in_ref, attn_ref))
    large = exchange(1, held_ref, other_ref, (send_sem, recv_sem))
    total = both_ref[me // 2].astype(f32)
    for i, copy in enumerate(away):
        copy.wait()
        total = total + far_ref[i].astype(f32)
    part_ref[0] = total.astype(bf16)
    for t in range(len(bits)):
        little = exchange(t, part_ref, part2_ref, (send2_sem, recv2_sem))
        if t > 0:
            settle(t, large, held_ref, other_ref, (in_ref, attn_ref))
            if t < len(bits) - 1:
                large = exchange(t + 1, held_ref, other_ref, (send_sem, recv_sem))
        settle(t, little, part_ref, part2_ref, (last_ref,))
    turned = last_ref[...].T
    deep = embed_ref.shape[1]
    embed_ref[...] = turned[0:VOCAB, 0:deep]
    conv_ref[...] = turned[VROWS : VROWS + 4, 0:deep]
    rest_ref[...] = turned[VROWS : VROWS + 16, 0:deep]


def finish(piece, small, replicas, shards):
    rows, wide = piece.shape
    half = rows // 2
    chips = shards // 2
    steps = replicas.bit_length() - 1
    vmem = pl.BlockSpec(memory_space=pltpu.VMEM)
    sems = lambda *shape: [pltpu.SemaphoreType.DMA(shape), pltpu.SemaphoreType.DMA(shape)]
    return pl.pallas_call(
        lambda *refs: finish_kernel(replicas, shards, *refs),
        out_shape=[
            jax.ShapeDtypeStruct((rows, 3 * D), f32),
            jax.ShapeDtypeStruct((rows, D), f32),
            jax.ShapeDtypeStruct((VOCAB, rows), f32),
            jax.ShapeDtypeStruct((4, rows), f32),
            jax.ShapeDtypeStruct((16, rows), f32),
        ],
        in_specs=[vmem] * 2,
        out_specs=[vmem] * 5,
        scratch_shapes=[
            pltpu.VMEM((chips, 2, half, SMALL), bf16),
            pltpu.VMEM((chips, 2, half, SMALL), bf16),
            pltpu.VMEM((chips - 1, 2, half, SMALL), bf16),
            pltpu.VMEM((steps, 2, half, wide), bf16),
            pltpu.VMEM((steps, 2, half, wide), bf16),
            pltpu.VMEM((steps, 2, half, SMALL), bf16),
            pltpu.VMEM((steps, 2, half, SMALL), bf16),
            pltpu.VMEM((128, SMALL), f32),
        ] + sems(chips) + sems(chips - 1) + sems(steps, 2) + sems(steps, 2),
        compiler_params=pltpu.CompilerParams(
            collective_id=2, has_side_effects=True, vmem_limit_bytes=VMEM_LIMIT),
        cost_estimate=cost(20, 4),
        name="finish_sums",
    )(piece.reshape(2, half, wide), small.reshape(shards, 2, half, SMALL))


def deliver_kernel(in_ref, attn_ref, embed_ref, conv_ref, rest_ref, in_out, attn_out, embed_out, conv_out, score_out, gain1_out, gain2_out, rel_out):
    in_out[...] = in_ref[...]
    attn_out[...] = attn_ref[...]
    embed_out[...] = embed_ref[...]
    conv_out[...] = conv_ref[...]
    for i, ref in enumerate((score_out, gain1_out, gain2_out)):
        ref[...] = rest_ref[4 + i : 5 + i, :].reshape(ref.shape)
    rel_out[...] = rest_ref[7 : 7 + rel_out.shape[0], 0 : rel_out.shape[1]]


def deliver(parts, rel_rows):
    deep = parts[0].shape[0]
    vmem = pl.BlockSpec(memory_space=pltpu.VMEM)
    line = jax.ShapeDtypeStruct((deep,), f32)
    return pl.pallas_call(
        deliver_kernel,
        out_shape=[jax.ShapeDtypeStruct(x.shape, f32) for x in parts[:4]]
        + [line] * 3 + [jax.ShapeDtypeStruct((rel_rows, HEADS), f32)],
        in_specs=[vmem] * 5,
        out_specs=[vmem] * 8,
        compiler_params=pltpu.CompilerParams(vmem_limit_bytes=VMEM_LIMIT),
        cost_estimate=cost(2, 2),
        name="deliver",
    )(*parts)


def unpack_kernel(shards, first_ref, first_other_ref, second_ref, second_other_ref, in_ref, out_ref):
    hs = FF // 2 // shards
    deep = in_ref.shape[0]
    owners = FT // hs
    for h in range(2):
        def load(start, count):
            rows = slice(start, start + count)
            mine, theirs = ((first_ref, first_other_ref), (second_ref, second_other_ref))[h]
            return mine[rows, :].astype(f32) + theirs[rows, :].astype(f32)

        row = 0
        for f in range(FF // 2 // FT):
            for g in range(2):
                x = load(row, deep)
                for o in range(owners):
                    start = g * FF + (f * owners + o) * 2 * hs + h * hs
                    in_ref[:, start : start + hs] = x[:, o * hs : (o + 1) * hs]
                row += deep
        for i in range(3):
            out_ref[h * hs : (h + 1) * hs, i * FT : (i + 1) * FT] = load(row, hs)
            row += hs


def unpack(first, first_other, second, second_other, shards):
    vmem = pl.BlockSpec(memory_space=pltpu.VMEM)
    return pl.pallas_call(
        lambda *refs: unpack_kernel(shards, *refs),
        out_shape=[
            jax.ShapeDtypeStruct((D // shards, 2 * FF), f32),
            jax.ShapeDtypeStruct((FF // shards, D), f32),
        ],
        in_specs=[vmem] * 4,
        out_specs=[vmem] * 2,
        compiler_params=pltpu.CompilerParams(vmem_limit_bytes=VMEM_LIMIT),
        cost_estimate=cost(3, 5),
        name="unpack",
    )(first, first_other, second, second_other)


def send_cotangent(slots, cotangent):
    replicas = lax.axis_size("rep")
    places = jnp.arange(replicas)
    rep = lax.axis_index("rep")
    asked = jnp.where(places[None, :] == rep, slots, 0).sum(axis=1) - 1
    turned = (places[None, :] == (rep + places[:, None]) % replicas) * asked[None, :]
    pieces = list(pick(jnp.maximum(turned.sum(axis=1), 0), cotangent))
    for shift in range(1, replicas):
        pieces[shift] = lax.ppermute(pieces[shift], "rep", [(r, (r + shift) % replicas) for r in range(replicas)])
    return pieces


def swap(x, bit):
    replicas = lax.axis_size("rep")
    return lax.ppermute(x, "rep", [(r, r ^ bit) for r in range(replicas)])


def add_low(a, b):
    return (a.astype(f32) + b.astype(f32)).astype(bf16)


def scatter_sum(grad):
    return lax.psum_scatter(grad, "shard", scatter_dimension=0, tiled=True)


def body(
    byte_ids, lengths, target, rel_bucket, cotangent, embed, conv_w, score_w, gain_attn,
    attn_in, attn_out, gain_ffn, ffn_in, ffn_out, rel_table,
):
    seqs = byte_ids.shape[0]
    replicas, shards = lax.axis_size("rep"), lax.axis_size("shard")
    attn_w = lax.all_gather(attn_in, "shard", axis=0, tiled=True)
    table, vecs, rel, slots, ids_col, ids_row, pack0, pack1 = prepare(
        lengths, target, embed, conv_w, score_w, gain_attn, gain_ffn, rel_table, byte_ids,
        attn_out, ffn_in, ffn_out, replicas, shards,
    )
    packs = [lax.all_gather(pack, "shard", axis=0) for pack in (pack0, pack1)]
    rows = bucket_rows(rel_bucket)

    hidden, normed, normed_t, convolved, weights, e_low, coefs = gbst_forward(lengths, ids_col, table, vecs)
    qkv = jnp.dot(normed, attn_w, preferred_element_type=f32).astype(bf16)
    qkv, slots = lax.optimization_barrier((qkv, slots))
    pieces = send_cotangent(slots[:, 0, :replicas], cotangent)
    ctx, lse = attn_forward(lengths, qkv, rel, rows)
    ctx, pieces = lax.optimization_barrier((ctx, pieces))
    shifts = (lax.axis_index("rep") - target // seqs // shards) % replicas
    attended, low, low_t, d_out, d_out_t = post_attention(
        lengths, shifts, ctx, packs[0], hidden, vecs, pieces, shards
    )
    g_half1, y1, dx1 = ffn_first(low, d_out, low_t, d_out_t, packs[0], shards)
    g_half2, out, d_att, d_ctx, g_attn_out, g_gain_ffn = ffn_second(
        lengths, low, d_out, low_t, d_out_t, packs[1], attended, y1, dx1, ctx, packs[0], vecs, shards
    )
    one, two = [scatter_sum(g.reshape(-1, FT)) for g in (g_half1, g_half2)]
    bits = [1 << b for b in range(replicas.bit_length() - 1)]
    dqkv, g_rel = attn_backward(lengths, qkv, d_ctx, ctx, lse, rel, rows, shards)
    dqkv, one = lax.optimization_barrier((dqkv, one))
    g_attn = qkv_grad(dqkv, normed_t, g_attn_out)
    g_attn, two = lax.optimization_barrier((g_attn, two))
    p_attn = scatter_sum(g_attn)
    turned = bits[1:] + bits[:1]
    others = swap(one, bits[0]), swap(two, turned[0])
    d_hidden, g_gain_attn = qkv_backward(dqkv, attn_w, hidden, d_att, vecs)
    d_hidden, others = lax.optimization_barrier((d_hidden, others))
    one, two = add_low(one, others[0]), add_low(two, others[1])
    for t in range(1, len(bits) - 1):
        one, two = add_low(one, swap(one, bits[t])), add_low(two, swap(two, turned[t]))
    d_hidden, one, two = lax.optimization_barrier((d_hidden, one, two))
    others = swap(one, bits[-1]), swap(two, turned[-1])
    input_grad, small = gbst_backward(
        ids_row, vecs, d_hidden, convolved, weights, e_low, coefs,
        g_gain_attn, g_gain_ffn, g_rel,
    )
    small, others = lax.optimization_barrier((small, others))
    parts = finish(p_attn, small, replicas, shards)
    s_ffn_in, s_ffn_out = unpack(one, others[0], two, others[1], shards)
    s_attn_in, s_attn_out, s_embed, s_conv, s_score, s_gain_attn, s_gain_ffn, s_rel = deliver(parts, rel_table.shape[0])
    return (
        out.reshape(seqs, TOK, D), input_grad, s_embed, s_conv, s_score, s_gain_attn, s_attn_in, s_attn_out,
        s_gain_ffn, s_ffn_in, s_ffn_out, s_rel,
    )


def solution(mesh):
    in_specs = (
        P(("rep", "shard"), None), P(("rep", "shard")), P(("rep", "shard")), P(),
        P(("rep", "shard"), None, None), P(None, "shard"), P(None, "shard"), P("shard"), P("shard"),
        P("shard", None), P("shard", None), P("shard"), P("shard", None), P("shard", None), P("shard", None),
    )
    out_specs = (
        P(("rep", "shard"), None, None), P(("rep", "shard"), None, None), P(None, "shard"), P(None, "shard"),
        P("shard"), P("shard"), P("shard", None), P("shard", None), P("shard"), P("shard", None),
        P("shard", None), P("shard", None),
    )
    return jax.shard_map(body, mesh=mesh, in_specs=in_specs, out_specs=out_specs, check_vma=False)
```

```python
import jax
import jax.numpy as jnp
from jax import lax
from jax.experimental import pallas as pl
from jax.experimental.pallas import tpu as pltpu
from jax.sharding import PartitionSpec as P

D = 768
VOCAB = 259
VROWS = 272
VMEM_LIMIT = 60 << 20
SMALL = 384
MAXLEN = 1024
TOK = 512
LANES = 128
QN = 88
R = 12
P_ROWS = QN * R
T_ROWS = 528
LT = D // LANES
epsilon = 1e-06
f32 = jnp.float32
bf16 = jnp.bfloat16


def cost(us, mib):
    return pl.CostEstimate(flops=int(us * 1e9), bytes_accessed=mib << 20, transcendentals=0)


def lane_iota(rows):
    return lax.broadcasted_iota(jnp.int32, (rows, LANES), 1)


def group_matrix(b):
    row = lax.broadcasted_iota(jnp.int32, (LANES, LANES), 0)
    col = lax.broadcasted_iota(jnp.int32, (LANES, LANES), 1)
    return jnp.where((row // b == col // b) & (row < R) & (col < R), 1.0, 0.0).astype(f32)


def exact_dot(a, b):
    return jnp.dot(a, b, precision=lax.Precision.HIGHEST, preferred_element_type=f32)


def place(columns, rows):
    lanes = lane_iota(rows)
    out = jnp.zeros((rows, LANES), f32)
    for r, column in enumerate(columns):
        out = jnp.where(lanes == r, column, out)
    return out


def gbst_masks(length):
    q = lax.broadcasted_iota(jnp.int32, (QN, LANES), 0)
    r = lax.broadcasted_iota(jnp.int32, (QN, LANES), 1)
    mask = jnp.where((q * R + r < length) & (r < R), 1.0, 0.0).astype(f32)
    inverse = [1.0 / jnp.maximum(exact_dot(mask, group_matrix(b)), 1.0) for b in (2, 3, 4)]
    pair = exact_dot(mask, group_matrix(2))
    alpha = mask / jnp.maximum(pair, 1.0)
    return mask, inverse, alpha


def gbst_weights(s1, inverse):
    sizes = [s1] + [exact_dot(s1, group_matrix(b)) * inv for b, inv in zip((2, 3, 4), inverse)]
    top = jnp.maximum(jnp.maximum(sizes[0], sizes[1]), jnp.maximum(sizes[2], sizes[3]))
    parts = [jnp.exp(s - top) for s in sizes]
    total = parts[0] + parts[1] + parts[2] + parts[3]
    return [p / total for p in parts]


def gbst_coefs(weights, inverse, alpha):
    a1 = weights[0] * alpha
    a2 = weights[1] * alpha * inverse[0]
    a3 = weights[2] * alpha * inverse[1]
    a4 = weights[3] * alpha * inverse[2]
    pair = group_matrix(2)
    a4s = exact_dot(a4, pair)
    own = a1 + exact_dot(a2, pair) + a4s
    return own, a3, a4s


def column(x, r):
    return jnp.broadcast_to(x[:, r : r + 1], (x.shape[0], LANES))


def hits_of(ids):
    lanes = lax.broadcasted_iota(jnp.int32, (P_ROWS, LANES), 1).astype(f32)
    return jnp.concatenate(
        [jnp.where(ids == lanes + float(i * LANES), 1.0, 0.0).astype(bf16) for i in range(SMALL // LANES)], axis=1)


def look_up(ids, table_ref):
    return lax.dot_general(
        hits_of(ids), table_ref[...].reshape(D, SMALL), (((1,), (1,)), ((), ())), preferred_element_type=f32)


def load_e(e_ref, r, lt):
    lanes = pl.ds(lt * LANES, LANES)
    if r < R:
        return e_ref[pl.ds(r * QN, QN), lanes]
    return e_ref[pl.ds((r - R) * QN + 1, QN), lanes]


def gbst_fwd_kernel(len_ref, ids_ref, table_ref, vec_ref, hlow_ref, normed_ref, turned_ref, c_ref, w_ref, elow_ref, kc_ref, e_ref, hid_ref, s_ref):
    k_ref = kc_ref.at[0]
    length = len_ref[pl.program_id(0)]
    rows_e = look_up(ids_ref[0], table_ref)
    e_ref[pl.ds(0, P_ROWS), :] = rows_e
    elow_ref[0] = rows_e.astype(bf16)
    e_ref[pl.ds(P_ROWS, 8), :] = jnp.zeros((8, D), f32)
    for lt in range(LT):
        lanes = pl.ds(lt * LANES, LANES)
        taps = [jnp.broadcast_to(vec_ref[j : j + 1, lanes], (QN, LANES)) for j in range(4)]
        sw = jnp.broadcast_to(vec_ref[4:5, lanes], (QN, LANES))
        for r in range(R):
            c = taps[0] * load_e(e_ref, r, lt)
            for j in range(1, 4):
                c = c + taps[j] * load_e(e_ref, r + j, lt)
            c_ref[0, pl.ds(r * QN, QN), lanes] = c
            part = c * sw
            rows = pl.ds(r * QN, QN)
            s_ref[rows, :] = part if lt == 0 else s_ref[rows, :] + part
    s1 = place([jnp.sum(s_ref[pl.ds(r * QN, QN), :], axis=1, keepdims=True) for r in range(R)], QN)
    mask, inverse, alpha = gbst_masks(length)
    weights = gbst_weights(s1, inverse)
    for b, kept in enumerate(weights + inverse + [alpha]):
        w_ref[0, b] = kept
    own, a3, a4s = gbst_coefs(weights, inverse, alpha)
    n = 0
    for r in range(R):
        k_ref[r] = column(own, r)
        k_ref[R + r] = column(a3, r)
    for k in range(6):
        k_ref[2 * R + k] = column(a4s, 2 * k)
    for r in range(R):
        k_ref[2 * R + 6 + r] = column(mask, r)
    for lt in range(LT):
        lanes = pl.ds(lt * LANES, LANES)
        for half in range(2):
            c = [c_ref[0, pl.ds((half * 6 + r) * QN, QN), lanes] for r in range(6)]
            base = half * 6
            s3 = [c[0] + c[1] + c[2], c[3] + c[4] + c[5]]
            for k in range(3):
                tok = half * 3 + k
                other = tok ^ 1
                rows = pl.ds(2 * other * QN, QN)
                rows1 = pl.ds((2 * other + 1) * QN, QN)
                s2 = c_ref[0, rows, lanes] + c_ref[0, rows1, lanes]
                h = k_ref[2 * tok] * c[2 * k] + k_ref[2 * tok + 1] * c[2 * k + 1] + k_ref[2 * R + tok] * s2
                if k == 1:
                    h = h + k_ref[R + 2 * tok] * s3[0] + k_ref[R + 2 * tok + 1] * s3[1]
                else:
                    h = h + (k_ref[R + 2 * tok] + k_ref[R + 2 * tok + 1]) * s3[0 if k == 0 else 1]
                hid_ref[lt, pl.ds(tok, QN, stride=6), :] = h
    total = jnp.zeros((TOK, LANES), f32)
    for lt in range(LT):
        x = hid_ref[lt, 0:TOK, :]
        total = total + x * x
    scale = lax.rsqrt(jnp.sum(total, axis=1, keepdims=True) * (1.0 / D) + epsilon)
    for lt in range(LT):
        lanes = pl.ds(lt * LANES, LANES)
        x = hid_ref[lt, 0:TOK, :]
        hlow_ref[:, lanes] = x.astype(bf16)
        normed = (x * scale * vec_ref[5:6, lanes]).astype(bf16)
        normed_ref[:, lanes] = normed
        turned_ref[lanes, :] = normed.T


def gbst_forward(lengths, ids_col, table, vecs):
    seqs = ids_col.shape[0]
    grid_spec = pltpu.PrefetchScalarGridSpec(
        num_scalar_prefetch=1,
        grid=(seqs,),
        in_specs=[
            pl.BlockSpec((1, P_ROWS, LANES), lambda s, n: (s, 0, 0)),
            pl.BlockSpec(table.shape, lambda s, n: (0, 0, 0)),
            pl.BlockSpec((8, D), lambda s, n: (0, 0)),
        ],
        out_specs=[
            pl.BlockSpec((TOK, D), lambda s, n: (s, 0)),
            pl.BlockSpec((TOK, D), lambda s, n: (s, 0)),
            pl.BlockSpec((D, TOK), lambda s, n: (0, s)),
            pl.BlockSpec((1, P_ROWS, D), lambda s, n: (s, 0, 0)),
            pl.BlockSpec((1, 8, QN, LANES), lambda s, n: (s, 0, 0, 0)),
            pl.BlockSpec((1, P_ROWS, D), lambda s, n: (s, 0, 0)),
            pl.BlockSpec((1, 3 * R + 6, QN, LANES), lambda s, n: (s, 0, 0, 0)),
        ],
        scratch_shapes=[
            pltpu.VMEM((P_ROWS + 8, D), f32),
            pltpu.VMEM((LT, T_ROWS, LANES), f32),
            pltpu.VMEM((P_ROWS, LANES), f32),
        ],
    )
    return pl.pallas_call(
        gbst_fwd_kernel,
        grid_spec=grid_spec,
        out_shape=[
            jax.ShapeDtypeStruct((seqs * TOK, D), bf16),
            jax.ShapeDtypeStruct((seqs * TOK, D), bf16),
            jax.ShapeDtypeStruct((D, seqs * TOK), bf16),
            jax.ShapeDtypeStruct((seqs, P_ROWS, D), f32),
            jax.ShapeDtypeStruct((seqs, 8, QN, LANES), f32),
            jax.ShapeDtypeStruct((seqs, P_ROWS, D), bf16),
            jax.ShapeDtypeStruct((seqs, 3 * R + 6, QN, LANES), f32),
        ],
        compiler_params=pltpu.CompilerParams(vmem_limit_bytes=VMEM_LIMIT),
        cost_estimate=cost(18, 30),
        name="gbst_forward",
    )(lengths, ids_col, table, vecs)


def gbst_bwd_kernel(row_ref, vec_ref, dh_ref, c_ref, w_ref, elow_ref, kc_ref, gain1_ref, gain2_ref, rel_ref,
                    ig_ref, small_ref, ge_ref, e_ref, dt_ref, dc_ref, s_ref, cf_ref, igs_ref):
    seq = pl.program_id(0)
    k_ref = kc_ref.at[0]

    @pl.when(seq == 0)
    def _():
        ge_ref[...] = jnp.zeros_like(ge_ref)

    e_ref[pl.ds(0, P_ROWS), :] = elow_ref[0].astype(f32)
    e_ref[pl.ds(P_ROWS, 8), :] = jnp.zeros((8, D), f32)
    for lt in range(LT):
        dt_ref[lt, 0:TOK, :] = dh_ref[:, pl.ds(lt * LANES, LANES)].astype(f32)
        dt_ref[lt, TOK:T_ROWS, :] = jnp.zeros((T_ROWS - TOK, LANES), f32)
    for lt in range(LT):
        lanes = pl.ds(lt * LANES, LANES)
        for half in range(2):
            c = [c_ref[0, pl.ds((half * 6 + r) * QN, QN), lanes] for r in range(6)]
            s3 = [c[0] + c[1] + c[2], c[3] + c[4] + c[5]]
            for k in range(3):
                tok = half * 3 + k
                other = tok ^ 1
                dh = dt_ref[lt, pl.ds(tok, QN, stride=6), :]
                s2 = c_ref[0, pl.ds(2 * other * QN, QN), lanes] + c_ref[0, pl.ds((2 * other + 1) * QN, QN), lanes]
                parts = [
                    (2 * tok, dh * c[2 * k]),
                    (2 * tok + 1, dh * c[2 * k + 1]),
                    (2 * R + tok, dh * s2),
                    (R + 2 * tok, dh * s3[0 if k < 2 else 1]),
                ]
                if k == 1:
                    parts.append((R + 2 * tok + 1, dh * s3[1]))
                for slot, part in parts:
                    s_ref[slot] = part if lt == 0 else s_ref[slot] + part

    def total(slot):
        return jnp.sum(s_ref[slot], axis=1, keepdims=True)

    d1, d3, dother = [], [], []
    for tok in range(6):
        d1 += [total(2 * tok), total(2 * tok + 1)]
        first = total(R + 2 * tok)
        d3 += [first, total(R + 2 * tok + 1) if tok % 3 == 1 else first]
        o = total(2 * R + tok)
        dother += [o, o]
    d1, d3, dother = place(d1, QN), place(d3, QN), place(dother, QN)
    weights = [w_ref[0, b] for b in range(4)]
    inverse = [w_ref[0, 4 + b] for b in range(3)]
    alpha = w_ref[0, 7]
    d2 = exact_dot(d1, group_matrix(2))
    g = [alpha * d1, alpha * d2 * inverse[0], alpha * d3 * inverse[1], alpha * (d2 + dother) * inverse[2]]
    mean = weights[0] * g[0] + weights[1] * g[1] + weights[2] * g[2] + weights[3] * g[3]
    d_size = [w * (x - mean) for w, x in zip(weights, g)]
    coef = d_size[0]
    for b, inv in zip((2, 3, 4), inverse):
        coef = coef + exact_dot(d_size[b - 1] * inv, group_matrix(b))
    for r in range(R):
        cf_ref[r] = column(coef, r)

    for lt in range(LT):
        lanes = pl.ds(lt * LANES, LANES)
        taps = [jnp.broadcast_to(vec_ref[j : j + 1, lanes], (QN, LANES)) for j in range(4)]
        sw = jnp.broadcast_to(vec_ref[4:5, lanes], (QN, LANES))
        gs = jnp.zeros((QN, LANES), f32)
        gc = [jnp.zeros((QN, LANES), f32) for _ in range(4)]
        for half in range(2):
            dh = [dt_ref[lt, pl.ds(half * 3 + k, QN, stride=6), :] for k in range(3)]
            a = R + half * 6
            t3 = [
                (k_ref[a] + k_ref[a + 1]) * dh[0] + k_ref[a + 2] * dh[1],
                k_ref[a + 3] * dh[1] + (k_ref[a + 4] + k_ref[a + 5]) * dh[2],
            ]
            for k in range(3):
                tok = half * 3 + k
                other = tok ^ 1
                dother_h = dt_ref[lt, pl.ds(other, QN, stride=6), :]
                cross = k_ref[2 * R + other] * dother_h
                for e in range(2):
                    r = 2 * tok + e
                    cf = cf_ref[r]
                    dc = k_ref[r] * dh[k] + cross + t3[(r % 6) // 3] + cf * sw
                    gs = gs + cf * c_ref[0, pl.ds(r * QN, QN), lanes]
                    dc_ref[r, pl.ds(8, QN), :] = dc
                    for j in range(4):
                        gc[j] = gc[j] + dc * load_e(e_ref, r + j, lt)
        ge_ref[VROWS + 4 : VROWS + 5, lanes] += jnp.sum(gs, axis=0, keepdims=True)
        for j in range(4):
            ge_ref[VROWS + j : VROWS + j + 1, lanes] += jnp.sum(gc[j], axis=0, keepdims=True)
        for r in range(R):
            dc_ref[r, 0:8, :] = jnp.zeros((8, LANES), f32)
        for r in range(R):
            x = taps[0] * dc_ref[r, pl.ds(8, QN), :]
            for j in range(1, 4):
                back = dc_ref[r - j, pl.ds(8, QN), :] if r >= j else dc_ref[r - j + R, pl.ds(7, QN), :]
                x = x + taps[j] * back
            igs_ref[lt, pl.ds(r, QN, stride=R), :] = x * k_ref[2 * R + 6 + r]
    for lt in range(LT):
        lanes = pl.ds(lt * LANES, LANES)
        ig_ref[0, :, lanes] = igs_ref[lt, 0:MAXLEN, :].astype(bf16)
    vocab = lax.broadcasted_iota(jnp.int32, (VROWS, MAXLEN), 0)
    row_hits = jnp.where(vocab == row_ref[0], 1.0, 0.0).astype(bf16)
    ge_ref[0:VROWS, :] += jnp.dot(row_hits, ig_ref[0], preferred_element_type=f32)

    @pl.when(seq == pl.num_programs(0) - 1)
    def _():
        ge_ref[VROWS + 5 : VROWS + 6, :] = gain1_ref[...]
        ge_ref[VROWS + 6 : VROWS + 7, :] = gain2_ref[...]
        ge_ref[VROWS + 7 : VROWS + 15, :] = rel_ref[...]
        for lt in range(LT):
            lanes = pl.ds(lt * LANES, LANES)
            small_ref[lanes, :] = ge_ref[:, lanes].T.astype(bf16)


def gbst_backward(ids_row, vecs, d_hidden, c, w, e_low, coefs, gain1, gain2, rel):
    seqs = ids_row.shape[0]
    per_seq = lambda *shape: pl.BlockSpec((1,) + shape, lambda s: (s,) + (0,) * len(shape))
    still = lambda *shape: pl.BlockSpec(shape, lambda s: (0,) * len(shape))
    return pl.pallas_call(
        gbst_bwd_kernel,
        grid=(seqs,),
        in_specs=[
            per_seq(1, MAXLEN), still(8, D), pl.BlockSpec((TOK, D), lambda s: (s, 0)), per_seq(P_ROWS, D),
            per_seq(8, QN, LANES), per_seq(P_ROWS, D), per_seq(3 * R + 6, QN, LANES),
            still(1, D), still(1, D), still(8, D),
        ],
        out_specs=[per_seq(MAXLEN, D), still(D, SMALL)],
        scratch_shapes=[
            pltpu.VMEM((SMALL, D), f32),
            pltpu.VMEM((P_ROWS + 8, D), f32),
            pltpu.VMEM((LT, T_ROWS, LANES), f32),
            pltpu.VMEM((R, QN + 8, LANES), f32),
            pltpu.VMEM((2 * R + 6, QN, LANES), f32),
            pltpu.VMEM((R, QN, LANES), f32),
            pltpu.VMEM((LT, P_ROWS, LANES), f32),
        ],
        out_shape=[
            jax.ShapeDtypeStruct((seqs, MAXLEN, D), bf16),
            jax.ShapeDtypeStruct((D, SMALL), bf16),
        ],
        compiler_params=pltpu.CompilerParams(vmem_limit_bytes=VMEM_LIMIT),
        cost_estimate=cost(26, 40),
        name="gbst_backward",
    )(ids_row, vecs, d_hidden, c, w, e_low, coefs, gain1, gain2, rel)


HEADS = 12
HD = 64
BUCKETS = 32
SPAN = 1024
HB = 4
WIDE = HB * HD
GROUPS = HEADS // HB
dead_score = -1e9


def nt(a, b):
    return lax.dot_general(a, b, (((1,), (1,)), ((), ())), preferred_element_type=f32)


def nn(a, b):
    return jnp.dot(a, b, preferred_element_type=f32)


def bucket_rows(buckets):
    def row(x):
        return jnp.concatenate([x[TOK - 1 :], x[:1], x[: TOK - 1]])

    return jnp.stack([row(buckets), row(buckets[::-1])])


def bucket_hits(row_ref, way):
    return jnp.where(lax.broadcasted_iota(jnp.int32, (BUCKETS, SPAN), 0) == row_ref[way : way + 1, :], 1.0, 0.0).astype(f32)


def spread_table(rel_ref, row_ref, z_ref, way):
    dims = (((0,), (0,)), ((), ()))
    z_ref[...] = lax.dot_general(
        rel_ref[...].astype(bf16), bucket_hits(row_ref, way).astype(bf16), dims, preferred_element_type=f32)


def build_bias(z_ref, bt_ref, group):
    for h in range(HB):
        row = jnp.broadcast_to(z_ref[pl.ds(group * HB + h, 1), :], (8, SPAN))
        z = pltpu.roll(row, 0, 1, stride=1, stride_axis=0)
        for g in range(TOK // 8):
            bt_ref[h, pl.ds(8 * g, 8), :] = (z if g == 0 else pltpu.roll(z, 8 * g, 1))[:, :TOK]


def pair_lanes(h):
    return slice(h // 2 * LANES, (h // 2 + 1) * LANES)


def own_lanes(h):
    return lax.broadcasted_iota(jnp.int32, (TOK, LANES), 1) // HD == h % 2


def head_parts(k, q, length, h):
    lanes = lax.broadcasted_iota(jnp.int32, (TOK, LANES), 1)
    rows = lax.broadcasted_iota(jnp.int32, (TOK, LANES), 0)
    spare = HD * (1 - h % 2)
    dead = jnp.where(2 * rows < length, 0.0, dead_score)
    kf = jnp.where(own_lanes(h), k[:, pair_lanes(h)].astype(f32), jnp.where(lanes == spare, dead, 0.0)).astype(bf16)
    qf = jnp.where(lanes == spare, 1.0, q[:, pair_lanes(h)].astype(f32)).astype(bf16)
    return kf, qf


def join_heads(parts):
    pairs = [jnp.where(own_lanes(0), parts[h], parts[h + 1]) for h in range(0, HB, 2)]
    return jnp.concatenate(pairs, axis=1).astype(bf16)


def attn_fwd_kernel(len_ref, q_ref, k_ref, v_ref, rel_ref, row_ref, ctx_ref, lse_ref, bias_ref, z_ref):
    length = len_ref[pl.program_id(1)]

    @pl.when((pl.program_id(0) == 0) & (pl.program_id(1) == 0))
    def _():
        spread_table(rel_ref, row_ref, z_ref, 0)

    @pl.when(pl.program_id(1) == 0)
    def _():
        build_bias(z_ref, bias_ref, pl.program_id(0))

    q, k, v = q_ref[...], k_ref[...], v_ref[...]

    def score(h):
        kf, qf = head_parts(k, q, length, h)
        return nt(qf, kf) + bias_ref[h]

    outs = []
    lanes = lax.broadcasted_iota(jnp.int32, (TOK, LANES), 1)
    lse = jnp.zeros((TOK, LANES), f32)
    s = score(0)
    for h in range(HB):
        later = score(h + 1) if h + 1 < HB else None
        top = jnp.max(s, axis=1, keepdims=True)
        p = jnp.exp(s - top)
        total = jnp.sum(p, axis=1, keepdims=True)
        outs.append(nn(p.astype(bf16), v[:, pair_lanes(h)]) * (1.0 / total))
        lse = jnp.where(lanes == h, top + jnp.log(total), lse)
        s = later
    ctx_ref[...] = join_heads(outs)
    lse_ref[0, 0] = lse.T[0:8]


def table_specs():
    return [
        pl.BlockSpec((BUCKETS, LANES), lambda hp, s, n: (0, 0)),
        pl.BlockSpec((2, SPAN), lambda hp, s, n: (0, 0)),
    ]


def attn_forward(lengths, qkv, rel, row):
    seqs = qkv.shape[0] // TOK
    spec = lambda off: pl.BlockSpec((TOK, WIDE), lambda hp, s, n: (s, off + hp))
    return pl.pallas_call(
        attn_fwd_kernel,
        grid_spec=pltpu.PrefetchScalarGridSpec(
            num_scalar_prefetch=1,
            grid=(GROUPS, seqs),
            in_specs=[spec(0), spec(GROUPS), spec(2 * GROUPS)] + table_specs(),
            out_specs=[spec(0), pl.BlockSpec((1, 1, 8, TOK), lambda hp, s, n: (hp, s, 0, 0))],
            scratch_shapes=[pltpu.VMEM((HB, TOK, TOK), f32), pltpu.VMEM((LANES, SPAN), f32)],
        ),
        out_shape=[
            jax.ShapeDtypeStruct((seqs * TOK, D), bf16),
            jax.ShapeDtypeStruct((GROUPS, seqs, 8, TOK), f32),
        ],
        compiler_params=pltpu.CompilerParams(vmem_limit_bytes=VMEM_LIMIT),
        cost_estimate=cost(27, 20),
        name="attn_forward",
    )(lengths, qkv, qkv, qkv, rel, row)


def attn_bwd_kernel(shards, len_ref, q_ref, k_ref, v_ref, do_ref, o_ref, lse_ref, rel_ref, row_ref, dqkv_ref, gt_ref, bt_ref, g_ref, z_ref, gz_ref):
    s_id = pl.program_id(1)
    length = len_ref[s_id]

    @pl.when((pl.program_id(0) == 0) & (s_id == 0))
    def _():
        spread_table(rel_ref, row_ref, z_ref, 1)
        gz_ref[...] = jnp.zeros_like(gz_ref)

    @pl.when(s_id == 0)
    def _():
        build_bias(z_ref, bt_ref, pl.program_id(0))
        g_ref[...] = jnp.zeros_like(g_ref)

    q, k, v, do = q_ref[...], k_ref[...], v_ref[...], do_ref[...]
    kt = k.astype(f32).T.astype(bf16)
    lanes8 = lax.broadcasted_iota(jnp.int32, (8, WIDE), 1)
    rows8 = lax.broadcasted_iota(jnp.int32, (8, WIDE), 0)
    pick = jnp.where(lanes8 // HD == rows8, 1.0, 0.0).astype(bf16)
    prod = do.astype(f32) * o_ref[...].astype(f32)
    upper = prod.astype(bf16)
    delta = nt(pick, upper) + nt(pick, (prod - upper.astype(f32)).astype(bf16))
    dq, dk, dv = [], [], []

    def first(h):
        kf, qf = head_parts(k, q, length, h)
        vf = jnp.where(own_lanes(h), v[:, pair_lanes(h)].astype(f32), 0.0).astype(bf16)
        return nt(kf, qf) + bt_ref[h], nt(vf, do[:, pair_lanes(h)])

    for h in range(HB):
        s, d_prob = first(h)
        p = jnp.exp(s - lse_ref[0, 0, h : h + 1, :])
        ds = p * (d_prob - delta[h : h + 1, :])
        g_ref[h] += ds
        low = ds.astype(bf16)
        dv.append(nn(p.astype(bf16), do[:, pair_lanes(h)]))
        dk.append(nn(low, q[:, pair_lanes(h)]))
        start = h % 2 * HD
        dq.append(nn(kt[pair_lanes(h)], low)[start : start + HD])
    dqkv_ref[0] = jnp.concatenate(dq, axis=0).T.astype(bf16)
    dqkv_ref[1] = join_heads(dk)
    dqkv_ref[2] = join_heads(dv)

    @pl.when(s_id == pl.num_programs(1) - 1)
    def _():
        for h in range(HB):
            total = jnp.zeros((8, SPAN), f32)
            for g in range(LANES // 8):
                tiles = [jnp.zeros((8, LANES), f32) for _ in range(SPAN // LANES)]
                for j in range(TOK // LANES):
                    x = g_ref[h, pl.ds(LANES * j + 8 * g, 8), :]
                    for t in range(TOK // LANES):
                        n = (t - j) % (SPAN // LANES)
                        tiles[n] = tiles[n] + x[:, t * LANES : (t + 1) * LANES]
                piece = jnp.concatenate(tiles, axis=1)
                total = total + (piece if g == 0 else pltpu.roll(piece, SPAN - 8 * g, 1))
            out = total[0:1]
            for s in range(1, 8):
                out = out + pltpu.roll(jnp.broadcast_to(total[s : s + 1], (8, SPAN)), SPAN - s, 1)[0:1]
            gz_ref[pl.ds(pl.program_id(0) * HB + h, 1), :] = out

    @pl.when((pl.program_id(0) == GROUPS - 1) & (s_id == pl.num_programs(1) - 1))
    def _():
        total = lax.dot_general(
            bucket_hits(row_ref, 1), gz_ref[...], (((1,), (1,)), ((), ())),
            precision=lax.Precision.HIGHEST, preferred_element_type=f32)
        gt_ref[...] = jnp.zeros_like(gt_ref)
        per = BUCKETS // shards
        for s in range(shards):
            start = s * (D // shards)
            gt_ref[0:per, start : start + HEADS] = total[s * per : (s + 1) * per, 0:HEADS]


def attn_backward(lengths, qkv, d_ctx, ctx, lse, rel, row, shards):
    seqs = qkv.shape[0] // TOK
    spec = lambda off: pl.BlockSpec((TOK, WIDE), lambda hp, s, n: (s, off + hp))
    return pl.pallas_call(
        lambda *refs: attn_bwd_kernel(shards, *refs),
        grid_spec=pltpu.PrefetchScalarGridSpec(
            num_scalar_prefetch=1,
            grid=(GROUPS, seqs),
            in_specs=[
                spec(0), spec(GROUPS), spec(2 * GROUPS), spec(0), spec(0),
                pl.BlockSpec((1, 1, 8, TOK), lambda hp, s, n: (hp, s, 0, 0)),
            ] + table_specs(),
            out_specs=[
                pl.BlockSpec((3, TOK, WIDE), lambda hp, s, n: (0, s, hp)),
                pl.BlockSpec((8, D), lambda hp, s, n: (0, 0)),
            ],
            scratch_shapes=[
                pltpu.VMEM((HB, TOK, TOK), f32), pltpu.VMEM((HB, TOK, TOK), f32),
                pltpu.VMEM((LANES, SPAN), f32), pltpu.VMEM((16, SPAN), f32),
            ],
        ),
        out_shape=[
            jax.ShapeDtypeStruct((3, seqs * TOK, D), bf16),
            jax.ShapeDtypeStruct((8, D), f32),
        ],
        compiler_params=pltpu.CompilerParams(vmem_limit_bytes=VMEM_LIMIT),
        cost_estimate=cost(46, 30),
        name="attn_backward",
    )(lengths, qkv, qkv, qkv, d_ctx, ctx, lse, rel, row)


FF = 2048
FT = 256
RC = 1024
MT = 512


def rms_scale(x):
    return lax.rsqrt(jnp.sum(x * x, axis=1, keepdims=True) * (1.0 / D) + epsilon)


def post_kernel(len_ref, shift_ref, ctx_ref, w_ref, hidden_ref, vec_ref, *refs):
    pieces, (att_ref, low_ref, low_t_ref, do_ref, do_t_ref) = refs[:-5], refs[-5:]
    s = pl.program_id(0)
    for i, piece in enumerate(pieces):
        @pl.when(shift_ref[s] == i)
        def _():
            do_ref[...] = piece[...]

    live = 2 * lax.broadcasted_iota(jnp.int32, (TOK, D), 0) < len_ref[s]
    d_out = jnp.where(live, do_ref[...].astype(f32), 0.0).astype(bf16)
    do_ref[...] = d_out
    do_t_ref[...] = d_out.T
    att = hidden_ref[...].astype(f32) + nn(ctx_ref[...], out_weights(w_ref))
    att_ref[...] = att.astype(bf16)
    low = (att * rms_scale(att) * vec_ref[6:7, :]).astype(bf16)
    low_ref[...] = low
    low_t_ref[...] = low.T


def rows_spec(width=D):
    return pl.BlockSpec((TOK, width), lambda s, *n: (s, 0))


def whole(*shape):
    return pl.BlockSpec(shape, lambda s, *n: (0,) * len(shape))


def out_block(shards):
    deep = D // shards
    return pl.BlockSpec((shards, 3 * deep, FT), lambda s, *n: (0, 4, 0))


def out_weights(ref):
    deep = ref.shape[1] // 3
    return jnp.concatenate([ref[:, i * deep : (i + 1) * deep, :].reshape(D, FT) for i in range(3)], axis=1)


def post_attention(lengths, shifts, ctx, pack, hidden, vecs, pieces, shards):
    rows = ctx.shape[0]
    cols_spec = pl.BlockSpec((D, TOK), lambda s, *n: (0, s))
    return pl.pallas_call(
        post_kernel,
        grid_spec=pltpu.PrefetchScalarGridSpec(
            num_scalar_prefetch=2,
            grid=(rows // TOK,),
            in_specs=[rows_spec(), out_block(shards), rows_spec(), whole(8, D)] + [whole(TOK, D)] * len(pieces),
            out_specs=[rows_spec(), rows_spec(), cols_spec, rows_spec(), cols_spec],
        ),
        out_shape=[
            jax.ShapeDtypeStruct((rows, D), bf16),
            jax.ShapeDtypeStruct((rows, D), bf16),
            jax.ShapeDtypeStruct((D, rows), bf16),
            jax.ShapeDtypeStruct((rows, D), bf16),
            jax.ShapeDtypeStruct((D, rows), bf16),
        ],
        compiler_params=pltpu.CompilerParams(vmem_limit_bytes=VMEM_LIMIT),
        cost_estimate=cost(10, 30),
        name="post_attention",
    )(lengths, shifts, ctx, pack, hidden, vecs, *pieces)


def gelu_parts(v):
    c = 0.7978845608
    v2 = v * v
    t = jnp.tanh(v * (c + (c * 0.044715) * v2))
    half = 0.5 + 0.5 * t
    gelu = v * half
    slope = half + (0.5 * v) * (1.0 - t * t) * (c + (3.0 * c * 0.044715) * v2)
    return gelu, slope


def ffn_steps(x_any, d_any, xt_any, dt_any, wgu_ref, wo_ref, grad_ref, y_any, dx_any,
              x_ref, d_ref, xt_ref, dt_ref, y_ref, dx_ref, a_ref, dg_ref, du_ref, gu_ref, go_ref, in_sem, out_sem, sems,
              low_ref=None):
    f = pl.program_id(0)
    steps = FF // 2 // FT
    rows_total = x_ref.shape[0]
    chunks = rows_total // RC
    shards, part = gu_ref.shape[1], gu_ref.shape[2]
    owners, deep = go_ref.shape[1], go_ref.shape[2]
    base = steps * part

    def copies(slot, step):
        return (
            pltpu.make_async_copy(
                gu_ref.at[slot], grad_ref.at[:, pl.ds(step * part, part), :], sems.at[0, slot]),
            pltpu.make_async_copy(
                go_ref.at[slot], grad_ref.at[pl.ds(step * owners, owners), pl.ds(base, deep), :], sems.at[1, slot]),
        )

    def row_loads(i):
        rows = pl.ds(i * RC, RC)
        return (
            pltpu.make_async_copy(x_any.at[rows], x_ref.at[rows], in_sem.at[0, i]),
            pltpu.make_async_copy(d_any.at[rows], d_ref.at[rows], in_sem.at[1, i]),
        )

    def turned_loads():
        return (
            pltpu.make_async_copy(xt_any, xt_ref, in_sem.at[2, 0]),
            pltpu.make_async_copy(dt_any, dt_ref, in_sem.at[2, 1]),
        )

    def row_stores(i):
        rows = pl.ds(i * RC, RC)
        return (
            pltpu.make_async_copy(low_ref.at[0, rows], y_any.at[rows], out_sem.at[0, i]),
            pltpu.make_async_copy(low_ref.at[1, rows], dx_any.at[rows], out_sem.at[1, i]),
        )

    @pl.when(f == 0)
    def _():
        for i in range(chunks):
            for copy in row_loads(i):
                copy.start()
        for copy in turned_loads():
            copy.start()

    d_rows = part // 2
    third = deep // 3
    wg = wgu_ref[:, 0:d_rows, :].reshape(D, FT)
    wu = wgu_ref[:, d_rows:part, :].reshape(D, FT)
    wgu = jnp.concatenate([wg, wu], axis=1)
    wo = jnp.concatenate(
        [wo_ref[:, i * third : (i + 1) * third, :].reshape(FT, FT) for i in range(3)], axis=1)

    def chunk(i, carry):
        @pl.when(f == 0)
        def _():
            for copy in row_loads(i):
                copy.wait()

        rows = pl.ds(pl.multiple_of(i * RC, RC), RC)
        x, d = x_ref[rows, :], d_ref[rows, :]
        gelu, slope = gelu_parts(nn(x, wg))
        up = nn(x, wu)
        da = nt(d, wo)
        act = (gelu * up).astype(bf16)
        dg = (da * up * slope).astype(bf16)
        du = (da * gelu).astype(bf16)
        a_ref[rows, :] = act
        dg_ref[rows, :] = dg
        du_ref[rows, :] = du
        y_ref[rows, :] = nn(act, wo) + jnp.where(f == 0, 0.0, y_ref[rows, :])
        dx_ref[rows, :] = nt(jnp.concatenate([dg, du], axis=1), wgu) + jnp.where(
            f == 0, 0.0, dx_ref[rows, :])
        return carry

    lax.fori_loop(0, chunks, chunk, 0)
    if y_any is not None:

        @pl.when(f == steps - 1)
        def _():
            for i in range(chunks):
                rows = pl.ds(i * RC, RC)
                low_ref[0, rows, :] = y_ref[rows, :].astype(bf16)
                low_ref[1, rows, :] = dx_ref[rows, :].astype(bf16)
                for copy in row_stores(i):
                    copy.start()

    slot = lax.rem(f, 2)

    @pl.when(f == 0)
    def _():
        for copy in turned_loads():
            copy.wait()

    @pl.when(f >= 2)
    def _():
        for copy in copies(slot, f - 2):
            copy.wait()

    gu_ref[slot, :, 0:d_rows, :] = nn(xt_ref[...], dg_ref[...]).astype(bf16).reshape(shards, d_rows, FT)
    gu_ref[slot, :, d_rows:part, :] = nn(xt_ref[...], du_ref[...]).astype(bf16).reshape(shards, d_rows, FT)
    go = nn(dt_ref[...], a_ref[...]).T.astype(bf16)
    for i in range(3):
        go_ref[slot, :, i * third : (i + 1) * third, :] = go[:, i * FT : (i + 1) * FT].reshape(owners, third, FT)
    for copy in copies(slot, f):
        copy.start()

    @pl.when(f == steps - 1)
    def _():
        for copy in copies(1 - slot, f - 1) + copies(slot, f):
            copy.wait()
        if y_any is not None:
            for i in range(chunks):
                for copy in row_stores(i):
                    copy.wait()


def first_kernel(x, d, xt, dt, wgu, wo, grad, y, dx, *scratch):
    ffn_steps(x, d, xt, dt, wgu, wo, grad, y, dx, *scratch)


def second_kernel(len_ref, x, d, xt, dt, wgu, wo, att_ref, y1_ref, dx1_ref, do_ref, ctx_ref, w_ref, vec_ref,
                  grad, out_ref, datt_ref, dctx_ref, gw_ref, gg_ref, acc_ref, flat_ref, *scratch):
    f = pl.program_id(0)
    steps = FF // 2 // FT

    @pl.when(f == 0)
    def _():
        acc_ref[...] = jnp.zeros_like(acc_ref)
        gg_ref[...] = jnp.zeros_like(gg_ref)
        flat_ref[...] = out_weights(w_ref)

    @pl.when(f < steps)
    def _():
        ffn_steps(x, d, xt, dt, wgu, wo, grad, None, None, *scratch)

    @pl.when(f >= steps)
    def _():
        tile = f - steps
        y_ref, dx_ref = scratch[4], scratch[5]
        rows = pl.ds(pl.multiple_of(tile * MT, MT), MT)
        per = TOK // MT
        length = len_ref[tile // per]
        place_in = lax.rem(tile, per) * MT + lax.broadcasted_iota(jnp.int32, (MT, 1), 0)
        live = jnp.where(2 * place_in < length, 1.0, 0.0).astype(f32)
        att = att_ref[...].astype(f32)
        out_ref[...] = ((att + y1_ref[...].astype(f32) + y_ref[rows, :]) * live).astype(bf16)
        back, gain_grad = norm_back(att, dx1_ref[...].astype(f32) + dx_ref[rows, :], vec_ref[6:7, :])
        gg_ref[...] += gain_grad
        d_att = do_ref[...].astype(f32) + back
        low = d_att.astype(bf16)
        datt_ref[...] = low
        dctx_ref[...] = nt(low, flat_ref[...]).astype(bf16)
        acc_ref[...] += nn(ctx_ref[...].T, low)

    @pl.when(f == pl.num_programs(0) - 1)
    def _():
        gw_ref[...] = acc_ref[...].astype(bf16)


def ffn_scratch(rows, shards):
    part, hs = 2 * D // shards, FF // 2 // shards
    return [
        pltpu.VMEM((rows, D), bf16),
        pltpu.VMEM((rows, D), bf16),
        pltpu.VMEM((D, rows), bf16),
        pltpu.VMEM((D, rows), bf16),
        pltpu.VMEM((rows, D), f32),
        pltpu.VMEM((rows, D), f32),
        pltpu.VMEM((rows, FT), bf16),
        pltpu.VMEM((rows, FT), bf16),
        pltpu.VMEM((rows, FT), bf16),
        pltpu.VMEM((2, shards, part, FT), bf16),
        pltpu.VMEM((2, FT // hs, 3 * hs, FT), bf16),
        pltpu.SemaphoreType.DMA((3, max(2, rows // RC))),
        pltpu.SemaphoreType.DMA((2, rows // RC)),
        pltpu.SemaphoreType.DMA((2, 2)),
    ]


def ffn_specs(tiles, shards):
    last = lambda f: jnp.minimum(f, tiles - 1)
    part, hs = 2 * D // shards, FF // 2 // shards
    return [pl.BlockSpec(memory_space=pl.ANY)] * 4 + [
        pl.BlockSpec((shards, part, FT), lambda f, *n: (0, last(f), 0)),
        pl.BlockSpec((FT // hs, 3 * hs, FT), lambda f, *n: (last(f), 2, 0)),
    ]


def grad_shape(shards):
    part, hs = 2 * D // shards, FF // 2 // shards
    return jax.ShapeDtypeStruct((shards, FF // 2 // FT * part + 3 * hs, FT), bf16)


def ffn_first(x, d_out, xt, dt, pack, shards):
    rows = x.shape[0]
    tiles = FF // 2 // FT
    anywhere = pl.BlockSpec(memory_space=pl.ANY)
    return pl.pallas_call(
        first_kernel,
        grid=(tiles,),
        in_specs=ffn_specs(tiles, shards),
        out_specs=[anywhere] * 3,
        out_shape=[
            grad_shape(shards),
            jax.ShapeDtypeStruct((rows, D), bf16),
            jax.ShapeDtypeStruct((rows, D), bf16),
        ],
        scratch_shapes=ffn_scratch(rows, shards) + [pltpu.VMEM((2, rows, D), bf16)],
        compiler_params=pltpu.CompilerParams(vmem_limit_bytes=VMEM_LIMIT),
        cost_estimate=cost(36, 40),
        name="ffn_first",
    )(x, d_out, xt, dt, pack, pack)


def ffn_second(lengths, x, d_out, xt, dt, pack, att, y1, dx1, ctx, pack0, vecs, shards):
    rows = x.shape[0]
    tiles = FF // 2 // FT
    tile_rows = pl.BlockSpec((MT, D), lambda f, n: (jnp.maximum(f - tiles, 0), 0))
    return pl.pallas_call(
        second_kernel,
        grid_spec=pltpu.PrefetchScalarGridSpec(
            num_scalar_prefetch=1,
            grid=(tiles + rows // MT,),
            in_specs=ffn_specs(tiles, shards) + [tile_rows] * 5 + [out_block(shards), whole(8, D)],
            out_specs=[pl.BlockSpec(memory_space=pl.ANY), tile_rows, tile_rows, tile_rows, whole(D, D), whole(1, D)],
            scratch_shapes=[
                pltpu.VMEM((D, D), f32), pltpu.VMEM((D, D), bf16),
            ] + ffn_scratch(rows, shards),
        ),
        out_shape=[
            grad_shape(shards),
            jax.ShapeDtypeStruct((rows, D), bf16),
            jax.ShapeDtypeStruct((rows, D), bf16),
            jax.ShapeDtypeStruct((rows, D), bf16),
            jax.ShapeDtypeStruct((D, D), bf16),
            jax.ShapeDtypeStruct((1, D), f32),
        ],
        compiler_params=pltpu.CompilerParams(vmem_limit_bytes=VMEM_LIMIT),
        cost_estimate=cost(46, 60),
        name="ffn_second",
    )(lengths, x, d_out, xt, dt, pack, pack, att, y1, dx1, d_out, ctx, pack0, vecs)


def norm_back(x, grad, gain):
    r = rms_scale(x)
    n = x * r
    u = gain * grad
    mean = jnp.sum(n * u, axis=1, keepdims=True) * (1.0 / D)
    return r * (u - n * mean), jnp.sum(n * grad, axis=0, keepdims=True)


def qkv_grad_kernel(dqkv_ref, normed_t_ref, go_ref, gw_ref):
    i = pl.program_id(0)

    @pl.when(i < 3)
    def _():
        gw_ref[...] = nn(normed_t_ref[...], dqkv_ref[0]).astype(bf16)

    @pl.when(i == 3)
    def _():
        gw_ref[...] = go_ref[...]


def qkv_grad(dqkv, normed_t, g_attn_out):
    rows = normed_t.shape[1]
    return pl.pallas_call(
        qkv_grad_kernel,
        grid=(4,),
        in_specs=[
            pl.BlockSpec((1, rows, D), lambda i: (jnp.minimum(i, 2), 0, 0)),
            whole(D, rows), whole(D, D),
        ],
        out_specs=pl.BlockSpec((D, D), lambda i: (0, i)),
        out_shape=jax.ShapeDtypeStruct((D, 4 * D), bf16),
        compiler_params=pltpu.CompilerParams(vmem_limit_bytes=VMEM_LIMIT),
        cost_estimate=cost(11, 20),
        name="qkv_grad",
    )(dqkv, normed_t, g_attn_out)


def qkv_back_kernel(dqkv_ref, w_ref, hidden_ref, datt_ref, vec_ref, dh_ref, gg_ref):
    @pl.when(pl.program_id(0) == 0)
    def _():
        gg_ref[...] = jnp.zeros_like(gg_ref)

    dn = nt(dqkv_ref[0], w_ref[:, 0:D])
    for i in range(1, 3):
        dn = dn + nt(dqkv_ref[i], w_ref[:, i * D : (i + 1) * D])
    back, gain_grad = norm_back(hidden_ref[...].astype(f32), dn, vec_ref[5:6, :])
    gg_ref[...] += gain_grad
    dh_ref[...] = (datt_ref[...].astype(f32) + back).astype(bf16)


def qkv_backward(dqkv, attn_w, hidden, d_att, vecs):
    rows = hidden.shape[0]
    tile = pl.BlockSpec((TOK, D), lambda s: (s, 0))
    return pl.pallas_call(
        qkv_back_kernel,
        grid=(rows // TOK,),
        in_specs=[
            pl.BlockSpec((3, TOK, D), lambda s: (0, s, 0)),
            pl.BlockSpec((D, 3 * D), lambda s: (0, 0)),
            tile, tile, whole(8, D),
        ],
        out_specs=[tile, whole(1, D)],
        out_shape=[jax.ShapeDtypeStruct((rows, D), bf16), jax.ShapeDtypeStruct((1, D), f32)],
        compiler_params=pltpu.CompilerParams(vmem_limit_bytes=VMEM_LIMIT),
        cost_estimate=cost(14, 40),
        name="qkv_backward",
    )(dqkv, attn_w, hidden, d_att, vecs)


MESH = pl.DeviceIdType.MESH


def greet(peers):
    barrier = pltpu.get_barrier_semaphore()
    for peer in peers:
        pl.semaphore_signal(barrier, inc=1, device_id=peer, device_id_type=MESH)
    pl.semaphore_wait(barrier, len(peers))


def pack_half(out_ref, ffn_in_ref, ffn_out_ref, h, shards):
    hs = FF // 2 // shards
    owners = FT // hs
    deep = ffn_in_ref.shape[0]
    row = 0
    for f in range(FF // 2 // FT):
        for g in range(2):
            starts = [g * FF + (f * owners + o) * 2 * hs + h * hs for o in range(owners)]
            out_ref[row : row + deep, :] = jnp.concatenate([ffn_in_ref[:, a : a + hs] for a in starts], axis=1)
            row += deep
    for i in range(3):
        out_ref[row : row + hs, :] = ffn_out_ref[h * hs : (h + 1) * hs, i * FT : (i + 1) * FT]
        row += hs
    return row


def prepare_kernel(replicas, shards, length_ref, target_ref, embed_ref, conv_ref, score_ref, gain1_ref, gain2_ref, rel_ref,
                   ids_ref, attn_out_ref, ffn_in_ref, ffn_out_ref,
                   table_ref, vec_ref, table_rel_ref, slots_ref, column_ref, row_ref, pack0_ref, pack1_ref,
                   own_ref, wide_ref, turn_ref, nat_ref, wanted_ref, send_sem, recv_sem):
    rep, me = lax.axis_index("rep"), lax.axis_index("shard")
    deep = embed_ref.shape[1]
    seqs = ids_ref.shape[0]
    twin = me + 1 - 2 * lax.rem(me, 2)
    far = [lax.rem(me + 2 * i, shards) for i in range(1, shards // 2)]
    others = [lax.rem(rep + i, replicas) for i in range(1, replicas)]
    greet([(rep, twin)] + [(rep, p) for p in far] + [(p, me) for p in others])

    def send(i, src, dst, device):
        copy = pltpu.make_async_remote_copy(
            src_ref=src, dst_ref=dst, send_sem=send_sem.at[i], recv_sem=recv_sem.at[i],
            device_id=device, device_id_type=MESH)
        copy.start()
        return copy

    wide_ref[...] = jnp.zeros_like(wide_ref)
    wide_ref[0:VOCAB, 0:deep] = embed_ref[...].astype(f32)
    wide_ref[VOCAB : VOCAB + 4, 0:deep] = conv_ref[...].astype(f32)
    for i, ref in enumerate((score_ref, gain1_ref, gain2_ref)):
        wide_ref[VOCAB + 4 + i : VOCAB + 5 + i, 0:deep] = ref[...].astype(f32).reshape(1, deep)
    rel_rows, heads = rel_ref.shape
    wide_ref[VOCAB + 7 : VOCAB + 7 + rel_rows, 0:heads] = rel_ref[...].astype(f32)
    own_ref[...] = wide_ref[...].T[0:deep].astype(bf16)
    near = [send(0, own_ref, table_ref.at[me], (rep, twin))]
    direct = [send(1 + i, own_ref, table_ref.at[me], (rep, p)) for i, p in enumerate(far)]
    lanes = lax.broadcasted_iota(jnp.int32, (8, 128), 1)
    wanted = jnp.zeros((8, 128), jnp.int32)
    for k in range(seqs):
        slot = target_ref[k] % seqs
        wanted = wanted + jnp.where(lanes == target_ref[k] // seqs // shards, slot + 1, 0)
    wanted_ref[...] = wanted
    base = shards
    asks = [send(base + i, wanted_ref, slots_ref.at[rep], (p, me)) for i, p in enumerate(others)]
    table_ref[me] = own_ref[...]
    slots_ref[rep] = wanted_ref[...]
    row = pack_half(pack0_ref, ffn_in_ref, ffn_out_ref, 0, shards)
    for i in range(3):
        pack0_ref[row : row + deep, :] = attn_out_ref[:, i * FT : (i + 1) * FT]
        row += deep
    pack_half(pack1_ref, ffn_in_ref, ffn_out_ref, 1, shards)
    base = base + replicas - 1
    for i, copy in enumerate(direct):
        copy.wait()
        source = lax.rem(me - 2 * (i + 1) + shards, shards)
        near.append(send(base + i, table_ref.at[source], table_ref.at[source], (rep, twin)))
    turn_ref[...] = jnp.full(turn_ref.shape, -1.0, f32)
    place = lax.broadcasted_iota(jnp.int32, (1, MAXLEN), 1)
    for s in range(seqs):
        live = jnp.where(place < length_ref[s], ids_ref[s : s + 1, :], -1)
        row_ref[s] = live
        turn_ref[s : s + 1, 0:MAXLEN] = live.astype(f32)
    nat_ref[...] = turn_ref[...].T
    for r in range(R):
        rows = nat_ref[pl.ds(r, QN, stride=R), :]
        for s in range(seqs):
            column_ref[s, r * QN : (r + 1) * QN, :] = jnp.broadcast_to(rows[:, s : s + 1], (QN, 128))
    for copy in near + asks:
        copy.wait()
    last = table_ref[:, :, SMALL - 128 :].astype(f32).reshape(D, 128).T
    first = VOCAB - (SMALL - 128)
    vec_ref[...] = last[first : first + 8]
    table_rel_ref[...] = jnp.zeros_like(table_rel_ref)
    for s in range(shards):
        block = last[first + 7 : first + 7 + rel_rows, s * deep : s * deep + heads]
        table_rel_ref[s * rel_rows : (s + 1) * rel_rows, 0:heads] = block


def prepare(lengths, target, embed, conv_w, score_w, gain_attn, gain_ffn, rel_table, ids, attn_out, ffn_in, ffn_out,
            replicas, shards):
    deep = embed.shape[1]
    seqs = ids.shape[0]
    part, hs = 2 * D // shards, FF // 2 // shards
    rows = FF // 2 // FT * part + 3 * hs
    sems = shards + replicas - 1 + shards // 2 - 1
    vmem = pl.BlockSpec(memory_space=pltpu.VMEM)
    smem = pl.BlockSpec(memory_space=pltpu.SMEM)
    return pl.pallas_call(
        lambda *refs: prepare_kernel(replicas, shards, *refs),
        out_shape=[
            jax.ShapeDtypeStruct((shards, deep, SMALL), bf16),
            jax.ShapeDtypeStruct((8, D), f32),
            jax.ShapeDtypeStruct((BUCKETS, 128), f32),
            jax.ShapeDtypeStruct((replicas, 8, 128), jnp.int32),
            jax.ShapeDtypeStruct((seqs, P_ROWS, 128), f32),
            jax.ShapeDtypeStruct((seqs, 1, MAXLEN), jnp.int32),
            jax.ShapeDtypeStruct((rows + 3 * deep, FT), bf16),
            jax.ShapeDtypeStruct((rows, FT), bf16),
        ],
        in_specs=[smem] * 2 + [vmem] * 10,
        out_specs=[vmem] * 8,
        scratch_shapes=[
            pltpu.VMEM((deep, SMALL), bf16),
            pltpu.VMEM((SMALL, 128), f32),
            pltpu.VMEM((128, 1152), f32),
            pltpu.VMEM((1152, 128), f32),
            pltpu.VMEM((8, 128), jnp.int32),
            pltpu.SemaphoreType.DMA((sems,)),
            pltpu.SemaphoreType.DMA((sems,)),
        ],
        compiler_params=pltpu.CompilerParams(collective_id=1, has_side_effects=True, vmem_limit_bytes=VMEM_LIMIT),
        cost_estimate=cost(12, 8),
        name="prepare",
    )(lengths, target, embed, conv_w, score_w, gain_attn, gain_ffn, rel_table, ids, attn_out, ffn_in, ffn_out)


def pick_kernel(order_ref, in_ref, *out_refs):
    for i, ref in enumerate(out_refs):
        @pl.when(pl.program_id(0) == i)
        def _():
            ref[...] = in_ref[0]


def pick(order, rows):
    count = order.shape[0]
    block = (rows.shape[1], rows.shape[2])
    return pl.pallas_call(
        pick_kernel,
        grid_spec=pltpu.PrefetchScalarGridSpec(
            num_scalar_prefetch=1,
            grid=(count,),
            in_specs=[pl.BlockSpec((1,) + block, lambda i, order: (order[i], 0, 0))],
            out_specs=[pl.BlockSpec(block, lambda i, order: (0, 0))] * count,
        ),
        out_shape=[jax.ShapeDtypeStruct(block, rows.dtype)] * count,
        compiler_params=pltpu.CompilerParams(vmem_limit_bytes=VMEM_LIMIT),
        cost_estimate=cost(4, 6),
        name="pick",
    )(order, rows)


def finish_kernel(replicas, shards, piece_ref, small_ref, in_ref, attn_ref, embed_ref, conv_ref, rest_ref,
                  twin_ref, both_ref, far_ref, held_ref, other_ref, part_ref, part2_ref, last_ref,
                  twin_send, twin_recv, far_send, far_recv, send_sem, recv_sem, send2_sem, recv2_sem):
    rep, me = lax.axis_index("rep"), lax.axis_index("shard")
    half = piece_ref.shape[1]
    chips = shards // 2
    core = lax.rem(me, 2)
    twin = me + 1 - 2 * core
    bits = [1 << b for b in range(replicas.bit_length() - 1)]
    orders = (bits, bits[::-1])
    far = [lax.rem(me + 2 * i, shards) for i in range(1, chips)]
    partners = {}
    for bit in bits:
        down = lax.rem(rep // bit, 2)
        partners[bit] = (rep + bit - 2 * bit * down, me)
    greet([(rep, twin)] + [(rep, p) for p in far] + [partners[bit] for bit in bits])

    def send(src, dst, sems, i, device):
        copy = pltpu.make_async_remote_copy(
            src_ref=src, dst_ref=dst, send_sem=sems[0].at[i], recv_sem=sems[1].at[i],
            device_id=device, device_id_type=MESH)
        copy.start()
        return copy

    near = [
        send(small_ref.at[2 * z + 1 - core], twin_ref.at[z], (twin_send, twin_recv), z, (rep, twin))
        for z in range(chips)
    ]

    def exchange(t, mine, theirs, sems):
        return [send(mine.at[t, h], theirs.at[t, h], sems, (t, h), partners[orders[h][t]]) for h in range(2)]

    held_ref[0] = piece_ref[...]
    large = exchange(0, held_ref, other_ref, (send_sem, recv_sem))
    for z, copy in enumerate(near):
        copy.wait()
        both_ref[z] = (small_ref[2 * z + core].astype(f32) + twin_ref[z].astype(f32)).astype(bf16)
    away = [send(both_ref.at[p // 2], far_ref.at[i], (far_send, far_recv), i, (rep, p)) for i, p in enumerate(far)]
    last_ref[...] = jnp.zeros_like(last_ref)

    def settle(t, copies, mine, theirs, outs):
        for h, copy in enumerate(copies):
            copy.wait()
            total = mine[t, h].astype(f32) + theirs[t, h].astype(f32)
            if t == len(bits) - 1:
                start = 0
                for out in outs:
                    width = out.shape[1]
                    out[h * half : (h + 1) * half, :] = total[:, start : start + width]
                    start += width
            else:
                mine[t + 1, h] = total.astype(bf16)

    settle(0, large, held_ref, other_ref, (in_ref, attn_ref))
    large = exchange(1, held_ref, other_ref, (send_sem, recv_sem))
    total = both_ref[me // 2].astype(f32)
    for i, copy in enumerate(away):
        copy.wait()
        total = total + far_ref[i].astype(f32)
    part_ref[0] = total.astype(bf16)
    for t in range(len(bits)):
        little = exchange(t, part_ref, part2_ref, (send2_sem, recv2_sem))
        if t > 0:
            settle(t, large, held_ref, other_ref, (in_ref, attn_ref))
            if t < len(bits) - 1:
                large = exchange(t + 1, held_ref, other_ref, (send_sem, recv_sem))
        settle(t, little, part_ref, part2_ref, (last_ref,))
    turned = last_ref[...].T
    deep = embed_ref.shape[1]
    embed_ref[...] = turned[0:VOCAB, 0:deep]
    conv_ref[...] = turned[VROWS : VROWS + 4, 0:deep]
    rest_ref[...] = turned[VROWS : VROWS + 16, 0:deep]


def finish(piece, small, replicas, shards):
    rows, wide = piece.shape
    half = rows // 2
    chips = shards // 2
    steps = replicas.bit_length() - 1
    vmem = pl.BlockSpec(memory_space=pltpu.VMEM)
    sems = lambda *shape: [pltpu.SemaphoreType.DMA(shape), pltpu.SemaphoreType.DMA(shape)]
    return pl.pallas_call(
        lambda *refs: finish_kernel(replicas, shards, *refs),
        out_shape=[
            jax.ShapeDtypeStruct((rows, 3 * D), f32),
            jax.ShapeDtypeStruct((rows, D), f32),
            jax.ShapeDtypeStruct((VOCAB, rows), f32),
            jax.ShapeDtypeStruct((4, rows), f32),
            jax.ShapeDtypeStruct((16, rows), f32),
        ],
        in_specs=[vmem] * 2,
        out_specs=[vmem] * 5,
        scratch_shapes=[
            pltpu.VMEM((chips, 2, half, SMALL), bf16),
            pltpu.VMEM((chips, 2, half, SMALL), bf16),
            pltpu.VMEM((chips - 1, 2, half, SMALL), bf16),
            pltpu.VMEM((steps, 2, half, wide), bf16),
            pltpu.VMEM((steps, 2, half, wide), bf16),
            pltpu.VMEM((steps, 2, half, SMALL), bf16),
            pltpu.VMEM((steps, 2, half, SMALL), bf16),
            pltpu.VMEM((128, SMALL), f32),
        ] + sems(chips) + sems(chips - 1) + sems(steps, 2) + sems(steps, 2),
        compiler_params=pltpu.CompilerParams(
            collective_id=2, has_side_effects=True, vmem_limit_bytes=VMEM_LIMIT),
        cost_estimate=cost(20, 4),
        name="finish_sums",
    )(piece.reshape(2, half, wide), small.reshape(shards, 2, half, SMALL))


def deliver_kernel(in_ref, attn_ref, embed_ref, conv_ref, rest_ref, in_out, attn_out, embed_out, conv_out, score_out, gain1_out, gain2_out, rel_out):
    in_out[...] = in_ref[...]
    attn_out[...] = attn_ref[...]
    embed_out[...] = embed_ref[...]
    conv_out[...] = conv_ref[...]
    for i, ref in enumerate((score_out, gain1_out, gain2_out)):
        ref[...] = rest_ref[4 + i : 5 + i, :].reshape(ref.shape)
    rel_out[...] = rest_ref[7 : 7 + rel_out.shape[0], 0 : rel_out.shape[1]]


def deliver(parts, rel_rows):
    deep = parts[0].shape[0]
    vmem = pl.BlockSpec(memory_space=pltpu.VMEM)
    line = jax.ShapeDtypeStruct((deep,), f32)
    return pl.pallas_call(
        deliver_kernel,
        out_shape=[jax.ShapeDtypeStruct(x.shape, f32) for x in parts[:4]]
        + [line] * 3 + [jax.ShapeDtypeStruct((rel_rows, HEADS), f32)],
        in_specs=[vmem] * 5,
        out_specs=[vmem] * 8,
        compiler_params=pltpu.CompilerParams(vmem_limit_bytes=VMEM_LIMIT),
        cost_estimate=cost(2, 2),
        name="deliver",
    )(*parts)


def unpack_kernel(shards, first_ref, first_other_ref, second_ref, second_other_ref, in_ref, out_ref):
    hs = FF // 2 // shards
    deep = in_ref.shape[0]
    owners = FT // hs
    for h in range(2):
        def load(start, count):
            rows = slice(start, start + count)
            mine, theirs = ((first_ref, first_other_ref), (second_ref, second_other_ref))[h]
            return mine[rows, :].astype(f32) + theirs[rows, :].astype(f32)

        row = 0
        for f in range(FF // 2 // FT):
            for g in range(2):
                x = load(row, deep)
                for o in range(owners):
                    start = g * FF + (f * owners + o) * 2 * hs + h * hs
                    in_ref[:, start : start + hs] = x[:, o * hs : (o + 1) * hs]
                row += deep
        for i in range(3):
            out_ref[h * hs : (h + 1) * hs, i * FT : (i + 1) * FT] = load(row, hs)
            row += hs


def unpack(first, first_other, second, second_other, shards):
    vmem = pl.BlockSpec(memory_space=pltpu.VMEM)
    return pl.pallas_call(
        lambda *refs: unpack_kernel(shards, *refs),
        out_shape=[
            jax.ShapeDtypeStruct((D // shards, 2 * FF), f32),
            jax.ShapeDtypeStruct((FF // shards, D), f32),
        ],
        in_specs=[vmem] * 4,
        out_specs=[vmem] * 2,
        compiler_params=pltpu.CompilerParams(vmem_limit_bytes=VMEM_LIMIT),
        cost_estimate=cost(3, 5),
        name="unpack",
    )(first, first_other, second, second_other)


def send_cotangent(slots, cotangent):
    replicas = lax.axis_size("rep")
    places = jnp.arange(replicas)
    rep = lax.axis_index("rep")
    asked = jnp.where(places[None, :] == rep, slots, 0).sum(axis=1) - 1
    turned = (places[None, :] == (rep + places[:, None]) % replicas) * asked[None, :]
    pieces = list(pick(jnp.maximum(turned.sum(axis=1), 0), cotangent))
    for shift in range(1, replicas):
        pieces[shift] = lax.ppermute(pieces[shift], "rep", [(r, (r + shift) % replicas) for r in range(replicas)])
    return pieces


def swap(x, bit):
    replicas = lax.axis_size("rep")
    return lax.ppermute(x, "rep", [(r, r ^ bit) for r in range(replicas)])


def add_low(a, b):
    return (a.astype(f32) + b.astype(f32)).astype(bf16)


def scatter_sum(grad):
    return lax.psum_scatter(grad, "shard", scatter_dimension=0, tiled=True)


def body(
    byte_ids, lengths, target, rel_bucket, cotangent, embed, conv_w, score_w, gain_attn,
    attn_in, attn_out, gain_ffn, ffn_in, ffn_out, rel_table,
):
    seqs = byte_ids.shape[0]
    replicas, shards = lax.axis_size("rep"), lax.axis_size("shard")
    attn_w = lax.all_gather(attn_in, "shard", axis=0, tiled=True)
    table, vecs, rel, slots, ids_col, ids_row, pack0, pack1 = prepare(
        lengths, target, embed, conv_w, score_w, gain_attn, gain_ffn, rel_table, byte_ids,
        attn_out, ffn_in, ffn_out, replicas, shards,
    )
    packs = [lax.all_gather(pack, "shard", axis=0) for pack in (pack0, pack1)]
    rows = bucket_rows(rel_bucket)

    hidden, normed, normed_t, convolved, weights, e_low, coefs = gbst_forward(lengths, ids_col, table, vecs)
    qkv = jnp.dot(normed, attn_w, preferred_element_type=f32).astype(bf16)
    qkv, slots = lax.optimization_barrier((qkv, slots))
    pieces = send_cotangent(slots[:, 0, :replicas], cotangent)
    ctx, lse = attn_forward(lengths, qkv, rel, rows)
    ctx, pieces = lax.optimization_barrier((ctx, pieces))
    shifts = (lax.axis_index("rep") - target // seqs // shards) % replicas
    attended, low, low_t, d_out, d_out_t = post_attention(
        lengths, shifts, ctx, packs[0], hidden, vecs, pieces, shards
    )
    g_half1, y1, dx1 = ffn_first(low, d_out, low_t, d_out_t, packs[0], shards)
    g_half2, out, d_att, d_ctx, g_attn_out, g_gain_ffn = ffn_second(
        lengths, low, d_out, low_t, d_out_t, packs[1], attended, y1, dx1, ctx, packs[0], vecs, shards
    )
    one, two = [scatter_sum(g.reshape(-1, FT)) for g in (g_half1, g_half2)]
    bits = [1 << b for b in range(replicas.bit_length() - 1)]
    dqkv, g_rel = attn_backward(lengths, qkv, d_ctx, ctx, lse, rel, rows, shards)
    dqkv, one = lax.optimization_barrier((dqkv, one))
    g_attn = qkv_grad(dqkv, normed_t, g_attn_out)
    g_attn, two = lax.optimization_barrier((g_attn, two))
    p_attn = scatter_sum(g_attn)
    turned = bits[1:] + bits[:1]
    others = swap(one, bits[0]), swap(two, turned[0])
    d_hidden, g_gain_attn = qkv_backward(dqkv, attn_w, hidden, d_att, vecs)
    d_hidden, others = lax.optimization_barrier((d_hidden, others))
    one, two = add_low(one, others[0]), add_low(two, others[1])
    for t in range(1, len(bits) - 1):
        one, two = add_low(one, swap(one, bits[t])), add_low(two, swap(two, turned[t]))
    d_hidden, one, two = lax.optimization_barrier((d_hidden, one, two))
    others = swap(one, bits[-1]), swap(two, turned[-1])
    input_grad, small = gbst_backward(
        ids_row, vecs, d_hidden, convolved, weights, e_low, coefs,
        g_gain_attn, g_gain_ffn, g_rel,
    )
    small, others = lax.optimization_barrier((small, others))
    parts = finish(p_attn, small, replicas, shards)
    s_ffn_in, s_ffn_out = unpack(one, others[0], two, others[1], shards)
    s_attn_in, s_attn_out, s_embed, s_conv, s_score, s_gain_attn, s_gain_ffn, s_rel = deliver(parts, rel_table.shape[0])
    return (
        out.reshape(seqs, TOK, D), input_grad, s_embed, s_conv, s_score, s_gain_attn, s_attn_in, s_attn_out,
        s_gain_ffn, s_ffn_in, s_ffn_out, s_rel,
    )


def solution(mesh):
    in_specs = (
        P(("rep", "shard"), None), P(("rep", "shard")), P(("rep", "shard")), P(),
        P(("rep", "shard"), None, None), P(None, "shard"), P(None, "shard"), P("shard"), P("shard"),
        P("shard", None), P("shard", None), P("shard"), P("shard", None), P("shard", None), P("shard", None),
    )
    out_specs = (
        P(("rep", "shard"), None, None), P(("rep", "shard"), None, None), P(None, "shard"), P(None, "shard"),
        P("shard"), P("shard"), P("shard", None), P("shard", None), P("shard"), P("shard", None),
        P("shard", None), P("shard", None),
    )
    return jax.shard_map(body, mesh=mesh, in_specs=in_specs, out_specs=out_specs, check_vma=False)
```
